32 devices in a mesh: rep: 8 (over y, x, core), shard: 4 (over z).
Axes of the slice: x: 2, y: 2, z: 4, core: 2. Of those that a mesh axis runs over, the one named last changes fastest.
Arguments:
- tokens: bfloat16 [4096, 768], P(('rep', 'shard')), may hold values from -6 to 6
- segment_ids: int32 [4096], P(('rep', 'shard')), may hold values from -1 to 4095, as said below
- cotangent: bfloat16 [4096, 768], P(('rep', 'shard')), may hold values from -6 to 6
- params: float32 [7090176], P('shard')
- moment_one: float32 [7090176], P(('shard', 'rep')), may hold values from -1.8 to 1.8
- moment_two: float32 [7090176], P(('shard', 'rep')), may hold values from 0.05 to 1
Outputs:
- output: float32 [4096, 768], P(('rep', 'shard'))
- grad_input: float32 [4096, 768], P(('rep', 'shard'))
- grad_params: float32 [7090176], P('shard')
- new_params: float32 [7090176], P('shard')
- new_moment_one: float32 [7090176], P(('shard', 'rep'))
- new_moment_two: float32 [7090176], P(('shard', 'rep'))
The draws below stay inside these ranges and needn't reach their ends.
Inputs may be any that keep to these rules, and one draw needn't show every extreme that they name: `segment_ids`: on each device's 128 slots the live slots come first and hold whole sequences, each slot marked by the global index of its sequence's first slot; the rest are padding, marked -1. Every device has at least 2/5 of its slots live; the last device is full and its last slot starts a sequence of one slot; the other devices are not full.
All inputs are finite; a program needn't handle non-finite values.
Results may differ from the reference program's by a relative error of at most 0.012.
Values may be sent and summed in bfloat16 or wider, within the bound.
No kernel may reach another device: no remote copies, remote signals or barrier semaphores. Data moves between devices by JAX's collectives and lax.ppermute only.
A program may use at most 192 MiB of HBM per device.

```python
import math
import jax
import jax.numpy as jnp
from jax import lax

D = 768
HEADS = 12
HD = 64
ROT = 16
FF = 3072
TOK_DEV = 128
DEVS = 32
TOKENS = 4096
RAW = 7087872
PARAMS = 7090176


def draw_segment_ids(key, part):
    key_perm, key_cut = jax.random.split(jax.random.fold_in(key, 11))
    others = jax.random.permutation(key_perm, DEVS - 1).astype(jnp.int32) + 1
    device_order = jnp.concatenate([others, jnp.zeros((1,), jnp.int32)])
    short_by = device_order * (3 * TOK_DEV // 5) // DEVS
    short_by = jnp.where(device_order > 0, jnp.maximum(short_by, 1), 0)
    live_slots = TOK_DEV - short_by
    slot_ids = jnp.arange(TOK_DEV, dtype=jnp.int32)[None, :]
    mean_length = max(TOK_DEV // 4, 2)
    global_ids = jnp.arange(DEVS, dtype=jnp.int32)[:, None] * TOK_DEV + slot_ids
    begins = (jax.random.randint(key_cut, (DEVS, TOK_DEV), 0, mean_length) == 0) | (slot_ids == 0) | (global_ids == DEVS * TOK_DEV - 1)
    marked = jnp.where(begins, global_ids, 0)
    starts = lax.cummax(marked, axis=1)
    segments = jnp.where(slot_ids < live_slots[:, None], starts, -1)
    return segments.reshape(DEVS * TOK_DEV).astype(jnp.int32)


def draw_params(key, part):
    q_width = HEADS * HD
    o_wqkv = 2 * D
    o_bqkv = o_wqkv + 3 * q_width * D
    o_wout = o_bqkv + 3 * q_width
    o_bout = o_wout + q_width * D
    o_gain2 = o_bout + D
    o_shift2 = o_gain2 + D
    o_win = o_shift2 + D
    o_bin = o_win + D * FF
    o_wout2 = o_bin + FF
    o_bout2 = o_wout2 + FF * D
    o_end = o_bout2 + D
    flat_index = jnp.arange(PARAMS, dtype=jnp.int32)
    base = jax.random.normal(jax.random.fold_in(key, 5), (PARAMS,), jnp.float32)
    in_gain = (flat_index < D) | (flat_index >= o_gain2) & (flat_index < o_shift2)
    in_shift = (flat_index >= D) & (flat_index < o_wqkv) | (flat_index >= o_shift2) & (flat_index < o_win)
    in_wqkv = (flat_index >= o_wqkv) & (flat_index < o_bqkv)
    in_bqkv = (flat_index >= o_bqkv) & (flat_index < o_wout)
    in_wout = (flat_index >= o_wout) & (flat_index < o_bout)
    in_bout = (flat_index >= o_bout) & (flat_index < o_gain2)
    in_win = (flat_index >= o_win) & (flat_index < o_bin)
    in_bin = (flat_index >= o_bin) & (flat_index < o_wout2)
    in_wout2 = (flat_index >= o_wout2) & (flat_index < o_bout2)
    in_bout2 = (flat_index >= o_bout2) & (flat_index < o_end)
    values = 0.02 * base
    values = jnp.where(in_gain, 1.0 + 0.1 * base, values)
    values = jnp.where(in_shift | in_bqkv | in_bout | in_bin | in_bout2, 0.2 * base, values)
    values = jnp.where(in_wqkv | in_win, base * D ** (-0.5), values)
    values = jnp.where(in_wout, base * 4.0 * q_width ** (-0.5), values)
    values = jnp.where(in_wout2, base * FF ** (-0.5), values)
    return values.astype(jnp.float32)


def levels(rng, shape, cuts, low, largest):
    level, own = 1.0, jax.random.fold_in(rng, 6)
    for axis_at, blocks in cuts:
        steps = jnp.exp(jax.random.uniform(jax.random.fold_in(own, axis_at), (blocks,), jnp.float32, low / len(cuts), largest / len(cuts)))
        level = level * jnp.repeat(steps, shape[axis_at] // blocks).reshape([-1 if axis == axis_at else 1 for axis in range(len(shape))])
    return level


def normal_values(own_key, dims, spread, reach, shards=(), kind=jnp.bfloat16):
    entries = spread * jax.random.normal(own_key, dims, jnp.float32)
    if shards:
        entries = entries * levels(own_key, dims, shards, -0.22, 0.18)
    return jnp.clip(entries, -reach, reach).astype(kind)


def setup_inputs(seed: int = 0) -> dict:
    seeds = jax.random.split(jax.random.key(seed), 7)
    return {
        "tokens": normal_values(seeds[0], (TOKENS, D), 1.0, 6.0, ((0, 32),)),
        "segment_ids": draw_segment_ids(jax.random.fold_in(seeds[6], 71), 0),
        "cotangent": normal_values(seeds[2], (TOKENS, D), 1.0, 6.0, ((0, 32),)),
        "params": draw_params(jax.random.fold_in(seeds[6], 71), 0),
        "moment_one": normal_values(seeds[4], (PARAMS,), 0.3, 1.8, ((0, 32),), jnp.float32),
        "moment_two": jnp.clip(jnp.exp(math.log(1.0) - 2.9957323 * jax.random.uniform(seeds[5], (PARAMS,), jnp.float32) ** levels(seeds[5], (PARAMS,), ((0, 32),), -0.2, 0.2)), 0.05, 1.0),
    }


EPS_NORM = 1e-05
ROPE_BASE = 10000.0
NEG_BIG = -1e+30
BETA_ONE = 0.9
BETA_TWO = 0.95
ADAM_STEP = 3.0
LEARN_RATE = 0.05
DECAY = 0.01
ADAM_EPS = 1e-08
INV_ROOT_TWO = 0.7071067811865476
INV_ROOT_TWO_PI = 0.3989422804014327

def layout_offsets():
    q_width = HEADS * HD
    o_wqkv = 2 * D
    o_bqkv = o_wqkv + 3 * q_width * D
    o_wout = o_bqkv + 3 * q_width
    o_bout = o_wout + q_width * D
    o_gain2 = o_bout + D
    o_shift2 = o_gain2 + D
    o_win = o_shift2 + D
    o_bin = o_win + D * FF
    o_wout2 = o_bin + FF
    o_bout2 = o_wout2 + FF * D
    return (o_wqkv, o_bqkv, o_wout, o_bout, o_gain2, o_shift2, o_win, o_bin, o_wout2, o_bout2, o_bout2 + D)

def split_params(flat16):
    q_width = HEADS * HD
    o_wqkv, o_bqkv, o_wout, o_bout, o_gain2, o_shift2, o_win, o_bin, o_wout2, o_bout2, o_end = layout_offsets()
    return (flat16[0:D], flat16[D:o_wqkv], flat16[o_wqkv:o_bqkv].reshape(D, 3 * q_width), flat16[o_bqkv:o_wout], flat16[o_wout:o_bout].reshape(q_width, D), flat16[o_bout:o_gain2], flat16[o_gain2:o_shift2], flat16[o_shift2:o_win], flat16[o_win:o_bin].reshape(D, FF), flat16[o_bin:o_wout2], flat16[o_wout2:o_bout2].reshape(FF, D), flat16[o_bout2:o_end])

def positions_of(segments):
    count = segments.shape[0]
    slot_ids = jnp.arange(count, dtype=jnp.int32)
    before = jnp.concatenate([jnp.full((1,), -2, jnp.int32), segments[:-1].astype(jnp.int32)])
    begins = segments.astype(jnp.int32) != before
    first_slot = lax.cummax(jnp.where(begins, slot_ids, 0), axis=0)
    return slot_ids - first_slot

def rotary_tables(positions):
    half = ROT // 2
    steps_j = jnp.arange(half, dtype=jnp.float32)
    freqs = jnp.power(jnp.float32(ROPE_BASE), -2.0 * steps_j / ROT)
    angle = positions.astype(jnp.float32)[:, None] * freqs[None, :]
    return (jnp.cos(angle)[:, None, :], jnp.sin(angle)[:, None, :])

def rotate(values, cosine, sine, sign):
    half = cosine.shape[-1]
    lower = values[..., :half]
    upper = values[..., half:2 * half]
    rest = values[..., 2 * half:]
    return jnp.concatenate([lower * cosine - sign * upper * sine, upper * cosine + sign * lower * sine, rest], axis=-1)

def gelu_exact(value):
    return value * 0.5 * (1.0 + lax.erf(value * INV_ROOT_TWO))

def gelu_slope(value):
    return 0.5 * (1.0 + lax.erf(value * INV_ROOT_TWO)) + value * jnp.exp(-0.5 * value * value) * INV_ROOT_TWO_PI

def masked_scores(q_blk, keys, seg_rows, seg_cols, begin_row):
    scale = q_blk.shape[-1] ** (-0.5)
    raw_scores = jnp.einsum('qhd,khd->hqk', q_blk, keys, preferred_element_type=jnp.float32) * scale
    row_ids = begin_row + jnp.arange(q_blk.shape[0], dtype=jnp.int32)
    col_ids = jnp.arange(keys.shape[0], dtype=jnp.int32)
    allowed = (seg_rows[:, None] == seg_cols[None, :]) & (col_ids[None, :] <= row_ids[:, None])
    return jnp.where(allowed[None], raw_scores, NEG_BIG)

def attend_forward(query16, key16, value16, segments):
    count = query16.shape[0]
    block = min(512, count)
    pieces_out = []
    lse_list = []
    for begin_row in range(0, count, block):
        stop_row = begin_row + block
        scores = masked_scores(query16[begin_row:stop_row], key16[:stop_row], segments[begin_row:stop_row], segments[:stop_row], begin_row)
        row_max = lax.optimization_barrier(jnp.max(scores, axis=-1, keepdims=True))
        expd = jnp.exp(scores - row_max)
        row_total = lax.optimization_barrier(jnp.sum(expd, axis=-1, keepdims=True))
        probs16 = (expd / row_total).astype(jnp.bfloat16)
        attn_blk = jnp.einsum('hqk,khd->qhd', probs16, value16[:stop_row], preferred_element_type=jnp.float32)
        pieces_out.append(attn_blk.astype(jnp.bfloat16))
        lse_list.append(row_max + jnp.log(row_total))
    return (jnp.concatenate(pieces_out, axis=0), lse_list)

def attend_backward(query16, key16, value16, attn16, lse_list, segments, grad_attn16):
    count = query16.shape[0]
    block = min(512, count)
    scale = query16.shape[-1] ** (-0.5)
    grad_query = []
    grad_key = jnp.zeros(key16.shape, jnp.float32)
    grad_value = jnp.zeros(value16.shape, jnp.float32)
    for turn, begin_row in enumerate(range(0, count, block)):
        stop_row = begin_row + block
        scores = masked_scores(query16[begin_row:stop_row], key16[:stop_row], segments[begin_row:stop_row], segments[:stop_row], begin_row)
        chances = jnp.exp(scores - lse_list[turn])
        chances16 = chances.astype(jnp.bfloat16)
        grad_out_blk = grad_attn16[begin_row:stop_row]
        grad_value = grad_value.at[:stop_row].add(jnp.einsum('hqk,qhd->khd', chances16, grad_out_blk, preferred_element_type=jnp.float32))
        grad_chance = jnp.einsum('qhd,khd->hqk', grad_out_blk, value16[:stop_row], preferred_element_type=jnp.float32)
        delta = lax.optimization_barrier(jnp.sum(grad_out_blk.astype(jnp.float32) * attn16[begin_row:stop_row].astype(jnp.float32), axis=-1))
        grad_scores = (chances * (grad_chance - jnp.transpose(delta)[:, :, None]) * scale).astype(jnp.bfloat16)
        grad_query.append(jnp.einsum('hqk,khd->qhd', grad_scores, key16[:stop_row], preferred_element_type=jnp.float32))
        grad_key = grad_key.at[:stop_row].add(jnp.einsum('hqk,qhd->khd', grad_scores, query16[begin_row:stop_row], preferred_element_type=jnp.float32))
    return (jnp.concatenate(grad_query, axis=0), grad_key, grad_value)

def norm_back(grad_act, normed, inv_std, gain):
    grad_gain = lax.optimization_barrier(jnp.sum(grad_act * normed, axis=0))
    grad_shift = lax.optimization_barrier(jnp.sum(grad_act, axis=0))
    grad_norm = grad_act * gain.astype(jnp.float32)
    grad_x = inv_std * (grad_norm - lax.optimization_barrier(jnp.mean(grad_norm, axis=1, keepdims=True)) - normed * lax.optimization_barrier(jnp.mean(grad_norm * normed, axis=1, keepdims=True)))
    return (grad_gain, grad_shift, grad_x)

def layer_forward(tokens, segments, pieces):
    gain_one, shift_one, w_qkv, b_qkv, w_out, b_out, gain_two, shift_two, w_in, b_in, w_out2, b_out2 = pieces
    count = tokens.shape[0]
    x_wide = tokens.astype(jnp.float32)
    row_mean = lax.optimization_barrier(jnp.mean(x_wide, axis=1, keepdims=True))
    centered = x_wide - row_mean
    variance = lax.optimization_barrier(jnp.mean(centered * centered, axis=1, keepdims=True))
    inv_std = lax.rsqrt(variance + EPS_NORM)
    normed = centered * inv_std
    act_one = (normed * gain_one.astype(jnp.float32) + shift_one.astype(jnp.float32)).astype(jnp.bfloat16)
    act_two = (normed * gain_two.astype(jnp.float32) + shift_two.astype(jnp.float32)).astype(jnp.bfloat16)
    mixed = jnp.dot(act_one, w_qkv, preferred_element_type=jnp.float32) + b_qkv.astype(jnp.float32)
    mixed = mixed.reshape(count, 3, HEADS, HD)
    cosine, sine = rotary_tables(positions_of(segments))
    query16 = rotate(mixed[:, 0], cosine, sine, 1.0).astype(jnp.bfloat16)
    key16 = rotate(mixed[:, 1], cosine, sine, 1.0).astype(jnp.bfloat16)
    value16 = mixed[:, 2].astype(jnp.bfloat16)
    attn16, lse_list = attend_forward(query16, key16, value16, segments)
    proj = jnp.dot(attn16.reshape(count, HEADS * HD), w_out, preferred_element_type=jnp.float32) + b_out.astype(jnp.float32)
    pre = jnp.dot(act_two, w_in, preferred_element_type=jnp.float32) + b_in.astype(jnp.float32)
    hidden16 = gelu_exact(pre).astype(jnp.bfloat16)
    feed = jnp.dot(hidden16, w_out2, preferred_element_type=jnp.float32) + b_out2.astype(jnp.float32)
    output = x_wide + proj + feed
    saved = (normed, inv_std, act_one, act_two, query16, key16, value16, attn16, lse_list, cosine, sine, pre, hidden16)
    return (output, saved)

def layer_backward(cotangent, segments, pieces, saved):
    gain_one, shift_one, w_qkv, b_qkv, w_out, b_out, gain_two, shift_two, w_in, b_in, w_out2, b_out2 = pieces
    normed, inv_std, act_one, act_two, query16, key16, value16, attn16, lse_list, cosine, sine, pre, hidden16 = saved
    count = cotangent.shape[0]
    contract_rows = (((0,), (0,)), ((), ()))
    contract_cols = (((1,), (1,)), ((), ()))
    live_rows = (segments >= 0).astype(jnp.float32)[:, None]
    grad_y = cotangent.astype(jnp.float32) * live_rows
    grad_y16 = grad_y.astype(jnp.bfloat16)
    grad_b_out = lax.optimization_barrier(jnp.sum(grad_y, axis=0))
    attn_flat = attn16.reshape(count, HEADS * HD)
    grad_w_out = lax.dot_general(attn_flat, grad_y16, contract_rows, preferred_element_type=jnp.float32)
    grad_w_out2 = lax.dot_general(hidden16, grad_y16, contract_rows, preferred_element_type=jnp.float32)
    grad_hidden = lax.dot_general(grad_y16, w_out2, contract_cols, preferred_element_type=jnp.float32)
    grad_pre = grad_hidden * gelu_slope(pre)
    grad_b_in = lax.optimization_barrier(jnp.sum(grad_pre, axis=0))
    grad_pre16 = grad_pre.astype(jnp.bfloat16)
    grad_w_in = lax.dot_general(act_two, grad_pre16, contract_rows, preferred_element_type=jnp.float32)
    grad_act_two = lax.dot_general(grad_pre16, w_in, contract_cols, preferred_element_type=jnp.float32)
    grad_attn16 = lax.dot_general(grad_y16, w_out, contract_cols, preferred_element_type=jnp.float32).astype(jnp.bfloat16).reshape(count, HEADS, HD)
    grad_query, grad_key, grad_value = attend_backward(query16, key16, value16, attn16, lse_list, segments, grad_attn16)
    grad_query = rotate(grad_query, cosine, sine, -1.0)
    grad_key = rotate(grad_key, cosine, sine, -1.0)
    grad_mixed = jnp.stack([grad_query, grad_key, grad_value], axis=1).reshape(count, 3 * HEADS * HD)
    grad_b_qkv = lax.optimization_barrier(jnp.sum(grad_mixed, axis=0))
    grad_mixed16 = grad_mixed.astype(jnp.bfloat16)
    grad_w_qkv = lax.dot_general(act_one, grad_mixed16, contract_rows, preferred_element_type=jnp.float32)
    grad_act_one = lax.dot_general(grad_mixed16, w_qkv, contract_cols, preferred_element_type=jnp.float32)
    gain_grad_one, shift_grad_one, grad_x_one = norm_back(grad_act_one, normed, inv_std, gain_one)
    gain_grad_two, shift_grad_two, grad_x_two = norm_back(grad_act_two, normed, inv_std, gain_two)
    grad_in = grad_y + grad_x_one + grad_x_two
    flat_parts = [gain_grad_one, shift_grad_one, grad_w_qkv.reshape(-1), grad_b_qkv, grad_w_out.reshape(-1), grad_b_out, gain_grad_two, shift_grad_two, grad_w_in.reshape(-1), grad_b_in, grad_w_out2.reshape(-1), grad_b_out]
    return (grad_in, [part.astype(jnp.bfloat16) for part in flat_parts])

def adam_update(weights, first_moment, second_moment, gradient):
    new_first = BETA_ONE * first_moment + (1.0 - BETA_ONE) * gradient
    new_second = BETA_TWO * second_moment + (1.0 - BETA_TWO) * gradient * gradient
    unbiased_first = new_first / (1.0 - BETA_ONE ** ADAM_STEP)
    unbiased_second = new_second / (1.0 - BETA_TWO ** ADAM_STEP)
    new_weights = weights - LEARN_RATE * (unbiased_first / (jnp.sqrt(unbiased_second) + ADAM_EPS) + DECAY * weights)
    return (new_weights, new_first, new_second)

def reference(tokens, segment_ids, cotangent, params, moment_one, moment_two):
    pieces = split_params(params.astype(jnp.bfloat16))
    token_blocks = tokens.reshape(DEVS, TOK_DEV, D)
    seg_blocks = segment_ids.reshape(DEVS, TOK_DEV)
    cot_blocks = cotangent.reshape(DEVS, TOK_DEV, D)

    def one_device(running, inputs):
        tok_blk, seg_blk, cot_blk = inputs
        out_blk, saved = layer_forward(tok_blk, seg_blk, pieces)
        grad_blk, flat_parts = layer_backward(cot_blk, seg_blk, pieces, saved)
        return (running + jnp.concatenate(flat_parts).astype(jnp.float32), (out_blk, grad_blk))
    running, (out_all, grad_all) = lax.scan(one_device, jnp.zeros((RAW,), jnp.float32), (token_blocks, seg_blocks, cot_blocks))
    total = jnp.concatenate([running, jnp.zeros((PARAMS - RAW,), jnp.float32)])
    grad_params = total * (1.0 / math.sqrt(TOKENS))
    new_params, new_first, new_second = adam_update(params, moment_one, moment_two, grad_params)
    return (out_all.reshape(TOKENS, D), grad_all.reshape(TOKENS, D), grad_params, new_params, new_first, new_second)
```

```python
import functools
import math

import jax
import jax.numpy as jnp
from jax import lax
from jax.experimental import pallas as pl
from jax.experimental.pallas import tpu as pltpu
from jax.sharding import PartitionSpec as P

D = 768
HEADS = 12
HD = 64
ROT = 16
FF = 3072


EPS_NORM = 1e-05
ROPE_BASE = 10000.0
NEG_BIG = -1e30
BETA_ONE = 0.9
BETA_TWO = 0.95
ADAM_STEP = 3.0
LEARN_RATE = 0.05
DECAY = 0.01
ADAM_EPS = 1e-08
INV_ROOT_TWO = 0.7071067811865476
INV_ROOT_TWO_PI = 0.3989422804014327


def layout_offsets():
    q_width = HEADS * HD
    o_wqkv = 2 * D
    o_bqkv = o_wqkv + 3 * q_width * D
    o_wout = o_bqkv + 3 * q_width
    o_bout = o_wout + q_width * D
    o_gain2 = o_bout + D
    o_shift2 = o_gain2 + D
    o_win = o_shift2 + D
    o_bin = o_win + D * FF
    o_wout2 = o_bin + FF
    o_bout2 = o_wout2 + FF * D
    return (
        o_wqkv,
        o_bqkv,
        o_wout,
        o_bout,
        o_gain2,
        o_shift2,
        o_win,
        o_bin,
        o_wout2,
        o_bout2,
        o_bout2 + D,
    )


def split_params(flat16):
    q_width = HEADS * HD
    o_wqkv, o_bqkv, o_wout, o_bout, o_gain2, o_shift2, o_win, o_bin, o_wout2, o_bout2, o_end = (
        layout_offsets()
    )
    return (
        flat16[0:D],
        flat16[D:o_wqkv],
        flat16[o_wqkv:o_bqkv].reshape(D, 3 * q_width),
        flat16[o_bqkv:o_wout],
        flat16[o_wout:o_bout].reshape(q_width, D),
        flat16[o_bout:o_gain2],
        flat16[o_gain2:o_shift2],
        flat16[o_shift2:o_win],
        flat16[o_win:o_bin].reshape(D, FF),
        flat16[o_bin:o_wout2],
        flat16[o_wout2:o_bout2].reshape(FF, D),
        flat16[o_bout2:o_end],
    )


def positions_of(segments):
    count = segments.shape[0]
    slot_ids = jnp.arange(count, dtype=jnp.int32)
    before = jnp.concatenate([jnp.full((1,), -2, jnp.int32), segments[:-1]])
    begins = segments != before
    first_slot = lax.cummax(jnp.where(begins, slot_ids, 0), axis=0)
    return slot_ids - first_slot


def rotary_tables(positions):
    half = ROT // 2
    steps_j = jnp.arange(half, dtype=jnp.float32)
    freqs = jnp.power(jnp.float32(ROPE_BASE), -2.0 * steps_j / ROT)
    angle = positions.astype(jnp.float32)[:, None] * freqs[None, :]
    return (jnp.cos(angle)[:, None, :], jnp.sin(angle)[:, None, :])


def rotate(values, cosine, sine, sign):
    half = cosine.shape[-1]
    lower = values[..., :half]
    upper = values[..., half : 2 * half]
    rest = values[..., 2 * half :]
    return jnp.concatenate(
        [lower * cosine - sign * upper * sine, upper * cosine + sign * lower * sine, rest], axis=-1
    )


def gelu_exact(value):
    return value * 0.5 * (1.0 + lax.erf(value * INV_ROOT_TWO))


def gelu_slope(value):
    return (
        0.5 * (1.0 + lax.erf(value * INV_ROOT_TWO))
        + value * jnp.exp(-0.5 * value * value) * INV_ROOT_TWO_PI
    )


def masked_scores(q_blk, keys, seg_rows, seg_cols, begin_row):
    scale = q_blk.shape[-1] ** (-0.5)
    raw_scores = jnp.einsum("qhd,khd->hqk", q_blk, keys, preferred_element_type=jnp.float32) * scale
    row_ids = begin_row + jnp.arange(q_blk.shape[0], dtype=jnp.int32)
    col_ids = jnp.arange(keys.shape[0], dtype=jnp.int32)
    allowed = (seg_rows[:, None] == seg_cols[None, :]) & (col_ids[None, :] <= row_ids[:, None])
    return jnp.where(allowed[None], raw_scores, NEG_BIG)


def attend_forward(query16, key16, value16, segments):
    scores = masked_scores(query16, key16, segments, segments, 0)
    row_max = jnp.max(scores, axis=-1, keepdims=True)
    expd = jnp.exp(scores - row_max)
    row_total = jnp.sum(expd, axis=-1, keepdims=True)
    probs16 = (expd / row_total).astype(jnp.bfloat16)
    attn_blk = jnp.einsum("hqk,khd->qhd", probs16, value16, preferred_element_type=jnp.float32)
    pieces_out = attn_blk.astype(jnp.bfloat16)
    lse_list = [row_max + jnp.log(row_total)]
    return (pieces_out, lse_list)


def attend_backward(query16, key16, value16, attn16, lse_list, segments, grad_attn16):
    count = query16.shape[0]
    block = min(512, count)
    scale = query16.shape[-1] ** (-0.5)
    grad_query = []
    grad_key = jnp.zeros(key16.shape, jnp.float32)
    grad_value = jnp.zeros(value16.shape, jnp.float32)
    for turn, begin_row in enumerate(range(0, count, block)):
        stop_row = begin_row + block
        scores = masked_scores(query16, key16, segments, segments, begin_row)
        chances = jnp.exp(scores - lse_list[turn])
        chances16 = chances.astype(jnp.bfloat16)
        grad_value = grad_value.at[:stop_row].add(
            jnp.einsum("hqk,qhd->khd", chances16, grad_attn16, preferred_element_type=jnp.float32)
        )
        grad_chance = jnp.einsum(
            "qhd,khd->hqk", grad_attn16, value16, preferred_element_type=jnp.float32
        )
        delta = jnp.sum(grad_attn16.astype(jnp.float32) * attn16.astype(jnp.float32), axis=-1)
        grad_scores = (chances * (grad_chance - jnp.transpose(delta)[:, :, None]) * scale).astype(
            jnp.bfloat16
        )
        grad_query.append(
            jnp.einsum("hqk,khd->qhd", grad_scores, key16, preferred_element_type=jnp.float32)
        )
        grad_key = grad_key.at[:stop_row].add(
            jnp.einsum("hqk,qhd->khd", grad_scores, query16, preferred_element_type=jnp.float32)
        )
    return (grad_query[0], grad_key, grad_value)


def norm_back(grad_act, normed, inv_std, gain):
    grad_gain = jnp.sum(grad_act * normed, axis=0)
    grad_shift = jnp.sum(grad_act, axis=0)
    grad_norm = grad_act * gain.astype(jnp.float32)
    grad_x = inv_std * (
        grad_norm
        - jnp.mean(grad_norm, axis=1, keepdims=True)
        - normed * jnp.mean(grad_norm * normed, axis=1, keepdims=True)
    )
    return (grad_gain, grad_shift, grad_x)


def layer_forward(tokens, segments, pieces):
    (
        gain_one,
        shift_one,
        w_qkv,
        b_qkv,
        w_out,
        b_out,
        gain_two,
        shift_two,
        w_in,
        b_in,
        w_out2,
        b_out2,
    ) = pieces
    count = tokens.shape[0]
    x_wide = tokens.astype(jnp.float32)
    row_mean = jnp.mean(x_wide, axis=1, keepdims=True)
    centered = x_wide - row_mean
    variance = jnp.mean(centered * centered, axis=1, keepdims=True)
    inv_std = lax.rsqrt(variance + EPS_NORM)
    normed = centered * inv_std
    act_one = (normed * gain_one.astype(jnp.float32) + shift_one.astype(jnp.float32)).astype(
        jnp.bfloat16
    )
    act_two = (normed * gain_two.astype(jnp.float32) + shift_two.astype(jnp.float32)).astype(
        jnp.bfloat16
    )
    mixed = jnp.dot(act_one, w_qkv, preferred_element_type=jnp.float32) + b_qkv.astype(jnp.float32)
    mixed = mixed.reshape(count, 3, HEADS, HD)
    cosine, sine = rotary_tables(positions_of(segments))
    query16 = rotate(mixed[:, 0], cosine, sine, 1.0).astype(jnp.bfloat16)
    key16 = rotate(mixed[:, 1], cosine, sine, 1.0).astype(jnp.bfloat16)
    value16 = mixed[:, 2].astype(jnp.bfloat16)
    attn16, lse_list = attend_forward(query16, key16, value16, segments)
    proj = jnp.dot(
        attn16.reshape(count, HEADS * HD), w_out, preferred_element_type=jnp.float32
    ) + b_out.astype(jnp.float32)
    pre = jnp.dot(act_two, w_in, preferred_element_type=jnp.float32) + b_in.astype(jnp.float32)
    hidden16 = gelu_exact(pre).astype(jnp.bfloat16)
    feed = jnp.dot(hidden16, w_out2, preferred_element_type=jnp.float32) + b_out2.astype(
        jnp.float32
    )
    output = x_wide + proj + feed
    saved = (
        normed,
        inv_std,
        act_one,
        act_two,
        query16,
        key16,
        value16,
        attn16,
        lse_list,
        cosine,
        sine,
        pre,
        hidden16,
    )
    return (output, saved)


def layer_backward(cotangent, segments, pieces, saved):
    (
        gain_one,
        shift_one,
        w_qkv,
        b_qkv,
        w_out,
        b_out,
        gain_two,
        shift_two,
        w_in,
        b_in,
        w_out2,
        b_out2,
    ) = pieces
    (
        normed,
        inv_std,
        act_one,
        act_two,
        query16,
        key16,
        value16,
        attn16,
        lse_list,
        cosine,
        sine,
        pre,
        hidden16,
    ) = saved
    count = cotangent.shape[0]
    contract_rows = (((0,), (0,)), ((), ()))
    contract_cols = (((1,), (1,)), ((), ()))
    live_rows = (segments >= 0).astype(jnp.float32)[:, None]
    grad_y = cotangent.astype(jnp.float32) * live_rows
    grad_y16 = grad_y.astype(jnp.bfloat16)
    grad_b_out = jnp.sum(grad_y, axis=0)
    attn_flat = attn16.reshape(count, HEADS * HD)
    grad_w_out = lax.dot_general(
        attn_flat, grad_y16, contract_rows, preferred_element_type=jnp.float32
    )
    grad_w_out2 = lax.dot_general(
        hidden16, grad_y16, contract_rows, preferred_element_type=jnp.float32
    )
    grad_hidden = lax.dot_general(
        grad_y16, w_out2, contract_cols, preferred_element_type=jnp.float32
    )
    grad_pre = grad_hidden * gelu_slope(pre)
    grad_b_in = jnp.sum(grad_pre, axis=0)
    grad_pre16 = grad_pre.astype(jnp.bfloat16)
    grad_w_in = lax.dot_general(
        act_two, grad_pre16, contract_rows, preferred_element_type=jnp.float32
    )
    grad_act_two = lax.dot_general(
        grad_pre16, w_in, contract_cols, preferred_element_type=jnp.float32
    )
    grad_attn16 = (
        lax.dot_general(grad_y16, w_out, contract_cols, preferred_element_type=jnp.float32)
        .astype(jnp.bfloat16)
        .reshape(count, HEADS, HD)
    )
    grad_query, grad_key, grad_value = attend_backward(
        query16, key16, value16, attn16, lse_list, segments, grad_attn16
    )
    grad_query = rotate(grad_query, cosine, sine, -1.0)
    grad_key = rotate(grad_key, cosine, sine, -1.0)
    grad_mixed = jnp.stack([grad_query, grad_key, grad_value], axis=1).reshape(
        count, 3 * HEADS * HD
    )
    grad_b_qkv = jnp.sum(grad_mixed, axis=0)
    grad_mixed16 = grad_mixed.astype(jnp.bfloat16)
    grad_w_qkv = lax.dot_general(
        act_one, grad_mixed16, contract_rows, preferred_element_type=jnp.float32
    )
    grad_act_one = lax.dot_general(
        grad_mixed16, w_qkv, contract_cols, preferred_element_type=jnp.float32
    )
    gain_grad_one, shift_grad_one, grad_x_one = norm_back(grad_act_one, normed, inv_std, gain_one)
    gain_grad_two, shift_grad_two, grad_x_two = norm_back(grad_act_two, normed, inv_std, gain_two)
    grad_in = grad_y + grad_x_one + grad_x_two
    return (
        grad_in,
        [
            gain_grad_one,
            shift_grad_one,
            grad_w_qkv,
            grad_b_qkv,
            grad_w_out,
            grad_b_out,
            gain_grad_two,
            shift_grad_two,
            grad_w_in,
            grad_b_in,
            grad_w_out2,
            grad_b_out,
        ],
    )


def flatten_grads(parts, total_len):
    used = layout_offsets()[-1]
    rounded = [part.astype(jnp.bfloat16).reshape(-1) for part in parts]
    return jnp.concatenate(rounded + [jnp.zeros((total_len - used,), jnp.bfloat16)])


def adam_update(weights, first_moment, second_moment, gradient):
    new_first = BETA_ONE * first_moment + (1.0 - BETA_ONE) * gradient
    new_second = BETA_TWO * second_moment + (1.0 - BETA_TWO) * gradient * gradient
    unbiased_first = new_first / (1.0 - BETA_ONE**ADAM_STEP)
    unbiased_second = new_second / (1.0 - BETA_TWO**ADAM_STEP)
    new_weights = weights - LEARN_RATE * (
        unbiased_first / (jnp.sqrt(unbiased_second) + ADAM_EPS) + DECAY * weights
    )
    return (new_weights, new_first, new_second)


def on_device(tokens, segment_ids, cotangent, params, moment_one, moment_two):
    gathered = lax.all_gather(params.astype(jnp.bfloat16), "shard", axis=0, tiled=True)
    total_len = gathered.shape[0]
    pieces = split_params(gathered)
    output, saved = layer_forward(tokens, segment_ids, pieces)
    grad_input, parts = layer_backward(cotangent, segment_ids, pieces, saved)
    local_grad = flatten_grads(parts, total_len)
    owned = lax.psum_scatter(local_grad, "shard", scatter_dimension=0, tiled=True).astype(
        jnp.float32
    )
    tokens_all = tokens.shape[0] * lax.axis_size("rep") * lax.axis_size("shard")
    factor = 1.0 / math.sqrt(tokens_all)
    width = moment_one.shape[0]
    begin = lax.axis_index("rep") * width
    param_share = lax.dynamic_slice_in_dim(params, begin, width)
    share = lax.psum_scatter(owned, "rep", scatter_dimension=0, tiled=True)
    grad_share = share * factor
    upd_params, upd_first, upd_second = adam_update(param_share, moment_one, moment_two, grad_share)
    grad_params, new_params = (
        lax.all_gather(grad_share, "rep", axis=0, tiled=True),
        lax.all_gather(upd_params, "rep", axis=0, tiled=True),
    )
    return (output, grad_input, grad_params, new_params, upd_first, upd_second)


LANES = 128
REPS = 8
SHARDS = 4
PIECE = 288
FLAT_ROWS = 13848
MOVED = PIECE * D // LANES


PARTS = (
    ((12, 1728, 96, 3, 0),),
    ((6, 576, 96, 1, 0), (4632, 1152, 48, 4, 96)),
    ((0, 1152, 48, 4, 0), (9240, 576, 96, 1, 192)),
    ((0, 1728, 288, 1, 0),),
)
VECTOR_ROWS = ((0, 1, 2306, 2307), (0, 769, 770, 771), (1536, 1537, 1538, 1539), (2304, 2305, 2306, 2307))


def pack_kernel(where, flat_ref, out_ref, held, sems):
    shard = where[0]
    rep = where[1]
    for z in range(SHARDS):

        @pl.when(shard == z)
        def _(z=z):
            copies = []
            at = 0
            for turn, (first, step, _, _, _) in enumerate(PARTS[z]):
                lead = first % 8
                count = step + (8 if lead else 0)
                begin = pl.multiple_of(first - lead + step * rep, 8)
                copies.append(
                    pltpu.make_async_copy(
                        flat_ref.at[pl.ds(begin, count)], held.at[pl.ds(at, count)], sems.at[turn]
                    )
                )
                at += count
            for copy in copies:
                copy.start()
            at = 0
            for copy, (first, step, rows, blocks, place) in zip(copies, PARTS[z]):
                copy.wait()
                lead = first % 8
                stride = 6 * blocks
                for block in range(blocks):
                    for col in range(6):
                        got = held[pl.ds(at + lead + 6 * block + col, rows, stride=stride), :]
                        out_ref[
                            place + rows * block : place + rows * (block + 1),
                            LANES * col : LANES * (col + 1),
                        ] = got.astype(jnp.bfloat16)
                at += step + (8 if lead else 0)


def pack_piece(params, shard, rep):
    return pl.pallas_call(
        pack_kernel,
        grid_spec=pltpu.PrefetchScalarGridSpec(
            num_scalar_prefetch=1,
            in_specs=[pl.BlockSpec(memory_space=pltpu.HBM)],
            out_specs=pl.BlockSpec(memory_space=pltpu.VMEM),
            scratch_shapes=[
                pltpu.VMEM((MOVED + 16, LANES), jnp.float32),
                pltpu.SemaphoreType.DMA((2,)),
            ],
        ),
        out_shape=jax.ShapeDtypeStruct((PIECE, D), jnp.bfloat16),
    )(jnp.stack([shard, rep]), params.reshape(FLAT_ROWS, LANES))


def unpack_kernel(factor, where, grad_ref, vec_ref, out_ref):
    shard = where[0]
    for z in range(SHARDS):

        @pl.when(shard == z)
        def _(z=z):
            for slot, row in enumerate(VECTOR_ROWS[z]):
                for col in range(6):
                    out_ref[6 * row + col : 6 * row + col + 1, :] = (
                        vec_ref[slot : slot + 1, LANES * col : LANES * (col + 1)] * factor
                    )
            for rep in range(REPS):
                for first, step, rows, blocks, place in PARTS[z]:
                    for block in range(blocks):
                        for col in range(6):
                            got = grad_ref[
                                rep,
                                place + rows * block : place + rows * (block + 1),
                                LANES * col : LANES * (col + 1),
                            ]
                            out_ref[
                                pl.ds(
                                    first + step * rep + 6 * block + col, rows, stride=6 * blocks
                                ),
                                :,
                            ] = got.astype(jnp.float32) * factor


def unpack_grads(grads, vectors, shard, factor):
    return pl.pallas_call(
        functools.partial(unpack_kernel, factor),
        grid_spec=pltpu.PrefetchScalarGridSpec(
            num_scalar_prefetch=1,
            in_specs=[pl.BlockSpec(memory_space=pltpu.VMEM)] * 2,
            out_specs=pl.BlockSpec(memory_space=pltpu.VMEM),
        ),
        out_shape=jax.ShapeDtypeStruct((FLAT_ROWS, LANES), jnp.float32),
        compiler_params=pltpu.CompilerParams(vmem_limit_bytes=32 * 2**20),
    )(jnp.stack([shard]), grads, vectors)


def shard_vectors(params, shard):
    rows = jnp.asarray(VECTOR_ROWS, jnp.int32)[shard]
    return jnp.stack([lax.dynamic_slice_in_dim(params, rows[i] * D, D) for i in range(4)])


def pieces_of(gathered, vectors):
    first, second, third, fourth = (gathered[z] for z in range(SHARDS))
    w_qkv = jnp.concatenate(
        [first[:, 96 * j : 96 * (j + 1)].reshape(D, D) for j in range(3)], axis=1
    )
    w_out = second[:, 0:96].reshape(D, D)
    w_in = jnp.concatenate(
        [
            jnp.concatenate(
                [
                    second[:, 96 + 48 * j : 144 + 48 * j].reshape(D // 2, D),
                    third[:, 48 * j : 48 * (j + 1)].reshape(D // 2, D),
                ],
                axis=0,
            )
            for j in range(4)
        ],
        axis=1,
    )
    w_out2 = jnp.concatenate([third[:, 192:288].reshape(D, D), fourth.reshape(3 * D, D)], axis=0)
    return (
        vectors[0, 0],
        vectors[0, 1],
        w_qkv,
        jnp.concatenate([vectors[0, 2], vectors[0, 3], vectors[1, 0]]),
        w_out,
        vectors[1, 1],
        vectors[1, 2],
        vectors[1, 3],
        w_in,
        vectors[2].reshape(-1),
        w_out2,
        vectors[3, 0],
    )


def grads_by_owner(parts):
    w_qkv, w_out, w_in, w_out2 = (part.astype(jnp.bfloat16) for part in parts)
    col = lambda w, j: w[:, D * j : D * (j + 1)]
    first = [col(w_qkv, j).reshape(REPS, 96, D) for j in range(3)]
    second = [w_out.reshape(REPS, 96, D)] + [
        col(w_in, j)[: D // 2].reshape(REPS, 48, D) for j in range(4)
    ]
    third = [col(w_in, j)[D // 2 :].reshape(REPS, 48, D) for j in range(4)] + [
        w_out2[:D].reshape(REPS, 96, D)
    ]
    fourth = [w_out2[D:].reshape(REPS, PIECE, D)]
    return jnp.stack(
        [jnp.concatenate(group, axis=1) for group in (first, second, third, fourth)]
    )


def on_device_rows(tokens, segment_ids, cotangent, params, moment_one, moment_two):
    shard = lax.axis_index("shard")
    rep = lax.axis_index("rep")
    piece = pack_piece(params, shard, rep)
    vectors = lax.all_gather(shard_vectors(params, shard).astype(jnp.bfloat16), "shard", axis=0)
    gathered = lax.all_gather(piece, ("shard", "rep"), axis=0, tiled=True)
    gathered = gathered.reshape(SHARDS, REPS, PIECE, D)
    pieces = pieces_of(gathered, vectors)
    output, saved = layer_forward(tokens, segment_ids, pieces)
    grad_input, parts = layer_backward(cotangent, segment_ids, pieces, saved)
    (g1, s1, gw_qkv, gb_qkv, gw_out, gb_out, g2, s2, gw_in, gb_in, gw_out2, gb_out2) = parts
    owned = lax.psum_scatter(
        grads_by_owner((gw_qkv, gw_out, gw_in, gw_out2)).reshape(SHARDS * REPS * PIECE, D),
        ("shard", "rep"),
        scatter_dimension=0,
        tiled=True,
    )
    zero = jnp.zeros((3 * D,), jnp.float32)
    vec_grads = jnp.concatenate([g1, s1, gb_qkv, gb_out, g2, s2, gb_in, gb_out2, zero])
    vec_grads = lax.psum(
        vec_grads.astype(jnp.bfloat16).astype(jnp.float32), ("shard", "rep")
    ).reshape(SHARDS, 4, D)
    own_vectors = lax.dynamic_index_in_dim(vec_grads, shard, 0, keepdims=False)
    grads = lax.all_gather(owned, "rep", axis=0, tiled=True).reshape(REPS, PIECE, D)
    tokens_all = tokens.shape[0] * lax.axis_size("rep") * lax.axis_size("shard")
    grad_params = unpack_grads(grads, own_vectors, shard, 1.0 / math.sqrt(tokens_all)).reshape(-1)
    width = moment_one.shape[0]
    begin = rep * width
    param_share = lax.dynamic_slice_in_dim(params, begin, width)
    grad_share = lax.dynamic_slice_in_dim(grad_params, begin, width)
    upd_params, upd_first, upd_second = adam_update(param_share, moment_one, moment_two, grad_share)
    new_params = lax.all_gather(upd_params, "rep", axis=0, tiled=True)
    return (output, grad_input, grad_params, new_params, upd_first, upd_second)


def solution(mesh):
    in_specs = (
        P(("rep", "shard"), None),
        P(("rep", "shard")),
        P(("rep", "shard"), None),
        P("shard"),
        P(("shard", "rep")),
        P(("shard", "rep")),
    )
    out_specs = (
        P(("rep", "shard"), None),
        P(("rep", "shard"), None),
        P("shard"),
        P("shard"),
        P(("shard", "rep")),
        P(("shard", "rep")),
    )
    in_rows = mesh.shape["rep"] == REPS and mesh.shape["shard"] == SHARDS
    return jax.shard_map(
        on_device_rows if in_rows else on_device, mesh=mesh, in_specs=in_specs, out_specs=out_specs, check_vma=False
    )
```

```python
import functools
import math

import jax
import jax.numpy as jnp
from jax import lax
from jax.experimental import pallas as pl
from jax.experimental.pallas import tpu as pltpu
from jax.sharding import Mesh
from jax.sharding import PartitionSpec as P

D = 768
HEADS = 12
HD = 64
ROT = 16
FF = 3072


EPS_NORM = 1e-05
ROPE_BASE = 10000.0
NEG_BIG = -1e30
BETA_ONE = 0.9
BETA_TWO = 0.95
ADAM_STEP = 3.0
LEARN_RATE = 0.05
DECAY = 0.01
ADAM_EPS = 1e-08
INV_ROOT_TWO = 0.7071067811865476
INV_ROOT_TWO_PI = 0.3989422804014327


def layout_offsets():
    q_width = HEADS * HD
    o_wqkv = 2 * D
    o_bqkv = o_wqkv + 3 * q_width * D
    o_wout = o_bqkv + 3 * q_width
    o_bout = o_wout + q_width * D
    o_gain2 = o_bout + D
    o_shift2 = o_gain2 + D
    o_win = o_shift2 + D
    o_bin = o_win + D * FF
    o_wout2 = o_bin + FF
    o_bout2 = o_wout2 + FF * D
    return (
        o_wqkv,
        o_bqkv,
        o_wout,
        o_bout,
        o_gain2,
        o_shift2,
        o_win,
        o_bin,
        o_wout2,
        o_bout2,
        o_bout2 + D,
    )


def split_params(flat16):
    q_width = HEADS * HD
    o_wqkv, o_bqkv, o_wout, o_bout, o_gain2, o_shift2, o_win, o_bin, o_wout2, o_bout2, o_end = (
        layout_offsets()
    )
    return (
        flat16[0:D],
        flat16[D:o_wqkv],
        flat16[o_wqkv:o_bqkv].reshape(D, 3 * q_width),
        flat16[o_bqkv:o_wout],
        flat16[o_wout:o_bout].reshape(q_width, D),
        flat16[o_bout:o_gain2],
        flat16[o_gain2:o_shift2],
        flat16[o_shift2:o_win],
        flat16[o_win:o_bin].reshape(D, FF),
        flat16[o_bin:o_wout2],
        flat16[o_wout2:o_bout2].reshape(FF, D),
        flat16[o_bout2:o_end],
    )


def positions_of(segments):
    count = segments.shape[0]
    slot_ids = jnp.arange(count, dtype=jnp.int32)
    before = jnp.concatenate([jnp.full((1,), -2, jnp.int32), segments[:-1]])
    begins = segments != before
    first_slot = lax.cummax(jnp.where(begins, slot_ids, 0), axis=0)
    return slot_ids - first_slot


def rotary_tables(positions):
    half = ROT // 2
    steps_j = jnp.arange(half, dtype=jnp.float32)
    freqs = jnp.power(jnp.float32(ROPE_BASE), -2.0 * steps_j / ROT)
    angle = positions.astype(jnp.float32)[:, None] * freqs[None, :]
    return (jnp.cos(angle)[:, None, :], jnp.sin(angle)[:, None, :])


def rotate(values, cosine, sine, sign):
    half = cosine.shape[-1]
    lower = values[..., :half]
    upper = values[..., half : 2 * half]
    rest = values[..., 2 * half :]
    return jnp.concatenate(
        [lower * cosine - sign * upper * sine, upper * cosine + sign * lower * sine, rest], axis=-1
    )


def gelu_exact(value):
    return value * 0.5 * (1.0 + lax.erf(value * INV_ROOT_TWO))


def gelu_slope(value):
    return (
        0.5 * (1.0 + lax.erf(value * INV_ROOT_TWO))
        + value * jnp.exp(-0.5 * value * value) * INV_ROOT_TWO_PI
    )


def masked_scores(q_blk, keys, seg_rows, seg_cols, begin_row):
    scale = q_blk.shape[-1] ** (-0.5)
    raw_scores = jnp.einsum("qhd,khd->hqk", q_blk, keys, preferred_element_type=jnp.float32) * scale
    row_ids = begin_row + jnp.arange(q_blk.shape[0], dtype=jnp.int32)
    col_ids = jnp.arange(keys.shape[0], dtype=jnp.int32)
    allowed = (seg_rows[:, None] == seg_cols[None, :]) & (col_ids[None, :] <= row_ids[:, None])
    return jnp.where(allowed[None], raw_scores, NEG_BIG)


def attend_forward(query16, key16, value16, segments):
    scores = masked_scores(query16, key16, segments, segments, 0)
    row_max = jnp.max(scores, axis=-1, keepdims=True)
    expd = jnp.exp(scores - row_max)
    row_total = jnp.sum(expd, axis=-1, keepdims=True)
    probs16 = (expd / row_total).astype(jnp.bfloat16)
    attn_blk = jnp.einsum("hqk,khd->qhd", probs16, value16, preferred_element_type=jnp.float32)
    pieces_out = attn_blk.astype(jnp.bfloat16)
    lse_list = [row_max + jnp.log(row_total)]
    return (pieces_out, lse_list)


def attend_backward(query16, key16, value16, attn16, lse_list, segments, grad_attn16):
    count = query16.shape[0]
    block = min(512, count)
    scale = query16.shape[-1] ** (-0.5)
    grad_query = []
    grad_key = jnp.zeros(key16.shape, jnp.float32)
    grad_value = jnp.zeros(value16.shape, jnp.float32)
    for turn, begin_row in enumerate(range(0, count, block)):
        stop_row = begin_row + block
        scores = masked_scores(query16, key16, segments, segments, begin_row)
        chances = jnp.exp(scores - lse_list[turn])
        chances16 = chances.astype(jnp.bfloat16)
        grad_value = grad_value.at[:stop_row].add(
            jnp.einsum("hqk,qhd->khd", chances16, grad_attn16, preferred_element_type=jnp.float32)
        )
        grad_chance = jnp.einsum(
            "qhd,khd->hqk", grad_attn16, value16, preferred_element_type=jnp.float32
        )
        delta = jnp.sum(grad_attn16.astype(jnp.float32) * attn16.astype(jnp.float32), axis=-1)
        grad_scores = (chances * (grad_chance - jnp.transpose(delta)[:, :, None]) * scale).astype(
            jnp.bfloat16
        )
        grad_query.append(
            jnp.einsum("hqk,khd->qhd", grad_scores, key16, preferred_element_type=jnp.float32)
        )
        grad_key = grad_key.at[:stop_row].add(
            jnp.einsum("hqk,qhd->khd", grad_scores, query16, preferred_element_type=jnp.float32)
        )
    return (grad_query[0], grad_key, grad_value)


def norm_back(grad_act, normed, inv_std, gain):
    grad_gain = jnp.sum(grad_act * normed, axis=0)
    grad_shift = jnp.sum(grad_act, axis=0)
    grad_norm = grad_act * gain.astype(jnp.float32)
    grad_x = inv_std * (
        grad_norm
        - jnp.mean(grad_norm, axis=1, keepdims=True)
        - normed * jnp.mean(grad_norm * normed, axis=1, keepdims=True)
    )
    return (grad_gain, grad_shift, grad_x)


def layer_forward(tokens, segments, pieces):
    (
        gain_one,
        shift_one,
        w_qkv,
        b_qkv,
        w_out,
        b_out,
        gain_two,
        shift_two,
        w_in,
        b_in,
        w_out2,
        b_out2,
    ) = pieces
    count = tokens.shape[0]
    x_wide = tokens.astype(jnp.float32)
    row_mean = jnp.mean(x_wide, axis=1, keepdims=True)
    centered = x_wide - row_mean
    variance = jnp.mean(centered * centered, axis=1, keepdims=True)
    inv_std = lax.rsqrt(variance + EPS_NORM)
    normed = centered * inv_std
    act_one = (normed * gain_one.astype(jnp.float32) + shift_one.astype(jnp.float32)).astype(
        jnp.bfloat16
    )
    act_two = (normed * gain_two.astype(jnp.float32) + shift_two.astype(jnp.float32)).astype(
        jnp.bfloat16
    )
    mixed = jnp.dot(act_one, w_qkv, preferred_element_type=jnp.float32) + b_qkv.astype(jnp.float32)
    mixed = mixed.reshape(count, 3, HEADS, HD)
    cosine, sine = rotary_tables(positions_of(segments))
    query16 = rotate(mixed[:, 0], cosine, sine, 1.0).astype(jnp.bfloat16)
    key16 = rotate(mixed[:, 1], cosine, sine, 1.0).astype(jnp.bfloat16)
    value16 = mixed[:, 2].astype(jnp.bfloat16)
    attn16, lse_list = attend_forward(query16, key16, value16, segments)
    proj = jnp.dot(
        attn16.reshape(count, HEADS * HD), w_out, preferred_element_type=jnp.float32
    ) + b_out.astype(jnp.float32)
    pre = jnp.dot(act_two, w_in, preferred_element_type=jnp.float32) + b_in.astype(jnp.float32)
    hidden16 = gelu_exact(pre).astype(jnp.bfloat16)
    feed = jnp.dot(hidden16, w_out2, preferred_element_type=jnp.float32) + b_out2.astype(
        jnp.float32
    )
    output = x_wide + proj + feed
    saved = (
        normed,
        inv_std,
        act_one,
        act_two,
        query16,
        key16,
        value16,
        attn16,
        lse_list,
        cosine,
        sine,
        pre,
        hidden16,
    )
    return (output, saved)


def layer_backward(cotangent, segments, pieces, saved):
    (
        gain_one,
        shift_one,
        w_qkv,
        b_qkv,
        w_out,
        b_out,
        gain_two,
        shift_two,
        w_in,
        b_in,
        w_out2,
        b_out2,
    ) = pieces
    (
        normed,
        inv_std,
        act_one,
        act_two,
        query16,
        key16,
        value16,
        attn16,
        lse_list,
        cosine,
        sine,
        pre,
        hidden16,
    ) = saved
    count = cotangent.shape[0]
    contract_rows = (((0,), (0,)), ((), ()))
    contract_cols = (((1,), (1,)), ((), ()))
    live_rows = (segments >= 0).astype(jnp.float32)[:, None]
    grad_y = cotangent.astype(jnp.float32) * live_rows
    grad_y16 = grad_y.astype(jnp.bfloat16)
    grad_b_out = jnp.sum(grad_y, axis=0)
    attn_flat = attn16.reshape(count, HEADS * HD)
    grad_w_out = lax.dot_general(
        attn_flat, grad_y16, contract_rows, preferred_element_type=jnp.float32
    )
    grad_w_out2 = lax.dot_general(
        hidden16, grad_y16, contract_rows, preferred_element_type=jnp.float32
    )
    grad_hidden = lax.dot_general(
        grad_y16, w_out2, contract_cols, preferred_element_type=jnp.float32
    )
    grad_pre = grad_hidden * gelu_slope(pre)
    grad_b_in = jnp.sum(grad_pre, axis=0)
    grad_pre16 = grad_pre.astype(jnp.bfloat16)
    grad_w_in = lax.dot_general(
        act_two, grad_pre16, contract_rows, preferred_element_type=jnp.float32
    )
    grad_act_two = lax.dot_general(
        grad_pre16, w_in, contract_cols, preferred_element_type=jnp.float32
    )
    grad_attn16 = (
        lax.dot_general(grad_y16, w_out, contract_cols, preferred_element_type=jnp.float32)
        .astype(jnp.bfloat16)
        .reshape(count, HEADS, HD)
    )
    grad_query, grad_key, grad_value = attend_backward(
        query16, key16, value16, attn16, lse_list, segments, grad_attn16
    )
    grad_query = rotate(grad_query, cosine, sine, -1.0)
    grad_key = rotate(grad_key, cosine, sine, -1.0)
    grad_mixed = jnp.stack([grad_query, grad_key, grad_value], axis=1).reshape(
        count, 3 * HEADS * HD
    )
    grad_b_qkv = jnp.sum(grad_mixed, axis=0)
    grad_mixed16 = grad_mixed.astype(jnp.bfloat16)
    grad_w_qkv = lax.dot_general(
        act_one, grad_mixed16, contract_rows, preferred_element_type=jnp.float32
    )
    grad_act_one = lax.dot_general(
        grad_mixed16, w_qkv, contract_cols, preferred_element_type=jnp.float32
    )
    gain_grad_one, shift_grad_one, grad_x_one = norm_back(grad_act_one, normed, inv_std, gain_one)
    gain_grad_two, shift_grad_two, grad_x_two = norm_back(grad_act_two, normed, inv_std, gain_two)
    grad_in = grad_y + grad_x_one + grad_x_two
    return (
        grad_in,
        [
            gain_grad_one,
            shift_grad_one,
            grad_w_qkv,
            grad_b_qkv,
            grad_w_out,
            grad_b_out,
            gain_grad_two,
            shift_grad_two,
            grad_w_in,
            grad_b_in,
            grad_w_out2,
            grad_b_out,
        ],
    )


def flatten_grads(parts, total_len):
    used = layout_offsets()[-1]
    rounded = [part.astype(jnp.bfloat16).reshape(-1) for part in parts]
    return jnp.concatenate(rounded + [jnp.zeros((total_len - used,), jnp.bfloat16)])


def adam_update(weights, first_moment, second_moment, gradient):
    new_first = BETA_ONE * first_moment + (1.0 - BETA_ONE) * gradient
    new_second = BETA_TWO * second_moment + (1.0 - BETA_TWO) * gradient * gradient
    unbiased_first = new_first / (1.0 - BETA_ONE**ADAM_STEP)
    unbiased_second = new_second / (1.0 - BETA_TWO**ADAM_STEP)
    new_weights = weights - LEARN_RATE * (
        unbiased_first / (jnp.sqrt(unbiased_second) + ADAM_EPS) + DECAY * weights
    )
    return (new_weights, new_first, new_second)


def on_device(tokens, segment_ids, cotangent, params, moment_one, moment_two):
    gathered = lax.all_gather(params.astype(jnp.bfloat16), "shard", axis=0, tiled=True)
    total_len = gathered.shape[0]
    pieces = split_params(gathered)
    output, saved = layer_forward(tokens, segment_ids, pieces)
    grad_input, parts = layer_backward(cotangent, segment_ids, pieces, saved)
    local_grad = flatten_grads(parts, total_len)
    owned = lax.psum_scatter(local_grad, "shard", scatter_dimension=0, tiled=True).astype(
        jnp.float32
    )
    tokens_all = tokens.shape[0] * lax.axis_size("rep") * lax.axis_size("shard")
    factor = 1.0 / math.sqrt(tokens_all)
    width = moment_one.shape[0]
    begin = lax.axis_index("rep") * width
    param_share = lax.dynamic_slice_in_dim(params, begin, width)
    share = lax.psum_scatter(owned, "rep", scatter_dimension=0, tiled=True)
    grad_share = share * factor
    upd_params, upd_first, upd_second = adam_update(param_share, moment_one, moment_two, grad_share)
    grad_params, new_params = (
        lax.all_gather(grad_share, "rep", axis=0, tiled=True),
        lax.all_gather(upd_params, "rep", axis=0, tiled=True),
    )
    return (output, grad_input, grad_params, new_params, upd_first, upd_second)


LANES = 128
REPS = 8
SHARDS = 4
PIECE = 288
FLAT_ROWS = 13848
MOVED = PIECE * D // LANES


PARTS = (
    ((12, 1728, 96, 3, 0),),
    ((6, 576, 96, 1, 0), (4632, 1152, 48, 4, 96)),
    ((0, 1152, 48, 4, 0), (9240, 576, 96, 1, 192)),
    ((0, 1728, 288, 1, 0),),
)
VECTOR_ROWS = ((0, 1, 2306, 2307), (0, 769, 770, 771), (1536, 1537, 1538, 1539), (2304, 2305, 2306, 2307))


PLANE = ("y", "x", "core")
EVERY = PLANE + ("z",)
HOPS = (1, 2, 3, 0)


def plane_permute(value, flips):
    return lax.ppermute(value, PLANE, [(i, i ^ flips[i % 2]) for i in range(REPS)])


def first_cross(value):
    return plane_permute(value, (2, 4))


def second_cross(value):
    return plane_permute(value, (4, 2))


def core_cross(value):
    return plane_permute(value, (1, 1))


def ring_step(value):
    return lax.ppermute(value, "z", [(i, (i + 1) % SHARDS) for i in range(SHARDS)])


def flips_of(rep):
    core = rep % 2
    first = 2 + 2 * core
    return (0, first, 6 - first, 6)


def spread_in_plane(piece):
    first = first_cross(piece)
    second = second_cross(piece)
    both = second_cross(first)
    mine = [piece, first, second, both]
    return mine + [core_cross(value) for value in mine]


def spread_ids(rep):
    other = rep ^ 1
    return [rep ^ flip for flip in flips_of(rep)] + [other ^ flip for flip in flips_of(other)]


def pack_kernel(where, flat_ref, out_ref, held, sems):
    shard = where[0]
    for z in range(SHARDS):

        @pl.when(shard == z)
        def _(z=z):
            def start(turn, slot):
                copies = []
                at = 0
                rep = where[1 + turn]
                for part, (first, step, _, _, _) in enumerate(PARTS[z]):
                    lead = first % 8
                    count = step + (8 if lead else 0)
                    begin = pl.multiple_of(first - lead + step * rep, 8)
                    copy = pltpu.make_async_copy(
                        flat_ref.at[pl.ds(begin, count)],
                        held.at[slot, pl.ds(at, count)],
                        sems.at[slot, part],
                    )
                    copy.start()
                    copies.append(copy)
                    at += count
                return copies

            turns = out_ref.shape[0]
            running = start(0, 0)
            for turn in range(turns):
                slot = turn % 2
                following = start(turn + 1, 1 - slot) if turn + 1 < turns else None
                rep = where[1 + turn] if turns > 1 else 0
                at = 0
                for copy, (first, step, rows, blocks, place) in zip(running, PARTS[z]):
                    copy.wait()
                    lead = first % 8
                    for block in range(blocks):
                        for col in range(6):
                            begin = at + lead + 6 * block + col
                            got = held[slot, pl.ds(begin, rows, stride=6 * blocks), :]
                            out_ref[
                                rep,
                                place + rows * block : place + rows * (block + 1),
                                LANES * col : LANES * (col + 1),
                            ] = got.astype(jnp.bfloat16)
                    at += step + (8 if lead else 0)
                running = following


def pack_pieces(params, shard, reps):
    return pl.pallas_call(
        pack_kernel,
        grid_spec=pltpu.PrefetchScalarGridSpec(
            num_scalar_prefetch=1,
            in_specs=[pl.BlockSpec(memory_space=pltpu.HBM)],
            out_specs=pl.BlockSpec(memory_space=pltpu.VMEM),
            scratch_shapes=[
                pltpu.VMEM((2, MOVED + 16, LANES), jnp.float32),
                pltpu.SemaphoreType.DMA((2, 2)),
            ],
        ),
        out_shape=jax.ShapeDtypeStruct((len(reps), PIECE, D), jnp.bfloat16),
        compiler_params=pltpu.CompilerParams(vmem_limit_bytes=16 * 2**20),
    )(jnp.stack([shard] + reps), params.reshape(FLAT_ROWS, LANES))


def place_kernel(where, *refs):
    out_ref, sem = refs[-2:]
    copies = []
    for turn, ref in enumerate(refs[:-2]):
        copies.append(pltpu.make_async_copy(ref, out_ref.at[where[turn]], sem.at[turn]))
    for copy in copies:
        copy.start()
    for copy in copies:
        copy.wait()


def place_pieces(blocks, ids, slots):
    return pl.pallas_call(
        place_kernel,
        grid_spec=pltpu.PrefetchScalarGridSpec(
            num_scalar_prefetch=1,
            in_specs=[pl.BlockSpec(memory_space=pltpu.HBM)] * len(blocks),
            out_specs=pl.BlockSpec(memory_space=pltpu.HBM),
            scratch_shapes=[pltpu.SemaphoreType.DMA((len(blocks),))],
        ),
        out_shape=jax.ShapeDtypeStruct((slots,) + blocks[0].shape, blocks[0].dtype),
    )(jnp.stack(ids), *blocks)


def order_kernel(where, in_ref, out_ref, sem):
    copies = []
    for turn in range(out_ref.shape[0]):
        copies.append(
            pltpu.make_async_copy(in_ref.at[where[turn]], out_ref.at[turn], sem.at[turn])
        )
    for copy in copies:
        copy.start()
    for copy in copies:
        copy.wait()


def order_pieces(pieces, ids):
    return pl.pallas_call(
        order_kernel,
        grid_spec=pltpu.PrefetchScalarGridSpec(
            num_scalar_prefetch=1,
            in_specs=[pl.BlockSpec(memory_space=pltpu.HBM)],
            out_specs=pl.BlockSpec(memory_space=pltpu.HBM),
            scratch_shapes=[pltpu.SemaphoreType.DMA((len(ids),))],
        ),
        out_shape=jax.ShapeDtypeStruct((len(ids),) + pieces.shape[1:], pieces.dtype),
    )(jnp.stack(ids), pieces)


def unpack_kernel(factor, where, *refs):
    vec_ref, out_ref, held, sems = refs[REPS:]
    copies = []
    for turn in range(REPS):
        copies.append(
            pltpu.make_async_copy(refs[turn], held.at[where[1 + turn]], sems.at[turn])
        )
    for copy in copies:
        copy.start()
    for copy in copies:
        copy.wait()
    shard = where[0]
    for z in range(SHARDS):

        @pl.when(shard == z)
        def _(z=z):
            for slot, row in enumerate(VECTOR_ROWS[z]):
                for col in range(6):
                    out_ref[6 * row + col : 6 * row + col + 1, :] = (
                        vec_ref[slot : slot + 1, LANES * col : LANES * (col + 1)] * factor
                    )

            @pl.loop(0, REPS)
            def _(rep):
                for first, step, rows, blocks, place in PARTS[z]:
                    for block in range(blocks):
                        for col in range(6):
                            got = held[
                                rep,
                                place + rows * block : place + rows * (block + 1),
                                LANES * col : LANES * (col + 1),
                            ]
                            begin = first + step * rep + 6 * block + col
                            out_ref[pl.ds(begin, rows, stride=6 * blocks), :] = (
                                got.astype(jnp.float32) * factor
                            )


def unpack_grads(blocks, ids, vectors, shard, factor):
    return pl.pallas_call(
        functools.partial(unpack_kernel, factor),
        grid_spec=pltpu.PrefetchScalarGridSpec(
            num_scalar_prefetch=1,
            in_specs=[pl.BlockSpec(memory_space=pltpu.HBM)] * REPS
            + [pl.BlockSpec(memory_space=pltpu.VMEM)],
            out_specs=pl.BlockSpec(memory_space=pltpu.VMEM),
            scratch_shapes=[
                pltpu.VMEM((REPS, PIECE, D), jnp.bfloat16),
                pltpu.SemaphoreType.DMA((REPS,)),
            ],
        ),
        out_shape=jax.ShapeDtypeStruct((FLAT_ROWS, LANES), jnp.float32),
        compiler_params=pltpu.CompilerParams(vmem_limit_bytes=32 * 2**20),
    )(jnp.stack([shard] + ids), *blocks, vectors)


def gather_matrices(params, shard, rep):
    piece = pack_pieces(params, shard, [rep])[0]
    own = pack_pieces(params, shard, [rep * 0 + turn for turn in range(REPS)])
    reps = spread_ids(rep)
    blocks, ids = [], []
    for hop in range(1, SHARDS):
        piece = ring_step(piece)
        owner = (shard + SHARDS - hop) % SHARDS
        blocks += spread_in_plane(piece)
        ids += [owner * REPS + which for which in reps]
    blocks += [own[turn] for turn in range(REPS)]
    ids += [shard * REPS + turn for turn in range(REPS)]
    return place_pieces(blocks, ids, SHARDS * REPS)


def slots_of(shard, rep):
    ids = []
    for base in (rep ^ 1, rep):
        own, first, second, both = (base ^ flip for flip in flips_of(base))
        for hop in HOPS:
            owner = (shard + SHARDS - hop) % SHARDS
            ids += [owner * REPS + which for which in (first, both, own, second)]
    return ids


def scatter_sums(ordered):
    sent, kept = ordered[0], ordered[1]
    carried = None
    for turn in range(SHARDS):
        chip = kept[turn] + core_cross(sent[turn])
        pair = chip[2:4] + first_cross(chip[0:2])
        total = pair[0] + second_cross(pair[1])
        if carried is not None:
            total = total + carried
        if turn < SHARDS - 1:
            carried = ring_step(total)
    return total


def shard_vectors(params, shard):
    rows = jnp.asarray(VECTOR_ROWS, jnp.int32)[shard]
    return jnp.stack([lax.dynamic_slice_in_dim(params, rows[i] * D, D) for i in range(4)])


def pieces_of(gathered, vectors):
    first, second, third, fourth = (gathered[z] for z in range(SHARDS))
    w_qkv = jnp.concatenate(
        [first[:, 96 * j : 96 * (j + 1)].reshape(D, D) for j in range(3)], axis=1
    )
    w_out = second[:, 0:96].reshape(D, D)
    w_in = jnp.concatenate(
        [
            jnp.concatenate(
                [
                    second[:, 96 + 48 * j : 144 + 48 * j].reshape(D // 2, D),
                    third[:, 48 * j : 48 * (j + 1)].reshape(D // 2, D),
                ],
                axis=0,
            )
            for j in range(4)
        ],
        axis=1,
    )
    w_out2 = jnp.concatenate([third[:, 192:288].reshape(D, D), fourth.reshape(3 * D, D)], axis=0)
    return (
        vectors[0, 0],
        vectors[0, 1],
        w_qkv,
        jnp.concatenate([vectors[0, 2], vectors[0, 3], vectors[1, 0]]),
        w_out,
        vectors[1, 1],
        vectors[1, 2],
        vectors[1, 3],
        w_in,
        vectors[2].reshape(-1),
        w_out2,
        vectors[3, 0],
    )


def grads_by_owner(parts):
    w_qkv, w_out, w_in, w_out2 = (part.astype(jnp.bfloat16) for part in parts)
    col = lambda w, j: w[:, D * j : D * (j + 1)]
    first = [col(w_qkv, j).reshape(REPS, 96, D) for j in range(3)]
    second = [w_out.reshape(REPS, 96, D)] + [
        col(w_in, j)[: D // 2].reshape(REPS, 48, D) for j in range(4)
    ]
    third = [col(w_in, j)[D // 2 :].reshape(REPS, 48, D) for j in range(4)] + [
        w_out2[:D].reshape(REPS, 96, D)
    ]
    fourth = [w_out2[D:].reshape(REPS, PIECE, D)]
    return jnp.stack(
        [jnp.concatenate(group, axis=1) for group in (first, second, third, fourth)]
    )


def on_device_rows(tokens, segment_ids, cotangent, params, moment_one, moment_two):
    shard = lax.axis_index("z")
    rep = lax.axis_index(PLANE)
    vectors = lax.all_gather(shard_vectors(params, shard).astype(jnp.bfloat16), "z", axis=0)
    gathered = gather_matrices(params, shard, rep).reshape(SHARDS, REPS, PIECE, D)
    pieces = pieces_of(gathered, vectors)
    output, saved = layer_forward(tokens, segment_ids, pieces)
    grad_input, parts = layer_backward(cotangent, segment_ids, pieces, saved)
    (g1, s1, gw_qkv, gb_qkv, gw_out, gb_out, g2, s2, gw_in, gb_in, gw_out2, gb_out2) = parts
    by_owner = grads_by_owner((gw_qkv, gw_out, gw_in, gw_out2))
    ordered = order_pieces(by_owner.reshape(SHARDS * REPS, PIECE, D), slots_of(shard, rep))
    owned = scatter_sums(ordered.reshape(2, SHARDS, 4, PIECE, D))
    zero = jnp.zeros((3 * D,), jnp.float32)
    vec_grads = jnp.concatenate([g1, s1, gb_qkv, gb_out, g2, s2, gb_in, gb_out2, zero])
    vec_grads = lax.psum(vec_grads.astype(jnp.bfloat16).astype(jnp.float32), EVERY)
    own_vectors = lax.dynamic_index_in_dim(
        vec_grads.reshape(SHARDS, 4, D), shard, 0, keepdims=False
    )
    tokens_all = tokens.shape[0] * lax.axis_size(EVERY)
    grad_params = unpack_grads(
        spread_in_plane(owned), spread_ids(rep), own_vectors, shard, 1.0 / math.sqrt(tokens_all)
    ).reshape(-1)
    width = moment_one.shape[0]
    begin = rep * width
    param_share = lax.dynamic_slice_in_dim(params, begin, width)
    grad_share = lax.dynamic_slice_in_dim(grad_params, begin, width)
    upd_params, upd_first, upd_second = adam_update(param_share, moment_one, moment_two, grad_share)
    new_params = lax.all_gather(upd_params, PLANE, axis=0, tiled=True)
    return (output, grad_input, grad_params, new_params, upd_first, upd_second)


def solution(mesh):
    in_rows = mesh.shape["rep"] == REPS and mesh.shape["shard"] == SHARDS
    if in_rows:
        rep, shard = PLANE, "z"
        mesh = Mesh(mesh.devices.reshape(2, 2, 2, SHARDS), EVERY)
        body = on_device_rows
    else:
        rep, shard = ("rep",), "shard"
        body = on_device
    rows = rep + (shard,)
    owner = (shard,) + rep
    in_specs = (P(rows, None), P(rows), P(rows, None), P(shard), P(owner), P(owner))
    out_specs = (P(rows, None), P(rows, None), P(shard), P(shard), P(owner), P(owner))
    return jax.shard_map(body, mesh=mesh, in_specs=in_specs, out_specs=out_specs, check_vma=False)
```

```python
import functools
import math

import jax
import jax.numpy as jnp
from jax import lax
from jax.experimental import pallas as pl
from jax.experimental.pallas import tpu as pltpu
from jax.sharding import Mesh
from jax.sharding import PartitionSpec as P

D = 768
HEADS = 12
HD = 64
ROT = 16
FF = 3072
TOK_DEV = 128


EPS_NORM = 1e-05
ROPE_BASE = 10000.0
NEG_BIG = -1e30
BETA_ONE = 0.9
BETA_TWO = 0.95
ADAM_STEP = 3.0
LEARN_RATE = 0.05
DECAY = 0.01
ADAM_EPS = 1e-08
INV_ROOT_TWO = 0.7071067811865476
INV_ROOT_TWO_PI = 0.3989422804014327


def layout_offsets():
    q_width = HEADS * HD
    o_wqkv = 2 * D
    o_bqkv = o_wqkv + 3 * q_width * D
    o_wout = o_bqkv + 3 * q_width
    o_bout = o_wout + q_width * D
    o_gain2 = o_bout + D
    o_shift2 = o_gain2 + D
    o_win = o_shift2 + D
    o_bin = o_win + D * FF
    o_wout2 = o_bin + FF
    o_bout2 = o_wout2 + FF * D
    return (
        o_wqkv,
        o_bqkv,
        o_wout,
        o_bout,
        o_gain2,
        o_shift2,
        o_win,
        o_bin,
        o_wout2,
        o_bout2,
        o_bout2 + D,
    )


def split_params(flat16):
    q_width = HEADS * HD
    o_wqkv, o_bqkv, o_wout, o_bout, o_gain2, o_shift2, o_win, o_bin, o_wout2, o_bout2, o_end = (
        layout_offsets()
    )
    return (
        flat16[0:D],
        flat16[D:o_wqkv],
        flat16[o_wqkv:o_bqkv].reshape(D, 3 * q_width),
        flat16[o_bqkv:o_wout],
        flat16[o_wout:o_bout].reshape(q_width, D),
        flat16[o_bout:o_gain2],
        flat16[o_gain2:o_shift2],
        flat16[o_shift2:o_win],
        flat16[o_win:o_bin].reshape(D, FF),
        flat16[o_bin:o_wout2],
        flat16[o_wout2:o_bout2].reshape(FF, D),
        flat16[o_bout2:o_end],
    )


def positions_of(segments):
    count = segments.shape[0]
    slot_ids = jnp.arange(count, dtype=jnp.int32)
    before = jnp.concatenate([jnp.full((1,), -2, jnp.int32), segments[:-1]])
    begins = segments != before
    first_slot = lax.cummax(jnp.where(begins, slot_ids, 0), axis=0)
    return slot_ids - first_slot


def rotary_tables(positions):
    half = ROT // 2
    steps_j = jnp.arange(half, dtype=jnp.float32)
    freqs = jnp.power(jnp.float32(ROPE_BASE), -2.0 * steps_j / ROT)
    angle = positions.astype(jnp.float32)[:, None] * freqs[None, :]
    return (jnp.cos(angle)[:, None, :], jnp.sin(angle)[:, None, :])


def rotate(values, cosine, sine, sign):
    half = cosine.shape[-1]
    lower = values[..., :half]
    upper = values[..., half : 2 * half]
    rest = values[..., 2 * half :]
    return jnp.concatenate(
        [lower * cosine - sign * upper * sine, upper * cosine + sign * lower * sine, rest], axis=-1
    )


def gelu_exact(value):
    return value * 0.5 * (1.0 + lax.erf(value * INV_ROOT_TWO))


def gelu_slope(value):
    return (
        0.5 * (1.0 + lax.erf(value * INV_ROOT_TWO))
        + value * jnp.exp(-0.5 * value * value) * INV_ROOT_TWO_PI
    )


def masked_scores(q_blk, keys, seg_rows, seg_cols, begin_row):
    scale = q_blk.shape[-1] ** (-0.5)
    raw_scores = jnp.einsum("qhd,khd->hqk", q_blk, keys, preferred_element_type=jnp.float32) * scale
    row_ids = begin_row + jnp.arange(q_blk.shape[0], dtype=jnp.int32)
    col_ids = jnp.arange(keys.shape[0], dtype=jnp.int32)
    allowed = (seg_rows[:, None] == seg_cols[None, :]) & (col_ids[None, :] <= row_ids[:, None])
    return jnp.where(allowed[None], raw_scores, NEG_BIG)


def attend_forward(query16, key16, value16, segments):
    scores = masked_scores(query16, key16, segments, segments, 0)
    row_max = jnp.max(scores, axis=-1, keepdims=True)
    expd = jnp.exp(scores - row_max)
    row_total = jnp.sum(expd, axis=-1, keepdims=True)
    probs16 = (expd / row_total).astype(jnp.bfloat16)
    attn_blk = jnp.einsum("hqk,khd->qhd", probs16, value16, preferred_element_type=jnp.float32)
    pieces_out = attn_blk.astype(jnp.bfloat16)
    lse_list = [row_max + jnp.log(row_total)]
    return (pieces_out, lse_list)


def attend_backward(query16, key16, value16, attn16, lse_list, segments, grad_attn16):
    count = query16.shape[0]
    block = min(512, count)
    scale = query16.shape[-1] ** (-0.5)
    grad_query = []
    grad_key = jnp.zeros(key16.shape, jnp.float32)
    grad_value = jnp.zeros(value16.shape, jnp.float32)
    for turn, begin_row in enumerate(range(0, count, block)):
        stop_row = begin_row + block
        scores = masked_scores(query16, key16, segments, segments, begin_row)
        chances = jnp.exp(scores - lse_list[turn])
        chances16 = chances.astype(jnp.bfloat16)
        grad_value = grad_value.at[:stop_row].add(
            jnp.einsum("hqk,qhd->khd", chances16, grad_attn16, preferred_element_type=jnp.float32)
        )
        grad_chance = jnp.einsum(
            "qhd,khd->hqk", grad_attn16, value16, preferred_element_type=jnp.float32
        )
        delta = jnp.sum(grad_attn16.astype(jnp.float32) * attn16.astype(jnp.float32), axis=-1)
        grad_scores = (chances * (grad_chance - jnp.transpose(delta)[:, :, None]) * scale).astype(
            jnp.bfloat16
        )
        grad_query.append(
            jnp.einsum("hqk,khd->qhd", grad_scores, key16, preferred_element_type=jnp.float32)
        )
        grad_key = grad_key.at[:stop_row].add(
            jnp.einsum("hqk,qhd->khd", grad_scores, query16, preferred_element_type=jnp.float32)
        )
    return (grad_query[0], grad_key, grad_value)


def norm_back(grad_act, normed, inv_std, gain):
    grad_gain = jnp.sum(grad_act * normed, axis=0)
    grad_shift = jnp.sum(grad_act, axis=0)
    grad_norm = grad_act * gain.astype(jnp.float32)
    grad_x = inv_std * (
        grad_norm
        - jnp.mean(grad_norm, axis=1, keepdims=True)
        - normed * jnp.mean(grad_norm * normed, axis=1, keepdims=True)
    )
    return (grad_gain, grad_shift, grad_x)


def layer_forward(tokens, segments, pieces):
    (
        gain_one,
        shift_one,
        w_qkv,
        b_qkv,
        w_out,
        b_out,
        gain_two,
        shift_two,
        w_in,
        b_in,
        w_out2,
        b_out2,
    ) = pieces
    count = tokens.shape[0]
    x_wide = tokens.astype(jnp.float32)
    row_mean = jnp.mean(x_wide, axis=1, keepdims=True)
    centered = x_wide - row_mean
    variance = jnp.mean(centered * centered, axis=1, keepdims=True)
    inv_std = lax.rsqrt(variance + EPS_NORM)
    normed = centered * inv_std
    act_one = (normed * gain_one.astype(jnp.float32) + shift_one.astype(jnp.float32)).astype(
        jnp.bfloat16
    )
    act_two = (normed * gain_two.astype(jnp.float32) + shift_two.astype(jnp.float32)).astype(
        jnp.bfloat16
    )
    mixed = jnp.dot(act_one, w_qkv, preferred_element_type=jnp.float32) + b_qkv.astype(jnp.float32)
    mixed = mixed.reshape(count, 3, HEADS, HD)
    cosine, sine = rotary_tables(positions_of(segments))
    query16 = rotate(mixed[:, 0], cosine, sine, 1.0).astype(jnp.bfloat16)
    key16 = rotate(mixed[:, 1], cosine, sine, 1.0).astype(jnp.bfloat16)
    value16 = mixed[:, 2].astype(jnp.bfloat16)
    attn16, lse_list = attend_forward(query16, key16, value16, segments)
    proj = jnp.dot(
        attn16.reshape(count, HEADS * HD), w_out, preferred_element_type=jnp.float32
    ) + b_out.astype(jnp.float32)
    pre = jnp.dot(act_two, w_in, preferred_element_type=jnp.float32) + b_in.astype(jnp.float32)
    hidden16 = gelu_exact(pre).astype(jnp.bfloat16)
    feed = jnp.dot(hidden16, w_out2, preferred_element_type=jnp.float32) + b_out2.astype(
        jnp.float32
    )
    output = x_wide + proj + feed
    saved = (
        normed,
        inv_std,
        act_one,
        act_two,
        query16,
        key16,
        value16,
        attn16,
        lse_list,
        cosine,
        sine,
        pre,
        hidden16,
    )
    return (output, saved)


def layer_backward(cotangent, segments, pieces, saved):
    (
        gain_one,
        shift_one,
        w_qkv,
        b_qkv,
        w_out,
        b_out,
        gain_two,
        shift_two,
        w_in,
        b_in,
        w_out2,
        b_out2,
    ) = pieces
    (
        normed,
        inv_std,
        act_one,
        act_two,
        query16,
        key16,
        value16,
        attn16,
        lse_list,
        cosine,
        sine,
        pre,
        hidden16,
    ) = saved
    count = cotangent.shape[0]
    contract_rows = (((0,), (0,)), ((), ()))
    contract_cols = (((1,), (1,)), ((), ()))
    live_rows = (segments >= 0).astype(jnp.float32)[:, None]
    grad_y = cotangent.astype(jnp.float32) * live_rows
    grad_y16 = grad_y.astype(jnp.bfloat16)
    grad_b_out = jnp.sum(grad_y, axis=0)
    attn_flat = attn16.reshape(count, HEADS * HD)
    grad_w_out = lax.dot_general(
        attn_flat, grad_y16, contract_rows, preferred_element_type=jnp.float32
    )
    grad_w_out2 = lax.dot_general(
        hidden16, grad_y16, contract_rows, preferred_element_type=jnp.float32
    )
    grad_hidden = lax.dot_general(
        grad_y16, w_out2, contract_cols, preferred_element_type=jnp.float32
    )
    grad_pre = grad_hidden * gelu_slope(pre)
    grad_b_in = jnp.sum(grad_pre, axis=0)
    grad_pre16 = grad_pre.astype(jnp.bfloat16)
    grad_w_in = lax.dot_general(
        act_two, grad_pre16, contract_rows, preferred_element_type=jnp.float32
    )
    grad_act_two = lax.dot_general(
        grad_pre16, w_in, contract_cols, preferred_element_type=jnp.float32
    )
    grad_attn16 = (
        lax.dot_general(grad_y16, w_out, contract_cols, preferred_element_type=jnp.float32)
        .astype(jnp.bfloat16)
        .reshape(count, HEADS, HD)
    )
    grad_query, grad_key, grad_value = attend_backward(
        query16, key16, value16, attn16, lse_list, segments, grad_attn16
    )
    grad_query = rotate(grad_query, cosine, sine, -1.0)
    grad_key = rotate(grad_key, cosine, sine, -1.0)
    grad_mixed = jnp.stack([grad_query, grad_key, grad_value], axis=1).reshape(
        count, 3 * HEADS * HD
    )
    grad_b_qkv = jnp.sum(grad_mixed, axis=0)
    grad_mixed16 = grad_mixed.astype(jnp.bfloat16)
    grad_w_qkv = lax.dot_general(
        act_one, grad_mixed16, contract_rows, preferred_element_type=jnp.float32
    )
    grad_act_one = lax.dot_general(
        grad_mixed16, w_qkv, contract_cols, preferred_element_type=jnp.float32
    )
    gain_grad_one, shift_grad_one, grad_x_one = norm_back(grad_act_one, normed, inv_std, gain_one)
    gain_grad_two, shift_grad_two, grad_x_two = norm_back(grad_act_two, normed, inv_std, gain_two)
    grad_in = grad_y + grad_x_one + grad_x_two
    return (
        grad_in,
        [
            gain_grad_one,
            shift_grad_one,
            grad_w_qkv,
            grad_b_qkv,
            grad_w_out,
            grad_b_out,
            gain_grad_two,
            shift_grad_two,
            grad_w_in,
            grad_b_in,
            grad_w_out2,
            grad_b_out,
        ],
    )


def flatten_grads(parts, total_len):
    used = layout_offsets()[-1]
    rounded = [part.astype(jnp.bfloat16).reshape(-1) for part in parts]
    return jnp.concatenate(rounded + [jnp.zeros((total_len - used,), jnp.bfloat16)])


def adam_update(weights, first_moment, second_moment, gradient):
    new_first = BETA_ONE * first_moment + (1.0 - BETA_ONE) * gradient
    new_second = BETA_TWO * second_moment + (1.0 - BETA_TWO) * gradient * gradient
    unbiased_first = new_first / (1.0 - BETA_ONE**ADAM_STEP)
    unbiased_second = new_second / (1.0 - BETA_TWO**ADAM_STEP)
    new_weights = weights - LEARN_RATE * (
        unbiased_first / (jnp.sqrt(unbiased_second) + ADAM_EPS) + DECAY * weights
    )
    return (new_weights, new_first, new_second)


def on_device(tokens, segment_ids, cotangent, params, moment_one, moment_two):
    gathered = lax.all_gather(params.astype(jnp.bfloat16), "shard", axis=0, tiled=True)
    total_len = gathered.shape[0]
    pieces = split_params(gathered)
    output, saved = layer_forward(tokens, segment_ids, pieces)
    grad_input, parts = layer_backward(cotangent, segment_ids, pieces, saved)
    local_grad = flatten_grads(parts, total_len)
    owned = lax.psum_scatter(local_grad, "shard", scatter_dimension=0, tiled=True).astype(
        jnp.float32
    )
    tokens_all = tokens.shape[0] * lax.axis_size("rep") * lax.axis_size("shard")
    factor = 1.0 / math.sqrt(tokens_all)
    width = moment_one.shape[0]
    begin = lax.axis_index("rep") * width
    param_share = lax.dynamic_slice_in_dim(params, begin, width)
    share = lax.psum_scatter(owned, "rep", scatter_dimension=0, tiled=True)
    grad_share = share * factor
    upd_params, upd_first, upd_second = adam_update(param_share, moment_one, moment_two, grad_share)
    grad_params, new_params = (
        lax.all_gather(grad_share, "rep", axis=0, tiled=True),
        lax.all_gather(upd_params, "rep", axis=0, tiled=True),
    )
    return (output, grad_input, grad_params, new_params, upd_first, upd_second)


LANES = 128
REPS = 8
SHARDS = 4
PIECE = 288
FLAT_ROWS = 13848
MOVED = PIECE * D // LANES


PARTS = (
    ((12, 1728, 96, 3, 0),),
    ((6, 576, 96, 1, 0), (4632, 1152, 48, 4, 96)),
    ((0, 1152, 48, 4, 0), (9240, 576, 96, 1, 192)),
    ((0, 1728, 288, 1, 0),),
)
VECTOR_ROWS = ((0, 1, 2306, 2307), (0, 769, 770, 771), (1536, 1537, 1538, 1539), (2304, 2305, 2306, 2307))


PLANE = ("y", "x", "core")
EVERY = PLANE + ("z",)
HOPS = (1, 2, 3, 0)


def plane_permute(value, flips):
    return lax.ppermute(value, PLANE, [(i, i ^ flips[i % 2]) for i in range(REPS)])


def first_cross(value):
    return plane_permute(value, (2, 4))


def second_cross(value):
    return plane_permute(value, (4, 2))


def core_cross(value):
    return plane_permute(value, (1, 1))


def ring_step(value):
    return lax.ppermute(value, "z", [(i, (i + 1) % SHARDS) for i in range(SHARDS)])


def flips_of(rep):
    core = rep % 2
    first = 2 + 2 * core
    return (0, first, 6 - first, 6)


def spread_in_plane(piece):
    first = first_cross(piece)
    second = second_cross(piece)
    both = second_cross(first)
    mine = [piece, first, second, both]
    return mine + [core_cross(value) for value in mine]


def spread_ids(rep):
    other = rep ^ 1
    return [rep ^ flip for flip in flips_of(rep)] + [other ^ flip for flip in flips_of(other)]


def pack_kernel(where, flat_ref, out_ref, held, sems):
    shard = where[0]
    turns = out_ref.shape[0]
    for z in range(SHARDS):

        @pl.when(shard == z)
        def _(z=z):
            def copies_of(turn):
                slot = turn % 2
                rep = where[1 + turn]
                copies = []
                at = 0
                for part, (first, step, _, _, _) in enumerate(PARTS[z]):
                    lead = first % 8
                    count = step + (8 if lead else 0)
                    begin = pl.multiple_of(first - lead + step * rep, 8)
                    copies.append(
                        pltpu.make_async_copy(
                            flat_ref.at[pl.ds(begin, count)],
                            held.at[slot, pl.ds(at, count)],
                            sems.at[slot, part],
                        )
                    )
                    at += count
                return copies

            for copy in copies_of(0):
                copy.start()

            @pl.loop(0, turns)
            def _(turn):
                @pl.when(turn + 1 < turns)
                def _():
                    for copy in copies_of(turn + 1):
                        copy.start()

                slot = turn % 2
                at = 0
                for copy, (first, step, rows, blocks, place) in zip(copies_of(turn), PARTS[z]):
                    copy.wait()
                    lead = first % 8
                    for block in range(blocks):
                        for col in range(6):
                            begin = at + lead + 6 * block + col
                            got = held[slot, pl.ds(begin, rows, stride=6 * blocks), :]
                            out_ref[
                                turn,
                                place + rows * block : place + rows * (block + 1),
                                LANES * col : LANES * (col + 1),
                            ] = got.astype(jnp.bfloat16)
                    at += step + (8 if lead else 0)


def pack_pieces(params, shard, reps):
    return pl.pallas_call(
        pack_kernel,
        grid_spec=pltpu.PrefetchScalarGridSpec(
            num_scalar_prefetch=1,
            in_specs=[pl.BlockSpec(memory_space=pltpu.HBM)],
            out_specs=pl.BlockSpec(memory_space=pltpu.VMEM),
            scratch_shapes=[
                pltpu.VMEM((2, MOVED + 16, LANES), jnp.float32),
                pltpu.SemaphoreType.DMA((2, 2)),
            ],
        ),
        out_shape=jax.ShapeDtypeStruct((len(reps), PIECE, D), jnp.bfloat16),
        compiler_params=pltpu.CompilerParams(vmem_limit_bytes=16 * 2**20),
    )(jnp.stack([shard] + reps), params.reshape(FLAT_ROWS, LANES))


PIECES = SHARDS * REPS
ALL_ROWS = PIECES * PIECE


def fetch_pieces(ids, blocks, own, shard, held, sems):
    copies = []
    for turn, block in enumerate(blocks):
        row = pl.multiple_of(ids[turn] * PIECE, 16)
        copies.append(pltpu.make_async_copy(block, held.at[pl.ds(row, PIECE)], sems.at[turn]))
    row = pl.multiple_of(shard * (REPS * PIECE), 16)
    copies.append(
        pltpu.make_async_copy(own, held.at[pl.ds(row, REPS * PIECE)], sems.at[len(blocks)])
    )
    for copy in copies:
        copy.start()
    return copies


def rows_of(held, shard, begin, rows):
    return jnp.concatenate(
        [held[pl.ds((shard * REPS + r) * PIECE + begin, rows), :] for r in range(REPS)], axis=0
    )


def w_qkv_of(held, j):
    return rows_of(held, 0, 96 * j, 96)


def w_out_of(held):
    return rows_of(held, 1, 0, 96)


def w_in_of(held, j):
    return jnp.concatenate([rows_of(held, 1, 96 + 48 * j, 48), rows_of(held, 2, 48 * j, 48)], axis=0)


def w_out2_of(held, j):
    if j == 0:
        return rows_of(held, 2, 192, 96)
    return held[pl.ds(3 * REPS * PIECE + D * (j - 1), D), :]


def dot32(a, b):
    return jnp.dot(a, b, preferred_element_type=jnp.float32)


def gradient_kernel(where, *refs):
    count = PIECES - REPS
    blocks, own = refs[:count], refs[count]
    (act_one, act_two, grad_y, vecs, rot_cos, rot_up, rot_down, bias) = refs[count + 1 : count + 9]
    outs = refs[count + 9 : count + 9 + 13]
    sent, kept = outs[0:4], outs[4:8]
    attn_out, hidden_out, pre_out, mixed_out, sums_out = outs[8:13]
    held, grads, query, key, value, grad_attn, sems, out_sems = refs[count + 22 :]
    shard = where[0]
    for copy in fetch_pieces([where[1 + t] for t in range(count)], blocks, own, shard, held, sems):
        copy.wait()
    slot_row = lambda z, r: pl.multiple_of(where[1 + count + z * REPS + r] * PIECE, 16)

    def keep_rows(z, begin, rows, part):
        for r in range(part.shape[0] // rows):
            grads[pl.ds(slot_row(z, r) + begin, rows), :] = part[rows * r : rows * (r + 1), :]

    act1 = act_one[...]
    for j, out in enumerate((query, key, value)):
        got = dot32(act1, w_qkv_of(held, j)) + vecs[2 + j : 3 + j, :]
        if j < 2:
            for p in range(6):
                lanes = slice(LANES * p, LANES * (p + 1))
                part = got[:, lanes]
                part = (
                    part * rot_cos[...]
                    + pltpu.roll(part, LANES - 8, 1) * rot_up[...]
                    + pltpu.roll(part, 8, 1) * rot_down[...]
                )
                out[:, lanes] = part.astype(jnp.bfloat16)
        else:
            out[...] = got.astype(jnp.bfloat16)
    gy_t = grad_y[...].T
    grad_attn[...] = dot32(w_out_of(held), gy_t).T.astype(jnp.bfloat16)

    low = lax.broadcasted_iota(jnp.int32, (LANES, LANES), 1) < HD
    scale = HD ** (-0.5)
    for p in range(6):
        lanes = slice(LANES * p, LANES * (p + 1))
        q2, k2, v2, g2 = (ref[:, lanes] for ref in (query, key, value, grad_attn))
        k2_t, v2_t = k2.T, v2.T
        attn_parts, value_parts, query_parts, key_parts = [], [], [], []
        for half in range(2):
            here = low if half == 0 else ~low
            zero = jnp.zeros_like(q2)
            scores = dot32(jnp.where(here, q2, zero), k2_t) * scale
            scores = jnp.where(bias[...] > 0.5, scores, NEG_BIG)
            expd = jnp.exp(scores - jnp.max(scores, axis=1, keepdims=True))
            chances = expd / jnp.sum(expd, axis=1, keepdims=True)
            chances16 = chances.astype(jnp.bfloat16)
            attn = dot32(chances16, v2)
            attn16 = attn.astype(jnp.bfloat16)
            masked = jnp.where(here, g2, zero)
            delta = jnp.sum(
                masked.astype(jnp.float32) * attn16.astype(jnp.float32), axis=1, keepdims=True
            )
            grad_chance = dot32(masked, v2_t)
            slope = (chances * (grad_chance - delta) * scale).astype(jnp.bfloat16)
            attn_parts.append(attn16)
            value_parts.append(dot32(chances16.T, g2))
            query_parts.append(dot32(slope, k2))
            key_parts.append(dot32(slope.T, q2))
        attn_out[:, lanes] = jnp.where(low, *attn_parts)
        for j, parts in enumerate((query_parts, key_parts, value_parts)):
            part = jnp.where(low, *parts)
            if j < 2:
                part = (
                    part * rot_cos[...]
                    - pltpu.roll(part, LANES - 8, 1) * rot_up[...]
                    - pltpu.roll(part, 8, 1) * rot_down[...]
                )
            wide = slice(D * j + LANES * p, D * j + LANES * (p + 1))
            sums_out[2 + j : 3 + j, lanes] = jnp.sum(part, axis=0, keepdims=True)
            mixed_out[:, wide] = part.astype(jnp.bfloat16)

    gy = grad_y[...]
    act1_t = act1.T
    for j in range(3):
        keep_rows(
            0, 96 * j, 96, dot32(act1_t, mixed_out[:, D * j : D * (j + 1)]).astype(jnp.bfloat16)
        )
    keep_rows(1, 0, 96, dot32(attn_out[...].T, gy).astype(jnp.bfloat16))

    act2 = act_two[...]
    act2_t = act2.T
    for j in range(4):
        wide = slice(D * j, D * (j + 1))
        pre = dot32(act2, w_in_of(held, j)) + vecs[8 + j : 9 + j, :]
        bell = 0.5 * (1.0 + lax.erf(pre * INV_ROOT_TWO))
        hidden = (pre * bell).astype(jnp.bfloat16)
        hidden_out[:, wide] = hidden
        grad_hidden = dot32(w_out2_of(held, j), gy_t).T
        grad_pre = grad_hidden * (bell + pre * jnp.exp(-0.5 * pre * pre) * INV_ROOT_TWO_PI)
        sums_out[8 + j : 9 + j, :] = jnp.sum(grad_pre, axis=0, keepdims=True)
        grad_pre16 = grad_pre.astype(jnp.bfloat16)
        pre_out[:, wide] = grad_pre16
        w2 = dot32(hidden.T, gy).astype(jnp.bfloat16)
        if j == 0:
            keep_rows(2, 192, 96, w2)
        else:
            at = D * (j - 1)
            while at < D * j:
                r, begin = divmod(at, PIECE)
                rows = min(PIECE - begin, D * j - at)
                grads[pl.ds(slot_row(3, r) + begin, rows), :] = w2[
                    at - D * (j - 1) : at - D * (j - 1) + rows, :
                ]
                at += rows
        w1 = dot32(act2_t, grad_pre16).astype(jnp.bfloat16)
        keep_rows(1, 96 + 48 * j, 48, w1[: D // 2])
        keep_rows(2, 48 * j, 48, w1[D // 2 :])
    copies = []
    for turn, out in enumerate(sent + kept):
        for p in range(4):
            copies.append(
                pltpu.make_async_copy(
                    grads.at[pl.ds((turn * 4 + p) * PIECE, PIECE)],
                    out.at[p],
                    out_sems.at[turn * 4 + p],
                )
            )
    for copy in copies:
        copy.start()
    for copy in copies:
        copy.wait()


def weight_gradients(scalars, blocks, own, small):
    hbm = pl.BlockSpec(memory_space=pltpu.HBM)
    vmem = pl.BlockSpec(memory_space=pltpu.VMEM)
    bf16 = jnp.bfloat16
    group = jax.ShapeDtypeStruct((4, PIECE, D), bf16)
    return pl.pallas_call(
        gradient_kernel,
        grid_spec=pltpu.PrefetchScalarGridSpec(
            num_scalar_prefetch=1,
            in_specs=[hbm] * (len(blocks) + 1) + [vmem] * len(small),
            out_specs=[hbm] * 8 + [vmem] * 5,
            scratch_shapes=[
                pltpu.VMEM((ALL_ROWS, D), bf16),
                pltpu.VMEM((ALL_ROWS, D), bf16),
                pltpu.VMEM((TOK_DEV, D), bf16),
                pltpu.VMEM((TOK_DEV, D), bf16),
                pltpu.VMEM((TOK_DEV, D), bf16),
                pltpu.VMEM((TOK_DEV, D), bf16),
                pltpu.SemaphoreType.DMA((PIECES,)),
                pltpu.SemaphoreType.DMA((PIECES,)),
            ],
        ),
        out_shape=[group] * 8
        + [
            jax.ShapeDtypeStruct((TOK_DEV, D), bf16),
            jax.ShapeDtypeStruct((TOK_DEV, FF), bf16),
            jax.ShapeDtypeStruct((TOK_DEV, FF), bf16),
            jax.ShapeDtypeStruct((TOK_DEV, 3 * D), bf16),
            jax.ShapeDtypeStruct((16, D), jnp.float32),
        ],
        compiler_params=pltpu.CompilerParams(vmem_limit_bytes=56 * 2**20),
    )(scalars, *blocks, own, *small)


def result_kernel(where, *refs):
    count = PIECES - REPS
    blocks, own = refs[:count], refs[count]
    (tokens, normed, inv_std, grad_y, vecs, attn, hidden, grad_pre, grad_mixed, sums) = refs[
        count + 1 : count + 11
    ]
    output, grad_input, vec_out, held, sems = refs[count + 11 :]
    shard = where[0]
    for copy in fetch_pieces([where[1 + t] for t in range(count)], blocks, own, shard, held, sems):
        copy.wait()
    total = dot32(attn[...], w_out_of(held)) + vecs[5:6, :]
    for j in range(4):
        total = total + dot32(hidden[:, D * j : D * (j + 1)], w_out2_of(held, j))
    output[...] = tokens[...].astype(jnp.float32) + (total + vecs[12:13, :])
    vec_out[...] = sums[...]
    gy = grad_y[...].astype(jnp.float32)
    total = gy
    for norm, (parts, width, weights) in enumerate(
        ((grad_mixed, 3, w_qkv_of), (grad_pre, 4, w_in_of))
    ):
        back = None
        for j in range(width):
            part = dot32(weights(held, j), parts[:, D * j : D * (j + 1)].T)
            back = part if back is None else back + part
        grad_act = back.T
        gain_row = 0 if norm == 0 else 6
        unit = normed[...]
        vec_out[gain_row : gain_row + 1, :] = jnp.sum(grad_act * unit, axis=0, keepdims=True)
        vec_out[gain_row + 1 : gain_row + 2, :] = jnp.sum(grad_act, axis=0, keepdims=True)
        grad_norm = grad_act * vecs[gain_row : gain_row + 1, :]
        total = total + inv_std[...] * (
            grad_norm
            - jnp.mean(grad_norm, axis=1, keepdims=True)
            - unit * jnp.mean(grad_norm * unit, axis=1, keepdims=True)
        )
    grad_input[...] = total
    bottom = jnp.sum(gy, axis=0, keepdims=True)
    vec_out[5:6, :] = bottom
    vec_out[12:13, :] = bottom
    vec_out[13:16, :] = jnp.zeros((3, D), jnp.float32)
    vec_out[...] = vec_out[...].astype(jnp.bfloat16).astype(jnp.float32)


def layer_results(scalars, blocks, own, small):
    hbm = pl.BlockSpec(memory_space=pltpu.HBM)
    vmem = pl.BlockSpec(memory_space=pltpu.VMEM)
    rows = jax.ShapeDtypeStruct((TOK_DEV, D), jnp.float32)
    return pl.pallas_call(
        result_kernel,
        grid_spec=pltpu.PrefetchScalarGridSpec(
            num_scalar_prefetch=1,
            in_specs=[hbm] * (len(blocks) + 1) + [vmem] * len(small),
            out_specs=[vmem] * 3,
            scratch_shapes=[
                pltpu.VMEM((ALL_ROWS, D), jnp.bfloat16),
                pltpu.SemaphoreType.DMA((PIECES,)),
            ],
        ),
        out_shape=[rows, rows, jax.ShapeDtypeStruct((16, D), jnp.float32)],
        compiler_params=pltpu.CompilerParams(vmem_limit_bytes=40 * 2**20),
    )(scalars, *blocks, own, *small)


def unpack_kernel(factor, where, *refs):
    vec_ref, out_ref, held, sems = refs[REPS:]
    copies = []
    for turn in range(REPS):
        copies.append(
            pltpu.make_async_copy(refs[turn], held.at[where[1 + turn]], sems.at[turn])
        )
    for copy in copies:
        copy.start()
    for copy in copies:
        copy.wait()
    shard = where[0]
    for z in range(SHARDS):

        @pl.when(shard == z)
        def _(z=z):
            for slot, row in enumerate(VECTOR_ROWS[z]):
                for col in range(6):
                    out_ref[6 * row + col : 6 * row + col + 1, :] = (
                        vec_ref[slot : slot + 1, LANES * col : LANES * (col + 1)] * factor
                    )

            @pl.loop(0, REPS)
            def _(rep):
                for first, step, rows, blocks, place in PARTS[z]:
                    for block in range(blocks):
                        for col in range(6):
                            got = held[
                                rep,
                                place + rows * block : place + rows * (block + 1),
                                LANES * col : LANES * (col + 1),
                            ]
                            begin = first + step * rep + 6 * block + col
                            out_ref[pl.ds(begin, rows, stride=6 * blocks), :] = (
                                got.astype(jnp.float32) * factor
                            )


def unpack_grads(blocks, ids, vectors, shard, factor):
    return pl.pallas_call(
        functools.partial(unpack_kernel, factor),
        grid_spec=pltpu.PrefetchScalarGridSpec(
            num_scalar_prefetch=1,
            in_specs=[pl.BlockSpec(memory_space=pltpu.HBM)] * REPS
            + [pl.BlockSpec(memory_space=pltpu.VMEM)],
            out_specs=pl.BlockSpec(memory_space=pltpu.VMEM),
            scratch_shapes=[
                pltpu.VMEM((REPS, PIECE, D), jnp.bfloat16),
                pltpu.SemaphoreType.DMA((REPS,)),
            ],
        ),
        out_shape=jax.ShapeDtypeStruct((FLAT_ROWS, LANES), jnp.float32),
        compiler_params=pltpu.CompilerParams(vmem_limit_bytes=32 * 2**20),
    )(jnp.stack([shard] + ids), *blocks, vectors)


def gather_matrices(params, shard, rep):
    piece = pack_pieces(params, shard, [rep])[0]
    own = pack_pieces(params, shard, [rep * 0 + turn for turn in range(REPS)])
    reps = spread_ids(rep)
    blocks, ids = [], []
    for hop in range(1, SHARDS):
        piece = ring_step(piece)
        owner = (shard + SHARDS - hop) % SHARDS
        blocks += spread_in_plane(piece)
        ids += [owner * REPS + which for which in reps]
    return blocks, own.reshape(REPS * PIECE, D), ids


def gather_vectors(params, shard):
    mine = shard_vectors(params, shard)
    held = [mine.astype(jnp.bfloat16)]
    for _ in range(1, SHARDS):
        held.append(ring_step(held[-1]))
    turned = jnp.stack(held).astype(jnp.float32)
    order = (shard + SHARDS - jnp.arange(SHARDS)) % SHARDS
    return jnp.take(turned, order, axis=0).reshape(16, D)


def sum_everywhere(value):
    for flips in ((1, 1), (2, 2), (4, 4)):
        value = value + plane_permute(value, flips)
    total, moving = value, value
    for _ in range(1, SHARDS):
        moving = ring_step(moving)
        total = total + moving
    return total


def slots_by_piece(shard, rep):
    slots = []
    for owner in range(SHARDS):
        hop = (shard + SHARDS - owner + 3) % SHARDS
        for which in range(REPS):
            apart = rep ^ which
            kept = 1 - apart % 2
            core = which % 2
            across = apart & 6
            first = 2 + 2 * core
            place = jnp.where(
                across == 0, 2, jnp.where(across == 6, 1, jnp.where(across == first, 0, 3))
            )
            slots.append((kept * SHARDS + hop) * 4 + place)
    return slots


def scatter_sums(sent, kept):
    carried = None
    for turn in range(SHARDS):
        chip = kept[turn] + core_cross(sent[turn])
        pair = chip[2:4] + first_cross(chip[0:2])
        total = pair[0] + second_cross(pair[1])
        if carried is not None:
            total = total + carried
        if turn < SHARDS - 1:
            carried = ring_step(total)
    return total


def shard_vectors(params, shard):
    rows = jnp.asarray(VECTOR_ROWS, jnp.int32)[shard]
    return jnp.stack([lax.dynamic_slice_in_dim(params, rows[i] * D, D) for i in range(4)])


def on_device_rows(tokens, segment_ids, cotangent, params, moment_one, moment_two):
    shard = lax.axis_index("z")
    rep = lax.axis_index(PLANE)
    vecs = gather_vectors(params, shard)
    blocks, own, ids = gather_matrices(params, shard, rep)
    x_wide = tokens.astype(jnp.float32)
    centered = x_wide - jnp.mean(x_wide, axis=1, keepdims=True)
    variance = jnp.mean(centered * centered, axis=1, keepdims=True)
    inv_std = lax.rsqrt(variance + EPS_NORM)
    normed = centered * inv_std
    act_one = (normed * vecs[0] + vecs[1]).astype(jnp.bfloat16)
    act_two = (normed * vecs[6] + vecs[7]).astype(jnp.bfloat16)
    live_rows = (segment_ids >= 0)[:, None]
    grad_y = jnp.where(live_rows, cotangent, jnp.zeros_like(cotangent))
    cosine, sine = rotary_tables(positions_of(segment_ids))
    cosine, sine = cosine[:, 0], sine[:, 0]
    rest = jnp.ones((TOK_DEV, HD - ROT), jnp.float32)
    none = jnp.zeros_like(rest)
    gap = jnp.zeros_like(sine)
    rot_cos = jnp.concatenate([cosine, cosine, rest] * 2, axis=1)
    rot_up = jnp.concatenate([-sine, gap, none] * 2, axis=1)
    rot_down = jnp.concatenate([gap, sine, none] * 2, axis=1)
    slot_ids = jnp.arange(TOK_DEV, dtype=jnp.int32)
    allowed = (segment_ids[:, None] == segment_ids[None, :]) & (
        slot_ids[None, :] <= slot_ids[:, None]
    )
    scalars = jnp.stack([shard] + ids + slots_by_piece(shard, rep))
    small = (act_one, act_two, grad_y, vecs, rot_cos, rot_up, rot_down, allowed.astype(jnp.float32))
    made = weight_gradients(scalars, blocks, own, small)
    sent, kept = made[0:4], made[4:8]
    attn, hidden, grad_pre, grad_mixed, sums = made[8:]
    owned = scatter_sums(sent, kept)
    small = (tokens, normed, inv_std, grad_y, vecs, attn, hidden, grad_pre, grad_mixed, sums)
    output, grad_input, vec_grads = layer_results(scalars, blocks, own, small)
    vec_grads = sum_everywhere(vec_grads)
    own_vectors = lax.dynamic_index_in_dim(
        vec_grads.reshape(SHARDS, 4, D), shard, 0, keepdims=False
    )
    tokens_all = tokens.shape[0] * lax.axis_size(EVERY)
    grad_params = unpack_grads(
        spread_in_plane(owned), spread_ids(rep), own_vectors, shard, 1.0 / math.sqrt(tokens_all)
    ).reshape(-1)
    width = moment_one.shape[0]
    begin = rep * width
    param_share = lax.dynamic_slice_in_dim(params, begin, width)
    grad_share = lax.dynamic_slice_in_dim(grad_params, begin, width)
    upd_params, upd_first, upd_second = adam_update(param_share, moment_one, moment_two, grad_share)
    new_params = lax.all_gather(upd_params, PLANE, axis=0, tiled=True)
    return (output, grad_input, grad_params, new_params, upd_first, upd_second)


def solution(mesh):
    in_rows = mesh.shape["rep"] == REPS and mesh.shape["shard"] == SHARDS
    if in_rows:
        rep, shard = PLANE, "z"
        mesh = Mesh(mesh.devices.reshape(2, 2, 2, SHARDS), EVERY)
        body = on_device_rows
    else:
        rep, shard = ("rep",), "shard"
        body = on_device
    rows = rep + (shard,)
    owner = (shard,) + rep
    in_specs = (P(rows, None), P(rows), P(rows, None), P(shard), P(owner), P(owner))
    out_specs = (P(rows, None), P(rows, None), P(shard), P(shard), P(owner), P(owner))
    return jax.shard_map(body, mesh=mesh, in_specs=in_specs, out_specs=out_specs, check_vma=False)
```

```python
import functools
import math

import jax
import jax.numpy as jnp
from jax import lax
from jax.experimental import pallas as pl
from jax.experimental.pallas import tpu as pltpu
from jax.sharding import Mesh
from jax.sharding import PartitionSpec as P

D = 768
HEADS = 12
HD = 64
ROT = 16
FF = 3072
TOK_DEV = 128


EPS_NORM = 1e-05
ROPE_BASE = 10000.0
NEG_BIG = -1e30
BETA_ONE = 0.9
BETA_TWO = 0.95
ADAM_STEP = 3.0
LEARN_RATE = 0.05
DECAY = 0.01
ADAM_EPS = 1e-08
INV_ROOT_TWO = 0.7071067811865476
INV_ROOT_TWO_PI = 0.3989422804014327


def layout_offsets():
    q_width = HEADS * HD
    o_wqkv = 2 * D
    o_bqkv = o_wqkv + 3 * q_width * D
    o_wout = o_bqkv + 3 * q_width
    o_bout = o_wout + q_width * D
    o_gain2 = o_bout + D
    o_shift2 = o_gain2 + D
    o_win = o_shift2 + D
    o_bin = o_win + D * FF
    o_wout2 = o_bin + FF
    o_bout2 = o_wout2 + FF * D
    return (
        o_wqkv,
        o_bqkv,
        o_wout,
        o_bout,
        o_gain2,
        o_shift2,
        o_win,
        o_bin,
        o_wout2,
        o_bout2,
        o_bout2 + D,
    )


def split_params(flat16):
    q_width = HEADS * HD
    o_wqkv, o_bqkv, o_wout, o_bout, o_gain2, o_shift2, o_win, o_bin, o_wout2, o_bout2, o_end = (
        layout_offsets()
    )
    return (
        flat16[0:D],
        flat16[D:o_wqkv],
        flat16[o_wqkv:o_bqkv].reshape(D, 3 * q_width),
        flat16[o_bqkv:o_wout],
        flat16[o_wout:o_bout].reshape(q_width, D),
        flat16[o_bout:o_gain2],
        flat16[o_gain2:o_shift2],
        flat16[o_shift2:o_win],
        flat16[o_win:o_bin].reshape(D, FF),
        flat16[o_bin:o_wout2],
        flat16[o_wout2:o_bout2].reshape(FF, D),
        flat16[o_bout2:o_end],
    )


def positions_of(segments):
    count = segments.shape[0]
    slot_ids = jnp.arange(count, dtype=jnp.int32)
    before = jnp.concatenate([jnp.full((1,), -2, jnp.int32), segments[:-1]])
    begins = segments != before
    first_slot = lax.cummax(jnp.where(begins, slot_ids, 0), axis=0)
    return slot_ids - first_slot


def rotary_tables(positions):
    half = ROT // 2
    steps_j = jnp.arange(half, dtype=jnp.float32)
    freqs = jnp.power(jnp.float32(ROPE_BASE), -2.0 * steps_j / ROT)
    angle = positions.astype(jnp.float32)[:, None] * freqs[None, :]
    return (jnp.cos(angle)[:, None, :], jnp.sin(angle)[:, None, :])


def rotate(values, cosine, sine, sign):
    half = cosine.shape[-1]
    lower = values[..., :half]
    upper = values[..., half : 2 * half]
    rest = values[..., 2 * half :]
    return jnp.concatenate(
        [lower * cosine - sign * upper * sine, upper * cosine + sign * lower * sine, rest], axis=-1
    )


def gelu_exact(value):
    return value * 0.5 * (1.0 + lax.erf(value * INV_ROOT_TWO))


def gelu_slope(value):
    return (
        0.5 * (1.0 + lax.erf(value * INV_ROOT_TWO))
        + value * jnp.exp(-0.5 * value * value) * INV_ROOT_TWO_PI
    )


def masked_scores(q_blk, keys, seg_rows, seg_cols, begin_row):
    scale = q_blk.shape[-1] ** (-0.5)
    raw_scores = jnp.einsum("qhd,khd->hqk", q_blk, keys, preferred_element_type=jnp.float32) * scale
    row_ids = begin_row + jnp.arange(q_blk.shape[0], dtype=jnp.int32)
    col_ids = jnp.arange(keys.shape[0], dtype=jnp.int32)
    allowed = (seg_rows[:, None] == seg_cols[None, :]) & (col_ids[None, :] <= row_ids[:, None])
    return jnp.where(allowed[None], raw_scores, NEG_BIG)


def attend_forward(query16, key16, value16, segments):
    scores = masked_scores(query16, key16, segments, segments, 0)
    row_max = jnp.max(scores, axis=-1, keepdims=True)
    expd = jnp.exp(scores - row_max)
    row_total = jnp.sum(expd, axis=-1, keepdims=True)
    probs16 = (expd / row_total).astype(jnp.bfloat16)
    attn_blk = jnp.einsum("hqk,khd->qhd", probs16, value16, preferred_element_type=jnp.float32)
    pieces_out = attn_blk.astype(jnp.bfloat16)
    lse_list = [row_max + jnp.log(row_total)]
    return (pieces_out, lse_list)


def attend_backward(query16, key16, value16, attn16, lse_list, segments, grad_attn16):
    count = query16.shape[0]
    block = min(512, count)
    scale = query16.shape[-1] ** (-0.5)
    grad_query = []
    grad_key = jnp.zeros(key16.shape, jnp.float32)
    grad_value = jnp.zeros(value16.shape, jnp.float32)
    for turn, begin_row in enumerate(range(0, count, block)):
        stop_row = begin_row + block
        scores = masked_scores(query16, key16, segments, segments, begin_row)
        chances = jnp.exp(scores - lse_list[turn])
        chances16 = chances.astype(jnp.bfloat16)
        grad_value = grad_value.at[:stop_row].add(
            jnp.einsum("hqk,qhd->khd", chances16, grad_attn16, preferred_element_type=jnp.float32)
        )
        grad_chance = jnp.einsum(
            "qhd,khd->hqk", grad_attn16, value16, preferred_element_type=jnp.float32
        )
        delta = jnp.sum(grad_attn16.astype(jnp.float32) * attn16.astype(jnp.float32), axis=-1)
        grad_scores = (chances * (grad_chance - jnp.transpose(delta)[:, :, None]) * scale).astype(
            jnp.bfloat16
        )
        grad_query.append(
            jnp.einsum("hqk,khd->qhd", grad_scores, key16, preferred_element_type=jnp.float32)
        )
        grad_key = grad_key.at[:stop_row].add(
            jnp.einsum("hqk,qhd->khd", grad_scores, query16, preferred_element_type=jnp.float32)
        )
    return (grad_query[0], grad_key, grad_value)


def norm_back(grad_act, normed, inv_std, gain):
    grad_gain = jnp.sum(grad_act * normed, axis=0)
    grad_shift = jnp.sum(grad_act, axis=0)
    grad_norm = grad_act * gain.astype(jnp.float32)
    grad_x = inv_std * (
        grad_norm
        - jnp.mean(grad_norm, axis=1, keepdims=True)
        - normed * jnp.mean(grad_norm * normed, axis=1, keepdims=True)
    )
    return (grad_gain, grad_shift, grad_x)


def layer_forward(tokens, segments, pieces):
    (
        gain_one,
        shift_one,
        w_qkv,
        b_qkv,
        w_out,
        b_out,
        gain_two,
        shift_two,
        w_in,
        b_in,
        w_out2,
        b_out2,
    ) = pieces
    count = tokens.shape[0]
    x_wide = tokens.astype(jnp.float32)
    row_mean = jnp.mean(x_wide, axis=1, keepdims=True)
    centered = x_wide - row_mean
    variance = jnp.mean(centered * centered, axis=1, keepdims=True)
    inv_std = lax.rsqrt(variance + EPS_NORM)
    normed = centered * inv_std
    act_one = (normed * gain_one.astype(jnp.float32) + shift_one.astype(jnp.float32)).astype(
        jnp.bfloat16
    )
    act_two = (normed * gain_two.astype(jnp.float32) + shift_two.astype(jnp.float32)).astype(
        jnp.bfloat16
    )
    mixed = jnp.dot(act_one, w_qkv, preferred_element_type=jnp.float32) + b_qkv.astype(jnp.float32)
    mixed = mixed.reshape(count, 3, HEADS, HD)
    cosine, sine = rotary_tables(positions_of(segments))
    query16 = rotate(mixed[:, 0], cosine, sine, 1.0).astype(jnp.bfloat16)
    key16 = rotate(mixed[:, 1], cosine, sine, 1.0).astype(jnp.bfloat16)
    value16 = mixed[:, 2].astype(jnp.bfloat16)
    attn16, lse_list = attend_forward(query16, key16, value16, segments)
    proj = jnp.dot(
        attn16.reshape(count, HEADS * HD), w_out, preferred_element_type=jnp.float32
    ) + b_out.astype(jnp.float32)
    pre = jnp.dot(act_two, w_in, preferred_element_type=jnp.float32) + b_in.astype(jnp.float32)
    hidden16 = gelu_exact(pre).astype(jnp.bfloat16)
    feed = jnp.dot(hidden16, w_out2, preferred_element_type=jnp.float32) + b_out2.astype(
        jnp.float32
    )
    output = x_wide + proj + feed
    saved = (
        normed,
        inv_std,
        act_one,
        act_two,
        query16,
        key16,
        value16,
        attn16,
        lse_list,
        cosine,
        sine,
        pre,
        hidden16,
    )
    return (output, saved)


def layer_backward(cotangent, segments, pieces, saved):
    (
        gain_one,
        shift_one,
        w_qkv,
        b_qkv,
        w_out,
        b_out,
        gain_two,
        shift_two,
        w_in,
        b_in,
        w_out2,
        b_out2,
    ) = pieces
    (
        normed,
        inv_std,
        act_one,
        act_two,
        query16,
        key16,
        value16,
        attn16,
        lse_list,
        cosine,
        sine,
        pre,
        hidden16,
    ) = saved
    count = cotangent.shape[0]
    contract_rows = (((0,), (0,)), ((), ()))
    contract_cols = (((1,), (1,)), ((), ()))
    live_rows = (segments >= 0).astype(jnp.float32)[:, None]
    grad_y = cotangent.astype(jnp.float32) * live_rows
    grad_y16 = grad_y.astype(jnp.bfloat16)
    grad_b_out = jnp.sum(grad_y, axis=0)
    attn_flat = attn16.reshape(count, HEADS * HD)
    grad_w_out = lax.dot_general(
        attn_flat, grad_y16, contract_rows, preferred_element_type=jnp.float32
    )
    grad_w_out2 = lax.dot_general(
        hidden16, grad_y16, contract_rows, preferred_element_type=jnp.float32
    )
    grad_hidden = lax.dot_general(
        grad_y16, w_out2, contract_cols, preferred_element_type=jnp.float32
    )
    grad_pre = grad_hidden * gelu_slope(pre)
    grad_b_in = jnp.sum(grad_pre, axis=0)
    grad_pre16 = grad_pre.astype(jnp.bfloat16)
    grad_w_in = lax.dot_general(
        act_two, grad_pre16, contract_rows, preferred_element_type=jnp.float32
    )
    grad_act_two = lax.dot_general(
        grad_pre16, w_in, contract_cols, preferred_element_type=jnp.float32
    )
    grad_attn16 = (
        lax.dot_general(grad_y16, w_out, contract_cols, preferred_element_type=jnp.float32)
        .astype(jnp.bfloat16)
        .reshape(count, HEADS, HD)
    )
    grad_query, grad_key, grad_value = attend_backward(
        query16, key16, value16, attn16, lse_list, segments, grad_attn16
    )
    grad_query = rotate(grad_query, cosine, sine, -1.0)
    grad_key = rotate(grad_key, cosine, sine, -1.0)
    grad_mixed = jnp.stack([grad_query, grad_key, grad_value], axis=1).reshape(
        count, 3 * HEADS * HD
    )
    grad_b_qkv = jnp.sum(grad_mixed, axis=0)
    grad_mixed16 = grad_mixed.astype(jnp.bfloat16)
    grad_w_qkv = lax.dot_general(
        act_one, grad_mixed16, contract_rows, preferred_element_type=jnp.float32
    )
    grad_act_one = lax.dot_general(
        grad_mixed16, w_qkv, contract_cols, preferred_element_type=jnp.float32
    )
    gain_grad_one, shift_grad_one, grad_x_one = norm_back(grad_act_one, normed, inv_std, gain_one)
    gain_grad_two, shift_grad_two, grad_x_two = norm_back(grad_act_two, normed, inv_std, gain_two)
    grad_in = grad_y + grad_x_one + grad_x_two
    return (
        grad_in,
        [
            gain_grad_one,
            shift_grad_one,
            grad_w_qkv,
            grad_b_qkv,
            grad_w_out,
            grad_b_out,
            gain_grad_two,
            shift_grad_two,
            grad_w_in,
            grad_b_in,
            grad_w_out2,
            grad_b_out,
        ],
    )


def flatten_grads(parts, total_len):
    used = layout_offsets()[-1]
    rounded = [part.astype(jnp.bfloat16).reshape(-1) for part in parts]
    return jnp.concatenate(rounded + [jnp.zeros((total_len - used,), jnp.bfloat16)])


def adam_update(weights, first_moment, second_moment, gradient):
    new_first = BETA_ONE * first_moment + (1.0 - BETA_ONE) * gradient
    new_second = BETA_TWO * second_moment + (1.0 - BETA_TWO) * gradient * gradient
    unbiased_first = new_first / (1.0 - BETA_ONE**ADAM_STEP)
    unbiased_second = new_second / (1.0 - BETA_TWO**ADAM_STEP)
    new_weights = weights - LEARN_RATE * (
        unbiased_first / (jnp.sqrt(unbiased_second) + ADAM_EPS) + DECAY * weights
    )
    return (new_weights, new_first, new_second)


def on_device(tokens, segment_ids, cotangent, params, moment_one, moment_two):
    gathered = lax.all_gather(params.astype(jnp.bfloat16), "shard", axis=0, tiled=True)
    total_len = gathered.shape[0]
    pieces = split_params(gathered)
    output, saved = layer_forward(tokens, segment_ids, pieces)
    grad_input, parts = layer_backward(cotangent, segment_ids, pieces, saved)
    local_grad = flatten_grads(parts, total_len)
    owned = lax.psum_scatter(local_grad, "shard", scatter_dimension=0, tiled=True).astype(
        jnp.float32
    )
    tokens_all = tokens.shape[0] * lax.axis_size("rep") * lax.axis_size("shard")
    factor = 1.0 / math.sqrt(tokens_all)
    width = moment_one.shape[0]
    begin = lax.axis_index("rep") * width
    param_share = lax.dynamic_slice_in_dim(params, begin, width)
    share = lax.psum_scatter(owned, "rep", scatter_dimension=0, tiled=True)
    grad_share = share * factor
    upd_params, upd_first, upd_second = adam_update(param_share, moment_one, moment_two, grad_share)
    grad_params, new_params = (
        lax.all_gather(grad_share, "rep", axis=0, tiled=True),
        lax.all_gather(upd_params, "rep", axis=0, tiled=True),
    )
    return (output, grad_input, grad_params, new_params, upd_first, upd_second)


LANES = 128
REPS = 8
SHARDS = 4
PIECE = 288
FLAT_ROWS = 13848
MOVED = PIECE * D // LANES


PARTS = (
    ((12, 1728, 96, 3, 0),),
    ((6, 576, 96, 1, 0), (4632, 1152, 48, 4, 96)),
    ((0, 1152, 48, 4, 0), (9240, 576, 96, 1, 192)),
    ((0, 1728, 288, 1, 0),),
)
VECTOR_ROWS = ((0, 1, 2306, 2307), (0, 769, 770, 771), (1536, 1537, 1538, 1539), (2304, 2305, 2306, 2307))


PLANE = ("y", "x", "core")
EVERY = PLANE + ("z",)
HOPS = (1, 2, 3, 0)


def plane_permute(value, flips):
    return lax.ppermute(value, PLANE, [(i, i ^ flips[i % 2]) for i in range(REPS)])


def first_cross(value):
    return plane_permute(value, (2, 4))


def second_cross(value):
    return plane_permute(value, (4, 2))


def core_cross(value):
    return plane_permute(value, (1, 1))


def ring_step(value):
    return lax.ppermute(value, "z", [(i, (i + 1) % SHARDS) for i in range(SHARDS)])


def flips_of(rep):
    core = rep % 2
    first = 2 + 2 * core
    return (0, first, 6 - first, 6)


def spread_in_plane(piece):
    first = first_cross(piece)
    second = second_cross(piece)
    both = second_cross(first)
    mine = [piece, first, second, both]
    return mine + [core_cross(value) for value in mine]


def spread_ids(rep):
    other = rep ^ 1
    return [rep ^ flip for flip in flips_of(rep)] + [other ^ flip for flip in flips_of(other)]


def pack_kernel(where, flat_ref, out_ref, held, sems):
    shard = where[0]
    turns = out_ref.shape[0]
    for z in range(SHARDS):

        @pl.when(shard == z)
        def _(z=z):
            def copies_of(turn):
                slot = turn % 2
                rep = where[1 + turn]
                copies = []
                at = 0
                for part, (first, step, _, _, _) in enumerate(PARTS[z]):
                    lead = first % 8
                    count = step + (8 if lead else 0)
                    begin = pl.multiple_of(first - lead + step * rep, 8)
                    copies.append(
                        pltpu.make_async_copy(
                            flat_ref.at[pl.ds(begin, count)],
                            held.at[slot, pl.ds(at, count)],
                            sems.at[slot, part],
                        )
                    )
                    at += count
                return copies

            for copy in copies_of(0):
                copy.start()

            @pl.loop(0, turns)
            def _(turn):
                @pl.when(turn + 1 < turns)
                def _():
                    for copy in copies_of(turn + 1):
                        copy.start()

                slot = turn % 2
                at = 0
                for copy, (first, step, rows, blocks, place) in zip(copies_of(turn), PARTS[z]):
                    copy.wait()
                    lead = first % 8
                    for block in range(blocks):
                        for col in range(6):
                            begin = at + lead + 6 * block + col
                            got = held[slot, pl.ds(begin, rows, stride=6 * blocks), :]
                            out_ref[
                                turn,
                                place + rows * block : place + rows * (block + 1),
                                LANES * col : LANES * (col + 1),
                            ] = got.astype(jnp.bfloat16)
                    at += step + (8 if lead else 0)


def pack_pieces(params, shard, reps):
    return pl.pallas_call(
        pack_kernel,
        grid_spec=pltpu.PrefetchScalarGridSpec(
            num_scalar_prefetch=1,
            in_specs=[pl.BlockSpec(memory_space=pltpu.HBM)],
            out_specs=pl.BlockSpec(memory_space=pltpu.VMEM),
            scratch_shapes=[
                pltpu.VMEM((2, MOVED + 16, LANES), jnp.float32),
                pltpu.SemaphoreType.DMA((2, 2)),
            ],
        ),
        out_shape=jax.ShapeDtypeStruct((len(reps), PIECE, D), jnp.bfloat16),
        compiler_params=pltpu.CompilerParams(vmem_limit_bytes=16 * 2**20),
    )(jnp.stack([shard] + reps), params.reshape(FLAT_ROWS, LANES))


PIECES = SHARDS * REPS
GROUPS = 9
ALL_ROWS = PIECES * PIECE


def fetch_pieces(ids, blocks, own, shard, held, sems):
    views = []
    for block in blocks:
        views += [block.at[p] for p in range(4)] if len(block.shape) == 3 else [block]
    ids = ids + [shard * REPS + r for r in range(REPS)]
    views += [own.at[pl.ds(r * PIECE, PIECE)] for r in range(REPS)]
    for which, view in zip(ids, views):
        row = pl.multiple_of(which * PIECE, 16)
        pltpu.make_async_copy(view, held.at[pl.ds(row, PIECE)], sems.at[which]).start()

    def arrive(owner):
        for r in range(REPS):
            at = owner * REPS + r
            pltpu.make_async_copy(
                own.at[pl.ds(0, PIECE)], held.at[pl.ds(at * PIECE, PIECE)], sems.at[at]
            ).wait()

    return arrive


def rows_of(held, shard, begin, rows):
    return jnp.concatenate(
        [held[pl.ds((shard * REPS + r) * PIECE + begin, rows), :] for r in range(REPS)], axis=0
    )


def w_qkv_of(held, j):
    return rows_of(held, 0, 96 * j, 96)


def w_out_of(held):
    return rows_of(held, 1, 0, 96)


def w_in_of(held, j):
    return jnp.concatenate([rows_of(held, 1, 96 + 48 * j, 48), rows_of(held, 2, 48 * j, 48)], axis=0)


def w_out2_of(held, j):
    if j == 0:
        return rows_of(held, 2, 192, 96)
    return held[pl.ds(3 * REPS * PIECE + D * (j - 1), D), :]


def dot32(a, b):
    return jnp.dot(a, b, preferred_element_type=jnp.float32)


def gradient_kernel(where, *refs):
    count = PIECES - REPS
    blocks, own = refs[:GROUPS], refs[GROUPS]
    (act_one, act_two, grad_y, vecs, rot_cos, rot_up, rot_down, bias) = refs[GROUPS + 1 : GROUPS + 9]
    outs = refs[GROUPS + 9 : GROUPS + 9 + 14]
    sent, kept = outs[0:4], outs[4:8]
    matrices, attn_out, hidden_out, pre_out, mixed_out, sums_out = outs[8:14]
    held, grads, query, key, value, grad_attn, sems, out_sems = refs[GROUPS + 23 :]
    shard = where[0]
    arrive = fetch_pieces([where[1 + t] for t in range(count)], blocks, own, shard, held, sems)
    slot_row = lambda z, r: pl.multiple_of(where[1 + count + z * REPS + r] * PIECE, 16)

    def keep_rows(z, begin, rows, part):
        for r in range(part.shape[0] // rows):
            grads[pl.ds(slot_row(z, r) + begin, rows), :] = part[rows * r : rows * (r + 1), :]

    arrive(0)
    act1 = act_one[...]
    for j, out in enumerate((query, key, value)):
        got = dot32(act1, w_qkv_of(held, j)) + vecs[2 + j : 3 + j, :]
        if j < 2:
            for p in range(6):
                lanes = slice(LANES * p, LANES * (p + 1))
                part = got[:, lanes]
                part = (
                    part * rot_cos[...]
                    + pltpu.roll(part, LANES - 8, 1) * rot_up[...]
                    + pltpu.roll(part, 8, 1) * rot_down[...]
                )
                out[:, lanes] = part.astype(jnp.bfloat16)
        else:
            out[...] = got.astype(jnp.bfloat16)
    gy_t = grad_y[...].T
    arrive(1)
    grad_attn[...] = dot32(w_out_of(held), gy_t).T.astype(jnp.bfloat16)

    arrive(2)
    arrive(3)
    saving = pltpu.make_async_copy(held, matrices, out_sems.at[PIECES])
    saving.start()
    low = lax.broadcasted_iota(jnp.int32, (LANES, LANES), 1) < HD
    scale = HD ** (-0.5)
    for p in range(6):
        lanes = slice(LANES * p, LANES * (p + 1))
        q2, k2, v2, g2 = (ref[:, lanes] for ref in (query, key, value, grad_attn))
        k2_t, v2_t = k2.T, v2.T
        attn_parts, value_parts, query_parts, key_parts = [], [], [], []
        for half in range(2):
            here = low if half == 0 else ~low
            zero = jnp.zeros_like(q2)
            scores = dot32(jnp.where(here, q2, zero), k2_t) * scale
            scores = jnp.where(bias[...] > 0.5, scores, NEG_BIG)
            expd = jnp.exp(scores - jnp.max(scores, axis=1, keepdims=True))
            chances = expd / jnp.sum(expd, axis=1, keepdims=True)
            chances16 = chances.astype(jnp.bfloat16)
            attn = dot32(chances16, v2)
            attn16 = attn.astype(jnp.bfloat16)
            masked = jnp.where(here, g2, zero)
            delta = jnp.sum(
                masked.astype(jnp.float32) * attn16.astype(jnp.float32), axis=1, keepdims=True
            )
            grad_chance = dot32(masked, v2_t)
            slope = (chances * (grad_chance - delta) * scale).astype(jnp.bfloat16)
            attn_parts.append(attn16)
            value_parts.append(dot32(chances16.T, g2))
            query_parts.append(dot32(slope, k2))
            key_parts.append(dot32(slope.T, q2))
        attn_out[:, lanes] = jnp.where(low, *attn_parts)
        for j, parts in enumerate((query_parts, key_parts, value_parts)):
            part = jnp.where(low, *parts)
            if j < 2:
                part = (
                    part * rot_cos[...]
                    - pltpu.roll(part, LANES - 8, 1) * rot_up[...]
                    - pltpu.roll(part, 8, 1) * rot_down[...]
                )
            wide = slice(D * j + LANES * p, D * j + LANES * (p + 1))
            sums_out[2 + j : 3 + j, lanes] = jnp.sum(part, axis=0, keepdims=True)
            mixed_out[:, wide] = part.astype(jnp.bfloat16)

    gy = grad_y[...]
    act1_t = act1.T
    for j in range(3):
        keep_rows(
            0, 96 * j, 96, dot32(act1_t, mixed_out[:, D * j : D * (j + 1)]).astype(jnp.bfloat16)
        )
    keep_rows(1, 0, 96, dot32(attn_out[...].T, gy).astype(jnp.bfloat16))

    act2 = act_two[...]
    act2_t = act2.T
    for j in range(4):
        wide = slice(D * j, D * (j + 1))
        pre = dot32(act2, w_in_of(held, j)) + vecs[8 + j : 9 + j, :]
        bell = 0.5 * (1.0 + lax.erf(pre * INV_ROOT_TWO))
        hidden = (pre * bell).astype(jnp.bfloat16)
        hidden_out[:, wide] = hidden
        grad_hidden = dot32(w_out2_of(held, j), gy_t).T
        grad_pre = grad_hidden * (bell + pre * jnp.exp(-0.5 * pre * pre) * INV_ROOT_TWO_PI)
        sums_out[8 + j : 9 + j, :] = jnp.sum(grad_pre, axis=0, keepdims=True)
        grad_pre16 = grad_pre.astype(jnp.bfloat16)
        pre_out[:, wide] = grad_pre16
        w2 = dot32(hidden.T, gy).astype(jnp.bfloat16)
        if j == 0:
            keep_rows(2, 192, 96, w2)
        else:
            at = D * (j - 1)
            while at < D * j:
                r, begin = divmod(at, PIECE)
                rows = min(PIECE - begin, D * j - at)
                grads[pl.ds(slot_row(3, r) + begin, rows), :] = w2[
                    at - D * (j - 1) : at - D * (j - 1) + rows, :
                ]
                at += rows
        w1 = dot32(act2_t, grad_pre16).astype(jnp.bfloat16)
        keep_rows(1, 96 + 48 * j, 48, w1[: D // 2])
        keep_rows(2, 48 * j, 48, w1[D // 2 :])
    copies = []
    for turn, out in enumerate(sent + kept):
        for p in range(4):
            copies.append(
                pltpu.make_async_copy(
                    grads.at[pl.ds((turn * 4 + p) * PIECE, PIECE)],
                    out.at[p],
                    out_sems.at[turn * 4 + p],
                )
            )
    for copy in copies:
        copy.start()
    for copy in copies:
        copy.wait()
    saving.wait()


def weight_gradients(scalars, blocks, own, small):
    hbm = pl.BlockSpec(memory_space=pl.ANY)
    vmem = pl.BlockSpec(memory_space=pltpu.VMEM)
    bf16 = jnp.bfloat16
    group = jax.ShapeDtypeStruct((4, PIECE, D), bf16)
    return pl.pallas_call(
        gradient_kernel,
        grid_spec=pltpu.PrefetchScalarGridSpec(
            num_scalar_prefetch=1,
            in_specs=[hbm] * (len(blocks) + 1) + [vmem] * len(small),
            out_specs=[hbm] * 9 + [vmem] * 5,
            scratch_shapes=[
                pltpu.VMEM((ALL_ROWS, D), bf16),
                pltpu.VMEM((ALL_ROWS, D), bf16),
                pltpu.VMEM((TOK_DEV, D), bf16),
                pltpu.VMEM((TOK_DEV, D), bf16),
                pltpu.VMEM((TOK_DEV, D), bf16),
                pltpu.VMEM((TOK_DEV, D), bf16),
                pltpu.SemaphoreType.DMA((PIECES,)),
                pltpu.SemaphoreType.DMA((PIECES + 1,)),
            ],
        ),
        out_shape=[group] * 8
        + [
            jax.ShapeDtypeStruct((ALL_ROWS, D), bf16),
            jax.ShapeDtypeStruct((TOK_DEV, D), bf16),
            jax.ShapeDtypeStruct((TOK_DEV, FF), bf16),
            jax.ShapeDtypeStruct((TOK_DEV, FF), bf16),
            jax.ShapeDtypeStruct((TOK_DEV, 3 * D), bf16),
            jax.ShapeDtypeStruct((16, D), jnp.float32),
        ],
        compiler_params=pltpu.CompilerParams(vmem_limit_bytes=56 * 2**20),
    )(scalars, *blocks, own, *small)


def result_kernel(matrices, *refs):
    (tokens, normed, inv_std, grad_y, vecs, attn, hidden, grad_pre, grad_mixed, sums) = refs[:10]
    output, grad_input, vec_out, held, sems = refs[10:]
    copies = []
    for z in range(SHARDS):
        rows = pl.ds(z * REPS * PIECE, REPS * PIECE)
        copies.append(pltpu.make_async_copy(matrices.at[rows], held.at[rows], sems.at[z]))
    for copy in copies:
        copy.start()
    for copy in copies:
        copy.wait()
    total = dot32(attn[...], w_out_of(held)) + vecs[5:6, :]
    for j in range(4):
        total = total + dot32(hidden[:, D * j : D * (j + 1)], w_out2_of(held, j))
    output[...] = tokens[...].astype(jnp.float32) + (total + vecs[12:13, :])
    vec_out[...] = sums[...]
    gy = grad_y[...].astype(jnp.float32)
    total = gy
    for norm, (parts, width, weights) in enumerate(
        ((grad_mixed, 3, w_qkv_of), (grad_pre, 4, w_in_of))
    ):
        back = None
        for j in range(width):
            part = dot32(weights(held, j), parts[:, D * j : D * (j + 1)].T)
            back = part if back is None else back + part
        grad_act = back.T
        gain_row = 0 if norm == 0 else 6
        unit = normed[...]
        vec_out[gain_row : gain_row + 1, :] = jnp.sum(grad_act * unit, axis=0, keepdims=True)
        vec_out[gain_row + 1 : gain_row + 2, :] = jnp.sum(grad_act, axis=0, keepdims=True)
        grad_norm = grad_act * vecs[gain_row : gain_row + 1, :]
        total = total + inv_std[...] * (
            grad_norm
            - jnp.mean(grad_norm, axis=1, keepdims=True)
            - unit * jnp.mean(grad_norm * unit, axis=1, keepdims=True)
        )
    grad_input[...] = total
    bottom = jnp.sum(gy, axis=0, keepdims=True)
    vec_out[5:6, :] = bottom
    vec_out[12:13, :] = bottom
    vec_out[13:16, :] = jnp.zeros((3, D), jnp.float32)
    vec_out[...] = vec_out[...].astype(jnp.bfloat16).astype(jnp.float32)


def layer_results(matrices, small):
    hbm = pl.BlockSpec(memory_space=pl.ANY)
    vmem = pl.BlockSpec(memory_space=pltpu.VMEM)
    rows = jax.ShapeDtypeStruct((TOK_DEV, D), jnp.float32)
    return pl.pallas_call(
        result_kernel,
        in_specs=[hbm] + [vmem] * len(small),
        out_specs=[vmem] * 3,
        scratch_shapes=[
            pltpu.VMEM((ALL_ROWS, D), jnp.bfloat16),
            pltpu.SemaphoreType.DMA((SHARDS,)),
        ],
        out_shape=[rows, rows, jax.ShapeDtypeStruct((16, D), jnp.float32)],
        compiler_params=pltpu.CompilerParams(vmem_limit_bytes=40 * 2**20),
    )(matrices, *small)


SHARE = FLAT_ROWS // REPS
BEGINS = tuple(SHARE * r // 16 * 16 for r in range(REPS)) + (FLAT_ROWS,)
SHARE_ROWS = 1760
STEP = 288


def align_kernel(where, one_ref, two_ref, out_ref, held):
    for r in range(REPS):

        @pl.when(where[0] == r)
        def _(r=r):
            lead = SHARE * r - BEGINS[r]
            for turn, ref in enumerate((one_ref, two_ref)):
                held[0:16, :] = jnp.zeros((16, LANES), jnp.float32)
                held[SHARE_ROWS - 32 :, :] = jnp.zeros((32, LANES), jnp.float32)
                held[lead : lead + SHARE, :] = ref[...]
                out_ref[turn] = held[...].astype(jnp.bfloat16)


def align_moments(moment_one, moment_two, rep):
    return pl.pallas_call(
        align_kernel,
        grid_spec=pltpu.PrefetchScalarGridSpec(
            num_scalar_prefetch=1,
            in_specs=[pl.BlockSpec(memory_space=pltpu.VMEM)] * 2,
            out_specs=pl.BlockSpec(memory_space=pltpu.VMEM),
            scratch_shapes=[pltpu.VMEM((SHARE_ROWS, LANES), jnp.float32)],
        ),
        out_shape=jax.ShapeDtypeStruct((2, SHARE_ROWS, LANES), jnp.bfloat16),
        compiler_params=pltpu.CompilerParams(vmem_limit_bytes=16 * 2**20),
    )(jnp.stack([rep]), moment_one.reshape(SHARE, LANES), moment_two.reshape(SHARE, LANES))


def update_kernel(factor, where, *refs):
    blocks = refs[:REPS]
    vec_ref, params, moments, grad_out, params_out = refs[REPS : REPS + 5]
    held, grad, weight, moment, sems, out_sems = refs[REPS + 5 :]
    copies = []
    for turn in range(REPS):
        copies.append(
            pltpu.make_async_copy(blocks[turn], held.at[where[1 + turn]], sems.at[turn])
        )
    copies.append(pltpu.make_async_copy(moments, moment, sems.at[REPS]))
    copies.append(pltpu.make_async_copy(params, weight, sems.at[REPS + 1]))
    for copy in copies:
        copy.start()
    for copy in copies[:REPS]:
        copy.wait()
    shard = where[0]
    for z in range(SHARDS):

        @pl.when(shard == z)
        def _(z=z):
            for slot, row in enumerate(VECTOR_ROWS[z]):
                for col in range(6):
                    grad[6 * row + col : 6 * row + col + 1, :] = (
                        vec_ref[slot : slot + 1, LANES * col : LANES * (col + 1)] * factor
                    )

            @pl.loop(0, REPS)
            def _(rep):
                for first, step, rows, blocks, place in PARTS[z]:
                    for block in range(blocks):
                        for col in range(6):
                            got = held[
                                rep,
                                place + rows * block : place + rows * (block + 1),
                                LANES * col : LANES * (col + 1),
                            ]
                            begin = first + step * rep + 6 * block + col
                            grad[pl.ds(begin, rows, stride=6 * blocks), :] = (
                                got.astype(jnp.float32) * factor
                            )

    saving = [pltpu.make_async_copy(grad, grad_out, out_sems.at[REPS])]
    saving[0].start()
    for copy in copies[REPS:]:
        copy.wait()
    for r in range(REPS):
        base = BEGINS[r]
        length = BEGINS[r + 1] - base
        if r > 0:
            tail = base - BEGINS[r - 1]
            moment[r, :, 0:16, :] = moment[r, :, 0:16, :] + moment[r - 1, :, tail : tail + 16, :]

        def renew(at, rows, r=r, base=base):
            here = pl.ds(pl.multiple_of(base + at, 8), rows)
            there = pl.ds(pl.multiple_of(at, 16), rows)
            updated, _, _ = adam_update(
                weight[here, :],
                moment[r, 0, there, :].astype(jnp.float32),
                moment[r, 1, there, :].astype(jnp.float32),
                grad[here, :],
            )
            weight[here, :] = updated

        @pl.loop(0, length // STEP)
        def _(turn):
            renew(turn * STEP, STEP)

        if length % STEP:
            renew(length // STEP * STEP, length % STEP)
        rows = pl.ds(base, length)
        saving.append(
            pltpu.make_async_copy(weight.at[rows], params_out.at[rows], out_sems.at[r])
        )
        saving[-1].start()
    for copy in saving:
        copy.wait()


def update_shard(blocks, ids, vectors, params, moments, shard, factor):
    anywhere = pl.BlockSpec(memory_space=pl.ANY)
    flat = jax.ShapeDtypeStruct((FLAT_ROWS, LANES), jnp.float32)
    return pl.pallas_call(
        functools.partial(update_kernel, factor),
        grid_spec=pltpu.PrefetchScalarGridSpec(
            num_scalar_prefetch=1,
            in_specs=[anywhere] * REPS + [pl.BlockSpec(memory_space=pltpu.VMEM)] + [anywhere] * 2,
            out_specs=[anywhere] * 2,
            scratch_shapes=[
                pltpu.VMEM((REPS, PIECE, D), jnp.bfloat16),
                pltpu.VMEM((FLAT_ROWS, LANES), jnp.float32),
                pltpu.VMEM((FLAT_ROWS, LANES), jnp.float32),
                pltpu.VMEM((REPS, 2, SHARE_ROWS, LANES), jnp.bfloat16),
                pltpu.SemaphoreType.DMA((REPS + 2,)),
                pltpu.SemaphoreType.DMA((REPS + 1,)),
            ],
        ),
        out_shape=[flat, flat],
        compiler_params=pltpu.CompilerParams(vmem_limit_bytes=40 * 2**20),
    )(jnp.stack([shard] + ids), *blocks, vectors, params.reshape(FLAT_ROWS, LANES), moments)


def gather_matrices(params, shard, rep):
    piece = pack_pieces(params, shard, [rep])[0]
    own = pack_pieces(params, shard, [rep * 0 + turn for turn in range(REPS)])
    reps = spread_ids(rep)
    blocks, ids = [], []
    for hop in range(1, SHARDS):
        piece = ring_step(piece)
        owner = (shard + SHARDS - hop) % SHARDS
        if hop < SHARDS - 1:
            first = first_cross(piece)
            mine = jnp.stack([piece, first, second_cross(piece), second_cross(first)])
            blocks += [mine, core_cross(mine)]
        else:
            blocks += spread_in_plane(piece)
        ids += [owner * REPS + which for which in reps]
    mine = jnp.stack(blocks[4:8])
    return blocks[:4] + [mine] + blocks[8:], own.reshape(REPS * PIECE, D), ids


def ring_shift(value, hop):
    return lax.ppermute(value, "z", [(i, (i + hop) % SHARDS) for i in range(SHARDS)])


def gather_vectors(params, shard):
    mine = shard_vectors(params, shard).astype(jnp.bfloat16)
    held = [mine] + [ring_shift(mine, hop) for hop in range(1, SHARDS)]
    turned = jnp.stack(held).astype(jnp.float32)
    order = (shard + SHARDS - jnp.arange(SHARDS)) % SHARDS
    return jnp.take(turned, order, axis=0).reshape(16, D)


def sum_in_plane(value):
    for flips in ((1, 1), (2, 2), (4, 4)):
        value = value + plane_permute(value, flips)
    return value


def sum_over_shards(value):
    return value + ring_shift(value, 1) + ring_shift(value, 2) + ring_shift(value, 3)


def slots_by_piece(shard, rep):
    slots = []
    for owner in range(SHARDS):
        hop = (shard + SHARDS - owner + 3) % SHARDS
        for which in range(REPS):
            apart = rep ^ which
            kept = 1 - apart % 2
            core = which % 2
            across = apart & 6
            first = 2 + 2 * core
            place = jnp.where(
                across == 0, 2, jnp.where(across == 6, 1, jnp.where(across == first, 0, 3))
            )
            slots.append((kept * SHARDS + hop) * 4 + place)
    return slots


def scatter_sums(sent, kept, small, results):
    carried = None
    for turn in range(SHARDS):
        chip = kept[turn] + core_cross(sent[turn])
        pair = chip[2:4] + first_cross(chip[0:2])
        if turn == 0:
            pair, small = lax.optimization_barrier((pair, small))
            output, grad_input, vectors = results(small)
        elif turn == 1:
            pair, vectors = lax.optimization_barrier((pair, vectors))
            vectors = sum_in_plane(vectors)
        elif turn == 2:
            pair, vectors = lax.optimization_barrier((pair, vectors))
            vectors = sum_over_shards(vectors)
        else:
            pair, vectors = lax.optimization_barrier((pair, vectors))
        total = pair[0] + second_cross(pair[1])
        if carried is not None:
            total = total + carried
        if turn < SHARDS - 1:
            carried = ring_step(total)
    return total, output, grad_input, vectors


def shard_vectors(params, shard):
    rows = jnp.asarray(VECTOR_ROWS, jnp.int32)[shard]
    return jnp.stack([lax.dynamic_slice_in_dim(params, rows[i] * D, D) for i in range(4)])


def on_device_rows(tokens, segment_ids, cotangent, params, moment_one, moment_two):
    shard = lax.axis_index("z")
    rep = lax.axis_index(PLANE)
    vecs = gather_vectors(params, shard)
    blocks, own, ids = gather_matrices(params, shard, rep)
    x_wide = tokens.astype(jnp.float32)
    centered = x_wide - jnp.mean(x_wide, axis=1, keepdims=True)
    variance = jnp.mean(centered * centered, axis=1, keepdims=True)
    inv_std = lax.rsqrt(variance + EPS_NORM)
    normed = centered * inv_std
    act_one = (normed * vecs[0] + vecs[1]).astype(jnp.bfloat16)
    act_two = (normed * vecs[6] + vecs[7]).astype(jnp.bfloat16)
    live_rows = (segment_ids >= 0)[:, None]
    grad_y = jnp.where(live_rows, cotangent, jnp.zeros_like(cotangent))
    cosine, sine = rotary_tables(positions_of(segment_ids))
    cosine, sine = cosine[:, 0], sine[:, 0]
    rest = jnp.ones((TOK_DEV, HD - ROT), jnp.float32)
    none = jnp.zeros_like(rest)
    gap = jnp.zeros_like(sine)
    rot_cos = jnp.concatenate([cosine, cosine, rest] * 2, axis=1)
    rot_up = jnp.concatenate([-sine, gap, none] * 2, axis=1)
    rot_down = jnp.concatenate([gap, sine, none] * 2, axis=1)
    slot_ids = jnp.arange(TOK_DEV, dtype=jnp.int32)
    allowed = (segment_ids[:, None] == segment_ids[None, :]) & (
        slot_ids[None, :] <= slot_ids[:, None]
    )
    scalars = jnp.stack([shard] + ids + slots_by_piece(shard, rep))
    small = (act_one, act_two, grad_y, vecs, rot_cos, rot_up, rot_down, allowed.astype(jnp.float32))
    moments = align_moments(moment_one, moment_two, rep).reshape(2 * SHARE_ROWS, LANES)
    moments, blocks[-1] = lax.optimization_barrier((moments, blocks[-1]))
    moments = lax.all_gather(moments, PLANE, axis=0, tiled=True)
    made = weight_gradients(scalars, blocks, own, small)
    sent, kept = made[0:4], made[4:8]
    matrices = made[8]
    small = (tokens, normed, inv_std, grad_y, vecs) + tuple(made[9:])
    owned, output, grad_input, vec_grads = scatter_sums(
        sent, kept, small, lambda small: layer_results(matrices, small)
    )
    own_vectors = lax.dynamic_index_in_dim(
        vec_grads.reshape(SHARDS, 4, D), shard, 0, keepdims=False
    )
    tokens_all = tokens.shape[0] * lax.axis_size(EVERY)
    grad_params, new_params = update_shard(
        spread_in_plane(owned),
        spread_ids(rep),
        own_vectors,
        params,
        moments.reshape(REPS, 2, SHARE_ROWS, LANES),
        shard,
        1.0 / math.sqrt(tokens_all),
    )
    grad_params = grad_params.reshape(-1)
    width = moment_one.shape[0]
    grad_share = lax.dynamic_slice_in_dim(grad_params, rep * width, width)
    _, upd_first, upd_second = adam_update(moment_one, moment_one, moment_two, grad_share)
    return (output, grad_input, grad_params, new_params.reshape(-1), upd_first, upd_second)


def solution(mesh):
    in_rows = mesh.shape["rep"] == REPS and mesh.shape["shard"] == SHARDS
    if in_rows:
        rep, shard = PLANE, "z"
        mesh = Mesh(mesh.devices.reshape(2, 2, 2, SHARDS), EVERY)
        body = on_device_rows
    else:
        rep, shard = ("rep",), "shard"
        body = on_device
    rows = rep + (shard,)
    owner = (shard,) + rep
    in_specs = (P(rows, None), P(rows), P(rows, None), P(shard), P(owner), P(owner))
    out_specs = (P(rows, None), P(rows, None), P(shard), P(shard), P(owner), P(owner))
    return jax.shard_map(body, mesh=mesh, in_specs=in_specs, out_specs=out_specs, check_vma=False)
```

```python
import functools
import math

import jax
import jax.numpy as jnp
from jax import lax
from jax.experimental import pallas as pl
from jax.experimental.pallas import tpu as pltpu
from jax.sharding import Mesh
from jax.sharding import PartitionSpec as P

D = 768
HEADS = 12
HD = 64
ROT = 16
FF = 3072
TOK_DEV = 128


EPS_NORM = 1e-05
ROPE_BASE = 10000.0
NEG_BIG = -1e30
BETA_ONE = 0.9
BETA_TWO = 0.95
ADAM_STEP = 3.0
LEARN_RATE = 0.05
DECAY = 0.01
ADAM_EPS = 1e-08
INV_ROOT_TWO = 0.7071067811865476
INV_ROOT_TWO_PI = 0.3989422804014327


def layout_offsets():
    q_width = HEADS * HD
    o_wqkv = 2 * D
    o_bqkv = o_wqkv + 3 * q_width * D
    o_wout = o_bqkv + 3 * q_width
    o_bout = o_wout + q_width * D
    o_gain2 = o_bout + D
    o_shift2 = o_gain2 + D
    o_win = o_shift2 + D
    o_bin = o_win + D * FF
    o_wout2 = o_bin + FF
    o_bout2 = o_wout2 + FF * D
    return (
        o_wqkv,
        o_bqkv,
        o_wout,
        o_bout,
        o_gain2,
        o_shift2,
        o_win,
        o_bin,
        o_wout2,
        o_bout2,
        o_bout2 + D,
    )


def split_params(flat16):
    q_width = HEADS * HD
    o_wqkv, o_bqkv, o_wout, o_bout, o_gain2, o_shift2, o_win, o_bin, o_wout2, o_bout2, o_end = (
        layout_offsets()
    )
    return (
        flat16[0:D],
        flat16[D:o_wqkv],
        flat16[o_wqkv:o_bqkv].reshape(D, 3 * q_width),
        flat16[o_bqkv:o_wout],
        flat16[o_wout:o_bout].reshape(q_width, D),
        flat16[o_bout:o_gain2],
        flat16[o_gain2:o_shift2],
        flat16[o_shift2:o_win],
        flat16[o_win:o_bin].reshape(D, FF),
        flat16[o_bin:o_wout2],
        flat16[o_wout2:o_bout2].reshape(FF, D),
        flat16[o_bout2:o_end],
    )


def positions_of(segments):
    count = segments.shape[0]
    slot_ids = jnp.arange(count, dtype=jnp.int32)
    before = jnp.concatenate([jnp.full((1,), -2, jnp.int32), segments[:-1]])
    begins = segments != before
    first_slot = lax.cummax(jnp.where(begins, slot_ids, 0), axis=0)
    return slot_ids - first_slot


def rotary_tables(positions):
    half = ROT // 2
    steps_j = jnp.arange(half, dtype=jnp.float32)
    freqs = jnp.power(jnp.float32(ROPE_BASE), -2.0 * steps_j / ROT)
    angle = positions.astype(jnp.float32)[:, None] * freqs[None, :]
    return (jnp.cos(angle)[:, None, :], jnp.sin(angle)[:, None, :])


def rotate(values, cosine, sine, sign):
    half = cosine.shape[-1]
    lower = values[..., :half]
    upper = values[..., half : 2 * half]
    rest = values[..., 2 * half :]
    return jnp.concatenate(
        [lower * cosine - sign * upper * sine, upper * cosine + sign * lower * sine, rest], axis=-1
    )


def gelu_exact(value):
    return value * 0.5 * (1.0 + lax.erf(value * INV_ROOT_TWO))


def gelu_slope(value):
    return (
        0.5 * (1.0 + lax.erf(value * INV_ROOT_TWO))
        + value * jnp.exp(-0.5 * value * value) * INV_ROOT_TWO_PI
    )


def masked_scores(q_blk, keys, seg_rows, seg_cols, begin_row):
    scale = q_blk.shape[-1] ** (-0.5)
    raw_scores = jnp.einsum("qhd,khd->hqk", q_blk, keys, preferred_element_type=jnp.float32) * scale
    row_ids = begin_row + jnp.arange(q_blk.shape[0], dtype=jnp.int32)
    col_ids = jnp.arange(keys.shape[0], dtype=jnp.int32)
    allowed = (seg_rows[:, None] == seg_cols[None, :]) & (col_ids[None, :] <= row_ids[:, None])
    return jnp.where(allowed[None], raw_scores, NEG_BIG)


def attend_forward(query16, key16, value16, segments):
    scores = masked_scores(query16, key16, segments, segments, 0)
    row_max = jnp.max(scores, axis=-1, keepdims=True)
    expd = jnp.exp(scores - row_max)
    row_total = jnp.sum(expd, axis=-1, keepdims=True)
    probs16 = (expd / row_total).astype(jnp.bfloat16)
    attn_blk = jnp.einsum("hqk,khd->qhd", probs16, value16, preferred_element_type=jnp.float32)
    pieces_out = attn_blk.astype(jnp.bfloat16)
    lse_list = [row_max + jnp.log(row_total)]
    return (pieces_out, lse_list)


def attend_backward(query16, key16, value16, attn16, lse_list, segments, grad_attn16):
    count = query16.shape[0]
    block = min(512, count)
    scale = query16.shape[-1] ** (-0.5)
    grad_query = []
    grad_key = jnp.zeros(key16.shape, jnp.float32)
    grad_value = jnp.zeros(value16.shape, jnp.float32)
    for turn, begin_row in enumerate(range(0, count, block)):
        stop_row = begin_row + block
        scores = masked_scores(query16, key16, segments, segments, begin_row)
        chances = jnp.exp(scores - lse_list[turn])
        chances16 = chances.astype(jnp.bfloat16)
        grad_value = grad_value.at[:stop_row].add(
            jnp.einsum("hqk,qhd->khd", chances16, grad_attn16, preferred_element_type=jnp.float32)
        )
        grad_chance = jnp.einsum(
            "qhd,khd->hqk", grad_attn16, value16, preferred_element_type=jnp.float32
        )
        delta = jnp.sum(grad_attn16.astype(jnp.float32) * attn16.astype(jnp.float32), axis=-1)
        grad_scores = (chances * (grad_chance - jnp.transpose(delta)[:, :, None]) * scale).astype(
            jnp.bfloat16
        )
        grad_query.append(
            jnp.einsum("hqk,khd->qhd", grad_scores, key16, preferred_element_type=jnp.float32)
        )
        grad_key = grad_key.at[:stop_row].add(
            jnp.einsum("hqk,qhd->khd", grad_scores, query16, preferred_element_type=jnp.float32)
        )
    return (grad_query[0], grad_key, grad_value)


def norm_back(grad_act, normed, inv_std, gain):
    grad_gain = jnp.sum(grad_act * normed, axis=0)
    grad_shift = jnp.sum(grad_act, axis=0)
    grad_norm = grad_act * gain.astype(jnp.float32)
    grad_x = inv_std * (
        grad_norm
        - jnp.mean(grad_norm, axis=1, keepdims=True)
        - normed * jnp.mean(grad_norm * normed, axis=1, keepdims=True)
    )
    return (grad_gain, grad_shift, grad_x)


def layer_forward(tokens, segments, pieces):
    (
        gain_one,
        shift_one,
        w_qkv,
        b_qkv,
        w_out,
        b_out,
        gain_two,
        shift_two,
        w_in,
        b_in,
        w_out2,
        b_out2,
    ) = pieces
    count = tokens.shape[0]
    x_wide = tokens.astype(jnp.float32)
    row_mean = jnp.mean(x_wide, axis=1, keepdims=True)
    centered = x_wide - row_mean
    variance = jnp.mean(centered * centered, axis=1, keepdims=True)
    inv_std = lax.rsqrt(variance + EPS_NORM)
    normed = centered * inv_std
    act_one = (normed * gain_one.astype(jnp.float32) + shift_one.astype(jnp.float32)).astype(
        jnp.bfloat16
    )
    act_two = (normed * gain_two.astype(jnp.float32) + shift_two.astype(jnp.float32)).astype(
        jnp.bfloat16
    )
    mixed = jnp.dot(act_one, w_qkv, preferred_element_type=jnp.float32) + b_qkv.astype(jnp.float32)
    mixed = mixed.reshape(count, 3, HEADS, HD)
    cosine, sine = rotary_tables(positions_of(segments))
    query16 = rotate(mixed[:, 0], cosine, sine, 1.0).astype(jnp.bfloat16)
    key16 = rotate(mixed[:, 1], cosine, sine, 1.0).astype(jnp.bfloat16)
    value16 = mixed[:, 2].astype(jnp.bfloat16)
    attn16, lse_list = attend_forward(query16, key16, value16, segments)
    proj = jnp.dot(
        attn16.reshape(count, HEADS * HD), w_out, preferred_element_type=jnp.float32
    ) + b_out.astype(jnp.float32)
    pre = jnp.dot(act_two, w_in, preferred_element_type=jnp.float32) + b_in.astype(jnp.float32)
    hidden16 = gelu_exact(pre).astype(jnp.bfloat16)
    feed = jnp.dot(hidden16, w_out2, preferred_element_type=jnp.float32) + b_out2.astype(
        jnp.float32
    )
    output = x_wide + proj + feed
    saved = (
        normed,
        inv_std,
        act_one,
        act_two,
        query16,
        key16,
        value16,
        attn16,
        lse_list,
        cosine,
        sine,
        pre,
        hidden16,
    )
    return (output, saved)


def layer_backward(cotangent, segments, pieces, saved):
    (
        gain_one,
        shift_one,
        w_qkv,
        b_qkv,
        w_out,
        b_out,
        gain_two,
        shift_two,
        w_in,
        b_in,
        w_out2,
        b_out2,
    ) = pieces
    (
        normed,
        inv_std,
        act_one,
        act_two,
        query16,
        key16,
        value16,
        attn16,
        lse_list,
        cosine,
        sine,
        pre,
        hidden16,
    ) = saved
    count = cotangent.shape[0]
    contract_rows = (((0,), (0,)), ((), ()))
    contract_cols = (((1,), (1,)), ((), ()))
    live_rows = (segments >= 0).astype(jnp.float32)[:, None]
    grad_y = cotangent.astype(jnp.float32) * live_rows
    grad_y16 = grad_y.astype(jnp.bfloat16)
    grad_b_out = jnp.sum(grad_y, axis=0)
    attn_flat = attn16.reshape(count, HEADS * HD)
    grad_w_out = lax.dot_general(
        attn_flat, grad_y16, contract_rows, preferred_element_type=jnp.float32
    )
    grad_w_out2 = lax.dot_general(
        hidden16, grad_y16, contract_rows, preferred_element_type=jnp.float32
    )
    grad_hidden = lax.dot_general(
        grad_y16, w_out2, contract_cols, preferred_element_type=jnp.float32
    )
    grad_pre = grad_hidden * gelu_slope(pre)
    grad_b_in = jnp.sum(grad_pre, axis=0)
    grad_pre16 = grad_pre.astype(jnp.bfloat16)
    grad_w_in = lax.dot_general(
        act_two, grad_pre16, contract_rows, preferred_element_type=jnp.float32
    )
    grad_act_two = lax.dot_general(
        grad_pre16, w_in, contract_cols, preferred_element_type=jnp.float32
    )
    grad_attn16 = (
        lax.dot_general(grad_y16, w_out, contract_cols, preferred_element_type=jnp.float32)
        .astype(jnp.bfloat16)
        .reshape(count, HEADS, HD)
    )
    grad_query, grad_key, grad_value = attend_backward(
        query16, key16, value16, attn16, lse_list, segments, grad_attn16
    )
    grad_query = rotate(grad_query, cosine, sine, -1.0)
    grad_key = rotate(grad_key, cosine, sine, -1.0)
    grad_mixed = jnp.stack([grad_query, grad_key, grad_value], axis=1).reshape(
        count, 3 * HEADS * HD
    )
    grad_b_qkv = jnp.sum(grad_mixed, axis=0)
    grad_mixed16 = grad_mixed.astype(jnp.bfloat16)
    grad_w_qkv = lax.dot_general(
        act_one, grad_mixed16, contract_rows, preferred_element_type=jnp.float32
    )
    grad_act_one = lax.dot_general(
        grad_mixed16, w_qkv, contract_cols, preferred_element_type=jnp.float32
    )
    gain_grad_one, shift_grad_one, grad_x_one = norm_back(grad_act_one, normed, inv_std, gain_one)
    gain_grad_two, shift_grad_two, grad_x_two = norm_back(grad_act_two, normed, inv_std, gain_two)
    grad_in = grad_y + grad_x_one + grad_x_two
    return (
        grad_in,
        [
            gain_grad_one,
            shift_grad_one,
            grad_w_qkv,
            grad_b_qkv,
            grad_w_out,
            grad_b_out,
            gain_grad_two,
            shift_grad_two,
            grad_w_in,
            grad_b_in,
            grad_w_out2,
            grad_b_out,
        ],
    )


def flatten_grads(parts, total_len):
    used = layout_offsets()[-1]
    rounded = [part.astype(jnp.bfloat16).reshape(-1) for part in parts]
    return jnp.concatenate(rounded + [jnp.zeros((total_len - used,), jnp.bfloat16)])


def adam_update(weights, first_moment, second_moment, gradient):
    new_first = BETA_ONE * first_moment + (1.0 - BETA_ONE) * gradient
    new_second = BETA_TWO * second_moment + (1.0 - BETA_TWO) * gradient * gradient
    unbiased_first = new_first / (1.0 - BETA_ONE**ADAM_STEP)
    unbiased_second = new_second / (1.0 - BETA_TWO**ADAM_STEP)
    new_weights = weights - LEARN_RATE * (
        unbiased_first / (jnp.sqrt(unbiased_second) + ADAM_EPS) + DECAY * weights
    )
    return (new_weights, new_first, new_second)


def on_device(tokens, segment_ids, cotangent, params, moment_one, moment_two):
    gathered = lax.all_gather(params.astype(jnp.bfloat16), "shard", axis=0, tiled=True)
    total_len = gathered.shape[0]
    pieces = split_params(gathered)
    output, saved = layer_forward(tokens, segment_ids, pieces)
    grad_input, parts = layer_backward(cotangent, segment_ids, pieces, saved)
    local_grad = flatten_grads(parts, total_len)
    owned = lax.psum_scatter(local_grad, "shard", scatter_dimension=0, tiled=True).astype(
        jnp.float32
    )
    tokens_all = tokens.shape[0] * lax.axis_size("rep") * lax.axis_size("shard")
    factor = 1.0 / math.sqrt(tokens_all)
    width = moment_one.shape[0]
    begin = lax.axis_index("rep") * width
    param_share = lax.dynamic_slice_in_dim(params, begin, width)
    share = lax.psum_scatter(owned, "rep", scatter_dimension=0, tiled=True)
    grad_share = share * factor
    upd_params, upd_first, upd_second = adam_update(param_share, moment_one, moment_two, grad_share)
    grad_params, new_params = (
        lax.all_gather(grad_share, "rep", axis=0, tiled=True),
        lax.all_gather(upd_params, "rep", axis=0, tiled=True),
    )
    return (output, grad_input, grad_params, new_params, upd_first, upd_second)


LANES = 128
REPS = 8
SHARDS = 4
PIECE = 288
FLAT_ROWS = 13848
MOVED = PIECE * D // LANES


PARTS = (
    ((12, 1728, 96, 3, 0),),
    ((6, 576, 96, 1, 0), (4632, 1152, 48, 4, 96)),
    ((0, 1152, 48, 4, 0), (9240, 576, 96, 1, 192)),
    ((0, 1728, 288, 1, 0),),
)
VECTOR_ROWS = ((0, 1, 2306, 2307), (0, 769, 770, 771), (1536, 1537, 1538, 1539), (2304, 2305, 2306, 2307))


PLANE = ("y", "x", "core")
EVERY = PLANE + ("z",)
HOPS = (1, 2, 3, 0)


def plane_permute(value, flips):
    return lax.ppermute(value, PLANE, [(i, i ^ flips[i % 2]) for i in range(REPS)])


def first_cross(value):
    return plane_permute(value, (2, 4))


def second_cross(value):
    return plane_permute(value, (4, 2))


def core_cross(value):
    return plane_permute(value, (1, 1))


def ring_step(value):
    return lax.ppermute(value, "z", [(i, (i + 1) % SHARDS) for i in range(SHARDS)])


def flips_of(rep):
    core = rep % 2
    first = 2 + 2 * core
    return (0, first, 6 - first, 6)


def spread_in_plane(piece):
    first = first_cross(piece)
    second = second_cross(piece)
    both = second_cross(first)
    mine = [piece, first, second, both]
    return mine + [core_cross(value) for value in mine]


def spread_ids(rep):
    other = rep ^ 1
    return [rep ^ flip for flip in flips_of(rep)] + [other ^ flip for flip in flips_of(other)]


def pack_kernel(where, flat_ref, out_ref, held, sems):
    shard = where[0]
    turns = out_ref.shape[0]
    for z in range(SHARDS):

        @pl.when(shard == z)
        def _(z=z):
            def copies_of(turn):
                slot = turn % 2
                rep = where[1 + turn]
                copies = []
                at = 0
                for part, (first, step, _, _, _) in enumerate(PARTS[z]):
                    lead = first % 8
                    count = step + (8 if lead else 0)
                    begin = pl.multiple_of(first - lead + step * rep, 8)
                    copies.append(
                        pltpu.make_async_copy(
                            flat_ref.at[pl.ds(begin, count)],
                            held.at[slot, pl.ds(at, count)],
                            sems.at[slot, part],
                        )
                    )
                    at += count
                return copies

            for copy in copies_of(0):
                copy.start()

            @pl.loop(0, turns)
            def _(turn):
                @pl.when(turn + 1 < turns)
                def _():
                    for copy in copies_of(turn + 1):
                        copy.start()

                slot = turn % 2
                at = 0
                for copy, (first, step, rows, blocks, place) in zip(copies_of(turn), PARTS[z]):
                    copy.wait()
                    lead = first % 8
                    for block in range(blocks):
                        for col in range(6):
                            begin = at + lead + 6 * block + col
                            got = held[slot, pl.ds(begin, rows, stride=6 * blocks), :]
                            out_ref[
                                turn,
                                place + rows * block : place + rows * (block + 1),
                                LANES * col : LANES * (col + 1),
                            ] = got.astype(jnp.bfloat16)
                    at += step + (8 if lead else 0)


def pack_pieces(params, shard, reps):
    return pl.pallas_call(
        pack_kernel,
        grid_spec=pltpu.PrefetchScalarGridSpec(
            num_scalar_prefetch=1,
            in_specs=[pl.BlockSpec(memory_space=pltpu.HBM)],
            out_specs=pl.BlockSpec(memory_space=pltpu.VMEM),
            scratch_shapes=[
                pltpu.VMEM((2, MOVED + 16, LANES), jnp.float32),
                pltpu.SemaphoreType.DMA((2, 2)),
            ],
        ),
        out_shape=jax.ShapeDtypeStruct((len(reps), PIECE, D), jnp.bfloat16),
        compiler_params=pltpu.CompilerParams(vmem_limit_bytes=56 * 2**20),
    )(jnp.stack([shard] + reps), params.reshape(FLAT_ROWS, LANES))


PIECES = SHARDS * REPS
GROUPS = 12
ALL_ROWS = PIECES * PIECE


def fetch_pieces(ids, blocks, own, shard, held, sems):
    views = []
    for block in blocks:
        views += [block.at[p] for p in range(4)] if len(block.shape) == 3 else [block]
    ids = ids + [shard * REPS + r for r in range(REPS)]
    views += [own.at[pl.ds(r * PIECE, PIECE)] for r in range(REPS)]
    for which, view in zip(ids, views):
        row = pl.multiple_of(which * PIECE, 16)
        pltpu.make_async_copy(view, held.at[pl.ds(row, PIECE)], sems.at[which]).start()

    def arrive(owner):
        for r in range(REPS):
            at = owner * REPS + r
            pltpu.make_async_copy(
                own.at[pl.ds(0, PIECE)], held.at[pl.ds(at * PIECE, PIECE)], sems.at[at]
            ).wait()

    return arrive


def rows_of(held, shard, begin, rows):
    return jnp.concatenate(
        [held[pl.ds((shard * REPS + r) * PIECE + begin, rows), :] for r in range(REPS)], axis=0
    )


def w_qkv_of(held, j):
    return rows_of(held, 0, 96 * j, 96)


def w_out_of(held):
    return rows_of(held, 1, 0, 96)


def w_in_of(held, j):
    return jnp.concatenate([rows_of(held, 1, 96 + 48 * j, 48), rows_of(held, 2, 48 * j, 48)], axis=0)


def w_out2_of(held, j):
    if j == 0:
        return rows_of(held, 2, 192, 96)
    return held[pl.ds(3 * REPS * PIECE + D * (j - 1), D), :]


def dot32(a, b):
    return jnp.dot(a, b, preferred_element_type=jnp.float32)


def attention_kernel(where, *refs):
    count = PIECES - REPS
    blocks, own = refs[:GROUPS], refs[GROUPS]
    (act_one, grad_y, vecs, rot_cos, rot_up, rot_down, bias) = refs[GROUPS + 1 : GROUPS + 8]
    matrices, attn_out, mixed_out, sums_out = refs[GROUPS + 8 : GROUPS + 12]
    held, query, key, value, grad_attn, sems, save_sem = refs[GROUPS + 12 :]
    shard = where[0]
    arrive = fetch_pieces([where[1 + t] for t in range(count)], blocks, own, shard, held, sems)
    sums_out[...] = jnp.zeros_like(sums_out)

    arrive(0)
    act1 = act_one[...]
    for j, out in enumerate((query, key, value)):
        got = dot32(act1, w_qkv_of(held, j)) + vecs[2 + j : 3 + j, :]
        if j < 2:
            for p in range(6):
                lanes = slice(LANES * p, LANES * (p + 1))
                part = got[:, lanes]
                part = (
                    part * rot_cos[...]
                    + pltpu.roll(part, LANES - 8, 1) * rot_up[...]
                    + pltpu.roll(part, 8, 1) * rot_down[...]
                )
                out[:, lanes] = part.astype(jnp.bfloat16)
        else:
            out[...] = got.astype(jnp.bfloat16)
    gy_t = grad_y[...].T
    arrive(1)
    grad_attn[...] = dot32(w_out_of(held), gy_t).T.astype(jnp.bfloat16)

    arrive(2)
    arrive(3)
    saving = pltpu.make_async_copy(held, matrices, save_sem)
    saving.start()
    low = lax.broadcasted_iota(jnp.int32, (LANES, LANES), 1) < HD
    scale = HD ** (-0.5)
    for p in range(6):
        lanes = slice(LANES * p, LANES * (p + 1))
        q2, k2, v2, g2 = (ref[:, lanes] for ref in (query, key, value, grad_attn))
        k2_t, v2_t = k2.T, v2.T
        attn_parts, value_parts, query_parts, key_parts = [], [], [], []
        for half in range(2):
            here = low if half == 0 else ~low
            zero = jnp.zeros_like(q2)
            scores = dot32(jnp.where(here, q2, zero), k2_t) * scale
            scores = jnp.where(bias[...] > 0.5, scores, NEG_BIG)
            expd = jnp.exp(scores - jnp.max(scores, axis=1, keepdims=True))
            chances = expd / jnp.sum(expd, axis=1, keepdims=True)
            chances16 = chances.astype(jnp.bfloat16)
            attn = dot32(chances16, v2)
            attn16 = attn.astype(jnp.bfloat16)
            masked = jnp.where(here, g2, zero)
            delta = jnp.sum(
                masked.astype(jnp.float32) * attn16.astype(jnp.float32), axis=1, keepdims=True
            )
            grad_chance = dot32(masked, v2_t)
            slope = (chances * (grad_chance - delta) * scale).astype(jnp.bfloat16)
            attn_parts.append(attn16)
            value_parts.append(dot32(chances16.T, g2))
            query_parts.append(dot32(slope, k2))
            key_parts.append(dot32(slope.T, q2))
        attn_out[:, lanes] = jnp.where(low, *attn_parts)
        for j, parts in enumerate((query_parts, key_parts, value_parts)):
            part = jnp.where(low, *parts)
            if j < 2:
                part = (
                    part * rot_cos[...]
                    - pltpu.roll(part, LANES - 8, 1) * rot_up[...]
                    - pltpu.roll(part, 8, 1) * rot_down[...]
                )
            wide = slice(D * j + LANES * p, D * j + LANES * (p + 1))
            sums_out[j : j + 1, lanes] = jnp.sum(part, axis=0, keepdims=True)
            mixed_out[:, wide] = part.astype(jnp.bfloat16)

    saving.wait()


def attention(scalars, blocks, own, small):
    anywhere = pl.BlockSpec(memory_space=pl.ANY)
    vmem = pl.BlockSpec(memory_space=pltpu.VMEM)
    bf16 = jnp.bfloat16
    return pl.pallas_call(
        attention_kernel,
        grid_spec=pltpu.PrefetchScalarGridSpec(
            num_scalar_prefetch=1,
            in_specs=[anywhere] * (len(blocks) + 1) + [vmem] * len(small),
            out_specs=[anywhere] + [vmem] * 3,
            scratch_shapes=[
                pltpu.VMEM((ALL_ROWS, D), bf16),
                pltpu.VMEM((TOK_DEV, D), bf16),
                pltpu.VMEM((TOK_DEV, D), bf16),
                pltpu.VMEM((TOK_DEV, D), bf16),
                pltpu.VMEM((TOK_DEV, D), bf16),
                pltpu.SemaphoreType.DMA((PIECES,)),
                pltpu.SemaphoreType.DMA,
            ],
        ),
        out_shape=[
            jax.ShapeDtypeStruct((ALL_ROWS, D), bf16),
            jax.ShapeDtypeStruct((TOK_DEV, D), bf16),
            jax.ShapeDtypeStruct((TOK_DEV, 3 * D), bf16),
            jax.ShapeDtypeStruct((8, D), jnp.float32),
        ],
        compiler_params=pltpu.CompilerParams(vmem_limit_bytes=40 * 2**20),
    )(scalars, *blocks, own, *small)


def gradient_kernel(where, matrices, *refs):
    (act_one, act_two, grad_y, vecs, attn_in, mixed_in) = refs[:6]
    outs = refs[6:22]
    hidden_out, pre_out, sums_out = refs[22:25]
    held, grads, sems, out_sems = refs[25:]
    copies = []
    for z in range(1, SHARDS):
        rows = pl.ds(z * REPS * PIECE, REPS * PIECE)
        copies.append(pltpu.make_async_copy(matrices.at[rows], held.at[rows], sems.at[z]))
    for copy in copies:
        copy.start()
    sums_out[...] = jnp.zeros_like(sums_out)
    slot_row = lambda z, r: pl.multiple_of(where[z * REPS + r] * PIECE, 16)

    def keep_rows(z, begin, rows, part):
        for r in range(part.shape[0] // rows):
            grads[pl.ds(slot_row(z, r) + begin, rows), :] = part[rows * r : rows * (r + 1), :]

    gy = grad_y[...]
    act1_t = act_one[...].T
    for j in range(3):
        keep_rows(
            0, 96 * j, 96, dot32(act1_t, mixed_in[:, D * j : D * (j + 1)]).astype(jnp.bfloat16)
        )
    keep_rows(1, 0, 96, dot32(attn_in[...].T, gy).astype(jnp.bfloat16))

    for copy in copies:
        copy.wait()
    gy_t = gy.T
    act2 = act_two[...]
    act2_t = act2.T
    for j in range(4):
        wide = slice(D * j, D * (j + 1))
        pre = dot32(act2, w_in_of(held, j)) + vecs[8 + j : 9 + j, :]
        bell = 0.5 * (1.0 + lax.erf(pre * INV_ROOT_TWO))
        hidden = (pre * bell).astype(jnp.bfloat16)
        hidden_out[:, wide] = hidden
        grad_hidden = dot32(w_out2_of(held, j), gy_t).T
        grad_pre = grad_hidden * (bell + pre * jnp.exp(-0.5 * pre * pre) * INV_ROOT_TWO_PI)
        sums_out[j : j + 1, :] = jnp.sum(grad_pre, axis=0, keepdims=True)
        grad_pre16 = grad_pre.astype(jnp.bfloat16)
        pre_out[:, wide] = grad_pre16
        w2 = dot32(hidden.T, gy).astype(jnp.bfloat16)
        if j == 0:
            keep_rows(2, 192, 96, w2)
        else:
            at = D * (j - 1)
            while at < D * j:
                r, begin = divmod(at, PIECE)
                rows = min(PIECE - begin, D * j - at)
                grads[pl.ds(slot_row(3, r) + begin, rows), :] = w2[
                    at - D * (j - 1) : at - D * (j - 1) + rows, :
                ]
                at += rows
        w1 = dot32(act2_t, grad_pre16).astype(jnp.bfloat16)
        keep_rows(1, 96 + 48 * j, 48, w1[: D // 2])
        keep_rows(2, 48 * j, 48, w1[D // 2 :])
    copies = []
    for turn, out in enumerate(outs):
        for p in range(2):
            copies.append(
                pltpu.make_async_copy(
                    grads.at[pl.ds((turn * 2 + p) * PIECE, PIECE)],
                    out.at[p],
                    out_sems.at[turn * 2 + p],
                )
            )
    for copy in copies:
        copy.start()
    for copy in copies:
        copy.wait()


def weight_gradients(slots, matrices, small):
    anywhere = pl.BlockSpec(memory_space=pl.ANY)
    vmem = pl.BlockSpec(memory_space=pltpu.VMEM)
    bf16 = jnp.bfloat16
    return pl.pallas_call(
        gradient_kernel,
        grid_spec=pltpu.PrefetchScalarGridSpec(
            num_scalar_prefetch=1,
            in_specs=[anywhere] + [vmem] * len(small),
            out_specs=[anywhere] * 16 + [vmem] * 3,
            scratch_shapes=[
                pltpu.VMEM((ALL_ROWS, D), bf16),
                pltpu.VMEM((ALL_ROWS, D), bf16),
                pltpu.SemaphoreType.DMA((SHARDS,)),
                pltpu.SemaphoreType.DMA((PIECES,)),
            ],
        ),
        out_shape=[jax.ShapeDtypeStruct((2, PIECE, D), bf16)] * 16
        + [
            jax.ShapeDtypeStruct((TOK_DEV, FF), bf16),
            jax.ShapeDtypeStruct((TOK_DEV, FF), bf16),
            jax.ShapeDtypeStruct((8, D), jnp.float32),
        ],
        compiler_params=pltpu.CompilerParams(vmem_limit_bytes=56 * 2**20),
    )(slots, matrices, *small)


def result_kernel(matrices, *refs):
    (tokens, normed, inv_std, grad_y, vecs, attn, grad_mixed, low_sums, hidden, grad_pre, high_sums) = (
        refs[:11]
    )
    output, grad_input, vec_out, held, sems = refs[11:]
    copies = []
    for z in range(SHARDS):
        rows = pl.ds(z * REPS * PIECE, REPS * PIECE)
        copies.append(pltpu.make_async_copy(matrices.at[rows], held.at[rows], sems.at[z]))
    for copy in copies:
        copy.start()
    for copy in copies:
        copy.wait()
    total = dot32(attn[...], w_out_of(held)) + vecs[5:6, :]
    for j in range(4):
        total = total + dot32(hidden[:, D * j : D * (j + 1)], w_out2_of(held, j))
    output[...] = tokens[...].astype(jnp.float32) + (total + vecs[12:13, :])
    vec_out[2:5, :] = low_sums[0:3, :]
    vec_out[8:12, :] = high_sums[0:4, :]
    gy = grad_y[...].astype(jnp.float32)
    total = gy
    for norm, (parts, width, weights) in enumerate(
        ((grad_mixed, 3, w_qkv_of), (grad_pre, 4, w_in_of))
    ):
        back = None
        for j in range(width):
            part = dot32(weights(held, j), parts[:, D * j : D * (j + 1)].T)
            back = part if back is None else back + part
        grad_act = back.T
        gain_row = 0 if norm == 0 else 6
        unit = normed[...]
        vec_out[gain_row : gain_row + 1, :] = jnp.sum(grad_act * unit, axis=0, keepdims=True)
        vec_out[gain_row + 1 : gain_row + 2, :] = jnp.sum(grad_act, axis=0, keepdims=True)
        grad_norm = grad_act * vecs[gain_row : gain_row + 1, :]
        total = total + inv_std[...] * (
            grad_norm
            - jnp.mean(grad_norm, axis=1, keepdims=True)
            - unit * jnp.mean(grad_norm * unit, axis=1, keepdims=True)
        )
    grad_input[...] = total
    bottom = jnp.sum(gy, axis=0, keepdims=True)
    vec_out[5:6, :] = bottom
    vec_out[12:13, :] = bottom
    vec_out[13:16, :] = jnp.zeros((3, D), jnp.float32)
    vec_out[...] = vec_out[...].astype(jnp.bfloat16).astype(jnp.float32)


def layer_results(matrices, small):
    hbm = pl.BlockSpec(memory_space=pl.ANY)
    vmem = pl.BlockSpec(memory_space=pltpu.VMEM)
    rows = jax.ShapeDtypeStruct((TOK_DEV, D), jnp.float32)
    return pl.pallas_call(
        result_kernel,
        in_specs=[hbm] + [vmem] * len(small),
        out_specs=[vmem] * 3,
        scratch_shapes=[
            pltpu.VMEM((ALL_ROWS, D), jnp.bfloat16),
            pltpu.SemaphoreType.DMA((SHARDS,)),
        ],
        out_shape=[rows, rows, jax.ShapeDtypeStruct((16, D), jnp.float32)],
        compiler_params=pltpu.CompilerParams(vmem_limit_bytes=40 * 2**20),
    )(matrices, *small)


SHARE = FLAT_ROWS // REPS
BEGINS = tuple(SHARE * r // 16 * 16 for r in range(REPS)) + (FLAT_ROWS,)
SHARE_ROWS = 1760
STEP = 288


def align_kernel(where, one_ref, two_ref, out_ref, held):
    for r in range(REPS):

        @pl.when(where[0] == r)
        def _(r=r):
            lead = SHARE * r - BEGINS[r]
            for turn, ref in enumerate((one_ref, two_ref)):
                held[0:16, :] = jnp.zeros((16, LANES), jnp.float32)
                held[SHARE_ROWS - 32 :, :] = jnp.zeros((32, LANES), jnp.float32)
                held[lead : lead + SHARE, :] = ref[...]
                out_ref[turn] = held[...].astype(jnp.bfloat16)


def align_moments(moment_one, moment_two, rep):
    return pl.pallas_call(
        align_kernel,
        grid_spec=pltpu.PrefetchScalarGridSpec(
            num_scalar_prefetch=1,
            in_specs=[pl.BlockSpec(memory_space=pltpu.VMEM)] * 2,
            out_specs=pl.BlockSpec(memory_space=pltpu.VMEM),
            scratch_shapes=[pltpu.VMEM((SHARE_ROWS, LANES), jnp.float32)],
        ),
        out_shape=jax.ShapeDtypeStruct((2, SHARE_ROWS, LANES), jnp.bfloat16),
        compiler_params=pltpu.CompilerParams(vmem_limit_bytes=16 * 2**20),
    )(jnp.stack([rep]), moment_one.reshape(SHARE, LANES), moment_two.reshape(SHARE, LANES))


def update_kernel(factor, where, *refs):
    blocks = refs[:REPS]
    moments = refs[REPS : 2 * REPS]
    vec_ref, params, grad_out, params_out = refs[2 * REPS : 2 * REPS + 4]
    held, grad, weight, moment, sems, out_sems = refs[2 * REPS + 4 :]
    copies = []
    for turn in range(REPS):
        copies.append(
            pltpu.make_async_copy(blocks[turn], held.at[where[1 + turn]], sems.at[turn])
        )
    copies.append(pltpu.make_async_copy(params, weight, sems.at[REPS]))
    for turn in range(REPS):
        copies.append(
            pltpu.make_async_copy(
                moments[turn], moment.at[where[1 + turn]], sems.at[REPS + 1 + turn]
            )
        )
    for copy in copies:
        copy.start()
    for copy in copies[:REPS]:
        copy.wait()
    shard = where[0]
    for z in range(SHARDS):

        @pl.when(shard == z)
        def _(z=z):
            for slot, row in enumerate(VECTOR_ROWS[z]):
                for col in range(6):
                    grad[6 * row + col : 6 * row + col + 1, :] = (
                        vec_ref[slot : slot + 1, LANES * col : LANES * (col + 1)] * factor
                    )

            @pl.loop(0, REPS)
            def _(rep):
                for first, step, rows, blocks, place in PARTS[z]:
                    for block in range(blocks):
                        for col in range(6):
                            got = held[
                                rep,
                                place + rows * block : place + rows * (block + 1),
                                LANES * col : LANES * (col + 1),
                            ]
                            begin = first + step * rep + 6 * block + col
                            grad[pl.ds(begin, rows, stride=6 * blocks), :] = (
                                got.astype(jnp.float32) * factor
                            )

    saving = [pltpu.make_async_copy(grad, grad_out, out_sems.at[REPS])]
    saving[0].start()
    for copy in copies[REPS:]:
        copy.wait()
    for r in range(REPS):
        base = BEGINS[r]
        length = BEGINS[r + 1] - base
        if r > 0:
            tail = base - BEGINS[r - 1]
            moment[r, :, 0:16, :] = moment[r, :, 0:16, :] + moment[r - 1, :, tail : tail + 16, :]

        def renew(at, rows, r=r, base=base):
            here = pl.ds(pl.multiple_of(base + at, 8), rows)
            there = pl.ds(pl.multiple_of(at, 16), rows)
            updated, _, _ = adam_update(
                weight[here, :],
                moment[r, 0, there, :].astype(jnp.float32),
                moment[r, 1, there, :].astype(jnp.float32),
                grad[here, :],
            )
            weight[here, :] = updated

        @pl.loop(0, length // STEP)
        def _(turn):
            renew(turn * STEP, STEP)

        if length % STEP:
            renew(length // STEP * STEP, length % STEP)
        rows = pl.ds(base, length)
        saving.append(
            pltpu.make_async_copy(weight.at[rows], params_out.at[rows], out_sems.at[r])
        )
        saving[-1].start()
    for copy in saving:
        copy.wait()


def update_shard(blocks, ids, vectors, params, moments, shard, factor):
    anywhere = pl.BlockSpec(memory_space=pl.ANY)
    flat = jax.ShapeDtypeStruct((FLAT_ROWS, LANES), jnp.float32)
    return pl.pallas_call(
        functools.partial(update_kernel, factor),
        grid_spec=pltpu.PrefetchScalarGridSpec(
            num_scalar_prefetch=1,
            in_specs=[anywhere] * (2 * REPS)
            + [pl.BlockSpec(memory_space=pltpu.VMEM), anywhere],
            out_specs=[anywhere] * 2,
            scratch_shapes=[
                pltpu.VMEM((REPS, PIECE, D), jnp.bfloat16),
                pltpu.VMEM((FLAT_ROWS, LANES), jnp.float32),
                pltpu.VMEM((FLAT_ROWS, LANES), jnp.float32),
                pltpu.VMEM((REPS, 2, SHARE_ROWS, LANES), jnp.bfloat16),
                pltpu.SemaphoreType.DMA((2 * REPS + 1,)),
                pltpu.SemaphoreType.DMA((REPS + 1,)),
            ],
        ),
        out_shape=[flat, flat],
        compiler_params=pltpu.CompilerParams(vmem_limit_bytes=56 * 2**20),
    )(jnp.stack([shard] + ids), *blocks, *moments, vectors, params.reshape(FLAT_ROWS, LANES))


def gather_matrices(params, shard, rep):
    piece = pack_pieces(params, shard, [rep])[0]
    own = pack_pieces(params, shard, [rep * 0 + turn for turn in range(REPS)])
    fence = lax.optimization_barrier
    one = ring_step(piece)
    one, own = fence((one, own))
    two, first_one, second_one = ring_step(one), first_cross(one), second_cross(one)
    two, first_one, second_one = fence((two, first_one, second_one))
    three, first_two, second_two = ring_step(two), first_cross(two), second_cross(two)
    both_one = second_cross(first_one)
    three, first_two, second_two, both_one = fence((three, first_two, second_two, both_one))
    first_three, second_three = first_cross(three), second_cross(three)
    both_two = second_cross(first_two)
    mine_one = jnp.stack([one, first_one, second_one, both_one])
    other_one = core_cross(mine_one)
    first_three, second_three, both_two, other_one = fence(
        (first_three, second_three, both_two, other_one)
    )
    both_three = second_cross(first_three)
    mine_two = jnp.stack([two, first_two, second_two, both_two])
    other_two = core_cross(mine_two)
    others = [core_cross(value) for value in (three, first_three, second_three)]
    others, both_three, other_two = fence((others, both_three, other_two))
    others.append(core_cross(both_three))
    threes = [three, first_three, second_three, both_three]
    blocks = [mine_one, other_one, mine_two, other_two] + threes + others
    ids = []
    for hop in range(1, SHARDS):
        owner = (shard + SHARDS - hop) % SHARDS
        ids += [owner * REPS + which for which in spread_ids(rep)]
    return blocks, own.reshape(REPS * PIECE, D), ids


def ring_shift(value, hop):
    return lax.ppermute(value, "z", [(i, (i + hop) % SHARDS) for i in range(SHARDS)])


def gather_vectors(params, shard):
    mine = shard_vectors(params, shard).astype(jnp.bfloat16)
    held = [mine] + [ring_shift(mine, hop) for hop in range(1, SHARDS)]
    turned = jnp.stack(held).astype(jnp.float32)
    order = (shard + SHARDS - jnp.arange(SHARDS)) % SHARDS
    return jnp.take(turned, order, axis=0).reshape(16, D)


def sum_in_plane(value):
    for flips in ((1, 1), (2, 2), (4, 4)):
        value = value + plane_permute(value, flips)
    return value


def sum_over_shards(value):
    return value + ring_shift(value, 1) + ring_shift(value, 2) + ring_shift(value, 3)


def slots_by_piece(shard, rep):
    slots = []
    for owner in range(SHARDS):
        hop = (shard + SHARDS - owner + 3) % SHARDS
        for which in range(REPS):
            apart = rep ^ which
            kept = 1 - apart % 2
            core = which % 2
            across = apart & 6
            first = 2 + 2 * core
            place = jnp.where(
                across == 0, 2, jnp.where(across == 6, 1, jnp.where(across == first, 0, 3))
            )
            slots.append((kept * SHARDS + hop) * 4 + place)
    return slots


def scatter_sums(parts, moments, small, results):
    carried = None
    for turn in range(SHARDS):
        sent_far, sent_near = parts[2 * turn], parts[2 * turn + 1]
        kept_far, kept_near = parts[8 + 2 * turn], parts[9 + 2 * turn]
        crossed = first_cross(kept_far + core_cross(sent_far))
        pair = kept_near + core_cross(sent_near) + crossed
        if turn == 1:
            pair, small = lax.optimization_barrier((pair, small))
            output, grad_input, vectors = results(small)
        elif turn == 2:
            pair, vectors, moments = lax.optimization_barrier((pair, vectors, moments))
            vectors = sum_over_shards(sum_in_plane(vectors))
            moments = moments + [core_cross(value) for value in moments]
        total = pair[0] + second_cross(pair[1])
        if carried is not None:
            total = total + carried
        if turn < SHARDS - 1:
            carried = ring_step(total)
    return total, moments, output, grad_input, vectors


def shard_vectors(params, shard):
    rows = jnp.asarray(VECTOR_ROWS, jnp.int32)[shard]
    return jnp.stack([lax.dynamic_slice_in_dim(params, rows[i] * D, D) for i in range(4)])


def on_device_rows(tokens, segment_ids, cotangent, params, moment_one, moment_two):
    shard = lax.axis_index("z")
    rep = lax.axis_index(PLANE)
    vecs = gather_vectors(params, shard)
    blocks, own, ids = gather_matrices(params, shard, rep)
    x_wide = tokens.astype(jnp.float32)
    centered = x_wide - jnp.mean(x_wide, axis=1, keepdims=True)
    variance = jnp.mean(centered * centered, axis=1, keepdims=True)
    inv_std = lax.rsqrt(variance + EPS_NORM)
    normed = centered * inv_std
    act_one = (normed * vecs[0] + vecs[1]).astype(jnp.bfloat16)
    act_two = (normed * vecs[6] + vecs[7]).astype(jnp.bfloat16)
    live_rows = (segment_ids >= 0)[:, None]
    grad_y = jnp.where(live_rows, cotangent, jnp.zeros_like(cotangent))
    cosine, sine = rotary_tables(positions_of(segment_ids))
    cosine, sine = cosine[:, 0], sine[:, 0]
    rest = jnp.ones((TOK_DEV, HD - ROT), jnp.float32)
    none = jnp.zeros_like(rest)
    gap = jnp.zeros_like(sine)
    rot_cos = jnp.concatenate([cosine, cosine, rest] * 2, axis=1)
    rot_up = jnp.concatenate([-sine, gap, none] * 2, axis=1)
    rot_down = jnp.concatenate([gap, sine, none] * 2, axis=1)
    slot_ids = jnp.arange(TOK_DEV, dtype=jnp.int32)
    allowed = (segment_ids[:, None] == segment_ids[None, :]) & (
        slot_ids[None, :] <= slot_ids[:, None]
    )
    small = (act_one, grad_y, vecs, rot_cos, rot_up, rot_down, allowed.astype(jnp.float32))
    moments = align_moments(moment_one, moment_two, rep)
    moments, blocks = lax.optimization_barrier((moments, blocks))
    first_moments = first_cross(moments)
    matrices, *attended = attention(jnp.stack([shard] + ids), blocks, own, small)
    moments, first_moments, attended = lax.optimization_barrier((moments, first_moments, attended))
    moments = [moments, first_moments, second_cross(moments), second_cross(first_moments)]
    small = (act_one, act_two, grad_y, vecs, attended[0], attended[1])
    made = weight_gradients(jnp.stack(slots_by_piece(shard, rep)), matrices, small)
    small = (tokens, normed, inv_std, grad_y, vecs) + tuple(attended) + tuple(made[16:])
    owned, moments, output, grad_input, vec_grads = scatter_sums(
        made[:16], moments, small, lambda small: layer_results(matrices, small)
    )
    own_vectors = lax.dynamic_index_in_dim(
        vec_grads.reshape(SHARDS, 4, D), shard, 0, keepdims=False
    )
    tokens_all = tokens.shape[0] * lax.axis_size(EVERY)
    grad_params, new_params = update_shard(
        spread_in_plane(owned),
        spread_ids(rep),
        own_vectors,
        params,
        moments,
        shard,
        1.0 / math.sqrt(tokens_all),
    )
    grad_params = grad_params.reshape(-1)
    width = moment_one.shape[0]
    grad_share = lax.dynamic_slice_in_dim(grad_params, rep * width, width)
    _, upd_first, upd_second = adam_update(moment_one, moment_one, moment_two, grad_share)
    return (output, grad_input, grad_params, new_params.reshape(-1), upd_first, upd_second)


def solution(mesh):
    in_rows = mesh.shape["rep"] == REPS and mesh.shape["shard"] == SHARDS
    if in_rows:
        rep, shard = PLANE, "z"
        mesh = Mesh(mesh.devices.reshape(2, 2, 2, SHARDS), EVERY)
        body = on_device_rows
    else:
        rep, shard = ("rep",), "shard"
        body = on_device
    rows = rep + (shard,)
    owner = (shard,) + rep
    in_specs = (P(rows, None), P(rows), P(rows, None), P(shard), P(owner), P(owner))
    out_specs = (P(rows, None), P(rows, None), P(shard), P(shard), P(owner), P(owner))
    return jax.shard_map(body, mesh=mesh, in_specs=in_specs, out_specs=out_specs, check_vma=False)
```

```python
import functools
import math

import jax
import jax.numpy as jnp
from jax import lax
from jax.experimental import pallas as pl
from jax.experimental.pallas import tpu as pltpu
from jax.sharding import Mesh
from jax.sharding import PartitionSpec as P

D = 768
HEADS = 12
HD = 64
ROT = 16
FF = 3072
TOK_DEV = 128


EPS_NORM = 1e-05
ROPE_BASE = 10000.0
NEG_BIG = -1e30
BETA_ONE = 0.9
BETA_TWO = 0.95
ADAM_STEP = 3.0
LEARN_RATE = 0.05
DECAY = 0.01
ADAM_EPS = 1e-08
INV_ROOT_TWO = 0.7071067811865476
INV_ROOT_TWO_PI = 0.3989422804014327


def layout_offsets():
    q_width = HEADS * HD
    o_wqkv = 2 * D
    o_bqkv = o_wqkv + 3 * q_width * D
    o_wout = o_bqkv + 3 * q_width
    o_bout = o_wout + q_width * D
    o_gain2 = o_bout + D
    o_shift2 = o_gain2 + D
    o_win = o_shift2 + D
    o_bin = o_win + D * FF
    o_wout2 = o_bin + FF
    o_bout2 = o_wout2 + FF * D
    return (
        o_wqkv,
        o_bqkv,
        o_wout,
        o_bout,
        o_gain2,
        o_shift2,
        o_win,
        o_bin,
        o_wout2,
        o_bout2,
        o_bout2 + D,
    )


def split_params(flat16):
    q_width = HEADS * HD
    o_wqkv, o_bqkv, o_wout, o_bout, o_gain2, o_shift2, o_win, o_bin, o_wout2, o_bout2, o_end = (
        layout_offsets()
    )
    return (
        flat16[0:D],
        flat16[D:o_wqkv],
        flat16[o_wqkv:o_bqkv].reshape(D, 3 * q_width),
        flat16[o_bqkv:o_wout],
        flat16[o_wout:o_bout].reshape(q_width, D),
        flat16[o_bout:o_gain2],
        flat16[o_gain2:o_shift2],
        flat16[o_shift2:o_win],
        flat16[o_win:o_bin].reshape(D, FF),
        flat16[o_bin:o_wout2],
        flat16[o_wout2:o_bout2].reshape(FF, D),
        flat16[o_bout2:o_end],
    )


def positions_of(segments):
    count = segments.shape[0]
    slot_ids = jnp.arange(count, dtype=jnp.int32)
    before = jnp.concatenate([jnp.full((1,), -2, jnp.int32), segments[:-1]])
    begins = segments != before
    first_slot = lax.cummax(jnp.where(begins, slot_ids, 0), axis=0)
    return slot_ids - first_slot


def rotary_tables(positions):
    half = ROT // 2
    steps_j = jnp.arange(half, dtype=jnp.float32)
    freqs = jnp.power(jnp.float32(ROPE_BASE), -2.0 * steps_j / ROT)
    angle = positions.astype(jnp.float32)[:, None] * freqs[None, :]
    return (jnp.cos(angle)[:, None, :], jnp.sin(angle)[:, None, :])


def rotate(values, cosine, sine, sign):
    half = cosine.shape[-1]
    lower = values[..., :half]
    upper = values[..., half : 2 * half]
    rest = values[..., 2 * half :]
    return jnp.concatenate(
        [lower * cosine - sign * upper * sine, upper * cosine + sign * lower * sine, rest], axis=-1
    )


def gelu_exact(value):
    return value * 0.5 * (1.0 + lax.erf(value * INV_ROOT_TWO))


def gelu_slope(value):
    return (
        0.5 * (1.0 + lax.erf(value * INV_ROOT_TWO))
        + value * jnp.exp(-0.5 * value * value) * INV_ROOT_TWO_PI
    )


def masked_scores(q_blk, keys, seg_rows, seg_cols, begin_row):
    scale = q_blk.shape[-1] ** (-0.5)
    raw_scores = jnp.einsum("qhd,khd->hqk", q_blk, keys, preferred_element_type=jnp.float32) * scale
    row_ids = begin_row + jnp.arange(q_blk.shape[0], dtype=jnp.int32)
    col_ids = jnp.arange(keys.shape[0], dtype=jnp.int32)
    allowed = (seg_rows[:, None] == seg_cols[None, :]) & (col_ids[None, :] <= row_ids[:, None])
    return jnp.where(allowed[None], raw_scores, NEG_BIG)


def attend_forward(query16, key16, value16, segments):
    scores = masked_scores(query16, key16, segments, segments, 0)
    row_max = jnp.max(scores, axis=-1, keepdims=True)
    expd = jnp.exp(scores - row_max)
    row_total = jnp.sum(expd, axis=-1, keepdims=True)
    probs16 = (expd / row_total).astype(jnp.bfloat16)
    attn_blk = jnp.einsum("hqk,khd->qhd", probs16, value16, preferred_element_type=jnp.float32)
    pieces_out = attn_blk.astype(jnp.bfloat16)
    lse_list = [row_max + jnp.log(row_total)]
    return (pieces_out, lse_list)


def attend_backward(query16, key16, value16, attn16, lse_list, segments, grad_attn16):
    count = query16.shape[0]
    block = min(512, count)
    scale = query16.shape[-1] ** (-0.5)
    grad_query = []
    grad_key = jnp.zeros(key16.shape, jnp.float32)
    grad_value = jnp.zeros(value16.shape, jnp.float32)
    for turn, begin_row in enumerate(range(0, count, block)):
        stop_row = begin_row + block
        scores = masked_scores(query16, key16, segments, segments, begin_row)
        chances = jnp.exp(scores - lse_list[turn])
        chances16 = chances.astype(jnp.bfloat16)
        grad_value = grad_value.at[:stop_row].add(
            jnp.einsum("hqk,qhd->khd", chances16, grad_attn16, preferred_element_type=jnp.float32)
        )
        grad_chance = jnp.einsum(
            "qhd,khd->hqk", grad_attn16, value16, preferred_element_type=jnp.float32
        )
        delta = jnp.sum(grad_attn16.astype(jnp.float32) * attn16.astype(jnp.float32), axis=-1)
        grad_scores = (chances * (grad_chance - jnp.transpose(delta)[:, :, None]) * scale).astype(
            jnp.bfloat16
        )
        grad_query.append(
            jnp.einsum("hqk,khd->qhd", grad_scores, key16, preferred_element_type=jnp.float32)
        )
        grad_key = grad_key.at[:stop_row].add(
            jnp.einsum("hqk,qhd->khd", grad_scores, query16, preferred_element_type=jnp.float32)
        )
    return (grad_query[0], grad_key, grad_value)


def norm_back(grad_act, normed, inv_std, gain):
    grad_gain = jnp.sum(grad_act * normed, axis=0)
    grad_shift = jnp.sum(grad_act, axis=0)
    grad_norm = grad_act * gain.astype(jnp.float32)
    grad_x = inv_std * (
        grad_norm
        - jnp.mean(grad_norm, axis=1, keepdims=True)
        - normed * jnp.mean(grad_norm * normed, axis=1, keepdims=True)
    )
    return (grad_gain, grad_shift, grad_x)


def layer_forward(tokens, segments, pieces):
    (
        gain_one,
        shift_one,
        w_qkv,
        b_qkv,
        w_out,
        b_out,
        gain_two,
        shift_two,
        w_in,
        b_in,
        w_out2,
        b_out2,
    ) = pieces
    count = tokens.shape[0]
    x_wide = tokens.astype(jnp.float32)
    row_mean = jnp.mean(x_wide, axis=1, keepdims=True)
    centered = x_wide - row_mean
    variance = jnp.mean(centered * centered, axis=1, keepdims=True)
    inv_std = lax.rsqrt(variance + EPS_NORM)
    normed = centered * inv_std
    act_one = (normed * gain_one.astype(jnp.float32) + shift_one.astype(jnp.float32)).astype(
        jnp.bfloat16
    )
    act_two = (normed * gain_two.astype(jnp.float32) + shift_two.astype(jnp.float32)).astype(
        jnp.bfloat16
    )
    mixed = jnp.dot(act_one, w_qkv, preferred_element_type=jnp.float32) + b_qkv.astype(jnp.float32)
    mixed = mixed.reshape(count, 3, HEADS, HD)
    cosine, sine = rotary_tables(positions_of(segments))
    query16 = rotate(mixed[:, 0], cosine, sine, 1.0).astype(jnp.bfloat16)
    key16 = rotate(mixed[:, 1], cosine, sine, 1.0).astype(jnp.bfloat16)
    value16 = mixed[:, 2].astype(jnp.bfloat16)
    attn16, lse_list = attend_forward(query16, key16, value16, segments)
    proj = jnp.dot(
        attn16.reshape(count, HEADS * HD), w_out, preferred_element_type=jnp.float32
    ) + b_out.astype(jnp.float32)
    pre = jnp.dot(act_two, w_in, preferred_element_type=jnp.float32) + b_in.astype(jnp.float32)
    hidden16 = gelu_exact(pre).astype(jnp.bfloat16)
    feed = jnp.dot(hidden16, w_out2, preferred_element_type=jnp.float32) + b_out2.astype(
        jnp.float32
    )
    output = x_wide + proj + feed
    saved = (
        normed,
        inv_std,
        act_one,
        act_two,
        query16,
        key16,
        value16,
        attn16,
        lse_list,
        cosine,
        sine,
        pre,
        hidden16,
    )
    return (output, saved)


def layer_backward(cotangent, segments, pieces, saved):
    (
        gain_one,
        shift_one,
        w_qkv,
        b_qkv,
        w_out,
        b_out,
        gain_two,
        shift_two,
        w_in,
        b_in,
        w_out2,
        b_out2,
    ) = pieces
    (
        normed,
        inv_std,
        act_one,
        act_two,
        query16,
        key16,
        value16,
        attn16,
        lse_list,
        cosine,
        sine,
        pre,
        hidden16,
    ) = saved
    count = cotangent.shape[0]
    contract_rows = (((0,), (0,)), ((), ()))
    contract_cols = (((1,), (1,)), ((), ()))
    live_rows = (segments >= 0).astype(jnp.float32)[:, None]
    grad_y = cotangent.astype(jnp.float32) * live_rows
    grad_y16 = grad_y.astype(jnp.bfloat16)
    grad_b_out = jnp.sum(grad_y, axis=0)
    attn_flat = attn16.reshape(count, HEADS * HD)
    grad_w_out = lax.dot_general(
        attn_flat, grad_y16, contract_rows, preferred_element_type=jnp.float32
    )
    grad_w_out2 = lax.dot_general(
        hidden16, grad_y16, contract_rows, preferred_element_type=jnp.float32
    )
    grad_hidden = lax.dot_general(
        grad_y16, w_out2, contract_cols, preferred_element_type=jnp.float32
    )
    grad_pre = grad_hidden * gelu_slope(pre)
    grad_b_in = jnp.sum(grad_pre, axis=0)
    grad_pre16 = grad_pre.astype(jnp.bfloat16)
    grad_w_in = lax.dot_general(
        act_two, grad_pre16, contract_rows, preferred_element_type=jnp.float32
    )
    grad_act_two = lax.dot_general(
        grad_pre16, w_in, contract_cols, preferred_element_type=jnp.float32
    )
    grad_attn16 = (
        lax.dot_general(grad_y16, w_out, contract_cols, preferred_element_type=jnp.float32)
        .astype(jnp.bfloat16)
        .reshape(count, HEADS, HD)
    )
    grad_query, grad_key, grad_value = attend_backward(
        query16, key16, value16, attn16, lse_list, segments, grad_attn16
    )
    grad_query = rotate(grad_query, cosine, sine, -1.0)
    grad_key = rotate(grad_key, cosine, sine, -1.0)
    grad_mixed = jnp.stack([grad_query, grad_key, grad_value], axis=1).reshape(
        count, 3 * HEADS * HD
    )
    grad_b_qkv = jnp.sum(grad_mixed, axis=0)
    grad_mixed16 = grad_mixed.astype(jnp.bfloat16)
    grad_w_qkv = lax.dot_general(
        act_one, grad_mixed16, contract_rows, preferred_element_type=jnp.float32
    )
    grad_act_one = lax.dot_general(
        grad_mixed16, w_qkv, contract_cols, preferred_element_type=jnp.float32
    )
    gain_grad_one, shift_grad_one, grad_x_one = norm_back(grad_act_one, normed, inv_std, gain_one)
    gain_grad_two, shift_grad_two, grad_x_two = norm_back(grad_act_two, normed, inv_std, gain_two)
    grad_in = grad_y + grad_x_one + grad_x_two
    return (
        grad_in,
        [
            gain_grad_one,
            shift_grad_one,
            grad_w_qkv,
            grad_b_qkv,
            grad_w_out,
            grad_b_out,
            gain_grad_two,
            shift_grad_two,
            grad_w_in,
            grad_b_in,
            grad_w_out2,
            grad_b_out,
        ],
    )


def flatten_grads(parts, total_len):
    used = layout_offsets()[-1]
    rounded = [part.astype(jnp.bfloat16).reshape(-1) for part in parts]
    return jnp.concatenate(rounded + [jnp.zeros((total_len - used,), jnp.bfloat16)])


def adam_update(weights, first_moment, second_moment, gradient):
    new_first = BETA_ONE * first_moment + (1.0 - BETA_ONE) * gradient
    new_second = BETA_TWO * second_moment + (1.0 - BETA_TWO) * gradient * gradient
    unbiased_first = new_first / (1.0 - BETA_ONE**ADAM_STEP)
    unbiased_second = new_second / (1.0 - BETA_TWO**ADAM_STEP)
    new_weights = weights - LEARN_RATE * (
        unbiased_first / (jnp.sqrt(unbiased_second) + ADAM_EPS) + DECAY * weights
    )
    return (new_weights, new_first, new_second)


def on_device(tokens, segment_ids, cotangent, params, moment_one, moment_two):
    gathered = lax.all_gather(params.astype(jnp.bfloat16), "shard", axis=0, tiled=True)
    total_len = gathered.shape[0]
    pieces = split_params(gathered)
    output, saved = layer_forward(tokens, segment_ids, pieces)
    grad_input, parts = layer_backward(cotangent, segment_ids, pieces, saved)
    local_grad = flatten_grads(parts, total_len)
    owned = lax.psum_scatter(local_grad, "shard", scatter_dimension=0, tiled=True).astype(
        jnp.float32
    )
    tokens_all = tokens.shape[0] * lax.axis_size("rep") * lax.axis_size("shard")
    factor = 1.0 / math.sqrt(tokens_all)
    width = moment_one.shape[0]
    begin = lax.axis_index("rep") * width
    param_share = lax.dynamic_slice_in_dim(params, begin, width)
    share = lax.psum_scatter(owned, "rep", scatter_dimension=0, tiled=True)
    grad_share = share * factor
    upd_params, upd_first, upd_second = adam_update(param_share, moment_one, moment_two, grad_share)
    grad_params, new_params = (
        lax.all_gather(grad_share, "rep", axis=0, tiled=True),
        lax.all_gather(upd_params, "rep", axis=0, tiled=True),
    )
    return (output, grad_input, grad_params, new_params, upd_first, upd_second)


LANES = 128
REPS = 8
SHARDS = 4
PIECE = 288
FLAT_ROWS = 13848
MOVED = PIECE * D // LANES


PARTS = (
    ((12, 1728, 96, 3, 0),),
    ((6, 576, 96, 1, 0), (4632, 1152, 48, 4, 96)),
    ((0, 1152, 48, 4, 0), (9240, 576, 96, 1, 192)),
    ((0, 1728, 288, 1, 0),),
)
VECTOR_ROWS = ((0, 1, 2306, 2307), (0, 769, 770, 771), (1536, 1537, 1538, 1539), (2304, 2305, 2306, 2307))


PLANE = ("y", "x", "core")
EVERY = PLANE + ("z",)
HOPS = (1, 2, 3, 0)


def plane_permute(value, flips):
    return lax.ppermute(value, PLANE, [(i, i ^ flips[i % 2]) for i in range(REPS)])


def first_cross(value):
    return plane_permute(value, (2, 4))


def second_cross(value):
    return plane_permute(value, (4, 2))


def core_cross(value):
    return plane_permute(value, (1, 1))


def ring_step(value):
    return lax.ppermute(value, "z", [(i, (i + 1) % SHARDS) for i in range(SHARDS)])


def flips_of(rep):
    core = rep % 2
    first = 2 + 2 * core
    return (0, first, 6 - first, 6)


def spread_ids(rep):
    other = rep ^ 1
    return [rep ^ flip for flip in flips_of(rep)] + [other ^ flip for flip in flips_of(other)]


def window_of(row):
    return min(6 * row // 8 * 8, FLAT_ROWS - 16)


def pack_kernel(where, flat_ref, out_ref, *rest):
    vec_ref = rest[0] if len(rest) == 4 else None
    held, windows, sems = rest[-3:]
    shard = where[0]
    turns = out_ref.shape[0]
    for z in range(SHARDS):

        @pl.when(shard == z)
        def _(z=z):
            def copies_of(turn):
                slot = turn % 2
                rep = where[1 + turn]
                copies = []
                at = 0
                for part, (first, step, _, _, _) in enumerate(PARTS[z]):
                    lead = first % 8
                    count = step + (8 if lead else 0)
                    begin = pl.multiple_of(first - lead + step * rep, 8)
                    copies.append(
                        pltpu.make_async_copy(
                            flat_ref.at[pl.ds(begin, count)],
                            held.at[slot, pl.ds(at, count)],
                            sems.at[slot, part],
                        )
                    )
                    at += count
                return copies

            for copy in copies_of(0):
                copy.start()
            if vec_ref is not None:
                cuts = []
                for slot, row in enumerate(VECTOR_ROWS[z]):
                    cuts.append(
                        pltpu.make_async_copy(
                            flat_ref.at[pl.ds(window_of(row), 16)],
                            windows.at[slot],
                            sems.at[2 + slot // 2, slot % 2],
                        )
                    )
                    cuts[-1].start()
                vec_ref[...] = jnp.zeros_like(vec_ref)
                for slot, row in enumerate(VECTOR_ROWS[z]):
                    cuts[slot].wait()
                    lead = 6 * row - window_of(row)
                    for col in range(6):
                        got = windows[slot, lead + col : lead + col + 1, :]
                        vec_ref[slot : slot + 1, LANES * col : LANES * (col + 1)] = got.astype(
                            jnp.bfloat16
                        ).astype(jnp.float32)

            @pl.loop(0, turns)
            def _(turn):
                @pl.when(turn + 1 < turns)
                def _():
                    for copy in copies_of(turn + 1):
                        copy.start()

                slot = turn % 2
                at = 0
                for copy, (first, step, rows, blocks, place) in zip(copies_of(turn), PARTS[z]):
                    copy.wait()
                    lead = first % 8
                    for block in range(blocks):
                        for col in range(6):
                            begin = at + lead + 6 * block + col
                            got = held[slot, pl.ds(begin, rows, stride=6 * blocks), :]
                            out_ref[
                                turn,
                                place + rows * block : place + rows * (block + 1),
                                LANES * col : LANES * (col + 1),
                            ] = got.astype(jnp.bfloat16)
                    at += step + (8 if lead else 0)


def pack_pieces(params, shard, reps, vectors):
    pieces = jax.ShapeDtypeStruct((len(reps), PIECE, D), jnp.bfloat16)
    rows = jax.ShapeDtypeStruct((8, D), jnp.float32)
    vmem = pl.BlockSpec(memory_space=pltpu.VMEM)
    return pl.pallas_call(
        pack_kernel,
        grid_spec=pltpu.PrefetchScalarGridSpec(
            num_scalar_prefetch=1,
            in_specs=[pl.BlockSpec(memory_space=pltpu.HBM)],
            out_specs=[vmem, vmem] if vectors else [vmem],
            scratch_shapes=[
                pltpu.VMEM((2, MOVED + 16, LANES), jnp.float32),
                pltpu.VMEM((4, 16, LANES), jnp.float32),
                pltpu.SemaphoreType.DMA((4, 2)),
            ],
        ),
        out_shape=[pieces, rows] if vectors else [pieces],
        compiler_params=pltpu.CompilerParams(vmem_limit_bytes=56 * 2**20),
    )(jnp.stack([shard] + reps), params.reshape(FLAT_ROWS, LANES))


def prepare_kernel(tokens, cotangent, ids, freqs, normed, spread, grad_y, tables):
    x_wide = tokens[...].astype(jnp.float32)
    centered = x_wide - jnp.mean(x_wide, axis=1, keepdims=True)
    variance = jnp.mean(centered * centered, axis=1, keepdims=True)
    inv_std = lax.rsqrt(variance + EPS_NORM)
    normed[...] = centered * inv_std
    spread[...] = jnp.broadcast_to(inv_std, spread.shape)
    square = (TOK_DEV, TOK_DEV)
    across = jnp.broadcast_to(ids[...].astype(jnp.float32), square)
    down = across.T
    lane = lax.broadcasted_iota(jnp.int32, square, 1)
    row = lax.broadcasted_iota(jnp.int32, square, 0)
    begins = (across != pltpu.roll(across, 1, 1)) | (lane == 0)
    before = jnp.where(begins & (lane <= row), lane.astype(jnp.float32), 0.0)
    position = row.astype(jnp.float32) - jnp.max(before, axis=1, keepdims=True)
    angle = position * freqs[...]
    cosine, sine = jnp.cos(angle), jnp.sin(angle)
    within = lane % HD
    tables[0] = jnp.where(within < ROT, cosine, 1.0)
    tables[1] = jnp.where(within < ROT // 2, -sine, 0.0)
    tables[2] = jnp.where((within >= ROT // 2) & (within < ROT), sine, 0.0)
    tables[3] = jnp.where((across == down) & (lane <= row), 1.0, 0.0)
    cot = cotangent[...].astype(jnp.float32)
    grad_y[...] = jnp.where(down[:, 0:1] >= 0, cot, 0.0).astype(jnp.bfloat16)


def prepare(tokens, cotangent, segment_ids):
    steps = jnp.arange(LANES, dtype=jnp.int32) % (ROT // 2)
    freqs = jnp.power(jnp.float32(ROPE_BASE), -2.0 * steps.astype(jnp.float32) / ROT)
    return pl.pallas_call(
        prepare_kernel,
        out_shape=[
            jax.ShapeDtypeStruct((TOK_DEV, D), jnp.float32),
            jax.ShapeDtypeStruct((TOK_DEV, LANES), jnp.float32),
            jax.ShapeDtypeStruct((TOK_DEV, D), jnp.bfloat16),
            jax.ShapeDtypeStruct((4, TOK_DEV, TOK_DEV), jnp.float32),
        ],
        compiler_params=pltpu.CompilerParams(vmem_limit_bytes=16 * 2**20),
    )(tokens, cotangent, segment_ids.reshape(1, TOK_DEV), freqs.reshape(1, LANES))


PIECES = SHARDS * REPS
GROUPS = 12
ALL_ROWS = PIECES * PIECE


def fetch_pieces(ids, blocks, own, shard, held, sems):
    views = []
    for block in blocks:
        views += [block.at[p] for p in range(4)] if len(block.shape) == 3 else [block]
    ids = ids + [shard * REPS + r for r in range(REPS)]
    views += [own.at[pl.ds(r * PIECE, PIECE)] for r in range(REPS)]
    for which, view in zip(ids, views):
        row = pl.multiple_of(which * PIECE, 16)
        pltpu.make_async_copy(view, held.at[pl.ds(row, PIECE)], sems.at[which]).start()

    def arrive(owner):
        for r in range(REPS):
            at = owner * REPS + r
            pltpu.make_async_copy(
                own.at[pl.ds(0, PIECE)], held.at[pl.ds(at * PIECE, PIECE)], sems.at[at]
            ).wait()

    return arrive


def rows_of(held, shard, begin, rows):
    return jnp.concatenate(
        [held[pl.ds((shard * REPS + r) * PIECE + begin, rows), :] for r in range(REPS)], axis=0
    )


def w_qkv_of(held, j):
    return rows_of(held, 0, 96 * j, 96)


def w_out_of(held):
    return rows_of(held, 1, 0, 96)


def w_in_of(held, j):
    return jnp.concatenate([rows_of(held, 1, 96 + 48 * j, 48), rows_of(held, 2, 48 * j, 48)], axis=0)


def w_out2_of(held, j):
    if j == 0:
        return rows_of(held, 2, 192, 96)
    return held[pl.ds(3 * REPS * PIECE + D * (j - 1), D), :]


def dot32(a, b):
    return jnp.dot(a, b, preferred_element_type=jnp.float32)


def attention_kernel(where, *refs):
    count = PIECES - REPS
    blocks, own = refs[:GROUPS], refs[GROUPS]
    normed, grad_y, tables = refs[GROUPS + 1 : GROUPS + 4]
    hops = refs[GROUPS + 4 : GROUPS + 8]
    matrices, attn_out, mixed_out, sums_out, vecs = refs[GROUPS + 8 : GROUPS + 13]
    held, query, key, value, grad_attn, sems, save_sem = refs[GROUPS + 13 :]
    rot_cos, rot_up, rot_down, bias = (tables.at[turn] for turn in range(4))
    shard = where[0]
    for owner in range(SHARDS):
        rows = jnp.zeros((4, D), jnp.float32)
        for hop in range(SHARDS):
            met = (shard + SHARDS - owner) % SHARDS == hop
            rows = jnp.where(met, hops[hop][0:4, :], rows)
        vecs[4 * owner : 4 * owner + 4, :] = rows
    arrive = fetch_pieces([where[1 + t] for t in range(count)], blocks, own, shard, held, sems)
    sums_out[...] = jnp.zeros_like(sums_out)

    arrive(0)
    act1 = (normed[...] * vecs[0:1, :] + vecs[1:2, :]).astype(jnp.bfloat16)
    for j, out in enumerate((query, key, value)):
        got = dot32(act1, w_qkv_of(held, j)) + vecs[2 + j : 3 + j, :]
        if j < 2:
            for p in range(6):
                lanes = slice(LANES * p, LANES * (p + 1))
                part = got[:, lanes]
                part = (
                    part * rot_cos[...]
                    + pltpu.roll(part, LANES - 8, 1) * rot_up[...]
                    + pltpu.roll(part, 8, 1) * rot_down[...]
                )
                out[:, lanes] = part.astype(jnp.bfloat16)
        else:
            out[...] = got.astype(jnp.bfloat16)
    gy_t = grad_y[...].T
    arrive(1)
    grad_attn[...] = dot32(w_out_of(held), gy_t).T.astype(jnp.bfloat16)

    arrive(2)
    arrive(3)
    saving = pltpu.make_async_copy(held, matrices, save_sem)
    saving.start()
    low = lax.broadcasted_iota(jnp.int32, (LANES, LANES), 1) < HD
    scale = HD ** (-0.5)
    for p in range(6):
        lanes = slice(LANES * p, LANES * (p + 1))
        q2, k2, v2, g2 = (ref[:, lanes] for ref in (query, key, value, grad_attn))
        k2_t, v2_t = k2.T, v2.T
        attn_parts, value_parts, query_parts, key_parts = [], [], [], []
        for half in range(2):
            here = low if half == 0 else ~low
            zero = jnp.zeros_like(q2)
            scores = dot32(jnp.where(here, q2, zero), k2_t) * scale
            scores = jnp.where(bias[...] > 0.5, scores, NEG_BIG)
            expd = jnp.exp(scores - jnp.max(scores, axis=1, keepdims=True))
            chances = expd / jnp.sum(expd, axis=1, keepdims=True)
            chances16 = chances.astype(jnp.bfloat16)
            attn = dot32(chances16, v2)
            attn16 = attn.astype(jnp.bfloat16)
            masked = jnp.where(here, g2, zero)
            delta = jnp.sum(
                masked.astype(jnp.float32) * attn16.astype(jnp.float32), axis=1, keepdims=True
            )
            grad_chance = dot32(masked, v2_t)
            slope = (chances * (grad_chance - delta) * scale).astype(jnp.bfloat16)
            attn_parts.append(attn16)
            value_parts.append(dot32(chances16.T, g2))
            query_parts.append(dot32(slope, k2))
            key_parts.append(dot32(slope.T, q2))
        attn_out[:, lanes] = jnp.where(low, *attn_parts)
        for j, parts in enumerate((query_parts, key_parts, value_parts)):
            part = jnp.where(low, *parts)
            if j < 2:
                part = (
                    part * rot_cos[...]
                    - pltpu.roll(part, LANES - 8, 1) * rot_up[...]
                    - pltpu.roll(part, 8, 1) * rot_down[...]
                )
            wide = slice(D * j + LANES * p, D * j + LANES * (p + 1))
            sums_out[j : j + 1, lanes] = jnp.sum(part, axis=0, keepdims=True)
            mixed_out[:, wide] = part.astype(jnp.bfloat16)

    saving.wait()


def attention(scalars, blocks, own, small):
    anywhere = pl.BlockSpec(memory_space=pl.ANY)
    vmem = pl.BlockSpec(memory_space=pltpu.VMEM)
    bf16 = jnp.bfloat16
    return pl.pallas_call(
        attention_kernel,
        grid_spec=pltpu.PrefetchScalarGridSpec(
            num_scalar_prefetch=1,
            in_specs=[anywhere] * (len(blocks) + 1) + [vmem] * len(small),
            out_specs=[anywhere] + [vmem] * 4,
            scratch_shapes=[
                pltpu.VMEM((ALL_ROWS, D), bf16),
                pltpu.VMEM((TOK_DEV, D), bf16),
                pltpu.VMEM((TOK_DEV, D), bf16),
                pltpu.VMEM((TOK_DEV, D), bf16),
                pltpu.VMEM((TOK_DEV, D), bf16),
                pltpu.SemaphoreType.DMA((PIECES,)),
                pltpu.SemaphoreType.DMA,
            ],
        ),
        out_shape=[
            jax.ShapeDtypeStruct((ALL_ROWS, D), bf16),
            jax.ShapeDtypeStruct((TOK_DEV, D), bf16),
            jax.ShapeDtypeStruct((TOK_DEV, 3 * D), bf16),
            jax.ShapeDtypeStruct((8, D), jnp.float32),
            jax.ShapeDtypeStruct((16, D), jnp.float32),
        ],
        compiler_params=pltpu.CompilerParams(vmem_limit_bytes=26 * 2**20),
        cost_estimate=pl.CostEstimate(
            flops=6 * 10**9, bytes_accessed=60 * 2**20, transcendentals=200000
        ),
    )(scalars, *blocks, own, *small)


def gradient_kernel(where, matrices, *refs):
    (normed, grad_y, attn_in, mixed_in, vecs) = refs[:5]
    outs = refs[5:21]
    hidden_out, pre_out, sums_out = refs[21:24]
    held, grads, sems, out_sems = refs[24:]
    copies = []
    for z in range(1, SHARDS):
        rows = pl.ds(z * REPS * PIECE, REPS * PIECE)
        copies.append(pltpu.make_async_copy(matrices.at[rows], held.at[rows], sems.at[z]))
    for copy in copies:
        copy.start()
    sums_out[...] = jnp.zeros_like(sums_out)
    slot_row = lambda z, r: pl.multiple_of(where[z * REPS + r] * PIECE, 16)

    def keep_rows(z, begin, rows, part):
        for r in range(part.shape[0] // rows):
            grads[pl.ds(slot_row(z, r) + begin, rows), :] = part[rows * r : rows * (r + 1), :]

    gy = grad_y[...]
    act1_t = (normed[...] * vecs[0:1, :] + vecs[1:2, :]).astype(jnp.bfloat16).T
    for j in range(3):
        keep_rows(
            0, 96 * j, 96, dot32(act1_t, mixed_in[:, D * j : D * (j + 1)]).astype(jnp.bfloat16)
        )
    keep_rows(1, 0, 96, dot32(attn_in[...].T, gy).astype(jnp.bfloat16))

    for copy in copies:
        copy.wait()
    gy_t = gy.T
    act2 = (normed[...] * vecs[6:7, :] + vecs[7:8, :]).astype(jnp.bfloat16)
    act2_t = act2.T
    for j in range(4):
        wide = slice(D * j, D * (j + 1))
        pre = dot32(act2, w_in_of(held, j)) + vecs[8 + j : 9 + j, :]
        bell = 0.5 * (1.0 + lax.erf(pre * INV_ROOT_TWO))
        hidden = (pre * bell).astype(jnp.bfloat16)
        hidden_out[:, wide] = hidden
        grad_hidden = dot32(w_out2_of(held, j), gy_t).T
        grad_pre = grad_hidden * (bell + pre * jnp.exp(-0.5 * pre * pre) * INV_ROOT_TWO_PI)
        sums_out[j : j + 1, :] = jnp.sum(grad_pre, axis=0, keepdims=True)
        grad_pre16 = grad_pre.astype(jnp.bfloat16)
        pre_out[:, wide] = grad_pre16
        w2 = dot32(hidden.T, gy).astype(jnp.bfloat16)
        if j == 0:
            keep_rows(2, 192, 96, w2)
        else:
            at = D * (j - 1)
            while at < D * j:
                r, begin = divmod(at, PIECE)
                rows = min(PIECE - begin, D * j - at)
                grads[pl.ds(slot_row(3, r) + begin, rows), :] = w2[
                    at - D * (j - 1) : at - D * (j - 1) + rows, :
                ]
                at += rows
        w1 = dot32(act2_t, grad_pre16).astype(jnp.bfloat16)
        keep_rows(1, 96 + 48 * j, 48, w1[: D // 2])
        keep_rows(2, 48 * j, 48, w1[D // 2 :])
    copies = []
    for turn, out in enumerate(outs):
        for p in range(2):
            copies.append(
                pltpu.make_async_copy(
                    grads.at[pl.ds((turn * 2 + p) * PIECE, PIECE)],
                    out.at[p],
                    out_sems.at[turn * 2 + p],
                )
            )
    for copy in copies:
        copy.start()
    for copy in copies:
        copy.wait()


def weight_gradients(slots, matrices, small):
    anywhere = pl.BlockSpec(memory_space=pl.ANY)
    vmem = pl.BlockSpec(memory_space=pltpu.VMEM)
    bf16 = jnp.bfloat16
    return pl.pallas_call(
        gradient_kernel,
        grid_spec=pltpu.PrefetchScalarGridSpec(
            num_scalar_prefetch=1,
            in_specs=[anywhere] + [vmem] * len(small),
            out_specs=[anywhere] * 16 + [vmem] * 3,
            scratch_shapes=[
                pltpu.VMEM((ALL_ROWS, D), bf16),
                pltpu.VMEM((ALL_ROWS, D), bf16),
                pltpu.SemaphoreType.DMA((SHARDS,)),
                pltpu.SemaphoreType.DMA((PIECES,)),
            ],
        ),
        out_shape=[jax.ShapeDtypeStruct((2, PIECE, D), bf16)] * 16
        + [
            jax.ShapeDtypeStruct((TOK_DEV, FF), bf16),
            jax.ShapeDtypeStruct((TOK_DEV, FF), bf16),
            jax.ShapeDtypeStruct((8, D), jnp.float32),
        ],
        compiler_params=pltpu.CompilerParams(vmem_limit_bytes=48 * 2**20),
        cost_estimate=pl.CostEstimate(
            flops=10**10, bytes_accessed=60 * 2**20, transcendentals=800000
        ),
    )(slots, matrices, *small)


def result_kernel(matrices, *refs):
    (tokens, normed, spread, grad_y, attn, grad_mixed, low_sums, vecs, hidden, grad_pre, high_sums) = (
        refs[:11]
    )
    output, grad_input, vec_out, held, sems = refs[11:]
    copies = []
    for z in range(SHARDS):
        rows = pl.ds(z * REPS * PIECE, REPS * PIECE)
        copies.append(pltpu.make_async_copy(matrices.at[rows], held.at[rows], sems.at[z]))
    for copy in copies:
        copy.start()
    for copy in copies:
        copy.wait()
    total = dot32(attn[...], w_out_of(held)) + vecs[5:6, :]
    for j in range(4):
        total = total + dot32(hidden[:, D * j : D * (j + 1)], w_out2_of(held, j))
    output[...] = tokens[...].astype(jnp.float32) + (total + vecs[12:13, :])
    vec_out[2:5, :] = low_sums[0:3, :]
    vec_out[8:12, :] = high_sums[0:4, :]
    gy = grad_y[...].astype(jnp.float32)
    total = gy
    for norm, (parts, width, weights) in enumerate(
        ((grad_mixed, 3, w_qkv_of), (grad_pre, 4, w_in_of))
    ):
        back = None
        for j in range(width):
            part = dot32(weights(held, j), parts[:, D * j : D * (j + 1)].T)
            back = part if back is None else back + part
        grad_act = back.T
        gain_row = 0 if norm == 0 else 6
        unit = normed[...]
        vec_out[gain_row : gain_row + 1, :] = jnp.sum(grad_act * unit, axis=0, keepdims=True)
        vec_out[gain_row + 1 : gain_row + 2, :] = jnp.sum(grad_act, axis=0, keepdims=True)
        grad_norm = grad_act * vecs[gain_row : gain_row + 1, :]
        total = total + spread[:, 0:1] * (
            grad_norm
            - jnp.mean(grad_norm, axis=1, keepdims=True)
            - unit * jnp.mean(grad_norm * unit, axis=1, keepdims=True)
        )
    grad_input[...] = total
    bottom = jnp.sum(gy, axis=0, keepdims=True)
    vec_out[5:6, :] = bottom
    vec_out[12:13, :] = bottom
    vec_out[13:16, :] = jnp.zeros((3, D), jnp.float32)
    vec_out[...] = vec_out[...].astype(jnp.bfloat16).astype(jnp.float32)


def layer_results(matrices, small):
    hbm = pl.BlockSpec(memory_space=pl.ANY)
    vmem = pl.BlockSpec(memory_space=pltpu.VMEM)
    rows = jax.ShapeDtypeStruct((TOK_DEV, D), jnp.float32)
    return pl.pallas_call(
        result_kernel,
        in_specs=[hbm] + [vmem] * len(small),
        out_specs=[vmem] * 3,
        scratch_shapes=[
            pltpu.VMEM((ALL_ROWS, D), jnp.bfloat16),
            pltpu.SemaphoreType.DMA((SHARDS,)),
        ],
        out_shape=[rows, rows, jax.ShapeDtypeStruct((16, D), jnp.float32)],
        compiler_params=pltpu.CompilerParams(vmem_limit_bytes=26 * 2**20),
        cost_estimate=pl.CostEstimate(
            flops=4 * 10**9, bytes_accessed=30 * 2**20, transcendentals=0
        ),
    )(matrices, *small)


SHARE = FLAT_ROWS // REPS
BEGINS = tuple(SHARE * r // 16 * 16 for r in range(REPS)) + (FLAT_ROWS,)
SHARE_ROWS = 1760
STEP = 288


def align_kernel(where, one_ref, two_ref, out_ref, held):
    for r in range(REPS):

        @pl.when(where[0] == r)
        def _(r=r):
            lead = SHARE * r - BEGINS[r]
            for turn, ref in enumerate((one_ref, two_ref)):
                held[0:16, :] = jnp.zeros((16, LANES), jnp.float32)
                held[SHARE_ROWS - 32 :, :] = jnp.zeros((32, LANES), jnp.float32)
                held[lead : lead + SHARE, :] = ref[...]
                out_ref[turn] = held[...].astype(jnp.bfloat16)


def align_moments(moment_one, moment_two, rep):
    return pl.pallas_call(
        align_kernel,
        grid_spec=pltpu.PrefetchScalarGridSpec(
            num_scalar_prefetch=1,
            in_specs=[pl.BlockSpec(memory_space=pltpu.VMEM)] * 2,
            out_specs=pl.BlockSpec(memory_space=pltpu.VMEM),
            scratch_shapes=[pltpu.VMEM((SHARE_ROWS, LANES), jnp.float32)],
        ),
        out_shape=jax.ShapeDtypeStruct((2, SHARE_ROWS, LANES), jnp.bfloat16),
        compiler_params=pltpu.CompilerParams(vmem_limit_bytes=16 * 2**20),
    )(jnp.stack([rep]), moment_one.reshape(SHARE, LANES), moment_two.reshape(SHARE, LANES))


def update_kernel(factor, where, *refs):
    blocks = refs[:REPS]
    moments = refs[REPS : 2 * REPS]
    vec_ref, params, grad_out, params_out = refs[2 * REPS : 2 * REPS + 4]
    held, grad, weight, moment, sems, out_sems = refs[2 * REPS + 4 :]
    copies = []
    for turn in range(REPS):
        copies.append(
            pltpu.make_async_copy(blocks[turn], held.at[where[1 + turn]], sems.at[turn])
        )
    copies.append(pltpu.make_async_copy(params, weight, sems.at[REPS]))
    for turn in range(REPS):
        copies.append(
            pltpu.make_async_copy(
                moments[turn], moment.at[where[1 + turn]], sems.at[REPS + 1 + turn]
            )
        )
    for copy in copies:
        copy.start()
    for copy in copies[:REPS]:
        copy.wait()
    shard = where[0]
    for z in range(SHARDS):

        @pl.when(shard == z)
        def _(z=z):
            for slot, row in enumerate(VECTOR_ROWS[z]):
                for col in range(6):
                    grad[6 * row + col : 6 * row + col + 1, :] = (
                        vec_ref[slot : slot + 1, LANES * col : LANES * (col + 1)] * factor
                    )

            @pl.loop(0, REPS)
            def _(rep):
                for first, step, rows, blocks, place in PARTS[z]:
                    for block in range(blocks):
                        for col in range(6):
                            got = held[
                                rep,
                                place + rows * block : place + rows * (block + 1),
                                LANES * col : LANES * (col + 1),
                            ]
                            begin = first + step * rep + 6 * block + col
                            grad[pl.ds(begin, rows, stride=6 * blocks), :] = (
                                got.astype(jnp.float32) * factor
                            )

    saving = [pltpu.make_async_copy(grad, grad_out, out_sems.at[REPS])]
    saving[0].start()
    for copy in copies[REPS:]:
        copy.wait()
    for r in range(REPS):
        base = BEGINS[r]
        length = BEGINS[r + 1] - base
        if r > 0:
            tail = base - BEGINS[r - 1]
            moment[r, :, 0:16, :] = moment[r, :, 0:16, :] + moment[r - 1, :, tail : tail + 16, :]

        def renew(at, rows, r=r, base=base):
            here = pl.ds(pl.multiple_of(base + at, 8), rows)
            there = pl.ds(pl.multiple_of(at, 16), rows)
            updated, _, _ = adam_update(
                weight[here, :],
                moment[r, 0, there, :].astype(jnp.float32),
                moment[r, 1, there, :].astype(jnp.float32),
                grad[here, :],
            )
            weight[here, :] = updated

        @pl.loop(0, length // STEP)
        def _(turn):
            renew(turn * STEP, STEP)

        if length % STEP:
            renew(length // STEP * STEP, length % STEP)
        rows = pl.ds(base, length)
        saving.append(
            pltpu.make_async_copy(weight.at[rows], params_out.at[rows], out_sems.at[r])
        )
        saving[-1].start()
    for copy in saving:
        copy.wait()


def update_shard(blocks, ids, vectors, params, moments, shard, factor):
    anywhere = pl.BlockSpec(memory_space=pl.ANY)
    flat = jax.ShapeDtypeStruct((FLAT_ROWS, LANES), jnp.float32)
    return pl.pallas_call(
        functools.partial(update_kernel, factor),
        grid_spec=pltpu.PrefetchScalarGridSpec(
            num_scalar_prefetch=1,
            in_specs=[anywhere] * (2 * REPS)
            + [pl.BlockSpec(memory_space=pltpu.VMEM), anywhere],
            out_specs=[anywhere] * 2,
            scratch_shapes=[
                pltpu.VMEM((REPS, PIECE, D), jnp.bfloat16),
                pltpu.VMEM((FLAT_ROWS, LANES), jnp.float32),
                pltpu.VMEM((FLAT_ROWS, LANES), jnp.float32),
                pltpu.VMEM((REPS, 2, SHARE_ROWS, LANES), jnp.bfloat16),
                pltpu.SemaphoreType.DMA((2 * REPS + 1,)),
                pltpu.SemaphoreType.DMA((REPS + 1,)),
            ],
        ),
        out_shape=[flat, flat],
        compiler_params=pltpu.CompilerParams(vmem_limit_bytes=56 * 2**20),
    )(jnp.stack([shard] + ids), *blocks, *moments, vectors, params.reshape(FLAT_ROWS, LANES))


def ring_shift(value, hop):
    return lax.ppermute(value, "z", [(i, (i + hop) % SHARDS) for i in range(SHARDS)])


fence = lax.optimization_barrier


def gather_matrices(params, shard, rep, early):
    piece = pack_pieces(params, shard, [rep], False)[0][0]
    own, vec = pack_pieces(params, shard, [rep * 0 + turn for turn in range(REPS)], True)
    one = ring_step(piece)
    one, own, vec = fence((one, own, vec))
    two, first_one, second_one = ring_step(one), first_cross(one), second_cross(one)
    vec_one = ring_step(vec)
    two, first_one, second_one, vec_one, early = fence(
        (two, first_one, second_one, vec_one, early)
    )
    three, first_two, second_two = ring_step(two), first_cross(two), second_cross(two)
    both_one = second_cross(first_one)
    vec_two = ring_step(vec_one)
    three, first_two, second_two, both_one, vec_two = fence(
        (three, first_two, second_two, both_one, vec_two)
    )
    first_three, second_three = first_cross(three), second_cross(three)
    both_two = second_cross(first_two)
    mine_one = jnp.stack([one, first_one, second_one, both_one])
    other_one = core_cross(mine_one)
    vec_three = ring_step(vec_two)
    first_three, second_three, both_two, other_one, vec_three = fence(
        (first_three, second_three, both_two, other_one, vec_three)
    )
    both_three = second_cross(first_three)
    mine_two = jnp.stack([two, first_two, second_two, both_two])
    other_two = core_cross(mine_two)
    others = [core_cross(value) for value in (three, first_three, second_three)]
    others, both_three, other_two = fence((others, both_three, other_two))
    others.append(core_cross(both_three))
    threes = [three, first_three, second_three, both_three]
    blocks = [mine_one, other_one, mine_two, other_two] + threes + others
    ids = []
    for hop in range(1, SHARDS):
        owner = (shard + SHARDS - hop) % SHARDS
        ids += [owner * REPS + which for which in spread_ids(rep)]
    hops = [vec, vec_one, vec_two, vec_three]
    return blocks, own.reshape(REPS * PIECE, D), ids, hops, early


def slots_by_piece(shard, rep):
    slots = []
    for owner in range(SHARDS):
        hop = (shard + SHARDS - owner + 3) % SHARDS
        for which in range(REPS):
            apart = rep ^ which
            kept = 1 - apart % 2
            core = which % 2
            across = apart & 6
            first = 2 + 2 * core
            place = jnp.where(
                across == 0, 2, jnp.where(across == 6, 1, jnp.where(across == first, 0, 3))
            )
            slots.append((kept * SHARDS + hop) * 4 + place)
    return slots


def scatter_sums(parts, moments, small, results):
    sent_far, sent_near, kept_far, kept_near = (
        [parts[8 * half + 2 * turn + near] for turn in range(SHARDS)]
        for half in range(2)
        for near in range(2)
    )
    cores = [core_cross(sent_far[0]), core_cross(sent_near[0]), core_cross(sent_far[1])]
    cores = list(fence(cores))
    far = [kept_far[0] + cores[0], kept_far[1] + cores[2]]
    crossed = first_cross(far[0])
    others = [core_cross(v) for v in (sent_near[1], sent_far[2], sent_near[2], sent_far[3])]
    crossed, others, small = fence((crossed, others, small))
    near = [kept_near[0] + cores[1], kept_near[1] + others[0], kept_near[2] + others[2]]
    far += [kept_far[2] + others[1], kept_far[3] + others[3]]

    pair = near[0] + crossed
    final = second_cross(pair[1])
    kept = pair[0]
    crossed = first_cross(far[1])
    last_near = core_cross(sent_near[3])
    output, grad_input, vectors = results(small)
    final, crossed, last_near, vectors = fence((final, crossed, last_near, vectors))
    near.append(kept_near[3] + last_near)

    carried = None
    for turn in range(1, SHARDS):
        total = kept + final
        if carried is not None:
            total = total + carried
        carried = ring_step(total)
        pair = near[turn] + crossed
        kept = pair[0]
        final = second_cross(pair[1])
        met = plane_permute(vectors, ((1, 1), (2, 2), (4, 4))[turn - 1])
        if turn < SHARDS - 1:
            crossed = first_cross(far[turn + 1])
            final, crossed, carried, met = fence((final, crossed, carried, met))
        else:
            others = [core_cross(value) for value in moments[:2]]
            final, carried, met, others = fence((final, carried, met, others))
        vectors = vectors + met
    total = kept + final + carried

    first, second = first_cross(total), second_cross(total)
    shifted = [ring_shift(vectors, hop) for hop in range(1, SHARDS)]
    first, second, shifted = fence((first, second, shifted))
    vectors = vectors + shifted[0] + shifted[1] + shifted[2]
    both = second_cross(first)
    mine = [total, first, second]
    spread = [core_cross(value) for value in mine]
    last = core_cross(moments[2])
    both, spread, last = fence((both, spread, last))
    spread.append(core_cross(both))
    others += [last, core_cross(moments[3])]
    return mine + [both] + spread, moments + others, output, grad_input, vectors


def on_device_rows(tokens, segment_ids, cotangent, params, moment_one, moment_two):
    shard = lax.axis_index("z")
    rep = lax.axis_index(PLANE)
    early = (prepare(tokens, cotangent, segment_ids), align_moments(moment_one, moment_two, rep))
    blocks, own, ids, hops, early = gather_matrices(params, shard, rep, early)
    (normed, inv_std, grad_y, tables), moments = early
    moments, blocks = fence((moments, blocks))
    first_moments = first_cross(moments)
    small = (normed, grad_y, tables, *hops)
    matrices, *attended = attention(jnp.stack([shard] + ids), blocks, own, small)
    moments, first_moments, attended = fence((moments, first_moments, attended))
    moments = [moments, first_moments, second_cross(moments), second_cross(first_moments)]
    attn, mixed, low_sums, vecs = attended
    made = weight_gradients(
        jnp.stack(slots_by_piece(shard, rep)), matrices, (normed, grad_y, attn, mixed, vecs)
    )
    made, moments = fence((made, moments))
    small = (tokens, normed, inv_std, grad_y, attn, mixed, low_sums, vecs) + tuple(made[16:])
    spread, moments, output, grad_input, vec_grads = scatter_sums(
        made[:16], moments, small, lambda small: layer_results(matrices, small)
    )
    own_vectors = lax.dynamic_index_in_dim(
        vec_grads.reshape(SHARDS, 4, D), shard, 0, keepdims=False
    )
    tokens_all = tokens.shape[0] * lax.axis_size(EVERY)
    grad_params, new_params = update_shard(
        spread,
        spread_ids(rep),
        own_vectors,
        params,
        moments,
        shard,
        1.0 / math.sqrt(tokens_all),
    )
    grad_params = grad_params.reshape(-1)
    width = moment_one.shape[0]
    grad_share = lax.dynamic_slice_in_dim(grad_params, rep * width, width)
    _, upd_first, upd_second = adam_update(moment_one, moment_one, moment_two, grad_share)
    return (output, grad_input, grad_params, new_params.reshape(-1), upd_first, upd_second)


def solution(mesh):
    in_rows = mesh.shape["rep"] == REPS and mesh.shape["shard"] == SHARDS
    if in_rows:
        rep, shard = PLANE, "z"
        mesh = Mesh(mesh.devices.reshape(2, 2, 2, SHARDS), EVERY)
        body = on_device_rows
    else:
        rep, shard = ("rep",), "shard"
        body = on_device
    rows = rep + (shard,)
    owner = (shard,) + rep
    in_specs = (P(rows, None), P(rows), P(rows, None), P(shard), P(owner), P(owner))
    out_specs = (P(rows, None), P(rows, None), P(shard), P(shard), P(owner), P(owner))
    return jax.shard_map(body, mesh=mesh, in_specs=in_specs, out_specs=out_specs, check_vma=False)
```

```python
import functools
import math

import jax
import jax.numpy as jnp
from jax import lax
from jax.experimental import pallas as pl
from jax.experimental.pallas import tpu as pltpu
from jax.sharding import Mesh
from jax.sharding import PartitionSpec as P

D = 768
HEADS = 12
HD = 64
ROT = 16
FF = 3072
TOK_DEV = 128


EPS_NORM = 1e-05
ROPE_BASE = 10000.0
NEG_BIG = -1e30
BETA_ONE = 0.9
BETA_TWO = 0.95
ADAM_STEP = 3.0
LEARN_RATE = 0.05
DECAY = 0.01
ADAM_EPS = 1e-08
INV_ROOT_TWO = 0.7071067811865476
INV_ROOT_TWO_PI = 0.3989422804014327


def layout_offsets():
    q_width = HEADS * HD
    o_wqkv = 2 * D
    o_bqkv = o_wqkv + 3 * q_width * D
    o_wout = o_bqkv + 3 * q_width
    o_bout = o_wout + q_width * D
    o_gain2 = o_bout + D
    o_shift2 = o_gain2 + D
    o_win = o_shift2 + D
    o_bin = o_win + D * FF
    o_wout2 = o_bin + FF
    o_bout2 = o_wout2 + FF * D
    return (
        o_wqkv,
        o_bqkv,
        o_wout,
        o_bout,
        o_gain2,
        o_shift2,
        o_win,
        o_bin,
        o_wout2,
        o_bout2,
        o_bout2 + D,
    )


def split_params(flat16):
    q_width = HEADS * HD
    o_wqkv, o_bqkv, o_wout, o_bout, o_gain2, o_shift2, o_win, o_bin, o_wout2, o_bout2, o_end = (
        layout_offsets()
    )
    return (
        flat16[0:D],
        flat16[D:o_wqkv],
        flat16[o_wqkv:o_bqkv].reshape(D, 3 * q_width),
        flat16[o_bqkv:o_wout],
        flat16[o_wout:o_bout].reshape(q_width, D),
        flat16[o_bout:o_gain2],
        flat16[o_gain2:o_shift2],
        flat16[o_shift2:o_win],
        flat16[o_win:o_bin].reshape(D, FF),
        flat16[o_bin:o_wout2],
        flat16[o_wout2:o_bout2].reshape(FF, D),
        flat16[o_bout2:o_end],
    )


def positions_of(segments):
    count = segments.shape[0]
    slot_ids = jnp.arange(count, dtype=jnp.int32)
    before = jnp.concatenate([jnp.full((1,), -2, jnp.int32), segments[:-1]])
    begins = segments != before
    first_slot = lax.cummax(jnp.where(begins, slot_ids, 0), axis=0)
    return slot_ids - first_slot


def rotary_tables(positions):
    half = ROT // 2
    steps_j = jnp.arange(half, dtype=jnp.float32)
    freqs = jnp.power(jnp.float32(ROPE_BASE), -2.0 * steps_j / ROT)
    angle = positions.astype(jnp.float32)[:, None] * freqs[None, :]
    return (jnp.cos(angle)[:, None, :], jnp.sin(angle)[:, None, :])


def rotate(values, cosine, sine, sign):
    half = cosine.shape[-1]
    lower = values[..., :half]
    upper = values[..., half : 2 * half]
    rest = values[..., 2 * half :]
    return jnp.concatenate(
        [lower * cosine - sign * upper * sine, upper * cosine + sign * lower * sine, rest], axis=-1
    )


def gelu_exact(value):
    return value * 0.5 * (1.0 + lax.erf(value * INV_ROOT_TWO))


def gelu_slope(value):
    return (
        0.5 * (1.0 + lax.erf(value * INV_ROOT_TWO))
        + value * jnp.exp(-0.5 * value * value) * INV_ROOT_TWO_PI
    )


def masked_scores(q_blk, keys, seg_rows, seg_cols, begin_row):
    scale = q_blk.shape[-1] ** (-0.5)
    raw_scores = jnp.einsum("qhd,khd->hqk", q_blk, keys, preferred_element_type=jnp.float32) * scale
    row_ids = begin_row + jnp.arange(q_blk.shape[0], dtype=jnp.int32)
    col_ids = jnp.arange(keys.shape[0], dtype=jnp.int32)
    allowed = (seg_rows[:, None] == seg_cols[None, :]) & (col_ids[None, :] <= row_ids[:, None])
    return jnp.where(allowed[None], raw_scores, NEG_BIG)


def attend_forward(query16, key16, value16, segments):
    scores = masked_scores(query16, key16, segments, segments, 0)
    row_max = jnp.max(scores, axis=-1, keepdims=True)
    expd = jnp.exp(scores - row_max)
    row_total = jnp.sum(expd, axis=-1, keepdims=True)
    probs16 = (expd / row_total).astype(jnp.bfloat16)
    attn_blk = jnp.einsum("hqk,khd->qhd", probs16, value16, preferred_element_type=jnp.float32)
    pieces_out = attn_blk.astype(jnp.bfloat16)
    lse_list = [row_max + jnp.log(row_total)]
    return (pieces_out, lse_list)


def attend_backward(query16, key16, value16, attn16, lse_list, segments, grad_attn16):
    count = query16.shape[0]
    block = min(512, count)
    scale = query16.shape[-1] ** (-0.5)
    grad_query = []
    grad_key = jnp.zeros(key16.shape, jnp.float32)
    grad_value = jnp.zeros(value16.shape, jnp.float32)
    for turn, begin_row in enumerate(range(0, count, block)):
        stop_row = begin_row + block
        scores = masked_scores(query16, key16, segments, segments, begin_row)
        chances = jnp.exp(scores - lse_list[turn])
        chances16 = chances.astype(jnp.bfloat16)
        grad_value = grad_value.at[:stop_row].add(
            jnp.einsum("hqk,qhd->khd", chances16, grad_attn16, preferred_element_type=jnp.float32)
        )
        grad_chance = jnp.einsum(
            "qhd,khd->hqk", grad_attn16, value16, preferred_element_type=jnp.float32
        )
        delta = jnp.sum(grad_attn16.astype(jnp.float32) * attn16.astype(jnp.float32), axis=-1)
        grad_scores = (chances * (grad_chance - jnp.transpose(delta)[:, :, None]) * scale).astype(
            jnp.bfloat16
        )
        grad_query.append(
            jnp.einsum("hqk,khd->qhd", grad_scores, key16, preferred_element_type=jnp.float32)
        )
        grad_key = grad_key.at[:stop_row].add(
            jnp.einsum("hqk,qhd->khd", grad_scores, query16, preferred_element_type=jnp.float32)
        )
    return (grad_query[0], grad_key, grad_value)


def norm_back(grad_act, normed, inv_std, gain):
    grad_gain = jnp.sum(grad_act * normed, axis=0)
    grad_shift = jnp.sum(grad_act, axis=0)
    grad_norm = grad_act * gain.astype(jnp.float32)
    grad_x = inv_std * (
        grad_norm
        - jnp.mean(grad_norm, axis=1, keepdims=True)
        - normed * jnp.mean(grad_norm * normed, axis=1, keepdims=True)
    )
    return (grad_gain, grad_shift, grad_x)


def layer_forward(tokens, segments, pieces):
    (
        gain_one,
        shift_one,
        w_qkv,
        b_qkv,
        w_out,
        b_out,
        gain_two,
        shift_two,
        w_in,
        b_in,
        w_out2,
        b_out2,
    ) = pieces
    count = tokens.shape[0]
    x_wide = tokens.astype(jnp.float32)
    row_mean = jnp.mean(x_wide, axis=1, keepdims=True)
    centered = x_wide - row_mean
    variance = jnp.mean(centered * centered, axis=1, keepdims=True)
    inv_std = lax.rsqrt(variance + EPS_NORM)
    normed = centered * inv_std
    act_one = (normed * gain_one.astype(jnp.float32) + shift_one.astype(jnp.float32)).astype(
        jnp.bfloat16
    )
    act_two = (normed * gain_two.astype(jnp.float32) + shift_two.astype(jnp.float32)).astype(
        jnp.bfloat16
    )
    mixed = jnp.dot(act_one, w_qkv, preferred_element_type=jnp.float32) + b_qkv.astype(jnp.float32)
    mixed = mixed.reshape(count, 3, HEADS, HD)
    cosine, sine = rotary_tables(positions_of(segments))
    query16 = rotate(mixed[:, 0], cosine, sine, 1.0).astype(jnp.bfloat16)
    key16 = rotate(mixed[:, 1], cosine, sine, 1.0).astype(jnp.bfloat16)
    value16 = mixed[:, 2].astype(jnp.bfloat16)
    attn16, lse_list = attend_forward(query16, key16, value16, segments)
    proj = jnp.dot(
        attn16.reshape(count, HEADS * HD), w_out, preferred_element_type=jnp.float32
    ) + b_out.astype(jnp.float32)
    pre = jnp.dot(act_two, w_in, preferred_element_type=jnp.float32) + b_in.astype(jnp.float32)
    hidden16 = gelu_exact(pre).astype(jnp.bfloat16)
    feed = jnp.dot(hidden16, w_out2, preferred_element_type=jnp.float32) + b_out2.astype(
        jnp.float32
    )
    output = x_wide + proj + feed
    saved = (
        normed,
        inv_std,
        act_one,
        act_two,
        query16,
        key16,
        value16,
        attn16,
        lse_list,
        cosine,
        sine,
        pre,
        hidden16,
    )
    return (output, saved)


def layer_backward(cotangent, segments, pieces, saved):
    (
        gain_one,
        shift_one,
        w_qkv,
        b_qkv,
        w_out,
        b_out,
        gain_two,
        shift_two,
        w_in,
        b_in,
        w_out2,
        b_out2,
    ) = pieces
    (
        normed,
        inv_std,
        act_one,
        act_two,
        query16,
        key16,
        value16,
        attn16,
        lse_list,
        cosine,
        sine,
        pre,
        hidden16,
    ) = saved
    count = cotangent.shape[0]
    contract_rows = (((0,), (0,)), ((), ()))
    contract_cols = (((1,), (1,)), ((), ()))
    live_rows = (segments >= 0).astype(jnp.float32)[:, None]
    grad_y = cotangent.astype(jnp.float32) * live_rows
    grad_y16 = grad_y.astype(jnp.bfloat16)
    grad_b_out = jnp.sum(grad_y, axis=0)
    attn_flat = attn16.reshape(count, HEADS * HD)
    grad_w_out = lax.dot_general(
        attn_flat, grad_y16, contract_rows, preferred_element_type=jnp.float32
    )
    grad_w_out2 = lax.dot_general(
        hidden16, grad_y16, contract_rows, preferred_element_type=jnp.float32
    )
    grad_hidden = lax.dot_general(
        grad_y16, w_out2, contract_cols, preferred_element_type=jnp.float32
    )
    grad_pre = grad_hidden * gelu_slope(pre)
    grad_b_in = jnp.sum(grad_pre, axis=0)
    grad_pre16 = grad_pre.astype(jnp.bfloat16)
    grad_w_in = lax.dot_general(
        act_two, grad_pre16, contract_rows, preferred_element_type=jnp.float32
    )
    grad_act_two = lax.dot_general(
        grad_pre16, w_in, contract_cols, preferred_element_type=jnp.float32
    )
    grad_attn16 = (
        lax.dot_general(grad_y16, w_out, contract_cols, preferred_element_type=jnp.float32)
        .astype(jnp.bfloat16)
        .reshape(count, HEADS, HD)
    )
    grad_query, grad_key, grad_value = attend_backward(
        query16, key16, value16, attn16, lse_list, segments, grad_attn16
    )
    grad_query = rotate(grad_query, cosine, sine, -1.0)
    grad_key = rotate(grad_key, cosine, sine, -1.0)
    grad_mixed = jnp.stack([grad_query, grad_key, grad_value], axis=1).reshape(
        count, 3 * HEADS * HD
    )
    grad_b_qkv = jnp.sum(grad_mixed, axis=0)
    grad_mixed16 = grad_mixed.astype(jnp.bfloat16)
    grad_w_qkv = lax.dot_general(
        act_one, grad_mixed16, contract_rows, preferred_element_type=jnp.float32
    )
    grad_act_one = lax.dot_general(
        grad_mixed16, w_qkv, contract_cols, preferred_element_type=jnp.float32
    )
    gain_grad_one, shift_grad_one, grad_x_one = norm_back(grad_act_one, normed, inv_std, gain_one)
    gain_grad_two, shift_grad_two, grad_x_two = norm_back(grad_act_two, normed, inv_std, gain_two)
    grad_in = grad_y + grad_x_one + grad_x_two
    return (
        grad_in,
        [
            gain_grad_one,
            shift_grad_one,
            grad_w_qkv,
            grad_b_qkv,
            grad_w_out,
            grad_b_out,
            gain_grad_two,
            shift_grad_two,
            grad_w_in,
            grad_b_in,
            grad_w_out2,
            grad_b_out,
        ],
    )


def flatten_grads(parts, total_len):
    used = layout_offsets()[-1]
    rounded = [part.astype(jnp.bfloat16).reshape(-1) for part in parts]
    return jnp.concatenate(rounded + [jnp.zeros((total_len - used,), jnp.bfloat16)])


def adam_update(weights, first_moment, second_moment, gradient):
    new_first = BETA_ONE * first_moment + (1.0 - BETA_ONE) * gradient
    new_second = BETA_TWO * second_moment + (1.0 - BETA_TWO) * gradient * gradient
    unbiased_first = new_first / (1.0 - BETA_ONE**ADAM_STEP)
    unbiased_second = new_second / (1.0 - BETA_TWO**ADAM_STEP)
    new_weights = weights - LEARN_RATE * (
        unbiased_first / (jnp.sqrt(unbiased_second) + ADAM_EPS) + DECAY * weights
    )
    return (new_weights, new_first, new_second)


def on_device(tokens, segment_ids, cotangent, params, moment_one, moment_two):
    gathered = lax.all_gather(params.astype(jnp.bfloat16), "shard", axis=0, tiled=True)
    total_len = gathered.shape[0]
    pieces = split_params(gathered)
    output, saved = layer_forward(tokens, segment_ids, pieces)
    grad_input, parts = layer_backward(cotangent, segment_ids, pieces, saved)
    local_grad = flatten_grads(parts, total_len)
    owned = lax.psum_scatter(local_grad, "shard", scatter_dimension=0, tiled=True).astype(
        jnp.float32
    )
    tokens_all = tokens.shape[0] * lax.axis_size("rep") * lax.axis_size("shard")
    factor = 1.0 / math.sqrt(tokens_all)
    width = moment_one.shape[0]
    begin = lax.axis_index("rep") * width
    param_share = lax.dynamic_slice_in_dim(params, begin, width)
    share = lax.psum_scatter(owned, "rep", scatter_dimension=0, tiled=True)
    grad_share = share * factor
    upd_params, upd_first, upd_second = adam_update(param_share, moment_one, moment_two, grad_share)
    grad_params, new_params = (
        lax.all_gather(grad_share, "rep", axis=0, tiled=True),
        lax.all_gather(upd_params, "rep", axis=0, tiled=True),
    )
    return (output, grad_input, grad_params, new_params, upd_first, upd_second)


LANES = 128
REPS = 8
SHARDS = 4
PIECE = 288
FLAT_ROWS = 13848
MOVED = PIECE * D // LANES


PARTS = (
    ((12, 1728, 96, 3, 0),),
    ((6, 576, 96, 1, 0), (4632, 1152, 48, 4, 96)),
    ((0, 1152, 48, 4, 0), (9240, 576, 96, 1, 192)),
    ((0, 1728, 288, 1, 0),),
)
VECTOR_ROWS = ((0, 1, 2306, 2307), (0, 769, 770, 771), (1536, 1537, 1538, 1539), (2304, 2305, 2306, 2307))


PLANE = ("y", "x", "core")
EVERY = PLANE + ("z",)
HOPS = (1, 2, 3, 0)


def plane_permute(value, flips):
    return lax.ppermute(value, PLANE, [(i, i ^ flips[i % 2]) for i in range(REPS)])


def first_cross(value):
    return plane_permute(value, (2, 4))


def second_cross(value):
    return plane_permute(value, (4, 2))


def core_cross(value):
    return plane_permute(value, (1, 1))


def ring_step(value):
    return lax.ppermute(value, "z", [(i, (i + 1) % SHARDS) for i in range(SHARDS)])


def flips_of(rep):
    core = rep % 2
    first = 2 + 2 * core
    return (0, first, 6 - first, 6)


def spread_ids(rep):
    other = rep ^ 1
    return [rep ^ flip for flip in flips_of(rep)] + [other ^ flip for flip in flips_of(other)]


def window_of(row):
    return min(6 * row // 8 * 8, FLAT_ROWS - 16)


def pack_kernel(where, flat_ref, out_ref, *rest):
    vec_ref = rest[0] if len(rest) == 4 else None
    held, windows, sems = rest[-3:]
    shard = where[0]
    turns = out_ref.shape[0]
    for z in range(SHARDS):

        @pl.when(shard == z)
        def _(z=z):
            def copies_of(turn):
                slot = turn % 2
                rep = where[1 + turn]
                copies = []
                at = 0
                for part, (first, step, _, _, _) in enumerate(PARTS[z]):
                    lead = first % 8
                    count = step + (8 if lead else 0)
                    begin = pl.multiple_of(first - lead + step * rep, 8)
                    copies.append(
                        pltpu.make_async_copy(
                            flat_ref.at[pl.ds(begin, count)],
                            held.at[slot, pl.ds(at, count)],
                            sems.at[slot, part],
                        )
                    )
                    at += count
                return copies

            for copy in copies_of(0):
                copy.start()
            if vec_ref is not None:
                cuts = []
                for slot, row in enumerate(VECTOR_ROWS[z]):
                    cuts.append(
                        pltpu.make_async_copy(
                            flat_ref.at[pl.ds(window_of(row), 16)],
                            windows.at[slot],
                            sems.at[2 + slot // 2, slot % 2],
                        )
                    )
                    cuts[-1].start()
                vec_ref[...] = jnp.zeros_like(vec_ref)
                for slot, row in enumerate(VECTOR_ROWS[z]):
                    cuts[slot].wait()
                    lead = 6 * row - window_of(row)
                    for col in range(6):
                        got = windows[slot, lead + col : lead + col + 1, :]
                        vec_ref[slot : slot + 1, LANES * col : LANES * (col + 1)] = got.astype(
                            jnp.bfloat16
                        ).astype(jnp.float32)

            @pl.loop(0, turns)
            def _(turn):
                @pl.when(turn + 1 < turns)
                def _():
                    for copy in copies_of(turn + 1):
                        copy.start()

                slot = turn % 2
                at = 0
                for copy, (first, step, rows, blocks, place) in zip(copies_of(turn), PARTS[z]):
                    copy.wait()
                    lead = first % 8
                    for block in range(blocks):
                        for col in range(6):
                            begin = at + lead + 6 * block + col
                            got = held[slot, pl.ds(begin, rows, stride=6 * blocks), :]
                            out_ref[
                                turn,
                                place + rows * block : place + rows * (block + 1),
                                LANES * col : LANES * (col + 1),
                            ] = got.astype(jnp.bfloat16)
                    at += step + (8 if lead else 0)


def pack_pieces(params, shard, reps, vectors):
    pieces = jax.ShapeDtypeStruct((len(reps), PIECE, D), jnp.bfloat16)
    rows = jax.ShapeDtypeStruct((8, D), jnp.float32)
    vmem = pl.BlockSpec(memory_space=pltpu.VMEM)
    return pl.pallas_call(
        pack_kernel,
        grid_spec=pltpu.PrefetchScalarGridSpec(
            num_scalar_prefetch=1,
            in_specs=[pl.BlockSpec(memory_space=pltpu.HBM)],
            out_specs=[vmem, vmem] if vectors else [vmem],
            scratch_shapes=[
                pltpu.VMEM((2, MOVED + 16, LANES), jnp.float32),
                pltpu.VMEM((4, 16, LANES), jnp.float32),
                pltpu.SemaphoreType.DMA((4, 2)),
            ],
        ),
        out_shape=[pieces, rows] if vectors else [pieces],
        compiler_params=pltpu.CompilerParams(vmem_limit_bytes=56 * 2**20),
    )(jnp.stack([shard] + reps), params.reshape(FLAT_ROWS, LANES))


def prepare_kernel(tokens, cotangent, ids, freqs, normed, spread, grad_y, tables):
    x_wide = tokens[...].astype(jnp.float32)
    centered = x_wide - jnp.mean(x_wide, axis=1, keepdims=True)
    variance = jnp.mean(centered * centered, axis=1, keepdims=True)
    inv_std = lax.rsqrt(variance + EPS_NORM)
    normed[...] = centered * inv_std
    spread[...] = jnp.broadcast_to(inv_std, spread.shape)
    square = (TOK_DEV, TOK_DEV)
    across = jnp.broadcast_to(ids[...].astype(jnp.float32), square)
    down = across.T
    lane = lax.broadcasted_iota(jnp.int32, square, 1)
    row = lax.broadcasted_iota(jnp.int32, square, 0)
    begins = (across != pltpu.roll(across, 1, 1)) | (lane == 0)
    before = jnp.where(begins & (lane <= row), lane.astype(jnp.float32), 0.0)
    position = row.astype(jnp.float32) - jnp.max(before, axis=1, keepdims=True)
    angle = position * freqs[...]
    cosine, sine = jnp.cos(angle), jnp.sin(angle)
    within = lane % HD
    tables[0] = jnp.where(within < ROT, cosine, 1.0)
    tables[1] = jnp.where(within < ROT // 2, -sine, 0.0)
    tables[2] = jnp.where((within >= ROT // 2) & (within < ROT), sine, 0.0)
    tables[3] = jnp.where((across == down) & (lane <= row), 1.0, 0.0)
    cot = cotangent[...].astype(jnp.float32)
    grad_y[...] = jnp.where(down[:, 0:1] >= 0, cot, 0.0).astype(jnp.bfloat16)


def prepare(tokens, cotangent, segment_ids):
    steps = jnp.arange(LANES, dtype=jnp.int32) % (ROT // 2)
    freqs = jnp.power(jnp.float32(ROPE_BASE), -2.0 * steps.astype(jnp.float32) / ROT)
    return pl.pallas_call(
        prepare_kernel,
        out_shape=[
            jax.ShapeDtypeStruct((TOK_DEV, D), jnp.float32),
            jax.ShapeDtypeStruct((TOK_DEV, LANES), jnp.float32),
            jax.ShapeDtypeStruct((TOK_DEV, D), jnp.bfloat16),
            jax.ShapeDtypeStruct((4, TOK_DEV, TOK_DEV), jnp.float32),
        ],
        compiler_params=pltpu.CompilerParams(vmem_limit_bytes=16 * 2**20),
    )(tokens, cotangent, segment_ids.reshape(1, TOK_DEV), freqs.reshape(1, LANES))


PIECES = SHARDS * REPS
GROUPS = 12
ALL_ROWS = PIECES * PIECE


def fetch_pieces(ids, blocks, own, shard, held, sems):
    views = []
    for block in blocks:
        views += [block.at[p] for p in range(4)] if len(block.shape) == 3 else [block]
    ids = ids + [shard * REPS + r for r in range(REPS)]
    views += [own.at[pl.ds(r * PIECE, PIECE)] for r in range(REPS)]
    for which, view in zip(ids, views):
        row = pl.multiple_of(which * PIECE, 16)
        pltpu.make_async_copy(view, held.at[pl.ds(row, PIECE)], sems.at[which]).start()

    def arrive(owner):
        for r in range(REPS):
            at = owner * REPS + r
            pltpu.make_async_copy(
                own.at[pl.ds(0, PIECE)], held.at[pl.ds(at * PIECE, PIECE)], sems.at[at]
            ).wait()

    return arrive


def rows_of(held, shard, begin, rows):
    return jnp.concatenate(
        [held[pl.ds((shard * REPS + r) * PIECE + begin, rows), :] for r in range(REPS)], axis=0
    )


def w_qkv_of(held, j):
    return rows_of(held, 0, 96 * j, 96)


def w_out_of(held):
    return rows_of(held, 1, 0, 96)


def w_in_of(held, j):
    return jnp.concatenate([rows_of(held, 1, 96 + 48 * j, 48), rows_of(held, 2, 48 * j, 48)], axis=0)


def w_out2_of(held, j):
    if j == 0:
        return rows_of(held, 2, 192, 96)
    return held[pl.ds(3 * REPS * PIECE + D * (j - 1), D), :]


def dot32(a, b):
    return jnp.dot(a, b, preferred_element_type=jnp.float32)


def attention_kernel(where, *refs):
    count = PIECES - REPS
    blocks, own = refs[:GROUPS], refs[GROUPS]
    normed, grad_y, tables = refs[GROUPS + 1 : GROUPS + 4]
    hops = refs[GROUPS + 4 : GROUPS + 8]
    matrices, attn_out, mixed_out, sums_out, vecs = refs[GROUPS + 8 : GROUPS + 13]
    held, query, key, value, grad_attn, sems, save_sem = refs[GROUPS + 13 :]
    rot_cos, rot_up, rot_down, bias = (tables.at[turn] for turn in range(4))
    shard = where[0]
    for owner in range(SHARDS):
        rows = jnp.zeros((4, D), jnp.float32)
        for hop in range(SHARDS):
            met = (shard + SHARDS - owner) % SHARDS == hop
            rows = jnp.where(met, hops[hop][0:4, :], rows)
        vecs[4 * owner : 4 * owner + 4, :] = rows
    arrive = fetch_pieces([where[1 + t] for t in range(count)], blocks, own, shard, held, sems)
    sums_out[...] = jnp.zeros_like(sums_out)

    arrive(0)
    act1 = (normed[...] * vecs[0:1, :] + vecs[1:2, :]).astype(jnp.bfloat16)
    for j, out in enumerate((query, key, value)):
        got = dot32(act1, w_qkv_of(held, j)) + vecs[2 + j : 3 + j, :]
        if j < 2:
            for p in range(6):
                lanes = slice(LANES * p, LANES * (p + 1))
                part = got[:, lanes]
                part = (
                    part * rot_cos[...]
                    + pltpu.roll(part, LANES - 8, 1) * rot_up[...]
                    + pltpu.roll(part, 8, 1) * rot_down[...]
                )
                out[:, lanes] = part.astype(jnp.bfloat16)
        else:
            out[...] = got.astype(jnp.bfloat16)
    gy_t = grad_y[...].T
    arrive(1)
    grad_attn[...] = dot32(w_out_of(held), gy_t).T.astype(jnp.bfloat16)

    arrive(2)
    arrive(3)
    saving = pltpu.make_async_copy(held, matrices, save_sem)
    saving.start()
    low = lax.broadcasted_iota(jnp.int32, (LANES, LANES), 1) < HD
    scale = HD ** (-0.5)
    for p in range(6):
        lanes = slice(LANES * p, LANES * (p + 1))
        q2, k2, v2, g2 = (ref[:, lanes] for ref in (query, key, value, grad_attn))
        k2_t, v2_t = k2.T, v2.T
        attn_parts, value_parts, query_parts, key_parts = [], [], [], []
        for half in range(2):
            here = low if half == 0 else ~low
            zero = jnp.zeros_like(q2)
            scores = dot32(jnp.where(here, q2, zero), k2_t) * scale
            scores = jnp.where(bias[...] > 0.5, scores, NEG_BIG)
            expd = jnp.exp(scores - jnp.max(scores, axis=1, keepdims=True))
            chances = expd / jnp.sum(expd, axis=1, keepdims=True)
            chances16 = chances.astype(jnp.bfloat16)
            attn = dot32(chances16, v2)
            attn16 = attn.astype(jnp.bfloat16)
            masked = jnp.where(here, g2, zero)
            delta = jnp.sum(
                masked.astype(jnp.float32) * attn16.astype(jnp.float32), axis=1, keepdims=True
            )
            grad_chance = dot32(masked, v2_t)
            slope = (chances * (grad_chance - delta) * scale).astype(jnp.bfloat16)
            attn_parts.append(attn16)
            value_parts.append(dot32(chances16.T, g2))
            query_parts.append(dot32(slope, k2))
            key_parts.append(dot32(slope.T, q2))
        attn_out[:, lanes] = jnp.where(low, *attn_parts)
        for j, parts in enumerate((query_parts, key_parts, value_parts)):
            part = jnp.where(low, *parts)
            if j < 2:
                part = (
                    part * rot_cos[...]
                    - pltpu.roll(part, LANES - 8, 1) * rot_up[...]
                    - pltpu.roll(part, 8, 1) * rot_down[...]
                )
            wide = slice(D * j + LANES * p, D * j + LANES * (p + 1))
            sums_out[j : j + 1, lanes] = jnp.sum(part, axis=0, keepdims=True)
            mixed_out[:, wide] = part.astype(jnp.bfloat16)

    saving.wait()


def attention(scalars, blocks, own, small):
    anywhere = pl.BlockSpec(memory_space=pl.ANY)
    vmem = pl.BlockSpec(memory_space=pltpu.VMEM)
    bf16 = jnp.bfloat16
    return pl.pallas_call(
        attention_kernel,
        grid_spec=pltpu.PrefetchScalarGridSpec(
            num_scalar_prefetch=1,
            in_specs=[anywhere] * (len(blocks) + 1) + [vmem] * len(small),
            out_specs=[anywhere] + [vmem] * 4,
            scratch_shapes=[
                pltpu.VMEM((ALL_ROWS, D), bf16),
                pltpu.VMEM((TOK_DEV, D), bf16),
                pltpu.VMEM((TOK_DEV, D), bf16),
                pltpu.VMEM((TOK_DEV, D), bf16),
                pltpu.VMEM((TOK_DEV, D), bf16),
                pltpu.SemaphoreType.DMA((PIECES,)),
                pltpu.SemaphoreType.DMA,
            ],
        ),
        out_shape=[
            jax.ShapeDtypeStruct((ALL_ROWS, D), bf16),
            jax.ShapeDtypeStruct((TOK_DEV, D), bf16),
            jax.ShapeDtypeStruct((TOK_DEV, 3 * D), bf16),
            jax.ShapeDtypeStruct((8, D), jnp.float32),
            jax.ShapeDtypeStruct((16, D), jnp.float32),
        ],
        compiler_params=pltpu.CompilerParams(vmem_limit_bytes=60 * 2**20),
        cost_estimate=pl.CostEstimate(
            flops=6 * 10**9, bytes_accessed=60 * 2**20, transcendentals=200000
        ),
    )(scalars, *blocks, own, *small)


def gradient_kernel(where, matrices, *refs):
    (normed, grad_y, attn_in, mixed_in, vecs) = refs[:5]
    outs = refs[5:21]
    hidden_out, pre_out, sums_out = refs[21:24]
    held, grads, sems, out_sems = refs[24:]
    copies = []
    for z in range(1, SHARDS):
        rows = pl.ds(z * REPS * PIECE, REPS * PIECE)
        copies.append(pltpu.make_async_copy(matrices.at[rows], held.at[rows], sems.at[z]))
    for copy in copies:
        copy.start()
    sums_out[...] = jnp.zeros_like(sums_out)
    slot_row = lambda z, r: pl.multiple_of(where[z * REPS + r] * PIECE, 16)

    def keep_rows(z, begin, rows, part):
        for r in range(part.shape[0] // rows):
            grads[pl.ds(slot_row(z, r) + begin, rows), :] = part[rows * r : rows * (r + 1), :]

    gy = grad_y[...]
    act1_t = (normed[...] * vecs[0:1, :] + vecs[1:2, :]).astype(jnp.bfloat16).T
    for j in range(3):
        keep_rows(
            0, 96 * j, 96, dot32(act1_t, mixed_in[:, D * j : D * (j + 1)]).astype(jnp.bfloat16)
        )
    keep_rows(1, 0, 96, dot32(attn_in[...].T, gy).astype(jnp.bfloat16))

    for copy in copies:
        copy.wait()
    gy_t = gy.T
    act2 = (normed[...] * vecs[6:7, :] + vecs[7:8, :]).astype(jnp.bfloat16)
    act2_t = act2.T
    for j in range(4):
        wide = slice(D * j, D * (j + 1))
        pre = dot32(act2, w_in_of(held, j)) + vecs[8 + j : 9 + j, :]
        bell = 0.5 * (1.0 + lax.erf(pre * INV_ROOT_TWO))
        hidden = (pre * bell).astype(jnp.bfloat16)
        hidden_out[:, wide] = hidden
        grad_hidden = dot32(w_out2_of(held, j), gy_t).T
        grad_pre = grad_hidden * (bell + pre * jnp.exp(-0.5 * pre * pre) * INV_ROOT_TWO_PI)
        sums_out[j : j + 1, :] = jnp.sum(grad_pre, axis=0, keepdims=True)
        grad_pre16 = grad_pre.astype(jnp.bfloat16)
        pre_out[:, wide] = grad_pre16
        w2 = dot32(hidden.T, gy).astype(jnp.bfloat16)
        if j == 0:
            keep_rows(2, 192, 96, w2)
        else:
            at = D * (j - 1)
            while at < D * j:
                r, begin = divmod(at, PIECE)
                rows = min(PIECE - begin, D * j - at)
                grads[pl.ds(slot_row(3, r) + begin, rows), :] = w2[
                    at - D * (j - 1) : at - D * (j - 1) + rows, :
                ]
                at += rows
        w1 = dot32(act2_t, grad_pre16).astype(jnp.bfloat16)
        keep_rows(1, 96 + 48 * j, 48, w1[: D // 2])
        keep_rows(2, 48 * j, 48, w1[D // 2 :])
    copies = []
    for turn, out in enumerate(outs):
        for p in range(2):
            copies.append(
                pltpu.make_async_copy(
                    grads.at[pl.ds((turn * 2 + p) * PIECE, PIECE)],
                    out.at[p],
                    out_sems.at[turn * 2 + p],
                )
            )
    for copy in copies:
        copy.start()
    for copy in copies:
        copy.wait()


def weight_gradients(slots, matrices, small):
    anywhere = pl.BlockSpec(memory_space=pl.ANY)
    vmem = pl.BlockSpec(memory_space=pltpu.VMEM)
    bf16 = jnp.bfloat16
    return pl.pallas_call(
        gradient_kernel,
        grid_spec=pltpu.PrefetchScalarGridSpec(
            num_scalar_prefetch=1,
            in_specs=[anywhere] + [vmem] * len(small),
            out_specs=[pl.BlockSpec(memory_space=pltpu.HBM)] * 16 + [vmem] * 3,
            scratch_shapes=[
                pltpu.VMEM((ALL_ROWS, D), bf16),
                pltpu.VMEM((ALL_ROWS, D), bf16),
                pltpu.SemaphoreType.DMA((SHARDS,)),
                pltpu.SemaphoreType.DMA((PIECES,)),
            ],
        ),
        out_shape=[jax.ShapeDtypeStruct((2, PIECE, D), bf16)] * 16
        + [
            jax.ShapeDtypeStruct((TOK_DEV, FF), bf16),
            jax.ShapeDtypeStruct((TOK_DEV, FF), bf16),
            jax.ShapeDtypeStruct((8, D), jnp.float32),
        ],
        compiler_params=pltpu.CompilerParams(vmem_limit_bytes=60 * 2**20),
        cost_estimate=pl.CostEstimate(
            flops=10**10, bytes_accessed=60 * 2**20, transcendentals=800000
        ),
    )(slots, matrices, *small)


def result_kernel(matrices, *refs):
    (tokens, normed, spread, grad_y, attn, grad_mixed, low_sums, vecs, hidden, grad_pre, high_sums) = (
        refs[:11]
    )
    output, grad_input, vec_out, held, sems = refs[11:]
    copies = []
    for z in range(SHARDS):
        rows = pl.ds(z * REPS * PIECE, REPS * PIECE)
        copies.append(pltpu.make_async_copy(matrices.at[rows], held.at[rows], sems.at[z]))
    for copy in copies:
        copy.start()
    for copy in copies:
        copy.wait()
    total = dot32(attn[...], w_out_of(held)) + vecs[5:6, :]
    for j in range(4):
        total = total + dot32(hidden[:, D * j : D * (j + 1)], w_out2_of(held, j))
    output[...] = tokens[...].astype(jnp.float32) + (total + vecs[12:13, :])
    vec_out[2:5, :] = low_sums[0:3, :]
    vec_out[8:12, :] = high_sums[0:4, :]
    gy = grad_y[...].astype(jnp.float32)
    total = gy
    for norm, (parts, width, weights) in enumerate(
        ((grad_mixed, 3, w_qkv_of), (grad_pre, 4, w_in_of))
    ):
        back = None
        for j in range(width):
            part = dot32(weights(held, j), parts[:, D * j : D * (j + 1)].T)
            back = part if back is None else back + part
        grad_act = back.T
        gain_row = 0 if norm == 0 else 6
        unit = normed[...]
        vec_out[gain_row : gain_row + 1, :] = jnp.sum(grad_act * unit, axis=0, keepdims=True)
        vec_out[gain_row + 1 : gain_row + 2, :] = jnp.sum(grad_act, axis=0, keepdims=True)
        grad_norm = grad_act * vecs[gain_row : gain_row + 1, :]
        total = total + spread[:, 0:1] * (
            grad_norm
            - jnp.mean(grad_norm, axis=1, keepdims=True)
            - unit * jnp.mean(grad_norm * unit, axis=1, keepdims=True)
        )
    grad_input[...] = total
    bottom = jnp.sum(gy, axis=0, keepdims=True)
    vec_out[5:6, :] = bottom
    vec_out[12:13, :] = bottom
    vec_out[13:16, :] = jnp.zeros((3, D), jnp.float32)
    vec_out[...] = vec_out[...].astype(jnp.bfloat16).astype(jnp.float32)


def layer_results(matrices, small):
    hbm = pl.BlockSpec(memory_space=pl.ANY)
    vmem = pl.BlockSpec(memory_space=pltpu.VMEM)
    rows = jax.ShapeDtypeStruct((TOK_DEV, D), jnp.float32)
    return pl.pallas_call(
        result_kernel,
        in_specs=[hbm] + [vmem] * len(small),
        out_specs=[vmem] * 3,
        scratch_shapes=[
            pltpu.VMEM((ALL_ROWS, D), jnp.bfloat16),
            pltpu.SemaphoreType.DMA((SHARDS,)),
        ],
        out_shape=[rows, rows, jax.ShapeDtypeStruct((16, D), jnp.float32)],
        compiler_params=pltpu.CompilerParams(vmem_limit_bytes=60 * 2**20),
        cost_estimate=pl.CostEstimate(
            flops=4 * 10**9, bytes_accessed=30 * 2**20, transcendentals=0
        ),
    )(matrices, *small)


SHARE = FLAT_ROWS // REPS
BEGINS = tuple(SHARE * r // 16 * 16 for r in range(REPS)) + (FLAT_ROWS,)
SHARE_ROWS = 1760
STEP = 288


def align_kernel(where, one_ref, two_ref, out_ref, held):
    for r in range(REPS):

        @pl.when(where[0] == r)
        def _(r=r):
            lead = SHARE * r - BEGINS[r]
            for turn, ref in enumerate((one_ref, two_ref)):
                held[0:16, :] = jnp.zeros((16, LANES), jnp.float32)
                held[SHARE_ROWS - 32 :, :] = jnp.zeros((32, LANES), jnp.float32)
                held[lead : lead + SHARE, :] = ref[...]
                out_ref[turn] = held[...].astype(jnp.bfloat16)


def align_moments(moment_one, moment_two, rep):
    return pl.pallas_call(
        align_kernel,
        grid_spec=pltpu.PrefetchScalarGridSpec(
            num_scalar_prefetch=1,
            in_specs=[pl.BlockSpec(memory_space=pltpu.VMEM)] * 2,
            out_specs=pl.BlockSpec(memory_space=pltpu.VMEM),
            scratch_shapes=[pltpu.VMEM((SHARE_ROWS, LANES), jnp.float32)],
        ),
        out_shape=jax.ShapeDtypeStruct((2, SHARE_ROWS, LANES), jnp.bfloat16),
        compiler_params=pltpu.CompilerParams(vmem_limit_bytes=16 * 2**20),
    )(jnp.stack([rep]), moment_one.reshape(SHARE, LANES), moment_two.reshape(SHARE, LANES))


def update_kernel(factor, where, *refs):
    blocks = refs[:REPS]
    moments = refs[REPS : 2 * REPS]
    vec_ref, params, grad_out, params_out = refs[2 * REPS : 2 * REPS + 4]
    held, grad, weight, moment, sems, out_sems = refs[2 * REPS + 4 :]
    copies = []
    for turn in range(REPS):
        copies.append(
            pltpu.make_async_copy(blocks[turn], held.at[where[1 + turn]], sems.at[turn])
        )
    copies.append(pltpu.make_async_copy(params, weight, sems.at[REPS]))
    for turn in range(REPS):
        copies.append(
            pltpu.make_async_copy(
                moments[turn], moment.at[where[1 + turn]], sems.at[REPS + 1 + turn]
            )
        )
    for copy in copies:
        copy.start()
    for copy in copies[:REPS]:
        copy.wait()
    shard = where[0]
    for z in range(SHARDS):

        @pl.when(shard == z)
        def _(z=z):
            for slot, row in enumerate(VECTOR_ROWS[z]):
                for col in range(6):
                    grad[6 * row + col : 6 * row + col + 1, :] = (
                        vec_ref[slot : slot + 1, LANES * col : LANES * (col + 1)] * factor
                    )

            @pl.loop(0, REPS)
            def _(rep):
                for first, step, rows, blocks, place in PARTS[z]:
                    for block in range(blocks):
                        for col in range(6):
                            got = held[
                                rep,
                                place + rows * block : place + rows * (block + 1),
                                LANES * col : LANES * (col + 1),
                            ]
                            begin = first + step * rep + 6 * block + col
                            grad[pl.ds(begin, rows, stride=6 * blocks), :] = (
                                got.astype(jnp.float32) * factor
                            )

    saving = [pltpu.make_async_copy(grad, grad_out, out_sems.at[REPS])]
    saving[0].start()
    for copy in copies[REPS:]:
        copy.wait()
    for r in range(REPS):
        base = BEGINS[r]
        length = BEGINS[r + 1] - base
        if r > 0:
            tail = base - BEGINS[r - 1]
            moment[r, :, 0:16, :] = moment[r, :, 0:16, :] + moment[r - 1, :, tail : tail + 16, :]

        def renew(at, rows, r=r, base=base):
            here = pl.ds(pl.multiple_of(base + at, 8), rows)
            there = pl.ds(pl.multiple_of(at, 16), rows)
            updated, _, _ = adam_update(
                weight[here, :],
                moment[r, 0, there, :].astype(jnp.float32),
                moment[r, 1, there, :].astype(jnp.float32),
                grad[here, :],
            )
            weight[here, :] = updated

        @pl.loop(0, length // STEP)
        def _(turn):
            renew(turn * STEP, STEP)

        if length % STEP:
            renew(length // STEP * STEP, length % STEP)
        rows = pl.ds(base, length)
        saving.append(
            pltpu.make_async_copy(weight.at[rows], params_out.at[rows], out_sems.at[r])
        )
        saving[-1].start()
    for copy in saving:
        copy.wait()


def update_shard(blocks, ids, vectors, params, moments, shard, factor):
    anywhere = pl.BlockSpec(memory_space=pl.ANY)
    flat = jax.ShapeDtypeStruct((FLAT_ROWS, LANES), jnp.float32)
    return pl.pallas_call(
        functools.partial(update_kernel, factor),
        grid_spec=pltpu.PrefetchScalarGridSpec(
            num_scalar_prefetch=1,
            in_specs=[anywhere] * (2 * REPS)
            + [pl.BlockSpec(memory_space=pltpu.VMEM), anywhere],
            out_specs=[anywhere] * 2,
            scratch_shapes=[
                pltpu.VMEM((REPS, PIECE, D), jnp.bfloat16),
                pltpu.VMEM((FLAT_ROWS, LANES), jnp.float32),
                pltpu.VMEM((FLAT_ROWS, LANES), jnp.float32),
                pltpu.VMEM((REPS, 2, SHARE_ROWS, LANES), jnp.bfloat16),
                pltpu.SemaphoreType.DMA((2 * REPS + 1,)),
                pltpu.SemaphoreType.DMA((REPS + 1,)),
            ],
        ),
        out_shape=[flat, flat],
        compiler_params=pltpu.CompilerParams(vmem_limit_bytes=60 * 2**20),
    )(jnp.stack([shard] + ids), *blocks, *moments, vectors, params.reshape(FLAT_ROWS, LANES))


def ring_shift(value, hop):
    return lax.ppermute(value, "z", [(i, (i + hop) % SHARDS) for i in range(SHARDS)])


fence = lax.optimization_barrier


def gather_matrices(params, shard, rep, early):
    piece = pack_pieces(params, shard, [rep], False)[0][0]
    own, vec = pack_pieces(params, shard, [rep * 0 + turn for turn in range(REPS)], True)
    one = ring_step(piece)
    one, own, vec = fence((one, own, vec))
    two, first_one, second_one = ring_step(one), first_cross(one), second_cross(one)
    vec_one = ring_step(vec)
    two, first_one, second_one, vec_one, early = fence(
        (two, first_one, second_one, vec_one, early)
    )
    three, first_two, second_two = ring_step(two), first_cross(two), second_cross(two)
    both_one = second_cross(first_one)
    vec_two = ring_step(vec_one)
    three, first_two, second_two, both_one, vec_two = fence(
        (three, first_two, second_two, both_one, vec_two)
    )
    first_three, second_three = first_cross(three), second_cross(three)
    both_two = second_cross(first_two)
    mine_one = jnp.stack([one, first_one, second_one, both_one])
    other_one = core_cross(mine_one)
    vec_three = ring_step(vec_two)
    first_three, second_three, both_two, other_one, vec_three = fence(
        (first_three, second_three, both_two, other_one, vec_three)
    )
    both_three = second_cross(first_three)
    mine_two = jnp.stack([two, first_two, second_two, both_two])
    other_two = core_cross(mine_two)
    others = [core_cross(value) for value in (three, first_three, second_three)]
    others, both_three, other_two = fence((others, both_three, other_two))
    others.append(core_cross(both_three))
    threes = [three, first_three, second_three, both_three]
    blocks = [mine_one, other_one, mine_two, other_two] + threes + others
    ids = []
    for hop in range(1, SHARDS):
        owner = (shard + SHARDS - hop) % SHARDS
        ids += [owner * REPS + which for which in spread_ids(rep)]
    hops = [vec, vec_one, vec_two, vec_three]
    return blocks, own.reshape(REPS * PIECE, D), ids, hops, early


def slots_by_piece(shard, rep):
    slots = []
    for owner in range(SHARDS):
        hop = (shard + SHARDS - owner + 3) % SHARDS
        for which in range(REPS):
            apart = rep ^ which
            kept = 1 - apart % 2
            core = which % 2
            across = apart & 6
            first = 2 + 2 * core
            place = jnp.where(
                across == 0, 2, jnp.where(across == 6, 1, jnp.where(across == first, 0, 3))
            )
            slots.append((kept * SHARDS + hop) * 4 + place)
    return slots


def scatter_sums(parts, moments, small, results):
    sent_far, sent_near, kept_far, kept_near = (
        [parts[8 * half + 2 * turn + near] for turn in range(SHARDS)]
        for half in range(2)
        for near in range(2)
    )
    cores = [core_cross(sent_far[0]), core_cross(sent_near[0]), core_cross(sent_far[1])]
    cores = list(fence(cores))
    far = [kept_far[0] + cores[0], kept_far[1] + cores[2]]
    crossed = first_cross(far[0])
    others = [core_cross(v) for v in (sent_near[1], sent_far[2], sent_near[2], sent_far[3])]
    crossed, others, small = fence((crossed, others, small))
    near = [kept_near[0] + cores[1], kept_near[1] + others[0], kept_near[2] + others[2]]
    far += [kept_far[2] + others[1], kept_far[3] + others[3]]

    pair = near[0] + crossed
    final = second_cross(pair[1])
    kept = pair[0]
    crossed = first_cross(far[1])
    last_near = core_cross(sent_near[3])
    others = [core_cross(value) for value in moments[:2]]
    output, grad_input, vectors = results(small)
    final, crossed, last_near, vectors, others = fence(
        (final, crossed, last_near, vectors, others)
    )
    near.append(kept_near[3] + last_near)

    carried = None
    for turn in range(1, SHARDS):
        total = kept + final
        if carried is not None:
            total = total + carried
        carried = ring_step(total)
        pair = near[turn] + crossed
        kept = pair[0]
        final = second_cross(pair[1])
        met = plane_permute(vectors, ((1, 1), (2, 2), (4, 4))[turn - 1])
        if turn < SHARDS - 1:
            crossed = first_cross(far[turn + 1])
            others.append(core_cross(moments[turn + 1]))
            final, crossed, carried, met, others = fence((final, crossed, carried, met, others))
        else:
            final, carried, met = fence((final, carried, met))
        vectors = vectors + met
    total = kept + final + carried

    first, second = first_cross(total), second_cross(total)
    shifted = [ring_shift(vectors, hop) for hop in range(1, SHARDS)]
    first, second, shifted = fence((first, second, shifted))
    vectors = vectors + shifted[0] + shifted[1] + shifted[2]
    both = second_cross(first)
    mine = [total, first, second]
    spread = [core_cross(value) for value in mine]
    both, spread = fence((both, spread))
    spread.append(core_cross(both))
    return mine + [both] + spread, moments + others, output, grad_input, vectors


def on_device_rows(tokens, segment_ids, cotangent, params, moment_one, moment_two):
    shard = lax.axis_index("z")
    rep = lax.axis_index(PLANE)
    early = (prepare(tokens, cotangent, segment_ids), align_moments(moment_one, moment_two, rep))
    blocks, own, ids, hops, early = gather_matrices(params, shard, rep, early)
    (normed, inv_std, grad_y, tables), moments = early
    moments, blocks = fence((moments, blocks))
    first_moments = first_cross(moments)
    small = (normed, grad_y, tables, *hops)
    matrices, *attended = attention(jnp.stack([shard] + ids), blocks, own, small)
    moments, first_moments, attended = fence((moments, first_moments, attended))
    moments = [moments, first_moments, second_cross(moments), second_cross(first_moments)]
    attn, mixed, low_sums, vecs = attended
    made = weight_gradients(
        jnp.stack(slots_by_piece(shard, rep)), matrices, (normed, grad_y, attn, mixed, vecs)
    )
    made, moments = fence((made, moments))
    small = (tokens, normed, inv_std, grad_y, attn, mixed, low_sums, vecs) + tuple(made[16:])
    spread, moments, output, grad_input, vec_grads = scatter_sums(
        made[:16], moments, small, lambda small: layer_results(matrices, small)
    )
    own_vectors = lax.dynamic_index_in_dim(
        vec_grads.reshape(SHARDS, 4, D), shard, 0, keepdims=False
    )
    tokens_all = tokens.shape[0] * lax.axis_size(EVERY)
    grad_params, new_params = update_shard(
        spread,
        spread_ids(rep),
        own_vectors,
        params,
        moments,
        shard,
        1.0 / math.sqrt(tokens_all),
    )
    grad_params = grad_params.reshape(-1)
    width = moment_one.shape[0]
    grad_share = lax.dynamic_slice_in_dim(grad_params, rep * width, width)
    _, upd_first, upd_second = adam_update(moment_one, moment_one, moment_two, grad_share)
    return (output, grad_input, grad_params, new_params.reshape(-1), upd_first, upd_second)


def solution(mesh):
    in_rows = mesh.shape["rep"] == REPS and mesh.shape["shard"] == SHARDS
    if in_rows:
        rep, shard = PLANE, "z"
        mesh = Mesh(mesh.devices.reshape(2, 2, 2, SHARDS), EVERY)
        body = on_device_rows
    else:
        rep, shard = ("rep",), "shard"
        body = on_device
    rows = rep + (shard,)
    owner = (shard,) + rep
    in_specs = (P(rows, None), P(rows), P(rows, None), P(shard), P(owner), P(owner))
    out_specs = (P(rows, None), P(rows, None), P(shard), P(shard), P(owner), P(owner))
    return jax.shard_map(body, mesh=mesh, in_specs=in_specs, out_specs=out_specs, check_vma=False)
```

```python
import functools
import math

import jax
import jax.numpy as jnp
from jax import lax
from jax.experimental import pallas as pl
from jax.experimental.pallas import tpu as pltpu
from jax.sharding import Mesh
from jax.sharding import PartitionSpec as P

D = 768
HEADS = 12
HD = 64
ROT = 16
FF = 3072
TOK_DEV = 128


EPS_NORM = 1e-05
ROPE_BASE = 10000.0
NEG_BIG = -1e30
BETA_ONE = 0.9
BETA_TWO = 0.95
ADAM_STEP = 3.0
LEARN_RATE = 0.05
DECAY = 0.01
ADAM_EPS = 1e-08
INV_ROOT_TWO = 0.7071067811865476
INV_ROOT_TWO_PI = 0.3989422804014327


def layout_offsets():
    q_width = HEADS * HD
    o_wqkv = 2 * D
    o_bqkv = o_wqkv + 3 * q_width * D
    o_wout = o_bqkv + 3 * q_width
    o_bout = o_wout + q_width * D
    o_gain2 = o_bout + D
    o_shift2 = o_gain2 + D
    o_win = o_shift2 + D
    o_bin = o_win + D * FF
    o_wout2 = o_bin + FF
    o_bout2 = o_wout2 + FF * D
    return (
        o_wqkv,
        o_bqkv,
        o_wout,
        o_bout,
        o_gain2,
        o_shift2,
        o_win,
        o_bin,
        o_wout2,
        o_bout2,
        o_bout2 + D,
    )


def split_params(flat16):
    q_width = HEADS * HD
    o_wqkv, o_bqkv, o_wout, o_bout, o_gain2, o_shift2, o_win, o_bin, o_wout2, o_bout2, o_end = (
        layout_offsets()
    )
    return (
        flat16[0:D],
        flat16[D:o_wqkv],
        flat16[o_wqkv:o_bqkv].reshape(D, 3 * q_width),
        flat16[o_bqkv:o_wout],
        flat16[o_wout:o_bout].reshape(q_width, D),
        flat16[o_bout:o_gain2],
        flat16[o_gain2:o_shift2],
        flat16[o_shift2:o_win],
        flat16[o_win:o_bin].reshape(D, FF),
        flat16[o_bin:o_wout2],
        flat16[o_wout2:o_bout2].reshape(FF, D),
        flat16[o_bout2:o_end],
    )


def positions_of(segments):
    count = segments.shape[0]
    slot_ids = jnp.arange(count, dtype=jnp.int32)
    before = jnp.concatenate([jnp.full((1,), -2, jnp.int32), segments[:-1]])
    begins = segments != before
    first_slot = lax.cummax(jnp.where(begins, slot_ids, 0), axis=0)
    return slot_ids - first_slot


def rotary_tables(positions):
    half = ROT // 2
    steps_j = jnp.arange(half, dtype=jnp.float32)
    freqs = jnp.power(jnp.float32(ROPE_BASE), -2.0 * steps_j / ROT)
    angle = positions.astype(jnp.float32)[:, None] * freqs[None, :]
    return (jnp.cos(angle)[:, None, :], jnp.sin(angle)[:, None, :])


def rotate(values, cosine, sine, sign):
    half = cosine.shape[-1]
    lower = values[..., :half]
    upper = values[..., half : 2 * half]
    rest = values[..., 2 * half :]
    return jnp.concatenate(
        [lower * cosine - sign * upper * sine, upper * cosine + sign * lower * sine, rest], axis=-1
    )


def gelu_exact(value):
    return value * 0.5 * (1.0 + lax.erf(value * INV_ROOT_TWO))


def gelu_slope(value):
    return (
        0.5 * (1.0 + lax.erf(value * INV_ROOT_TWO))
        + value * jnp.exp(-0.5 * value * value) * INV_ROOT_TWO_PI
    )


def masked_scores(q_blk, keys, seg_rows, seg_cols, begin_row):
    scale = q_blk.shape[-1] ** (-0.5)
    raw_scores = jnp.einsum("qhd,khd->hqk", q_blk, keys, preferred_element_type=jnp.float32) * scale
    row_ids = begin_row + jnp.arange(q_blk.shape[0], dtype=jnp.int32)
    col_ids = jnp.arange(keys.shape[0], dtype=jnp.int32)
    allowed = (seg_rows[:, None] == seg_cols[None, :]) & (col_ids[None, :] <= row_ids[:, None])
    return jnp.where(allowed[None], raw_scores, NEG_BIG)


def attend_forward(query16, key16, value16, segments):
    scores = masked_scores(query16, key16, segments, segments, 0)
    row_max = jnp.max(scores, axis=-1, keepdims=True)
    expd = jnp.exp(scores - row_max)
    row_total = jnp.sum(expd, axis=-1, keepdims=True)
    probs16 = (expd / row_total).astype(jnp.bfloat16)
    attn_blk = jnp.einsum("hqk,khd->qhd", probs16, value16, preferred_element_type=jnp.float32)
    pieces_out = attn_blk.astype(jnp.bfloat16)
    lse_list = [row_max + jnp.log(row_total)]
    return (pieces_out, lse_list)


def attend_backward(query16, key16, value16, attn16, lse_list, segments, grad_attn16):
    count = query16.shape[0]
    block = min(512, count)
    scale = query16.shape[-1] ** (-0.5)
    grad_query = []
    grad_key = jnp.zeros(key16.shape, jnp.float32)
    grad_value = jnp.zeros(value16.shape, jnp.float32)
    for turn, begin_row in enumerate(range(0, count, block)):
        stop_row = begin_row + block
        scores = masked_scores(query16, key16, segments, segments, begin_row)
        chances = jnp.exp(scores - lse_list[turn])
        chances16 = chances.astype(jnp.bfloat16)
        grad_value = grad_value.at[:stop_row].add(
            jnp.einsum("hqk,qhd->khd", chances16, grad_attn16, preferred_element_type=jnp.float32)
        )
        grad_chance = jnp.einsum(
            "qhd,khd->hqk", grad_attn16, value16, preferred_element_type=jnp.float32
        )
        delta = jnp.sum(grad_attn16.astype(jnp.float32) * attn16.astype(jnp.float32), axis=-1)
        grad_scores = (chances * (grad_chance - jnp.transpose(delta)[:, :, None]) * scale).astype(
            jnp.bfloat16
        )
        grad_query.append(
            jnp.einsum("hqk,khd->qhd", grad_scores, key16, preferred_element_type=jnp.float32)
        )
        grad_key = grad_key.at[:stop_row].add(
            jnp.einsum("hqk,qhd->khd", grad_scores, query16, preferred_element_type=jnp.float32)
        )
    return (grad_query[0], grad_key, grad_value)


def norm_back(grad_act, normed, inv_std, gain):
    grad_gain = jnp.sum(grad_act * normed, axis=0)
    grad_shift = jnp.sum(grad_act, axis=0)
    grad_norm = grad_act * gain.astype(jnp.float32)
    grad_x = inv_std * (
        grad_norm
        - jnp.mean(grad_norm, axis=1, keepdims=True)
        - normed * jnp.mean(grad_norm * normed, axis=1, keepdims=True)
    )
    return (grad_gain, grad_shift, grad_x)


def layer_forward(tokens, segments, pieces):
    (
        gain_one,
        shift_one,
        w_qkv,
        b_qkv,
        w_out,
        b_out,
        gain_two,
        shift_two,
        w_in,
        b_in,
        w_out2,
        b_out2,
    ) = pieces
    count = tokens.shape[0]
    x_wide = tokens.astype(jnp.float32)
    row_mean = jnp.mean(x_wide, axis=1, keepdims=True)
    centered = x_wide - row_mean
    variance = jnp.mean(centered * centered, axis=1, keepdims=True)
    inv_std = lax.rsqrt(variance + EPS_NORM)
    normed = centered * inv_std
    act_one = (normed * gain_one.astype(jnp.float32) + shift_one.astype(jnp.float32)).astype(
        jnp.bfloat16
    )
    act_two = (normed * gain_two.astype(jnp.float32) + shift_two.astype(jnp.float32)).astype(
        jnp.bfloat16
    )
    mixed = jnp.dot(act_one, w_qkv, preferred_element_type=jnp.float32) + b_qkv.astype(jnp.float32)
    mixed = mixed.reshape(count, 3, HEADS, HD)
    cosine, sine = rotary_tables(positions_of(segments))
    query16 = rotate(mixed[:, 0], cosine, sine, 1.0).astype(jnp.bfloat16)
    key16 = rotate(mixed[:, 1], cosine, sine, 1.0).astype(jnp.bfloat16)
    value16 = mixed[:, 2].astype(jnp.bfloat16)
    attn16, lse_list = attend_forward(query16, key16, value16, segments)
    proj = jnp.dot(
        attn16.reshape(count, HEADS * HD), w_out, preferred_element_type=jnp.float32
    ) + b_out.astype(jnp.float32)
    pre = jnp.dot(act_two, w_in, preferred_element_type=jnp.float32) + b_in.astype(jnp.float32)
    hidden16 = gelu_exact(pre).astype(jnp.bfloat16)
    feed = jnp.dot(hidden16, w_out2, preferred_element_type=jnp.float32) + b_out2.astype(
        jnp.float32
    )
    output = x_wide + proj + feed
    saved = (
        normed,
        inv_std,
        act_one,
        act_two,
        query16,
        key16,
        value16,
        attn16,
        lse_list,
        cosine,
        sine,
        pre,
        hidden16,
    )
    return (output, saved)


def layer_backward(cotangent, segments, pieces, saved):
    (
        gain_one,
        shift_one,
        w_qkv,
        b_qkv,
        w_out,
        b_out,
        gain_two,
        shift_two,
        w_in,
        b_in,
        w_out2,
        b_out2,
    ) = pieces
    (
        normed,
        inv_std,
        act_one,
        act_two,
        query16,
        key16,
        value16,
        attn16,
        lse_list,
        cosine,
        sine,
        pre,
        hidden16,
    ) = saved
    count = cotangent.shape[0]
    contract_rows = (((0,), (0,)), ((), ()))
    contract_cols = (((1,), (1,)), ((), ()))
    live_rows = (segments >= 0).astype(jnp.float32)[:, None]
    grad_y = cotangent.astype(jnp.float32) * live_rows
    grad_y16 = grad_y.astype(jnp.bfloat16)
    grad_b_out = jnp.sum(grad_y, axis=0)
    attn_flat = attn16.reshape(count, HEADS * HD)
    grad_w_out = lax.dot_general(
        attn_flat, grad_y16, contract_rows, preferred_element_type=jnp.float32
    )
    grad_w_out2 = lax.dot_general(
        hidden16, grad_y16, contract_rows, preferred_element_type=jnp.float32
    )
    grad_hidden = lax.dot_general(
        grad_y16, w_out2, contract_cols, preferred_element_type=jnp.float32
    )
    grad_pre = grad_hidden * gelu_slope(pre)
    grad_b_in = jnp.sum(grad_pre, axis=0)
    grad_pre16 = grad_pre.astype(jnp.bfloat16)
    grad_w_in = lax.dot_general(
        act_two, grad_pre16, contract_rows, preferred_element_type=jnp.float32
    )
    grad_act_two = lax.dot_general(
        grad_pre16, w_in, contract_cols, preferred_element_type=jnp.float32
    )
    grad_attn16 = (
        lax.dot_general(grad_y16, w_out, contract_cols, preferred_element_type=jnp.float32)
        .astype(jnp.bfloat16)
        .reshape(count, HEADS, HD)
    )
    grad_query, grad_key, grad_value = attend_backward(
        query16, key16, value16, attn16, lse_list, segments, grad_attn16
    )
    grad_query = rotate(grad_query, cosine, sine, -1.0)
    grad_key = rotate(grad_key, cosine, sine, -1.0)
    grad_mixed = jnp.stack([grad_query, grad_key, grad_value], axis=1).reshape(
        count, 3 * HEADS * HD
    )
    grad_b_qkv = jnp.sum(grad_mixed, axis=0)
    grad_mixed16 = grad_mixed.astype(jnp.bfloat16)
    grad_w_qkv = lax.dot_general(
        act_one, grad_mixed16, contract_rows, preferred_element_type=jnp.float32
    )
    grad_act_one = lax.dot_general(
        grad_mixed16, w_qkv, contract_cols, preferred_element_type=jnp.float32
    )
    gain_grad_one, shift_grad_one, grad_x_one = norm_back(grad_act_one, normed, inv_std, gain_one)
    gain_grad_two, shift_grad_two, grad_x_two = norm_back(grad_act_two, normed, inv_std, gain_two)
    grad_in = grad_y + grad_x_one + grad_x_two
    return (
        grad_in,
        [
            gain_grad_one,
            shift_grad_one,
            grad_w_qkv,
            grad_b_qkv,
            grad_w_out,
            grad_b_out,
            gain_grad_two,
            shift_grad_two,
            grad_w_in,
            grad_b_in,
            grad_w_out2,
            grad_b_out,
        ],
    )


def flatten_grads(parts, total_len):
    used = layout_offsets()[-1]
    rounded = [part.astype(jnp.bfloat16).reshape(-1) for part in parts]
    return jnp.concatenate(rounded + [jnp.zeros((total_len - used,), jnp.bfloat16)])


def adam_update(weights, first_moment, second_moment, gradient):
    new_first = BETA_ONE * first_moment + (1.0 - BETA_ONE) * gradient
    new_second = BETA_TWO * second_moment + (1.0 - BETA_TWO) * gradient * gradient
    unbiased_first = new_first / (1.0 - BETA_ONE**ADAM_STEP)
    unbiased_second = new_second / (1.0 - BETA_TWO**ADAM_STEP)
    new_weights = weights - LEARN_RATE * (
        unbiased_first / (jnp.sqrt(unbiased_second) + ADAM_EPS) + DECAY * weights
    )
    return (new_weights, new_first, new_second)


def on_device(tokens, segment_ids, cotangent, params, moment_one, moment_two):
    gathered = lax.all_gather(params.astype(jnp.bfloat16), "shard", axis=0, tiled=True)
    total_len = gathered.shape[0]
    pieces = split_params(gathered)
    output, saved = layer_forward(tokens, segment_ids, pieces)
    grad_input, parts = layer_backward(cotangent, segment_ids, pieces, saved)
    local_grad = flatten_grads(parts, total_len)
    owned = lax.psum_scatter(local_grad, "shard", scatter_dimension=0, tiled=True).astype(
        jnp.float32
    )
    tokens_all = tokens.shape[0] * lax.axis_size("rep") * lax.axis_size("shard")
    factor = 1.0 / math.sqrt(tokens_all)
    width = moment_one.shape[0]
    begin = lax.axis_index("rep") * width
    param_share = lax.dynamic_slice_in_dim(params, begin, width)
    share = lax.psum_scatter(owned, "rep", scatter_dimension=0, tiled=True)
    grad_share = share * factor
    upd_params, upd_first, upd_second = adam_update(param_share, moment_one, moment_two, grad_share)
    grad_params, new_params = (
        lax.all_gather(grad_share, "rep", axis=0, tiled=True),
        lax.all_gather(upd_params, "rep", axis=0, tiled=True),
    )
    return (output, grad_input, grad_params, new_params, upd_first, upd_second)


LANES = 128
REPS = 8
SHARDS = 4
PIECE = 288
FLAT_ROWS = 13848
MOVED = PIECE * D // LANES


PARTS = (
    ((12, 1728, 96, 3, 0),),
    ((6, 576, 96, 1, 0), (4632, 1152, 48, 4, 96)),
    ((0, 1152, 48, 4, 0), (9240, 576, 96, 1, 192)),
    ((0, 1728, 288, 1, 0),),
)
VECTOR_ROWS = ((0, 1, 2306, 2307), (0, 769, 770, 771), (1536, 1537, 1538, 1539), (2304, 2305, 2306, 2307))


PLANE = ("y", "x", "core")
EVERY = PLANE + ("z",)
HOPS = (1, 2, 3, 0)


def plane_permute(value, flips):
    return lax.ppermute(value, PLANE, [(i, i ^ flips[i % 2]) for i in range(REPS)])


def first_cross(value):
    return plane_permute(value, (2, 4))


def second_cross(value):
    return plane_permute(value, (4, 2))


def core_cross(value):
    return plane_permute(value, (1, 1))


def ring_step(value):
    return lax.ppermute(value, "z", [(i, (i + 1) % SHARDS) for i in range(SHARDS)])


def flips_of(rep):
    core = rep % 2
    first = 2 + 2 * core
    return (0, first, 6 - first, 6)


def spread_ids(rep):
    other = rep ^ 1
    return [rep ^ flip for flip in flips_of(rep)] + [other ^ flip for flip in flips_of(other)]


def window_of(row):
    return min(6 * row // 8 * 8, FLAT_ROWS - 16)


def pack_kernel(where, flat_ref, out_ref, *rest):
    vec_ref = rest[0] if len(rest) == 4 else None
    held, windows, sems = rest[-3:]
    shard = where[0]
    turns = out_ref.shape[0]
    for z in range(SHARDS):

        @pl.when(shard == z)
        def _(z=z):
            def copies_of(turn):
                slot = turn % 2
                rep = where[1 + turn]
                copies = []
                at = 0
                for part, (first, step, _, _, _) in enumerate(PARTS[z]):
                    lead = first % 8
                    count = step + (8 if lead else 0)
                    begin = pl.multiple_of(first - lead + step * rep, 8)
                    copies.append(
                        pltpu.make_async_copy(
                            flat_ref.at[pl.ds(begin, count)],
                            held.at[slot, pl.ds(at, count)],
                            sems.at[slot, part],
                        )
                    )
                    at += count
                return copies

            for copy in copies_of(0):
                copy.start()
            if vec_ref is not None:
                cuts = []
                for slot, row in enumerate(VECTOR_ROWS[z]):
                    cuts.append(
                        pltpu.make_async_copy(
                            flat_ref.at[pl.ds(window_of(row), 16)],
                            windows.at[slot],
                            sems.at[2 + slot // 2, slot % 2],
                        )
                    )
                    cuts[-1].start()
                vec_ref[...] = jnp.zeros_like(vec_ref)
                for slot, row in enumerate(VECTOR_ROWS[z]):
                    cuts[slot].wait()
                    lead = 6 * row - window_of(row)
                    for col in range(6):
                        got = windows[slot, lead + col : lead + col + 1, :]
                        vec_ref[slot : slot + 1, LANES * col : LANES * (col + 1)] = got.astype(
                            jnp.bfloat16
                        ).astype(jnp.float32)

            @pl.loop(0, turns)
            def _(turn):
                @pl.when(turn + 1 < turns)
                def _():
                    for copy in copies_of(turn + 1):
                        copy.start()

                slot = turn % 2
                at = 0
                for copy, (first, step, rows, blocks, place) in zip(copies_of(turn), PARTS[z]):
                    copy.wait()
                    lead = first % 8
                    for block in range(blocks):
                        for col in range(6):
                            begin = at + lead + 6 * block + col
                            got = held[slot, pl.ds(begin, rows, stride=6 * blocks), :]
                            out_ref[
                                turn,
                                place + rows * block : place + rows * (block + 1),
                                LANES * col : LANES * (col + 1),
                            ] = got.astype(jnp.bfloat16)
                    at += step + (8 if lead else 0)


def pack_pieces(params, shard, reps, vectors):
    pieces = jax.ShapeDtypeStruct((len(reps), PIECE, D), jnp.bfloat16)
    rows = jax.ShapeDtypeStruct((8, D), jnp.float32)
    vmem = pl.BlockSpec(memory_space=pltpu.VMEM)
    return pl.pallas_call(
        pack_kernel,
        grid_spec=pltpu.PrefetchScalarGridSpec(
            num_scalar_prefetch=1,
            in_specs=[pl.BlockSpec(memory_space=pltpu.HBM)],
            out_specs=[vmem, vmem] if vectors else [vmem],
            scratch_shapes=[
                pltpu.VMEM((2, MOVED + 16, LANES), jnp.float32),
                pltpu.VMEM((4, 16, LANES), jnp.float32),
                pltpu.SemaphoreType.DMA((4, 2)),
            ],
        ),
        out_shape=[pieces, rows] if vectors else [pieces],
        compiler_params=pltpu.CompilerParams(vmem_limit_bytes=56 * 2**20),
    )(jnp.stack([shard] + reps), params.reshape(FLAT_ROWS, LANES))


def prepare_kernel(tokens, cotangent, ids, freqs, normed, spread, grad_y, tables):
    x_wide = tokens[...].astype(jnp.float32)
    centered = x_wide - jnp.mean(x_wide, axis=1, keepdims=True)
    variance = jnp.mean(centered * centered, axis=1, keepdims=True)
    inv_std = lax.rsqrt(variance + EPS_NORM)
    normed[...] = centered * inv_std
    spread[...] = jnp.broadcast_to(inv_std, spread.shape)
    square = (TOK_DEV, TOK_DEV)
    across = jnp.broadcast_to(ids[...].astype(jnp.float32), square)
    down = across.T
    lane = lax.broadcasted_iota(jnp.int32, square, 1)
    row = lax.broadcasted_iota(jnp.int32, square, 0)
    begins = (across != pltpu.roll(across, 1, 1)) | (lane == 0)
    before = jnp.where(begins & (lane <= row), lane.astype(jnp.float32), 0.0)
    position = row.astype(jnp.float32) - jnp.max(before, axis=1, keepdims=True)
    angle = position * freqs[...]
    cosine, sine = jnp.cos(angle), jnp.sin(angle)
    within = lane % HD
    tables[0] = jnp.where(within < ROT, cosine, 1.0)
    tables[1] = jnp.where(within < ROT // 2, -sine, 0.0)
    tables[2] = jnp.where((within >= ROT // 2) & (within < ROT), sine, 0.0)
    tables[3] = jnp.where((across == down) & (lane <= row), 1.0, 0.0)
    cot = cotangent[...].astype(jnp.float32)
    grad_y[...] = jnp.where(down[:, 0:1] >= 0, cot, 0.0).astype(jnp.bfloat16)


def prepare(tokens, cotangent, segment_ids):
    steps = jnp.arange(LANES, dtype=jnp.int32) % (ROT // 2)
    freqs = jnp.power(jnp.float32(ROPE_BASE), -2.0 * steps.astype(jnp.float32) / ROT)
    return pl.pallas_call(
        prepare_kernel,
        out_shape=[
            jax.ShapeDtypeStruct((TOK_DEV, D), jnp.float32),
            jax.ShapeDtypeStruct((TOK_DEV, LANES), jnp.float32),
            jax.ShapeDtypeStruct((TOK_DEV, D), jnp.bfloat16),
            jax.ShapeDtypeStruct((4, TOK_DEV, TOK_DEV), jnp.float32),
        ],
        compiler_params=pltpu.CompilerParams(vmem_limit_bytes=16 * 2**20),
    )(tokens, cotangent, segment_ids.reshape(1, TOK_DEV), freqs.reshape(1, LANES))


PIECES = SHARDS * REPS
GROUPS = 12
ALL_ROWS = PIECES * PIECE


def fetch_pieces(ids, blocks, own, shard, held, sems):
    views = []
    for block in blocks:
        views += [block.at[p] for p in range(4)] if len(block.shape) == 3 else [block]
    ids = ids + [shard * REPS + r for r in range(REPS)]
    views += [own.at[pl.ds(r * PIECE, PIECE)] for r in range(REPS)]
    for early in (True, False):
        for which, view in zip(ids, views):

            @pl.when((which < 2 * REPS) == early)
            def _(which=which, view=view):
                row = pl.multiple_of(which * PIECE, 16)
                pltpu.make_async_copy(view, held.at[pl.ds(row, PIECE)], sems.at[which]).start()

    def arrive(owner):
        for r in range(REPS):
            at = owner * REPS + r
            pltpu.make_async_copy(
                own.at[pl.ds(0, PIECE)], held.at[pl.ds(at * PIECE, PIECE)], sems.at[at]
            ).wait()

    return arrive


def rows_of(held, shard, begin, rows):
    return jnp.concatenate(
        [held[pl.ds((shard * REPS + r) * PIECE + begin, rows), :] for r in range(REPS)], axis=0
    )


def w_qkv_of(held, j):
    return rows_of(held, 0, 96 * j, 96)


def w_out_of(held):
    return rows_of(held, 1, 0, 96)


def w_in_of(held, j):
    return jnp.concatenate([rows_of(held, 1, 96 + 48 * j, 48), rows_of(held, 2, 48 * j, 48)], axis=0)


def w_out2_of(held, j):
    if j == 0:
        return rows_of(held, 2, 192, 96)
    return held[pl.ds(3 * REPS * PIECE + D * (j - 1), D), :]


def dot32(a, b):
    return jnp.dot(a, b, preferred_element_type=jnp.float32)


def attention_kernel(where, *refs):
    count = PIECES - REPS
    blocks, own = refs[:GROUPS], refs[GROUPS]
    normed, grad_y, tables = refs[GROUPS + 1 : GROUPS + 4]
    hops = refs[GROUPS + 4 : GROUPS + 8]
    matrices, attn_out, mixed_out, sums_out, vecs = refs[GROUPS + 8 : GROUPS + 13]
    held, query, key, value, grad_attn, sems, save_sem = refs[GROUPS + 13 :]
    rot_cos, rot_up, rot_down, bias = (tables.at[turn] for turn in range(4))
    shard = where[0]
    for owner in range(SHARDS):
        rows = jnp.zeros((4, D), jnp.float32)
        for hop in range(SHARDS):
            met = (shard + SHARDS - owner) % SHARDS == hop
            rows = jnp.where(met, hops[hop][0:4, :], rows)
        vecs[4 * owner : 4 * owner + 4, :] = rows
    arrive = fetch_pieces([where[1 + t] for t in range(count)], blocks, own, shard, held, sems)
    sums_out[...] = jnp.zeros_like(sums_out)

    arrive(0)
    act1 = (normed[...] * vecs[0:1, :] + vecs[1:2, :]).astype(jnp.bfloat16)
    for j, out in enumerate((query, key, value)):
        got = dot32(act1, w_qkv_of(held, j)) + vecs[2 + j : 3 + j, :]
        if j < 2:
            for p in range(6):
                lanes = slice(LANES * p, LANES * (p + 1))
                part = got[:, lanes]
                part = (
                    part * rot_cos[...]
                    + pltpu.roll(part, LANES - 8, 1) * rot_up[...]
                    + pltpu.roll(part, 8, 1) * rot_down[...]
                )
                out[:, lanes] = part.astype(jnp.bfloat16)
        else:
            out[...] = got.astype(jnp.bfloat16)
    gy_t = grad_y[...].T
    arrive(1)
    grad_attn[...] = dot32(w_out_of(held), gy_t).T.astype(jnp.bfloat16)

    arrive(2)
    arrive(3)
    saving = pltpu.make_async_copy(held, matrices, save_sem)
    saving.start()
    low = lax.broadcasted_iota(jnp.int32, (LANES, LANES), 1) < HD
    scale = HD ** (-0.5)
    for p in range(6):
        lanes = slice(LANES * p, LANES * (p + 1))
        q2, k2, v2, g2 = (ref[:, lanes] for ref in (query, key, value, grad_attn))
        k2_t, v2_t = k2.T, v2.T
        attn_parts, value_parts, query_parts, key_parts = [], [], [], []
        for half in range(2):
            here = low if half == 0 else ~low
            zero = jnp.zeros_like(q2)
            scores = dot32(jnp.where(here, q2, zero), k2_t) * scale
            scores = jnp.where(bias[...] > 0.5, scores, NEG_BIG)
            expd = jnp.exp(scores - jnp.max(scores, axis=1, keepdims=True))
            chances = expd / jnp.sum(expd, axis=1, keepdims=True)
            chances16 = chances.astype(jnp.bfloat16)
            attn = dot32(chances16, v2)
            attn16 = attn.astype(jnp.bfloat16)
            masked = jnp.where(here, g2, zero)
            delta = jnp.sum(
                masked.astype(jnp.float32) * attn16.astype(jnp.float32), axis=1, keepdims=True
            )
            grad_chance = dot32(masked, v2_t)
            slope = (chances * (grad_chance - delta) * scale).astype(jnp.bfloat16)
            attn_parts.append(attn16)
            value_parts.append(dot32(chances16.T, g2))
            query_parts.append(dot32(slope, k2))
            key_parts.append(dot32(slope.T, q2))
        attn_out[:, lanes] = jnp.where(low, *attn_parts)
        for j, parts in enumerate((query_parts, key_parts, value_parts)):
            part = jnp.where(low, *parts)
            if j < 2:
                part = (
                    part * rot_cos[...]
                    - pltpu.roll(part, LANES - 8, 1) * rot_up[...]
                    - pltpu.roll(part, 8, 1) * rot_down[...]
                )
            wide = slice(D * j + LANES * p, D * j + LANES * (p + 1))
            sums_out[j : j + 1, lanes] = jnp.sum(part, axis=0, keepdims=True)
            mixed_out[:, wide] = part.astype(jnp.bfloat16)

    saving.wait()


def attention(scalars, blocks, own, small):
    anywhere = pl.BlockSpec(memory_space=pl.ANY)
    vmem = pl.BlockSpec(memory_space=pltpu.VMEM)
    bf16 = jnp.bfloat16
    return pl.pallas_call(
        attention_kernel,
        grid_spec=pltpu.PrefetchScalarGridSpec(
            num_scalar_prefetch=1,
            in_specs=[anywhere] * (len(blocks) + 1) + [vmem] * len(small),
            out_specs=[anywhere] + [vmem] * 4,
            scratch_shapes=[
                pltpu.VMEM((ALL_ROWS, D), bf16),
                pltpu.VMEM((TOK_DEV, D), bf16),
                pltpu.VMEM((TOK_DEV, D), bf16),
                pltpu.VMEM((TOK_DEV, D), bf16),
                pltpu.VMEM((TOK_DEV, D), bf16),
                pltpu.SemaphoreType.DMA((PIECES,)),
                pltpu.SemaphoreType.DMA,
            ],
        ),
        out_shape=[
            jax.ShapeDtypeStruct((ALL_ROWS, D), bf16),
            jax.ShapeDtypeStruct((TOK_DEV, D), bf16),
            jax.ShapeDtypeStruct((TOK_DEV, 3 * D), bf16),
            jax.ShapeDtypeStruct((8, D), jnp.float32),
            jax.ShapeDtypeStruct((16, D), jnp.float32),
        ],
        compiler_params=pltpu.CompilerParams(vmem_limit_bytes=60 * 2**20),
        cost_estimate=pl.CostEstimate(
            flops=6 * 10**9, bytes_accessed=60 * 2**20, transcendentals=200000
        ),
    )(scalars, *blocks, own, *small)


def gradient_kernel(where, matrices, *refs):
    (normed, grad_y, attn_in, mixed_in, vecs) = refs[:5]
    outs = refs[5:21]
    hidden_out, pre_out, sums_out = refs[21:24]
    held, grads, sems, out_sems = refs[24:]
    copies = []
    for z in range(1, SHARDS):
        rows = pl.ds(z * REPS * PIECE, REPS * PIECE)
        copies.append(pltpu.make_async_copy(matrices.at[rows], held.at[rows], sems.at[z]))
    for copy in copies:
        copy.start()
    sums_out[...] = jnp.zeros_like(sums_out)
    shard = where[PIECES]

    def send_off(owner):
        for hop in range(SHARDS):

            @pl.when((shard + SHARDS - HOPS[hop]) % SHARDS == owner)
            def _(hop=hop):
                for turn in (2 * hop, 2 * hop + 1, 8 + 2 * hop, 9 + 2 * hop):
                    pltpu.make_async_copy(
                        grads.at[pl.ds(turn * 2 * PIECE, 2 * PIECE)],
                        outs[turn],
                        out_sems.at[turn],
                    ).start()

    slot_row = lambda z, r: pl.multiple_of(where[z * REPS + r] * PIECE, 16)

    def keep_rows(z, begin, rows, part):
        for r in range(part.shape[0] // rows):
            grads[pl.ds(slot_row(z, r) + begin, rows), :] = part[rows * r : rows * (r + 1), :]

    gy = grad_y[...]
    act1_t = (normed[...] * vecs[0:1, :] + vecs[1:2, :]).astype(jnp.bfloat16).T
    for j in range(3):
        keep_rows(
            0, 96 * j, 96, dot32(act1_t, mixed_in[:, D * j : D * (j + 1)]).astype(jnp.bfloat16)
        )
    send_off(0)
    keep_rows(1, 0, 96, dot32(attn_in[...].T, gy).astype(jnp.bfloat16))

    for copy in copies:
        copy.wait()
    gy_t = gy.T
    act2 = (normed[...] * vecs[6:7, :] + vecs[7:8, :]).astype(jnp.bfloat16)
    act2_t = act2.T
    for j in range(4):
        wide = slice(D * j, D * (j + 1))
        pre = dot32(act2, w_in_of(held, j)) + vecs[8 + j : 9 + j, :]
        bell = 0.5 * (1.0 + lax.erf(pre * INV_ROOT_TWO))
        hidden = (pre * bell).astype(jnp.bfloat16)
        hidden_out[:, wide] = hidden
        grad_hidden = dot32(w_out2_of(held, j), gy_t).T
        grad_pre = grad_hidden * (bell + pre * jnp.exp(-0.5 * pre * pre) * INV_ROOT_TWO_PI)
        sums_out[j : j + 1, :] = jnp.sum(grad_pre, axis=0, keepdims=True)
        grad_pre16 = grad_pre.astype(jnp.bfloat16)
        pre_out[:, wide] = grad_pre16
        w2 = dot32(hidden.T, gy).astype(jnp.bfloat16)
        if j == 0:
            keep_rows(2, 192, 96, w2)
        else:
            at = D * (j - 1)
            while at < D * j:
                r, begin = divmod(at, PIECE)
                rows = min(PIECE - begin, D * j - at)
                grads[pl.ds(slot_row(3, r) + begin, rows), :] = w2[
                    at - D * (j - 1) : at - D * (j - 1) + rows, :
                ]
                at += rows
    send_off(3)
    for half, owner in enumerate((1, 2)):
        side = act2_t[D // 2 * half : D // 2 * (half + 1), :]
        for j in range(4):
            w1 = dot32(side, pre_out[:, D * j : D * (j + 1)]).astype(jnp.bfloat16)
            keep_rows(owner, (96 if owner == 1 else 0) + 48 * j, 48, w1)
        send_off(owner)
    for turn, out in enumerate(outs):
        pltpu.make_async_copy(
            grads.at[pl.ds(turn * 2 * PIECE, 2 * PIECE)], out, out_sems.at[turn]
        ).wait()


def weight_gradients(slots, matrices, small):
    anywhere = pl.BlockSpec(memory_space=pl.ANY)
    vmem = pl.BlockSpec(memory_space=pltpu.VMEM)
    bf16 = jnp.bfloat16
    return pl.pallas_call(
        gradient_kernel,
        grid_spec=pltpu.PrefetchScalarGridSpec(
            num_scalar_prefetch=1,
            in_specs=[anywhere] + [vmem] * len(small),
            out_specs=[pl.BlockSpec(memory_space=pltpu.HBM)] * 16 + [vmem] * 3,
            scratch_shapes=[
                pltpu.VMEM((ALL_ROWS, D), bf16),
                pltpu.VMEM((ALL_ROWS, D), bf16),
                pltpu.SemaphoreType.DMA((SHARDS,)),
                pltpu.SemaphoreType.DMA((PIECES,)),
            ],
        ),
        out_shape=[jax.ShapeDtypeStruct((2 * PIECE, D), bf16)] * 16
        + [
            jax.ShapeDtypeStruct((TOK_DEV, FF), bf16),
            jax.ShapeDtypeStruct((TOK_DEV, FF), bf16),
            jax.ShapeDtypeStruct((8, D), jnp.float32),
        ],
        compiler_params=pltpu.CompilerParams(vmem_limit_bytes=60 * 2**20),
        cost_estimate=pl.CostEstimate(
            flops=10**10, bytes_accessed=60 * 2**20, transcendentals=800000
        ),
    )(slots, matrices, *small)


def result_kernel(matrices, *refs):
    (tokens, normed, spread, grad_y, attn, grad_mixed, low_sums, vecs, hidden, grad_pre, high_sums) = (
        refs[:11]
    )
    output, grad_input, vec_out, held, sems = refs[11:]
    copies = []
    for z in range(SHARDS):
        rows = pl.ds(z * REPS * PIECE, REPS * PIECE)
        copies.append(pltpu.make_async_copy(matrices.at[rows], held.at[rows], sems.at[z]))
    for copy in copies:
        copy.start()
    for copy in copies:
        copy.wait()
    total = dot32(attn[...], w_out_of(held)) + vecs[5:6, :]
    for j in range(4):
        total = total + dot32(hidden[:, D * j : D * (j + 1)], w_out2_of(held, j))
    output[...] = tokens[...].astype(jnp.float32) + (total + vecs[12:13, :])
    vec_out[2:5, :] = low_sums[0:3, :]
    vec_out[8:12, :] = high_sums[0:4, :]
    gy = grad_y[...].astype(jnp.float32)
    total = gy
    for norm, (parts, width, weights) in enumerate(
        ((grad_mixed, 3, w_qkv_of), (grad_pre, 4, w_in_of))
    ):
        back = None
        for j in range(width):
            part = dot32(weights(held, j), parts[:, D * j : D * (j + 1)].T)
            back = part if back is None else back + part
        grad_act = back.T
        gain_row = 0 if norm == 0 else 6
        unit = normed[...]
        vec_out[gain_row : gain_row + 1, :] = jnp.sum(grad_act * unit, axis=0, keepdims=True)
        vec_out[gain_row + 1 : gain_row + 2, :] = jnp.sum(grad_act, axis=0, keepdims=True)
        grad_norm = grad_act * vecs[gain_row : gain_row + 1, :]
        total = total + spread[:, 0:1] * (
            grad_norm
            - jnp.mean(grad_norm, axis=1, keepdims=True)
            - unit * jnp.mean(grad_norm * unit, axis=1, keepdims=True)
        )
    grad_input[...] = total
    bottom = jnp.sum(gy, axis=0, keepdims=True)
    vec_out[5:6, :] = bottom
    vec_out[12:13, :] = bottom
    vec_out[13:16, :] = jnp.zeros((3, D), jnp.float32)
    vec_out[...] = vec_out[...].astype(jnp.bfloat16).astype(jnp.float32)


def layer_results(matrices, small):
    hbm = pl.BlockSpec(memory_space=pl.ANY)
    vmem = pl.BlockSpec(memory_space=pltpu.VMEM)
    rows = jax.ShapeDtypeStruct((TOK_DEV, D), jnp.float32)
    return pl.pallas_call(
        result_kernel,
        in_specs=[hbm] + [vmem] * len(small),
        out_specs=[vmem] * 3,
        scratch_shapes=[
            pltpu.VMEM((ALL_ROWS, D), jnp.bfloat16),
            pltpu.SemaphoreType.DMA((SHARDS,)),
        ],
        out_shape=[rows, rows, jax.ShapeDtypeStruct((16, D), jnp.float32)],
        compiler_params=pltpu.CompilerParams(vmem_limit_bytes=20 * 2**20),
        cost_estimate=pl.CostEstimate(
            flops=4 * 10**9, bytes_accessed=30 * 2**20, transcendentals=0
        ),
    )(matrices, *small)


SHARE = FLAT_ROWS // REPS
BEGINS = tuple(SHARE * r // 16 * 16 for r in range(REPS)) + (FLAT_ROWS,)
SHARE_ROWS = 1760
STEP = 96


def align_kernel(where, one_ref, two_ref, out_ref, held):
    for r in range(REPS):

        @pl.when(where[0] == r)
        def _(r=r):
            lead = SHARE * r - BEGINS[r]
            for turn, ref in enumerate((one_ref, two_ref)):
                held[0:16, :] = jnp.zeros((16, LANES), jnp.float32)
                held[SHARE_ROWS - 32 :, :] = jnp.zeros((32, LANES), jnp.float32)
                held[lead : lead + SHARE, :] = ref[...]
                out_ref[turn] = held[...].astype(jnp.bfloat16)


def align_moments(moment_one, moment_two, rep):
    return pl.pallas_call(
        align_kernel,
        grid_spec=pltpu.PrefetchScalarGridSpec(
            num_scalar_prefetch=1,
            in_specs=[pl.BlockSpec(memory_space=pltpu.VMEM)] * 2,
            out_specs=pl.BlockSpec(memory_space=pltpu.VMEM),
            scratch_shapes=[pltpu.VMEM((SHARE_ROWS, LANES), jnp.float32)],
        ),
        out_shape=jax.ShapeDtypeStruct((2, SHARE_ROWS, LANES), jnp.bfloat16),
        compiler_params=pltpu.CompilerParams(vmem_limit_bytes=16 * 2**20),
    )(jnp.stack([rep]), moment_one.reshape(SHARE, LANES), moment_two.reshape(SHARE, LANES))


def update_kernel(factor, where, *refs):
    blocks = refs[:REPS]
    moments = refs[REPS : 2 * REPS]
    vec_ref, params, grad_out, params_out = refs[2 * REPS : 2 * REPS + 4]
    held, grad, weight, moment, sems, out_sems = refs[2 * REPS + 4 :]
    copies = []
    for turn in range(REPS):
        copies.append(
            pltpu.make_async_copy(blocks[turn], held.at[where[1 + turn]], sems.at[turn])
        )
    copies.append(pltpu.make_async_copy(params, weight, sems.at[REPS]))
    for turn in range(REPS):
        copies.append(
            pltpu.make_async_copy(
                moments[turn], moment.at[where[1 + turn]], sems.at[REPS + 1 + turn]
            )
        )
    for copy in copies[:REPS]:
        copy.start()
    for copy in copies[:REPS]:
        copy.wait()
    for copy in copies[REPS:]:
        copy.start()
    shard = where[0]
    for z in range(SHARDS):

        @pl.when(shard == z)
        def _(z=z):
            for slot, row in enumerate(VECTOR_ROWS[z]):
                for col in range(6):
                    grad[6 * row + col : 6 * row + col + 1, :] = (
                        vec_ref[slot : slot + 1, LANES * col : LANES * (col + 1)] * factor
                    )

            @pl.loop(0, REPS)
            def _(rep):
                for first, step, rows, blocks, place in PARTS[z]:
                    for block in range(blocks):
                        for col in range(6):
                            got = held[
                                rep,
                                place + rows * block : place + rows * (block + 1),
                                LANES * col : LANES * (col + 1),
                            ]
                            begin = first + step * rep + 6 * block + col
                            grad[pl.ds(begin, rows, stride=6 * blocks), :] = (
                                got.astype(jnp.float32) * factor
                            )

    saving = [pltpu.make_async_copy(grad, grad_out, out_sems.at[REPS])]
    saving[0].start()
    for copy in copies[REPS:]:
        copy.wait()
    for r in range(REPS):
        base = BEGINS[r]
        length = BEGINS[r + 1] - base
        if r > 0:
            tail = base - BEGINS[r - 1]
            moment[r, :, 0:16, :] = moment[r, :, 0:16, :] + moment[r - 1, :, tail : tail + 16, :]

        def renew(at, rows, r=r, base=base):
            here = pl.ds(pl.multiple_of(base + at, 8), rows)
            there = pl.ds(pl.multiple_of(at, 16), rows)
            updated, _, _ = adam_update(
                weight[here, :],
                moment[r, 0, there, :].astype(jnp.float32),
                moment[r, 1, there, :].astype(jnp.float32),
                grad[here, :],
            )
            weight[here, :] = updated

        @pl.loop(0, length // STEP)
        def _(turn):
            renew(turn * STEP, STEP)

        if length % STEP:
            renew(length // STEP * STEP, length % STEP)
        rows = pl.ds(base, length)
        saving.append(
            pltpu.make_async_copy(weight.at[rows], params_out.at[rows], out_sems.at[r])
        )
        saving[-1].start()
    for copy in saving:
        copy.wait()


def update_shard(blocks, ids, vectors, params, moments, shard, factor):
    anywhere = pl.BlockSpec(memory_space=pl.ANY)
    flat = jax.ShapeDtypeStruct((FLAT_ROWS, LANES), jnp.float32)
    return pl.pallas_call(
        functools.partial(update_kernel, factor),
        grid_spec=pltpu.PrefetchScalarGridSpec(
            num_scalar_prefetch=1,
            in_specs=[anywhere] * (2 * REPS)
            + [pl.BlockSpec(memory_space=pltpu.VMEM), anywhere],
            out_specs=[anywhere] * 2,
            scratch_shapes=[
                pltpu.VMEM((REPS, PIECE, D), jnp.bfloat16),
                pltpu.VMEM((FLAT_ROWS, LANES), jnp.float32),
                pltpu.VMEM((FLAT_ROWS, LANES), jnp.float32),
                pltpu.VMEM((REPS, 2, SHARE_ROWS, LANES), jnp.bfloat16),
                pltpu.SemaphoreType.DMA((2 * REPS + 1,)),
                pltpu.SemaphoreType.DMA((REPS + 1,)),
            ],
        ),
        out_shape=[flat, flat],
        compiler_params=pltpu.CompilerParams(vmem_limit_bytes=60 * 2**20),
    )(jnp.stack([shard] + ids), *blocks, *moments, vectors, params.reshape(FLAT_ROWS, LANES))


def ring_shift(value, hop):
    return lax.ppermute(value, "z", [(i, (i + hop) % SHARDS) for i in range(SHARDS)])


fence = lax.optimization_barrier


def gather_matrices(params, shard, rep, early):
    piece = pack_pieces(params, shard, [rep], False)[0][0]
    own, vec = pack_pieces(params, shard, [rep * 0 + turn for turn in range(REPS)], True)
    one = ring_step(piece)
    one, own, vec = fence((one, own, vec))
    two, first_one, second_one = ring_step(one), first_cross(one), second_cross(one)
    vec_one = ring_step(vec)
    two, first_one, second_one, vec_one, early = fence(
        (two, first_one, second_one, vec_one, early)
    )
    three, first_two, second_two = ring_step(two), first_cross(two), second_cross(two)
    both_one = second_cross(first_one)
    vec_two = ring_step(vec_one)
    three, first_two, second_two, both_one, vec_two = fence(
        (three, first_two, second_two, both_one, vec_two)
    )
    first_three, second_three = first_cross(three), second_cross(three)
    both_two = second_cross(first_two)
    mine_one = jnp.stack([one, first_one, second_one, both_one])
    other_one = core_cross(mine_one)
    vec_three = ring_step(vec_two)
    first_three, second_three, both_two, other_one, vec_three = fence(
        (first_three, second_three, both_two, other_one, vec_three)
    )
    both_three = second_cross(first_three)
    mine_two = jnp.stack([two, first_two, second_two, both_two])
    other_two = core_cross(mine_two)
    others = [core_cross(value) for value in (three, first_three, second_three)]
    others, both_three, other_two = fence((others, both_three, other_two))
    others.append(core_cross(both_three))
    threes = [three, first_three, second_three, both_three]
    blocks = [mine_one, other_one, mine_two, other_two] + threes + others
    ids = []
    for hop in range(1, SHARDS):
        owner = (shard + SHARDS - hop) % SHARDS
        ids += [owner * REPS + which for which in spread_ids(rep)]
    hops = [vec, vec_one, vec_two, vec_three]
    return blocks, own.reshape(REPS * PIECE, D), ids, hops, early


def slots_by_piece(shard, rep):
    slots = []
    for owner in range(SHARDS):
        hop = (shard + SHARDS - owner + 3) % SHARDS
        for which in range(REPS):
            apart = rep ^ which
            kept = 1 - apart % 2
            core = which % 2
            across = apart & 6
            first = 2 + 2 * core
            place = jnp.where(
                across == 0, 2, jnp.where(across == 6, 1, jnp.where(across == first, 0, 3))
            )
            slots.append((kept * SHARDS + hop) * 4 + place)
    return slots


def scatter_sums(parts, moments, small, results):
    sent_far, sent_near, kept_far, kept_near = (
        [parts[8 * half + 2 * turn + near] for turn in range(SHARDS)]
        for half in range(2)
        for near in range(2)
    )
    cores = [core_cross(sent_far[0]), core_cross(sent_near[0]), core_cross(sent_far[1])]
    cores = list(fence(cores))
    far = [kept_far[0] + cores[0], kept_far[1] + cores[2]]
    crossed = first_cross(far[0])
    others = [core_cross(v) for v in (sent_near[1], sent_far[2], sent_near[2], sent_far[3])]
    crossed, others, small = fence((crossed, others, small))
    near = [kept_near[0] + cores[1], kept_near[1] + others[0], kept_near[2] + others[2]]
    far += [kept_far[2] + others[1], kept_far[3] + others[3]]

    pair = near[0] + crossed
    final = second_cross(pair[1])
    kept = pair[0]
    crossed = first_cross(far[1])
    last_near = core_cross(sent_near[3])
    output, grad_input, vectors = results(small)
    final, crossed, last_near, vectors = fence((final, crossed, last_near, vectors))
    near.append(kept_near[3] + last_near)

    carried = None
    for turn in range(1, SHARDS):
        total = kept + final
        if carried is not None:
            total = total + carried
        carried = ring_step(total)
        pair = near[turn] + crossed
        kept = pair[0]
        final = second_cross(pair[1])
        met = plane_permute(vectors, ((1, 1), (2, 2), (4, 4))[turn - 1])
        if turn < SHARDS - 1:
            crossed = first_cross(far[turn + 1])
            final, crossed, carried, met, moments = fence(
                (final, crossed, carried, met, moments)
            )
        else:
            final, carried, met = fence((final, carried, met))
        if turn > 1:
            moments.append(core_cross(moments[turn]))
        vectors = vectors + met
    total = kept + final + carried

    first, second = first_cross(total), second_cross(total)
    shifted = [ring_shift(vectors, hop) for hop in range(1, SHARDS)]
    first, second, shifted = fence((first, second, shifted))
    vectors = vectors + shifted[0] + shifted[1] + shifted[2]
    both = second_cross(first)
    mine = [total, first, second]
    spread = [core_cross(value) for value in mine]
    both, spread = fence((both, spread))
    spread.append(core_cross(both))
    return mine + [both] + spread, moments, output, grad_input, vectors


def on_device_rows(tokens, segment_ids, cotangent, params, moment_one, moment_two):
    shard = lax.axis_index("z")
    rep = lax.axis_index(PLANE)
    early = (prepare(tokens, cotangent, segment_ids), align_moments(moment_one, moment_two, rep))
    blocks, own, ids, hops, early = gather_matrices(params, shard, rep, early)
    (normed, inv_std, grad_y, tables), moments = early
    moments, blocks = fence((moments, blocks))
    first_moments = first_cross(moments)
    small = (normed, grad_y, tables, *hops)
    matrices, *attended = attention(jnp.stack([shard] + ids), blocks, own, small)
    moments, first_moments, attended = fence((moments, first_moments, attended))
    moments = [moments, first_moments, second_cross(moments), second_cross(first_moments)]
    moments += [core_cross(value) for value in moments[:2]]
    attn, mixed, low_sums, vecs = attended
    made = weight_gradients(
        jnp.stack(slots_by_piece(shard, rep) + [shard]), matrices, (normed, grad_y, attn, mixed, vecs)
    )
    made, moments = fence((made, moments))
    small = (tokens, normed, inv_std, grad_y, attn, mixed, low_sums, vecs) + tuple(made[16:])
    spread, moments, output, grad_input, vec_grads = scatter_sums(
        [part.reshape(2, PIECE, D) for part in made[:16]], moments, small, lambda small: layer_results(matrices, small)
    )
    own_vectors = lax.dynamic_index_in_dim(
        vec_grads.reshape(SHARDS, 4, D), shard, 0, keepdims=False
    )
    tokens_all = tokens.shape[0] * lax.axis_size(EVERY)
    grad_params, new_params = update_shard(
        spread,
        spread_ids(rep),
        own_vectors,
        params,
        moments,
        shard,
        1.0 / math.sqrt(tokens_all),
    )
    grad_params = grad_params.reshape(-1)
    width = moment_one.shape[0]
    grad_share = lax.dynamic_slice_in_dim(grad_params, rep * width, width)
    _, upd_first, upd_second = adam_update(moment_one, moment_one, moment_two, grad_share)
    return (output, grad_input, grad_params, new_params.reshape(-1), upd_first, upd_second)


def solution(mesh):
    in_rows = mesh.shape["rep"] == REPS and mesh.shape["shard"] == SHARDS
    if in_rows:
        rep, shard = PLANE, "z"
        mesh = Mesh(mesh.devices.reshape(2, 2, 2, SHARDS), EVERY)
        body = on_device_rows
    else:
        rep, shard = ("rep",), "shard"
        body = on_device
    rows = rep + (shard,)
    owner = (shard,) + rep
    in_specs = (P(rows, None), P(rows), P(rows, None), P(shard), P(owner), P(owner))
    out_specs = (P(rows, None), P(rows, None), P(shard), P(shard), P(owner), P(owner))
    return jax.shard_map(body, mesh=mesh, in_specs=in_specs, out_specs=out_specs, check_vma=False)
```

```python
import functools
import math

import jax
import jax.numpy as jnp
from jax import lax
from jax.experimental import pallas as pl
from jax.experimental.pallas import tpu as pltpu
from jax.sharding import Mesh
from jax.sharding import PartitionSpec as P

D = 768
HEADS = 12
HD = 64
ROT = 16
FF = 3072
TOK_DEV = 128


EPS_NORM = 1e-05
ROPE_BASE = 10000.0
NEG_BIG = -1e30
BETA_ONE = 0.9
BETA_TWO = 0.95
ADAM_STEP = 3.0
LEARN_RATE = 0.05
DECAY = 0.01
ADAM_EPS = 1e-08
INV_ROOT_TWO = 0.7071067811865476
INV_ROOT_TWO_PI = 0.3989422804014327


def layout_offsets():
    q_width = HEADS * HD
    o_wqkv = 2 * D
    o_bqkv = o_wqkv + 3 * q_width * D
    o_wout = o_bqkv + 3 * q_width
    o_bout = o_wout + q_width * D
    o_gain2 = o_bout + D
    o_shift2 = o_gain2 + D
    o_win = o_shift2 + D
    o_bin = o_win + D * FF
    o_wout2 = o_bin + FF
    o_bout2 = o_wout2 + FF * D
    return (
        o_wqkv,
        o_bqkv,
        o_wout,
        o_bout,
        o_gain2,
        o_shift2,
        o_win,
        o_bin,
        o_wout2,
        o_bout2,
        o_bout2 + D,
    )


def split_params(flat16):
    q_width = HEADS * HD
    o_wqkv, o_bqkv, o_wout, o_bout, o_gain2, o_shift2, o_win, o_bin, o_wout2, o_bout2, o_end = (
        layout_offsets()
    )
    return (
        flat16[0:D],
        flat16[D:o_wqkv],
        flat16[o_wqkv:o_bqkv].reshape(D, 3 * q_width),
        flat16[o_bqkv:o_wout],
        flat16[o_wout:o_bout].reshape(q_width, D),
        flat16[o_bout:o_gain2],
        flat16[o_gain2:o_shift2],
        flat16[o_shift2:o_win],
        flat16[o_win:o_bin].reshape(D, FF),
        flat16[o_bin:o_wout2],
        flat16[o_wout2:o_bout2].reshape(FF, D),
        flat16[o_bout2:o_end],
    )


def positions_of(segments):
    count = segments.shape[0]
    slot_ids = jnp.arange(count, dtype=jnp.int32)
    before = jnp.concatenate([jnp.full((1,), -2, jnp.int32), segments[:-1]])
    begins = segments != before
    first_slot = lax.cummax(jnp.where(begins, slot_ids, 0), axis=0)
    return slot_ids - first_slot


def rotary_tables(positions):
    half = ROT // 2
    steps_j = jnp.arange(half, dtype=jnp.float32)
    freqs = jnp.power(jnp.float32(ROPE_BASE), -2.0 * steps_j / ROT)
    angle = positions.astype(jnp.float32)[:, None] * freqs[None, :]
    return (jnp.cos(angle)[:, None, :], jnp.sin(angle)[:, None, :])


def rotate(values, cosine, sine, sign):
    half = cosine.shape[-1]
    lower = values[..., :half]
    upper = values[..., half : 2 * half]
    rest = values[..., 2 * half :]
    return jnp.concatenate(
        [lower * cosine - sign * upper * sine, upper * cosine + sign * lower * sine, rest], axis=-1
    )


def gelu_exact(value):
    return value * 0.5 * (1.0 + lax.erf(value * INV_ROOT_TWO))


def gelu_slope(value):
    return (
        0.5 * (1.0 + lax.erf(value * INV_ROOT_TWO))
        + value * jnp.exp(-0.5 * value * value) * INV_ROOT_TWO_PI
    )


def masked_scores(q_blk, keys, seg_rows, seg_cols, begin_row):
    scale = q_blk.shape[-1] ** (-0.5)
    raw_scores = jnp.einsum("qhd,khd->hqk", q_blk, keys, preferred_element_type=jnp.float32) * scale
    row_ids = begin_row + jnp.arange(q_blk.shape[0], dtype=jnp.int32)
    col_ids = jnp.arange(keys.shape[0], dtype=jnp.int32)
    allowed = (seg_rows[:, None] == seg_cols[None, :]) & (col_ids[None, :] <= row_ids[:, None])
    return jnp.where(allowed[None], raw_scores, NEG_BIG)


def attend_forward(query16, key16, value16, segments):
    scores = masked_scores(query16, key16, segments, segments, 0)
    row_max = jnp.max(scores, axis=-1, keepdims=True)
    expd = jnp.exp(scores - row_max)
    row_total = jnp.sum(expd, axis=-1, keepdims=True)
    probs16 = (expd / row_total).astype(jnp.bfloat16)
    attn_blk = jnp.einsum("hqk,khd->qhd", probs16, value16, preferred_element_type=jnp.float32)
    pieces_out = attn_blk.astype(jnp.bfloat16)
    lse_list = [row_max + jnp.log(row_total)]
    return (pieces_out, lse_list)


def attend_backward(query16, key16, value16, attn16, lse_list, segments, grad_attn16):
    count = query16.shape[0]
    block = min(512, count)
    scale = query16.shape[-1] ** (-0.5)
    grad_query = []
    grad_key = jnp.zeros(key16.shape, jnp.float32)
    grad_value = jnp.zeros(value16.shape, jnp.float32)
    for turn, begin_row in enumerate(range(0, count, block)):
        stop_row = begin_row + block
        scores = masked_scores(query16, key16, segments, segments, begin_row)
        chances = jnp.exp(scores - lse_list[turn])
        chances16 = chances.astype(jnp.bfloat16)
        grad_value = grad_value.at[:stop_row].add(
            jnp.einsum("hqk,qhd->khd", chances16, grad_attn16, preferred_element_type=jnp.float32)
        )
        grad_chance = jnp.einsum(
            "qhd,khd->hqk", grad_attn16, value16, preferred_element_type=jnp.float32
        )
        delta = jnp.sum(grad_attn16.astype(jnp.float32) * attn16.astype(jnp.float32), axis=-1)
        grad_scores = (chances * (grad_chance - jnp.transpose(delta)[:, :, None]) * scale).astype(
            jnp.bfloat16
        )
        grad_query.append(
            jnp.einsum("hqk,khd->qhd", grad_scores, key16, preferred_element_type=jnp.float32)
        )
        grad_key = grad_key.at[:stop_row].add(
            jnp.einsum("hqk,qhd->khd", grad_scores, query16, preferred_element_type=jnp.float32)
        )
    return (grad_query[0], grad_key, grad_value)


def norm_back(grad_act, normed, inv_std, gain):
    grad_gain = jnp.sum(grad_act * normed, axis=0)
    grad_shift = jnp.sum(grad_act, axis=0)
    grad_norm = grad_act * gain.astype(jnp.float32)
    grad_x = inv_std * (
        grad_norm
        - jnp.mean(grad_norm, axis=1, keepdims=True)
        - normed * jnp.mean(grad_norm * normed, axis=1, keepdims=True)
    )
    return (grad_gain, grad_shift, grad_x)


def layer_forward(tokens, segments, pieces):
    (
        gain_one,
        shift_one,
        w_qkv,
        b_qkv,
        w_out,
        b_out,
        gain_two,
        shift_two,
        w_in,
        b_in,
        w_out2,
        b_out2,
    ) = pieces
    count = tokens.shape[0]
    x_wide = tokens.astype(jnp.float32)
    row_mean = jnp.mean(x_wide, axis=1, keepdims=True)
    centered = x_wide - row_mean
    variance = jnp.mean(centered * centered, axis=1, keepdims=True)
    inv_std = lax.rsqrt(variance + EPS_NORM)
    normed = centered * inv_std
    act_one = (normed * gain_one.astype(jnp.float32) + shift_one.astype(jnp.float32)).astype(
        jnp.bfloat16
    )
    act_two = (normed * gain_two.astype(jnp.float32) + shift_two.astype(jnp.float32)).astype(
        jnp.bfloat16
    )
    mixed = jnp.dot(act_one, w_qkv, preferred_element_type=jnp.float32) + b_qkv.astype(jnp.float32)
    mixed = mixed.reshape(count, 3, HEADS, HD)
    cosine, sine = rotary_tables(positions_of(segments))
    query16 = rotate(mixed[:, 0], cosine, sine, 1.0).astype(jnp.bfloat16)
    key16 = rotate(mixed[:, 1], cosine, sine, 1.0).astype(jnp.bfloat16)
    value16 = mixed[:, 2].astype(jnp.bfloat16)
    attn16, lse_list = attend_forward(query16, key16, value16, segments)
    proj = jnp.dot(
        attn16.reshape(count, HEADS * HD), w_out, preferred_element_type=jnp.float32
    ) + b_out.astype(jnp.float32)
    pre = jnp.dot(act_two, w_in, preferred_element_type=jnp.float32) + b_in.astype(jnp.float32)
    hidden16 = gelu_exact(pre).astype(jnp.bfloat16)
    feed = jnp.dot(hidden16, w_out2, preferred_element_type=jnp.float32) + b_out2.astype(
        jnp.float32
    )
    output = x_wide + proj + feed
    saved = (
        normed,
        inv_std,
        act_one,
        act_two,
        query16,
        key16,
        value16,
        attn16,
        lse_list,
        cosine,
        sine,
        pre,
        hidden16,
    )
    return (output, saved)


def layer_backward(cotangent, segments, pieces, saved):
    (
        gain_one,
        shift_one,
        w_qkv,
        b_qkv,
        w_out,
        b_out,
        gain_two,
        shift_two,
        w_in,
        b_in,
        w_out2,
        b_out2,
    ) = pieces
    (
        normed,
        inv_std,
        act_one,
        act_two,
        query16,
        key16,
        value16,
        attn16,
        lse_list,
        cosine,
        sine,
        pre,
        hidden16,
    ) = saved
    count = cotangent.shape[0]
    contract_rows = (((0,), (0,)), ((), ()))
    contract_cols = (((1,), (1,)), ((), ()))
    live_rows = (segments >= 0).astype(jnp.float32)[:, None]
    grad_y = cotangent.astype(jnp.float32) * live_rows
    grad_y16 = grad_y.astype(jnp.bfloat16)
    grad_b_out = jnp.sum(grad_y, axis=0)
    attn_flat = attn16.reshape(count, HEADS * HD)
    grad_w_out = lax.dot_general(
        attn_flat, grad_y16, contract_rows, preferred_element_type=jnp.float32
    )
    grad_w_out2 = lax.dot_general(
        hidden16, grad_y16, contract_rows, preferred_element_type=jnp.float32
    )
    grad_hidden = lax.dot_general(
        grad_y16, w_out2, contract_cols, preferred_element_type=jnp.float32
    )
    grad_pre = grad_hidden * gelu_slope(pre)
    grad_b_in = jnp.sum(grad_pre, axis=0)
    grad_pre16 = grad_pre.astype(jnp.bfloat16)
    grad_w_in = lax.dot_general(
        act_two, grad_pre16, contract_rows, preferred_element_type=jnp.float32
    )
    grad_act_two = lax.dot_general(
        grad_pre16, w_in, contract_cols, preferred_element_type=jnp.float32
    )
    grad_attn16 = (
        lax.dot_general(grad_y16, w_out, contract_cols, preferred_element_type=jnp.float32)
        .astype(jnp.bfloat16)
        .reshape(count, HEADS, HD)
    )
    grad_query, grad_key, grad_value = attend_backward(
        query16, key16, value16, attn16, lse_list, segments, grad_attn16
    )
    grad_query = rotate(grad_query, cosine, sine, -1.0)
    grad_key = rotate(grad_key, cosine, sine, -1.0)
    grad_mixed = jnp.stack([grad_query, grad_key, grad_value], axis=1).reshape(
        count, 3 * HEADS * HD
    )
    grad_b_qkv = jnp.sum(grad_mixed, axis=0)
    grad_mixed16 = grad_mixed.astype(jnp.bfloat16)
    grad_w_qkv = lax.dot_general(
        act_one, grad_mixed16, contract_rows, preferred_element_type=jnp.float32
    )
    grad_act_one = lax.dot_general(
        grad_mixed16, w_qkv, contract_cols, preferred_element_type=jnp.float32
    )
    gain_grad_one, shift_grad_one, grad_x_one = norm_back(grad_act_one, normed, inv_std, gain_one)
    gain_grad_two, shift_grad_two, grad_x_two = norm_back(grad_act_two, normed, inv_std, gain_two)
    grad_in = grad_y + grad_x_one + grad_x_two
    return (
        grad_in,
        [
            gain_grad_one,
            shift_grad_one,
            grad_w_qkv,
            grad_b_qkv,
            grad_w_out,
            grad_b_out,
            gain_grad_two,
            shift_grad_two,
            grad_w_in,
            grad_b_in,
            grad_w_out2,
            grad_b_out,
        ],
    )


def flatten_grads(parts, total_len):
    used = layout_offsets()[-1]
    rounded = [part.astype(jnp.bfloat16).reshape(-1) for part in parts]
    return jnp.concatenate(rounded + [jnp.zeros((total_len - used,), jnp.bfloat16)])


def adam_update(weights, first_moment, second_moment, gradient):
    new_first = BETA_ONE * first_moment + (1.0 - BETA_ONE) * gradient
    new_second = BETA_TWO * second_moment + (1.0 - BETA_TWO) * gradient * gradient
    unbiased_first = new_first / (1.0 - BETA_ONE**ADAM_STEP)
    unbiased_second = new_second / (1.0 - BETA_TWO**ADAM_STEP)
    new_weights = weights - LEARN_RATE * (
        unbiased_first / (jnp.sqrt(unbiased_second) + ADAM_EPS) + DECAY * weights
    )
    return (new_weights, new_first, new_second)


def on_device(tokens, segment_ids, cotangent, params, moment_one, moment_two):
    gathered = lax.all_gather(params.astype(jnp.bfloat16), "shard", axis=0, tiled=True)
    total_len = gathered.shape[0]
    pieces = split_params(gathered)
    output, saved = layer_forward(tokens, segment_ids, pieces)
    grad_input, parts = layer_backward(cotangent, segment_ids, pieces, saved)
    local_grad = flatten_grads(parts, total_len)
    owned = lax.psum_scatter(local_grad, "shard", scatter_dimension=0, tiled=True).astype(
        jnp.float32
    )
    tokens_all = tokens.shape[0] * lax.axis_size("rep") * lax.axis_size("shard")
    factor = 1.0 / math.sqrt(tokens_all)
    width = moment_one.shape[0]
    begin = lax.axis_index("rep") * width
    param_share = lax.dynamic_slice_in_dim(params, begin, width)
    share = lax.psum_scatter(owned, "rep", scatter_dimension=0, tiled=True)
    grad_share = share * factor
    upd_params, upd_first, upd_second = adam_update(param_share, moment_one, moment_two, grad_share)
    grad_params, new_params = (
        lax.all_gather(grad_share, "rep", axis=0, tiled=True),
        lax.all_gather(upd_params, "rep", axis=0, tiled=True),
    )
    return (output, grad_input, grad_params, new_params, upd_first, upd_second)


LANES = 128
REPS = 8
SHARDS = 4
PIECE = 288
FLAT_ROWS = 13848
MOVED = PIECE * D // LANES


PARTS = (
    ((12, 1728, 96, 3, 0),),
    ((6, 576, 96, 1, 0), (4632, 1152, 48, 4, 96)),
    ((0, 1152, 48, 4, 0), (9240, 576, 96, 1, 192)),
    ((0, 1728, 288, 1, 0),),
)
VECTOR_ROWS = ((0, 1, 2306, 2307), (0, 769, 770, 771), (1536, 1537, 1538, 1539), (2304, 2305, 2306, 2307))


PLANE = ("y", "x", "core")
EVERY = PLANE + ("z",)
HOPS = (1, 2, 3, 0)


def plane_permute(value, flips):
    return lax.ppermute(value, PLANE, [(i, i ^ flips[i % 2]) for i in range(REPS)])


def first_cross(value):
    return plane_permute(value, (2, 4))


def second_cross(value):
    return plane_permute(value, (4, 2))


def core_cross(value):
    return plane_permute(value, (1, 1))


def ring_step(value):
    return lax.ppermute(value, "z", [(i, (i + 1) % SHARDS) for i in range(SHARDS)])


def flips_of(rep):
    core = rep % 2
    first = 2 + 2 * core
    return (0, first, 6 - first, 6)


def spread_ids(rep):
    other = rep ^ 1
    return [rep ^ flip for flip in flips_of(rep)] + [other ^ flip for flip in flips_of(other)]


def window_of(row):
    return min(6 * row // 8 * 8, FLAT_ROWS - 16)


def pack_kernel(where, flat_ref, out_ref, *rest):
    vec_ref = rest[0] if len(rest) == 4 else None
    held, windows, sems = rest[-3:]
    shard = where[0]
    turns = out_ref.shape[0]
    for z in range(SHARDS):

        @pl.when(shard == z)
        def _(z=z):
            def copies_of(turn):
                slot = turn % 2
                rep = where[1 + turn]
                copies = []
                at = 0
                for part, (first, step, _, _, _) in enumerate(PARTS[z]):
                    lead = first % 8
                    count = step + (8 if lead else 0)
                    begin = pl.multiple_of(first - lead + step * rep, 8)
                    copies.append(
                        pltpu.make_async_copy(
                            flat_ref.at[pl.ds(begin, count)],
                            held.at[slot, pl.ds(at, count)],
                            sems.at[slot, part],
                        )
                    )
                    at += count
                return copies

            for copy in copies_of(0):
                copy.start()
            if vec_ref is not None:
                cuts = []
                for slot, row in enumerate(VECTOR_ROWS[z]):
                    cuts.append(
                        pltpu.make_async_copy(
                            flat_ref.at[pl.ds(window_of(row), 16)],
                            windows.at[slot],
                            sems.at[2 + slot // 2, slot % 2],
                        )
                    )
                    cuts[-1].start()
                vec_ref[...] = jnp.zeros_like(vec_ref)
                for slot, row in enumerate(VECTOR_ROWS[z]):
                    cuts[slot].wait()
                    lead = 6 * row - window_of(row)
                    for col in range(6):
                        got = windows[slot, lead + col : lead + col + 1, :]
                        vec_ref[slot : slot + 1, LANES * col : LANES * (col + 1)] = got.astype(
                            jnp.bfloat16
                        ).astype(jnp.float32)

            @pl.loop(0, turns)
            def _(turn):
                @pl.when(turn + 1 < turns)
                def _():
                    for copy in copies_of(turn + 1):
                        copy.start()

                slot = turn % 2
                at = 0
                for copy, (first, step, rows, blocks, place) in zip(copies_of(turn), PARTS[z]):
                    copy.wait()
                    lead = first % 8
                    for block in range(blocks):
                        for col in range(6):
                            begin = at + lead + 6 * block + col
                            got = held[slot, pl.ds(begin, rows, stride=6 * blocks), :]
                            out_ref[
                                turn,
                                place + rows * block : place + rows * (block + 1),
                                LANES * col : LANES * (col + 1),
                            ] = got.astype(jnp.bfloat16)
                    at += step + (8 if lead else 0)


def pack_pieces(params, shard, reps, vectors):
    pieces = jax.ShapeDtypeStruct((len(reps), PIECE, D), jnp.bfloat16)
    rows = jax.ShapeDtypeStruct((8, D), jnp.float32)
    vmem = pl.BlockSpec(memory_space=pltpu.VMEM)
    return pl.pallas_call(
        pack_kernel,
        grid_spec=pltpu.PrefetchScalarGridSpec(
            num_scalar_prefetch=1,
            in_specs=[pl.BlockSpec(memory_space=pltpu.HBM)],
            out_specs=[vmem, vmem] if vectors else [vmem],
            scratch_shapes=[
                pltpu.VMEM((2, MOVED + 16, LANES), jnp.float32),
                pltpu.VMEM((4, 16, LANES), jnp.float32),
                pltpu.SemaphoreType.DMA((4, 2)),
            ],
        ),
        out_shape=[pieces, rows] if vectors else [pieces],
        compiler_params=pltpu.CompilerParams(vmem_limit_bytes=56 * 2**20),
    )(jnp.stack([shard] + reps), params.reshape(FLAT_ROWS, LANES))


def prepare_kernel(tokens, cotangent, ids, freqs, normed, spread, grad_y, tables):
    x_wide = tokens[...].astype(jnp.float32)
    centered = x_wide - jnp.mean(x_wide, axis=1, keepdims=True)
    variance = jnp.mean(centered * centered, axis=1, keepdims=True)
    inv_std = lax.rsqrt(variance + EPS_NORM)
    normed[...] = centered * inv_std
    spread[...] = jnp.broadcast_to(inv_std, spread.shape)
    square = (TOK_DEV, TOK_DEV)
    across = jnp.broadcast_to(ids[...].astype(jnp.float32), square)
    down = across.T
    lane = lax.broadcasted_iota(jnp.int32, square, 1)
    row = lax.broadcasted_iota(jnp.int32, square, 0)
    begins = (across != pltpu.roll(across, 1, 1)) | (lane == 0)
    before = jnp.where(begins & (lane <= row), lane.astype(jnp.float32), 0.0)
    position = row.astype(jnp.float32) - jnp.max(before, axis=1, keepdims=True)
    angle = position * freqs[...]
    cosine, sine = jnp.cos(angle), jnp.sin(angle)
    within = lane % HD
    tables[0] = jnp.where(within < ROT, cosine, 1.0)
    tables[1] = jnp.where(within < ROT // 2, -sine, 0.0)
    tables[2] = jnp.where((within >= ROT // 2) & (within < ROT), sine, 0.0)
    tables[3] = jnp.where((across == down) & (lane <= row), 1.0, 0.0)
    cot = cotangent[...].astype(jnp.float32)
    grad_y[...] = jnp.where(down[:, 0:1] >= 0, cot, 0.0).astype(jnp.bfloat16)


def prepare(tokens, cotangent, segment_ids):
    steps = jnp.arange(LANES, dtype=jnp.int32) % (ROT // 2)
    freqs = jnp.power(jnp.float32(ROPE_BASE), -2.0 * steps.astype(jnp.float32) / ROT)
    return pl.pallas_call(
        prepare_kernel,
        out_shape=[
            jax.ShapeDtypeStruct((TOK_DEV, D), jnp.float32),
            jax.ShapeDtypeStruct((TOK_DEV, LANES), jnp.float32),
            jax.ShapeDtypeStruct((TOK_DEV, D), jnp.bfloat16),
            jax.ShapeDtypeStruct((4, TOK_DEV, TOK_DEV), jnp.float32),
        ],
        compiler_params=pltpu.CompilerParams(vmem_limit_bytes=16 * 2**20),
    )(tokens, cotangent, segment_ids.reshape(1, TOK_DEV), freqs.reshape(1, LANES))


PIECES = SHARDS * REPS
GROUPS = 12
ALL_ROWS = PIECES * PIECE


def fetch_pieces(ids, blocks, own, shard, held, sems):
    views = []
    for block in blocks:
        views += [block.at[p] for p in range(4)] if len(block.shape) == 3 else [block]
    ids = ids + [shard * REPS + r for r in range(REPS)]
    views += [own.at[pl.ds(r * PIECE, PIECE)] for r in range(REPS)]
    for early in (True, False):
        for which, view in zip(ids, views):

            @pl.when((which < 2 * REPS) == early)
            def _(which=which, view=view):
                row = pl.multiple_of(which * PIECE, 16)
                pltpu.make_async_copy(view, held.at[pl.ds(row, PIECE)], sems.at[which]).start()

    def arrive(owner):
        for r in range(REPS):
            at = owner * REPS + r
            pltpu.make_async_copy(
                own.at[pl.ds(0, PIECE)], held.at[pl.ds(at * PIECE, PIECE)], sems.at[at]
            ).wait()

    return arrive


def rows_of(held, shard, begin, rows):
    return jnp.concatenate(
        [held[pl.ds((shard * REPS + r) * PIECE + begin, rows), :] for r in range(REPS)], axis=0
    )


def w_qkv_of(held, j):
    return rows_of(held, 0, 96 * j, 96)


def w_out_of(held):
    return rows_of(held, 1, 0, 96)


def w_in_of(held, j):
    return jnp.concatenate([rows_of(held, 1, 96 + 48 * j, 48), rows_of(held, 2, 48 * j, 48)], axis=0)


def w_out2_of(held, j):
    if j == 0:
        return rows_of(held, 2, 192, 96)
    return held[pl.ds(3 * REPS * PIECE + D * (j - 1), D), :]


def dot32(a, b):
    return jnp.dot(a, b, preferred_element_type=jnp.float32)


def attention_kernel(where, *refs):
    count = PIECES - REPS
    blocks, own = refs[:GROUPS], refs[GROUPS]
    normed, grad_y, tables = refs[GROUPS + 1 : GROUPS + 4]
    hops = refs[GROUPS + 4 : GROUPS + 8]
    matrices, attn_out, mixed_out, sums_out, vecs = refs[GROUPS + 8 : GROUPS + 13]
    held, query, key, value, grad_attn, sems, save_sem = refs[GROUPS + 13 :]
    rot_cos, rot_up, rot_down, bias = (tables.at[turn] for turn in range(4))
    shard = where[0]
    for owner in range(SHARDS):
        rows = jnp.zeros((4, D), jnp.float32)
        for hop in range(SHARDS):
            met = (shard + SHARDS - owner) % SHARDS == hop
            rows = jnp.where(met, hops[hop][0:4, :], rows)
        vecs[4 * owner : 4 * owner + 4, :] = rows
    arrive = fetch_pieces([where[1 + t] for t in range(count)], blocks, own, shard, held, sems)
    sums_out[...] = jnp.zeros_like(sums_out)

    arrive(0)
    act1 = (normed[...] * vecs[0:1, :] + vecs[1:2, :]).astype(jnp.bfloat16)
    for j, out in enumerate((query, key, value)):
        got = dot32(act1, w_qkv_of(held, j)) + vecs[2 + j : 3 + j, :]
        if j < 2:
            for p in range(6):
                lanes = slice(LANES * p, LANES * (p + 1))
                part = got[:, lanes]
                part = (
                    part * rot_cos[...]
                    + pltpu.roll(part, LANES - 8, 1) * rot_up[...]
                    + pltpu.roll(part, 8, 1) * rot_down[...]
                )
                out[:, lanes] = part.astype(jnp.bfloat16)
        else:
            out[...] = got.astype(jnp.bfloat16)
    gy_t = grad_y[...].T
    arrive(1)
    grad_attn[...] = dot32(w_out_of(held), gy_t).T.astype(jnp.bfloat16)

    arrive(2)
    arrive(3)
    saving = pltpu.make_async_copy(held, matrices, save_sem)
    saving.start()
    low = lax.broadcasted_iota(jnp.int32, (LANES, LANES), 1) < HD
    scale = HD ** (-0.5)
    for p in range(6):
        lanes = slice(LANES * p, LANES * (p + 1))
        q2, k2, v2, g2 = (ref[:, lanes] for ref in (query, key, value, grad_attn))
        k2_t, v2_t = k2.T, v2.T
        attn_parts, value_parts, query_parts, key_parts = [], [], [], []
        for half in range(2):
            here = low if half == 0 else ~low
            zero = jnp.zeros_like(q2)
            scores = dot32(jnp.where(here, q2, zero), k2_t) * scale
            scores = jnp.where(bias[...] > 0.5, scores, NEG_BIG)
            expd = jnp.exp(scores - jnp.max(scores, axis=1, keepdims=True))
            chances = expd / jnp.sum(expd, axis=1, keepdims=True)
            chances16 = chances.astype(jnp.bfloat16)
            attn = dot32(chances16, v2)
            attn16 = attn.astype(jnp.bfloat16)
            masked = jnp.where(here, g2, zero)
            delta = jnp.sum(
                masked.astype(jnp.float32) * attn16.astype(jnp.float32), axis=1, keepdims=True
            )
            grad_chance = dot32(masked, v2_t)
            slope = (chances * (grad_chance - delta) * scale).astype(jnp.bfloat16)
            attn_parts.append(attn16)
            value_parts.append(dot32(chances16.T, g2))
            query_parts.append(dot32(slope, k2))
            key_parts.append(dot32(slope.T, q2))
        attn_out[:, lanes] = jnp.where(low, *attn_parts)
        for j, parts in enumerate((query_parts, key_parts, value_parts)):
            part = jnp.where(low, *parts)
            if j < 2:
                part = (
                    part * rot_cos[...]
                    - pltpu.roll(part, LANES - 8, 1) * rot_up[...]
                    - pltpu.roll(part, 8, 1) * rot_down[...]
                )
            wide = slice(D * j + LANES * p, D * j + LANES * (p + 1))
            sums_out[j : j + 1, lanes] = jnp.sum(part, axis=0, keepdims=True)
            mixed_out[:, wide] = part.astype(jnp.bfloat16)

    saving.wait()


def attention(scalars, blocks, own, small):
    anywhere = pl.BlockSpec(memory_space=pl.ANY)
    vmem = pl.BlockSpec(memory_space=pltpu.VMEM)
    bf16 = jnp.bfloat16
    return pl.pallas_call(
        attention_kernel,
        grid_spec=pltpu.PrefetchScalarGridSpec(
            num_scalar_prefetch=1,
            in_specs=[anywhere] * (len(blocks) + 1) + [vmem] * len(small),
            out_specs=[anywhere] + [vmem] * 4,
            scratch_shapes=[
                pltpu.VMEM((ALL_ROWS, D), bf16),
                pltpu.VMEM((TOK_DEV, D), bf16),
                pltpu.VMEM((TOK_DEV, D), bf16),
                pltpu.VMEM((TOK_DEV, D), bf16),
                pltpu.VMEM((TOK_DEV, D), bf16),
                pltpu.SemaphoreType.DMA((PIECES,)),
                pltpu.SemaphoreType.DMA,
            ],
        ),
        out_shape=[
            jax.ShapeDtypeStruct((ALL_ROWS, D), bf16),
            jax.ShapeDtypeStruct((TOK_DEV, D), bf16),
            jax.ShapeDtypeStruct((TOK_DEV, 3 * D), bf16),
            jax.ShapeDtypeStruct((8, D), jnp.float32),
            jax.ShapeDtypeStruct((16, D), jnp.float32),
        ],
        compiler_params=pltpu.CompilerParams(vmem_limit_bytes=60 * 2**20),
        cost_estimate=pl.CostEstimate(
            flops=6 * 10**9, bytes_accessed=60 * 2**20, transcendentals=200000
        ),
    )(scalars, *blocks, own, *small)


def gradient_kernel(where, matrices, *refs):
    (normed, grad_y, attn_in, mixed_in, vecs) = refs[:5]
    outs = refs[5:21]
    hidden_out, pre_out, sums_out = refs[21:24]
    held, grads, sems, out_sems = refs[24:]
    copies = []
    for z in range(1, SHARDS):
        rows = pl.ds(z * REPS * PIECE, REPS * PIECE)
        copies.append(pltpu.make_async_copy(matrices.at[rows], held.at[rows], sems.at[z]))
    for copy in copies:
        copy.start()
    sums_out[...] = jnp.zeros_like(sums_out)
    shard = where[PIECES]

    def send_off(owner):
        for hop in range(SHARDS):

            @pl.when((shard + SHARDS - HOPS[hop]) % SHARDS == owner)
            def _(hop=hop):
                for turn in (2 * hop, 2 * hop + 1, 8 + 2 * hop, 9 + 2 * hop):
                    pltpu.make_async_copy(
                        grads.at[pl.ds(turn * 2 * PIECE, 2 * PIECE)],
                        outs[turn],
                        out_sems.at[turn],
                    ).start()

    slot_row = lambda z, r: pl.multiple_of(where[z * REPS + r] * PIECE, 16)

    def keep_rows(z, begin, rows, part):
        for r in range(part.shape[0] // rows):
            grads[pl.ds(slot_row(z, r) + begin, rows), :] = part[rows * r : rows * (r + 1), :]

    gy = grad_y[...]
    act1_t = (normed[...] * vecs[0:1, :] + vecs[1:2, :]).astype(jnp.bfloat16).T
    for j in range(3):
        keep_rows(
            0, 96 * j, 96, dot32(act1_t, mixed_in[:, D * j : D * (j + 1)]).astype(jnp.bfloat16)
        )
    send_off(0)
    keep_rows(1, 0, 96, dot32(attn_in[...].T, gy).astype(jnp.bfloat16))

    for copy in copies:
        copy.wait()
    gy_t = gy.T
    act2 = (normed[...] * vecs[6:7, :] + vecs[7:8, :]).astype(jnp.bfloat16)
    act2_t = act2.T
    for j in range(4):
        wide = slice(D * j, D * (j + 1))
        pre = dot32(act2, w_in_of(held, j)) + vecs[8 + j : 9 + j, :]
        bell = 0.5 * (1.0 + lax.erf(pre * INV_ROOT_TWO))
        hidden = (pre * bell).astype(jnp.bfloat16)
        hidden_out[:, wide] = hidden
        grad_hidden = dot32(w_out2_of(held, j), gy_t).T
        grad_pre = grad_hidden * (bell + pre * jnp.exp(-0.5 * pre * pre) * INV_ROOT_TWO_PI)
        sums_out[j : j + 1, :] = jnp.sum(grad_pre, axis=0, keepdims=True)
        grad_pre16 = grad_pre.astype(jnp.bfloat16)
        pre_out[:, wide] = grad_pre16
        w2 = dot32(hidden.T, gy).astype(jnp.bfloat16)
        if j == 0:
            keep_rows(2, 192, 96, w2)
        else:
            at = D * (j - 1)
            while at < D * j:
                r, begin = divmod(at, PIECE)
                rows = min(PIECE - begin, D * j - at)
                grads[pl.ds(slot_row(3, r) + begin, rows), :] = w2[
                    at - D * (j - 1) : at - D * (j - 1) + rows, :
                ]
                at += rows
    send_off(3)
    for half, owner in enumerate((1, 2)):
        side = act2_t[D // 2 * half : D // 2 * (half + 1), :]
        for j in range(4):
            w1 = dot32(side, pre_out[:, D * j : D * (j + 1)]).astype(jnp.bfloat16)
            keep_rows(owner, (96 if owner == 1 else 0) + 48 * j, 48, w1)
        send_off(owner)
    for turn, out in enumerate(outs):
        pltpu.make_async_copy(
            grads.at[pl.ds(turn * 2 * PIECE, 2 * PIECE)], out, out_sems.at[turn]
        ).wait()


def weight_gradients(slots, matrices, small):
    anywhere = pl.BlockSpec(memory_space=pl.ANY)
    vmem = pl.BlockSpec(memory_space=pltpu.VMEM)
    bf16 = jnp.bfloat16
    return pl.pallas_call(
        gradient_kernel,
        grid_spec=pltpu.PrefetchScalarGridSpec(
            num_scalar_prefetch=1,
            in_specs=[anywhere] + [vmem] * len(small),
            out_specs=[pl.BlockSpec(memory_space=pltpu.HBM)] * 16 + [vmem] * 3,
            scratch_shapes=[
                pltpu.VMEM((ALL_ROWS, D), bf16),
                pltpu.VMEM((ALL_ROWS, D), bf16),
                pltpu.SemaphoreType.DMA((SHARDS,)),
                pltpu.SemaphoreType.DMA((PIECES,)),
            ],
        ),
        out_shape=[jax.ShapeDtypeStruct((2 * PIECE, D), bf16)] * 16
        + [
            jax.ShapeDtypeStruct((TOK_DEV, FF), bf16),
            jax.ShapeDtypeStruct((TOK_DEV, FF), bf16),
            jax.ShapeDtypeStruct((8, D), jnp.float32),
        ],
        compiler_params=pltpu.CompilerParams(vmem_limit_bytes=60 * 2**20),
        cost_estimate=pl.CostEstimate(
            flops=10**10, bytes_accessed=60 * 2**20, transcendentals=800000
        ),
    )(slots, matrices, *small)


def result_kernel(matrices, *refs):
    (tokens, normed, spread, grad_y, attn, grad_mixed, low_sums, vecs, hidden, grad_pre, high_sums) = (
        refs[:11]
    )
    output, grad_input, vec_out, held, sems = refs[11:]
    copies = []
    for z in range(SHARDS):
        rows = pl.ds(z * REPS * PIECE, REPS * PIECE)
        copies.append(pltpu.make_async_copy(matrices.at[rows], held.at[rows], sems.at[z]))
    for copy in copies:
        copy.start()
    for copy in copies:
        copy.wait()
    total = dot32(attn[...], w_out_of(held)) + vecs[5:6, :]
    for j in range(4):
        total = total + dot32(hidden[:, D * j : D * (j + 1)], w_out2_of(held, j))
    output[...] = tokens[...].astype(jnp.float32) + (total + vecs[12:13, :])
    vec_out[2:5, :] = low_sums[0:3, :]
    vec_out[8:12, :] = high_sums[0:4, :]
    gy = grad_y[...].astype(jnp.float32)
    total = gy
    for norm, (parts, width, weights) in enumerate(
        ((grad_mixed, 3, w_qkv_of), (grad_pre, 4, w_in_of))
    ):
        back = None
        for j in range(width):
            part = dot32(weights(held, j), parts[:, D * j : D * (j + 1)].T)
            back = part if back is None else back + part
        grad_act = back.T
        gain_row = 0 if norm == 0 else 6
        unit = normed[...]
        vec_out[gain_row : gain_row + 1, :] = jnp.sum(grad_act * unit, axis=0, keepdims=True)
        vec_out[gain_row + 1 : gain_row + 2, :] = jnp.sum(grad_act, axis=0, keepdims=True)
        grad_norm = grad_act * vecs[gain_row : gain_row + 1, :]
        total = total + spread[:, 0:1] * (
            grad_norm
            - jnp.mean(grad_norm, axis=1, keepdims=True)
            - unit * jnp.mean(grad_norm * unit, axis=1, keepdims=True)
        )
    grad_input[...] = total
    bottom = jnp.sum(gy, axis=0, keepdims=True)
    vec_out[5:6, :] = bottom
    vec_out[12:13, :] = bottom
    vec_out[13:16, :] = jnp.zeros((3, D), jnp.float32)
    vec_out[...] = vec_out[...].astype(jnp.bfloat16).astype(jnp.float32)


def layer_results(matrices, small):
    hbm = pl.BlockSpec(memory_space=pl.ANY)
    vmem = pl.BlockSpec(memory_space=pltpu.VMEM)
    rows = jax.ShapeDtypeStruct((TOK_DEV, D), jnp.float32)
    return pl.pallas_call(
        result_kernel,
        in_specs=[hbm] + [vmem] * len(small),
        out_specs=[vmem] * 3,
        scratch_shapes=[
            pltpu.VMEM((ALL_ROWS, D), jnp.bfloat16),
            pltpu.SemaphoreType.DMA((SHARDS,)),
        ],
        out_shape=[rows, rows, jax.ShapeDtypeStruct((16, D), jnp.float32)],
        compiler_params=pltpu.CompilerParams(vmem_limit_bytes=20 * 2**20),
        cost_estimate=pl.CostEstimate(
            flops=4 * 10**9, bytes_accessed=30 * 2**20, transcendentals=0
        ),
    )(matrices, *small)


SHARE = FLAT_ROWS // REPS
BEGINS = tuple(SHARE * r // 16 * 16 for r in range(REPS)) + (FLAT_ROWS,)
SHARE_ROWS = 1760
STEP = 576


def align_kernel(where, one_ref, two_ref, out_ref, held):
    for r in range(REPS):

        @pl.when(where[0] == r)
        def _(r=r):
            lead = SHARE * r - BEGINS[r]
            for turn, ref in enumerate((one_ref, two_ref)):
                held[0:16, :] = jnp.zeros((16, LANES), jnp.float32)
                held[SHARE_ROWS - 32 :, :] = jnp.zeros((32, LANES), jnp.float32)
                held[lead : lead + SHARE, :] = ref[...]
                out_ref[turn] = held[...].astype(jnp.bfloat16)


def align_moments(moment_one, moment_two, rep):
    return pl.pallas_call(
        align_kernel,
        grid_spec=pltpu.PrefetchScalarGridSpec(
            num_scalar_prefetch=1,
            in_specs=[pl.BlockSpec(memory_space=pltpu.VMEM)] * 2,
            out_specs=pl.BlockSpec(memory_space=pltpu.VMEM),
            scratch_shapes=[pltpu.VMEM((SHARE_ROWS, LANES), jnp.float32)],
        ),
        out_shape=jax.ShapeDtypeStruct((2, SHARE_ROWS, LANES), jnp.bfloat16),
        compiler_params=pltpu.CompilerParams(vmem_limit_bytes=16 * 2**20),
    )(jnp.stack([rep]), moment_one.reshape(SHARE, LANES), moment_two.reshape(SHARE, LANES))


def update_kernel(factor, where, *refs):
    blocks = refs[:REPS]
    moments = refs[REPS : 2 * REPS]
    vec_ref, params, grad_out, params_out = refs[2 * REPS : 2 * REPS + 4]
    held, grad, weight, moment, sems, out_sems = refs[2 * REPS + 4 :]
    copies = []
    for turn in range(REPS):
        copies.append(
            pltpu.make_async_copy(blocks[turn], held.at[where[1 + turn]], sems.at[turn])
        )
    fetched = []
    for r in range(REPS):
        rows = pl.ds(BEGINS[r], BEGINS[r + 1] - BEGINS[r])
        fetched.append(
            pltpu.make_async_copy(params.at[rows], weight.at[rows], sems.at[REPS + r])
        )
    for turn in range(REPS):
        which = where[1 + turn]
        copies.append(
            pltpu.make_async_copy(
                moments[turn], moment.at[which], sems.at[2 * REPS + which]
            )
        )
    for copy in copies + fetched:
        copy.start()
    for copy in copies[:REPS]:
        copy.wait()
    shard = where[0]
    for z in range(SHARDS):

        @pl.when(shard == z)
        def _(z=z):
            for slot, row in enumerate(VECTOR_ROWS[z]):
                for col in range(6):
                    grad[6 * row + col : 6 * row + col + 1, :] = (
                        vec_ref[slot : slot + 1, LANES * col : LANES * (col + 1)] * factor
                    )

            @pl.loop(0, REPS)
            def _(rep):
                for first, step, rows, blocks, place in PARTS[z]:
                    for block in range(blocks):
                        for col in range(6):
                            got = held[
                                rep,
                                place + rows * block : place + rows * (block + 1),
                                LANES * col : LANES * (col + 1),
                            ]
                            begin = first + step * rep + 6 * block + col
                            grad[pl.ds(begin, rows, stride=6 * blocks), :] = (
                                got.astype(jnp.float32) * factor
                            )

    saving = []
    for r in range(REPS):
        rows = pl.ds(BEGINS[r], BEGINS[r + 1] - BEGINS[r])
        saving.append(
            pltpu.make_async_copy(grad.at[rows], grad_out.at[rows], out_sems.at[REPS + r])
        )
        saving[-1].start()
    for r in range(REPS):
        base = BEGINS[r]
        length = BEGINS[r + 1] - base
        pltpu.make_async_copy(moments[0], moment.at[r], sems.at[2 * REPS + r]).wait()
        fetched[r].wait()
        if r > 0:
            tail = base - BEGINS[r - 1]
            moment[r, :, 0:16, :] = moment[r, :, 0:16, :] + moment[r - 1, :, tail : tail + 16, :]

        def renew(at, rows, r=r, base=base):
            here = pl.ds(pl.multiple_of(base + at, 8), rows)
            there = pl.ds(pl.multiple_of(at, 16), rows)
            updated, _, _ = adam_update(
                weight[here, :],
                moment[r, 0, there, :].astype(jnp.float32),
                moment[r, 1, there, :].astype(jnp.float32),
                grad[here, :],
            )
            weight[here, :] = updated

        @pl.loop(0, length // STEP)
        def _(turn):
            renew(turn * STEP, STEP)

        if length % STEP:
            renew(length // STEP * STEP, length % STEP)
        rows = pl.ds(base, length)
        saving.append(
            pltpu.make_async_copy(weight.at[rows], params_out.at[rows], out_sems.at[r])
        )
        saving[-1].start()
    for copy in saving:
        copy.wait()


def update_shard(blocks, ids, vectors, params, moments, shard, factor):
    anywhere = pl.BlockSpec(memory_space=pl.ANY)
    flat = jax.ShapeDtypeStruct((FLAT_ROWS, LANES), jnp.float32)
    return pl.pallas_call(
        functools.partial(update_kernel, factor),
        grid_spec=pltpu.PrefetchScalarGridSpec(
            num_scalar_prefetch=1,
            in_specs=[anywhere] * (2 * REPS)
            + [pl.BlockSpec(memory_space=pltpu.VMEM), anywhere],
            out_specs=[anywhere] * 2,
            scratch_shapes=[
                pltpu.VMEM((REPS, PIECE, D), jnp.bfloat16),
                pltpu.VMEM((FLAT_ROWS, LANES), jnp.float32),
                pltpu.VMEM((FLAT_ROWS, LANES), jnp.float32),
                pltpu.VMEM((REPS, 2, SHARE_ROWS, LANES), jnp.bfloat16),
                pltpu.SemaphoreType.DMA((3 * REPS,)),
                pltpu.SemaphoreType.DMA((2 * REPS,)),
            ],
        ),
        out_shape=[flat, flat],
        compiler_params=pltpu.CompilerParams(vmem_limit_bytes=60 * 2**20),
    )(jnp.stack([shard] + ids), *blocks, *moments, vectors, params.reshape(FLAT_ROWS, LANES))


def ring_shift(value, hop):
    return lax.ppermute(value, "z", [(i, (i + hop) % SHARDS) for i in range(SHARDS)])


fence = lax.optimization_barrier


def gather_matrices(params, shard, rep, early):
    piece = pack_pieces(params, shard, [rep], False)[0][0]
    own, vec = pack_pieces(params, shard, [rep * 0 + turn for turn in range(REPS)], True)
    one = ring_step(piece)
    one, own, vec = fence((one, own, vec))
    two, first_one, second_one = ring_step(one), first_cross(one), second_cross(one)
    vec_one = ring_step(vec)
    two, first_one, second_one, vec_one, early = fence(
        (two, first_one, second_one, vec_one, early)
    )
    three, first_two, second_two = ring_step(two), first_cross(two), second_cross(two)
    both_one = second_cross(first_one)
    vec_two = ring_step(vec_one)
    three, first_two, second_two, both_one, vec_two = fence(
        (three, first_two, second_two, both_one, vec_two)
    )
    first_three, second_three = first_cross(three), second_cross(three)
    both_two = second_cross(first_two)
    mine_one = jnp.stack([one, first_one, second_one, both_one])
    other_one = core_cross(mine_one)
    vec_three = ring_step(vec_two)
    first_three, second_three, both_two, other_one, vec_three = fence(
        (first_three, second_three, both_two, other_one, vec_three)
    )
    both_three = second_cross(first_three)
    mine_two = jnp.stack([two, first_two, second_two, both_two])
    other_two = core_cross(mine_two)
    others = [core_cross(value) for value in (three, first_three, second_three)]
    others, both_three, other_two = fence((others, both_three, other_two))
    others.append(core_cross(both_three))
    threes = [three, first_three, second_three, both_three]
    blocks = [mine_one, other_one, mine_two, other_two] + threes + others
    ids = []
    for hop in range(1, SHARDS):
        owner = (shard + SHARDS - hop) % SHARDS
        ids += [owner * REPS + which for which in spread_ids(rep)]
    hops = [vec, vec_one, vec_two, vec_three]
    return blocks, own.reshape(REPS * PIECE, D), ids, hops, early


def slots_by_piece(shard, rep):
    slots = []
    for owner in range(SHARDS):
        hop = (shard + SHARDS - owner + 3) % SHARDS
        for which in range(REPS):
            apart = rep ^ which
            kept = 1 - apart % 2
            core = which % 2
            across = apart & 6
            first = 2 + 2 * core
            place = jnp.where(
                across == 0, 2, jnp.where(across == 6, 1, jnp.where(across == first, 0, 3))
            )
            slots.append((kept * SHARDS + hop) * 4 + place)
    return slots


def scatter_sums(parts, moments, small, results):
    sent_far, sent_near, kept_far, kept_near = (
        [parts[8 * half + 2 * turn + near] for turn in range(SHARDS)]
        for half in range(2)
        for near in range(2)
    )
    cores = [core_cross(sent_far[0]), core_cross(sent_near[0]), core_cross(sent_far[1])]
    cores = list(fence(cores))
    far = [kept_far[0] + cores[0], kept_far[1] + cores[2]]
    crossed = first_cross(far[0])
    others = [core_cross(v) for v in (sent_near[1], sent_far[2], sent_near[2], sent_far[3])]
    crossed, others, small = fence((crossed, others, small))
    near = [kept_near[0] + cores[1], kept_near[1] + others[0], kept_near[2] + others[2]]
    far += [kept_far[2] + others[1], kept_far[3] + others[3]]

    pair = near[0] + crossed
    final = second_cross(pair[1])
    kept = pair[0]
    crossed = first_cross(far[1])
    last_near = core_cross(sent_near[3])
    output, grad_input, vectors = results(small)
    final, crossed, last_near, vectors = fence((final, crossed, last_near, vectors))
    near.append(kept_near[3] + last_near)

    carried = None
    for turn in range(1, SHARDS):
        total = kept + final
        if carried is not None:
            total = total + carried
        carried = ring_step(total)
        pair = near[turn] + crossed
        kept = pair[0]
        final = second_cross(pair[1])
        met = plane_permute(vectors, ((1, 1), (2, 2), (4, 4))[turn - 1])
        if turn < SHARDS - 1:
            crossed = first_cross(far[turn + 1])
            final, crossed, carried, met, moments = fence(
                (final, crossed, carried, met, moments)
            )
        else:
            final, carried, met = fence((final, carried, met))
        if turn > 1:
            moments.append(core_cross(moments[turn]))
        vectors = vectors + met
    total = kept + final + carried

    first, second = first_cross(total), second_cross(total)
    shifted = [ring_shift(vectors, hop) for hop in range(1, SHARDS)]
    first, second, shifted = fence((first, second, shifted))
    vectors = vectors + shifted[0] + shifted[1] + shifted[2]
    both = second_cross(first)
    mine = [total, first, second]
    spread = [core_cross(value) for value in mine]
    both, spread = fence((both, spread))
    spread.append(core_cross(both))
    return mine + [both] + spread, moments, output, grad_input, vectors


def on_device_rows(tokens, segment_ids, cotangent, params, moment_one, moment_two):
    shard = lax.axis_index("z")
    rep = lax.axis_index(PLANE)
    early = (prepare(tokens, cotangent, segment_ids), align_moments(moment_one, moment_two, rep))
    blocks, own, ids, hops, early = gather_matrices(params, shard, rep, early)
    (normed, inv_std, grad_y, tables), moments = early
    moments, blocks = fence((moments, blocks))
    first_moments = first_cross(moments)
    small = (normed, grad_y, tables, *hops)
    matrices, *attended = attention(jnp.stack([shard] + ids), blocks, own, small)
    moments, first_moments, attended = fence((moments, first_moments, attended))
    moments = [moments, first_moments, second_cross(moments), second_cross(first_moments)]
    moments += [core_cross(value) for value in moments[:2]]
    attn, mixed, low_sums, vecs = attended
    made = weight_gradients(
        jnp.stack(slots_by_piece(shard, rep) + [shard]), matrices, (normed, grad_y, attn, mixed, vecs)
    )
    made, moments = fence((made, moments))
    small = (tokens, normed, inv_std, grad_y, attn, mixed, low_sums, vecs) + tuple(made[16:])
    spread, moments, output, grad_input, vec_grads = scatter_sums(
        [part.reshape(2, PIECE, D) for part in made[:16]], moments, small, lambda small: layer_results(matrices, small)
    )
    own_vectors = lax.dynamic_index_in_dim(
        vec_grads.reshape(SHARDS, 4, D), shard, 0, keepdims=False
    )
    tokens_all = tokens.shape[0] * lax.axis_size(EVERY)
    grad_params, new_params = update_shard(
        spread,
        spread_ids(rep),
        own_vectors,
        params,
        moments,
        shard,
        1.0 / math.sqrt(tokens_all),
    )
    grad_params = grad_params.reshape(-1)
    width = moment_one.shape[0]
    grad_share = lax.dynamic_slice_in_dim(grad_params, rep * width, width)
    _, upd_first, upd_second = adam_update(moment_one, moment_one, moment_two, grad_share)
    return (output, grad_input, grad_params, new_params.reshape(-1), upd_first, upd_second)


def solution(mesh):
    in_rows = mesh.shape["rep"] == REPS and mesh.shape["shard"] == SHARDS
    if in_rows:
        rep, shard = PLANE, "z"
        mesh = Mesh(mesh.devices.reshape(2, 2, 2, SHARDS), EVERY)
        body = on_device_rows
    else:
        rep, shard = ("rep",), "shard"
        body = on_device
    rows = rep + (shard,)
    owner = (shard,) + rep
    in_specs = (P(rows, None), P(rows), P(rows, None), P(shard), P(owner), P(owner))
    out_specs = (P(rows, None), P(rows, None), P(shard), P(shard), P(owner), P(owner))
    return jax.shard_map(body, mesh=mesh, in_specs=in_specs, out_specs=out_specs, check_vma=False)
```

```python
import functools
import math

import jax
import jax.numpy as jnp
from jax import lax
from jax.experimental import pallas as pl
from jax.experimental.pallas import tpu as pltpu
from jax.sharding import Mesh
from jax.sharding import PartitionSpec as P

D = 768
HEADS = 12
HD = 64
ROT = 16
FF = 3072
TOK_DEV = 128


EPS_NORM = 1e-05
ROPE_BASE = 10000.0
NEG_BIG = -1e30
BETA_ONE = 0.9
BETA_TWO = 0.95
ADAM_STEP = 3.0
LEARN_RATE = 0.05
DECAY = 0.01
ADAM_EPS = 1e-08
INV_ROOT_TWO = 0.7071067811865476
INV_ROOT_TWO_PI = 0.3989422804014327


def layout_offsets():
    q_width = HEADS * HD
    o_wqkv = 2 * D
    o_bqkv = o_wqkv + 3 * q_width * D
    o_wout = o_bqkv + 3 * q_width
    o_bout = o_wout + q_width * D
    o_gain2 = o_bout + D
    o_shift2 = o_gain2 + D
    o_win = o_shift2 + D
    o_bin = o_win + D * FF
    o_wout2 = o_bin + FF
    o_bout2 = o_wout2 + FF * D
    return (
        o_wqkv,
        o_bqkv,
        o_wout,
        o_bout,
        o_gain2,
        o_shift2,
        o_win,
        o_bin,
        o_wout2,
        o_bout2,
        o_bout2 + D,
    )


def split_params(flat16):
    q_width = HEADS * HD
    o_wqkv, o_bqkv, o_wout, o_bout, o_gain2, o_shift2, o_win, o_bin, o_wout2, o_bout2, o_end = (
        layout_offsets()
    )
    return (
        flat16[0:D],
        flat16[D:o_wqkv],
        flat16[o_wqkv:o_bqkv].reshape(D, 3 * q_width),
        flat16[o_bqkv:o_wout],
        flat16[o_wout:o_bout].reshape(q_width, D),
        flat16[o_bout:o_gain2],
        flat16[o_gain2:o_shift2],
        flat16[o_shift2:o_win],
        flat16[o_win:o_bin].reshape(D, FF),
        flat16[o_bin:o_wout2],
        flat16[o_wout2:o_bout2].reshape(FF, D),
        flat16[o_bout2:o_end],
    )


def positions_of(segments):
    count = segments.shape[0]
    slot_ids = jnp.arange(count, dtype=jnp.int32)
    before = jnp.concatenate([jnp.full((1,), -2, jnp.int32), segments[:-1]])
    begins = segments != before
    first_slot = lax.cummax(jnp.where(begins, slot_ids, 0), axis=0)
    return slot_ids - first_slot


def rotary_tables(positions):
    half = ROT // 2
    steps_j = jnp.arange(half, dtype=jnp.float32)
    freqs = jnp.power(jnp.float32(ROPE_BASE), -2.0 * steps_j / ROT)
    angle = positions.astype(jnp.float32)[:, None] * freqs[None, :]
    return (jnp.cos(angle)[:, None, :], jnp.sin(angle)[:, None, :])


def rotate(values, cosine, sine, sign):
    half = cosine.shape[-1]
    lower = values[..., :half]
    upper = values[..., half : 2 * half]
    rest = values[..., 2 * half :]
    return jnp.concatenate(
        [lower * cosine - sign * upper * sine, upper * cosine + sign * lower * sine, rest], axis=-1
    )


def gelu_exact(value):
    return value * 0.5 * (1.0 + lax.erf(value * INV_ROOT_TWO))


def gelu_slope(value):
    return (
        0.5 * (1.0 + lax.erf(value * INV_ROOT_TWO))
        + value * jnp.exp(-0.5 * value * value) * INV_ROOT_TWO_PI
    )


def masked_scores(q_blk, keys, seg_rows, seg_cols, begin_row):
    scale = q_blk.shape[-1] ** (-0.5)
    raw_scores = jnp.einsum("qhd,khd->hqk", q_blk, keys, preferred_element_type=jnp.float32) * scale
    row_ids = begin_row + jnp.arange(q_blk.shape[0], dtype=jnp.int32)
    col_ids = jnp.arange(keys.shape[0], dtype=jnp.int32)
    allowed = (seg_rows[:, None] == seg_cols[None, :]) & (col_ids[None, :] <= row_ids[:, None])
    return jnp.where(allowed[None], raw_scores, NEG_BIG)


def attend_forward(query16, key16, value16, segments):
    scores = masked_scores(query16, key16, segments, segments, 0)
    row_max = jnp.max(scores, axis=-1, keepdims=True)
    expd = jnp.exp(scores - row_max)
    row_total = jnp.sum(expd, axis=-1, keepdims=True)
    probs16 = (expd / row_total).astype(jnp.bfloat16)
    attn_blk = jnp.einsum("hqk,khd->qhd", probs16, value16, preferred_element_type=jnp.float32)
    pieces_out = attn_blk.astype(jnp.bfloat16)
    lse_list = [row_max + jnp.log(row_total)]
    return (pieces_out, lse_list)


def attend_backward(query16, key16, value16, attn16, lse_list, segments, grad_attn16):
    count = query16.shape[0]
    block = min(512, count)
    scale = query16.shape[-1] ** (-0.5)
    grad_query = []
    grad_key = jnp.zeros(key16.shape, jnp.float32)
    grad_value = jnp.zeros(value16.shape, jnp.float32)
    for turn, begin_row in enumerate(range(0, count, block)):
        stop_row = begin_row + block
        scores = masked_scores(query16, key16, segments, segments, begin_row)
        chances = jnp.exp(scores - lse_list[turn])
        chances16 = chances.astype(jnp.bfloat16)
        grad_value = grad_value.at[:stop_row].add(
            jnp.einsum("hqk,qhd->khd", chances16, grad_attn16, preferred_element_type=jnp.float32)
        )
        grad_chance = jnp.einsum(
            "qhd,khd->hqk", grad_attn16, value16, preferred_element_type=jnp.float32
        )
        delta = jnp.sum(grad_attn16.astype(jnp.float32) * attn16.astype(jnp.float32), axis=-1)
        grad_scores = (chances * (grad_chance - jnp.transpose(delta)[:, :, None]) * scale).astype(
            jnp.bfloat16
        )
        grad_query.append(
            jnp.einsum("hqk,khd->qhd", grad_scores, key16, preferred_element_type=jnp.float32)
        )
        grad_key = grad_key.at[:stop_row].add(
            jnp.einsum("hqk,qhd->khd", grad_scores, query16, preferred_element_type=jnp.float32)
        )
    return (grad_query[0], grad_key, grad_value)


def norm_back(grad_act, normed, inv_std, gain):
    grad_gain = jnp.sum(grad_act * normed, axis=0)
    grad_shift = jnp.sum(grad_act, axis=0)
    grad_norm = grad_act * gain.astype(jnp.float32)
    grad_x = inv_std * (
        grad_norm
        - jnp.mean(grad_norm, axis=1, keepdims=True)
        - normed * jnp.mean(grad_norm * normed, axis=1, keepdims=True)
    )
    return (grad_gain, grad_shift, grad_x)


def layer_forward(tokens, segments, pieces):
    (
        gain_one,
        shift_one,
        w_qkv,
        b_qkv,
        w_out,
        b_out,
        gain_two,
        shift_two,
        w_in,
        b_in,
        w_out2,
        b_out2,
    ) = pieces
    count = tokens.shape[0]
    x_wide = tokens.astype(jnp.float32)
    row_mean = jnp.mean(x_wide, axis=1, keepdims=True)
    centered = x_wide - row_mean
    variance = jnp.mean(centered * centered, axis=1, keepdims=True)
    inv_std = lax.rsqrt(variance + EPS_NORM)
    normed = centered * inv_std
    act_one = (normed * gain_one.astype(jnp.float32) + shift_one.astype(jnp.float32)).astype(
        jnp.bfloat16
    )
    act_two = (normed * gain_two.astype(jnp.float32) + shift_two.astype(jnp.float32)).astype(
        jnp.bfloat16
    )
    mixed = jnp.dot(act_one, w_qkv, preferred_element_type=jnp.float32) + b_qkv.astype(jnp.float32)
    mixed = mixed.reshape(count, 3, HEADS, HD)
    cosine, sine = rotary_tables(positions_of(segments))
    query16 = rotate(mixed[:, 0], cosine, sine, 1.0).astype(jnp.bfloat16)
    key16 = rotate(mixed[:, 1], cosine, sine, 1.0).astype(jnp.bfloat16)
    value16 = mixed[:, 2].astype(jnp.bfloat16)
    attn16, lse_list = attend_forward(query16, key16, value16, segments)
    proj = jnp.dot(
        attn16.reshape(count, HEADS * HD), w_out, preferred_element_type=jnp.float32
    ) + b_out.astype(jnp.float32)
    pre = jnp.dot(act_two, w_in, preferred_element_type=jnp.float32) + b_in.astype(jnp.float32)
    hidden16 = gelu_exact(pre).astype(jnp.bfloat16)
    feed = jnp.dot(hidden16, w_out2, preferred_element_type=jnp.float32) + b_out2.astype(
        jnp.float32
    )
    output = x_wide + proj + feed
    saved = (
        normed,
        inv_std,
        act_one,
        act_two,
        query16,
        key16,
        value16,
        attn16,
        lse_list,
        cosine,
        sine,
        pre,
        hidden16,
    )
    return (output, saved)


def layer_backward(cotangent, segments, pieces, saved):
    (
        gain_one,
        shift_one,
        w_qkv,
        b_qkv,
        w_out,
        b_out,
        gain_two,
        shift_two,
        w_in,
        b_in,
        w_out2,
        b_out2,
    ) = pieces
    (
        normed,
        inv_std,
        act_one,
        act_two,
        query16,
        key16,
        value16,
        attn16,
        lse_list,
        cosine,
        sine,
        pre,
        hidden16,
    ) = saved
    count = cotangent.shape[0]
    contract_rows = (((0,), (0,)), ((), ()))
    contract_cols = (((1,), (1,)), ((), ()))
    live_rows = (segments >= 0).astype(jnp.float32)[:, None]
    grad_y = cotangent.astype(jnp.float32) * live_rows
    grad_y16 = grad_y.astype(jnp.bfloat16)
    grad_b_out = jnp.sum(grad_y, axis=0)
    attn_flat = attn16.reshape(count, HEADS * HD)
    grad_w_out = lax.dot_general(
        attn_flat, grad_y16, contract_rows, preferred_element_type=jnp.float32
    )
    grad_w_out2 = lax.dot_general(
        hidden16, grad_y16, contract_rows, preferred_element_type=jnp.float32
    )
    grad_hidden = lax.dot_general(
        grad_y16, w_out2, contract_cols, preferred_element_type=jnp.float32
    )
    grad_pre = grad_hidden * gelu_slope(pre)
    grad_b_in = jnp.sum(grad_pre, axis=0)
    grad_pre16 = grad_pre.astype(jnp.bfloat16)
    grad_w_in = lax.dot_general(
        act_two, grad_pre16, contract_rows, preferred_element_type=jnp.float32
    )
    grad_act_two = lax.dot_general(
        grad_pre16, w_in, contract_cols, preferred_element_type=jnp.float32
    )
    grad_attn16 = (
        lax.dot_general(grad_y16, w_out, contract_cols, preferred_element_type=jnp.float32)
        .astype(jnp.bfloat16)
        .reshape(count, HEADS, HD)
    )
    grad_query, grad_key, grad_value = attend_backward(
        query16, key16, value16, attn16, lse_list, segments, grad_attn16
    )
    grad_query = rotate(grad_query, cosine, sine, -1.0)
    grad_key = rotate(grad_key, cosine, sine, -1.0)
    grad_mixed = jnp.stack([grad_query, grad_key, grad_value], axis=1).reshape(
        count, 3 * HEADS * HD
    )
    grad_b_qkv = jnp.sum(grad_mixed, axis=0)
    grad_mixed16 = grad_mixed.astype(jnp.bfloat16)
    grad_w_qkv = lax.dot_general(
        act_one, grad_mixed16, contract_rows, preferred_element_type=jnp.float32
    )
    grad_act_one = lax.dot_general(
        grad_mixed16, w_qkv, contract_cols, preferred_element_type=jnp.float32
    )
    gain_grad_one, shift_grad_one, grad_x_one = norm_back(grad_act_one, normed, inv_std, gain_one)
    gain_grad_two, shift_grad_two, grad_x_two = norm_back(grad_act_two, normed, inv_std, gain_two)
    grad_in = grad_y + grad_x_one + grad_x_two
    return (
        grad_in,
        [
            gain_grad_one,
            shift_grad_one,
            grad_w_qkv,
            grad_b_qkv,
            grad_w_out,
            grad_b_out,
            gain_grad_two,
            shift_grad_two,
            grad_w_in,
            grad_b_in,
            grad_w_out2,
            grad_b_out,
        ],
    )


def flatten_grads(parts, total_len):
    used = layout_offsets()[-1]
    rounded = [part.astype(jnp.bfloat16).reshape(-1) for part in parts]
    return jnp.concatenate(rounded + [jnp.zeros((total_len - used,), jnp.bfloat16)])


def adam_update(weights, first_moment, second_moment, gradient):
    new_first = BETA_ONE * first_moment + (1.0 - BETA_ONE) * gradient
    new_second = BETA_TWO * second_moment + (1.0 - BETA_TWO) * gradient * gradient
    unbiased_first = new_first / (1.0 - BETA_ONE**ADAM_STEP)
    unbiased_second = new_second / (1.0 - BETA_TWO**ADAM_STEP)
    new_weights = weights - LEARN_RATE * (
        unbiased_first / (jnp.sqrt(unbiased_second) + ADAM_EPS) + DECAY * weights
    )
    return (new_weights, new_first, new_second)


def on_device(tokens, segment_ids, cotangent, params, moment_one, moment_two):
    gathered = lax.all_gather(params.astype(jnp.bfloat16), "shard", axis=0, tiled=True)
    total_len = gathered.shape[0]
    pieces = split_params(gathered)
    output, saved = layer_forward(tokens, segment_ids, pieces)
    grad_input, parts = layer_backward(cotangent, segment_ids, pieces, saved)
    local_grad = flatten_grads(parts, total_len)
    owned = lax.psum_scatter(local_grad, "shard", scatter_dimension=0, tiled=True).astype(
        jnp.float32
    )
    tokens_all = tokens.shape[0] * lax.axis_size("rep") * lax.axis_size("shard")
    factor = 1.0 / math.sqrt(tokens_all)
    width = moment_one.shape[0]
    begin = lax.axis_index("rep") * width
    param_share = lax.dynamic_slice_in_dim(params, begin, width)
    share = lax.psum_scatter(owned, "rep", scatter_dimension=0, tiled=True)
    grad_share = share * factor
    upd_params, upd_first, upd_second = adam_update(param_share, moment_one, moment_two, grad_share)
    grad_params, new_params = (
        lax.all_gather(grad_share, "rep", axis=0, tiled=True),
        lax.all_gather(upd_params, "rep", axis=0, tiled=True),
    )
    return (output, grad_input, grad_params, new_params, upd_first, upd_second)


LANES = 128
REPS = 8
SHARDS = 4
PIECE = 288
FLAT_ROWS = 13848
MOVED = PIECE * D // LANES


PARTS = (
    ((12, 1728, 96, 3, 0),),
    ((6, 576, 96, 1, 0), (4632, 1152, 48, 4, 96)),
    ((0, 1152, 48, 4, 0), (9240, 576, 96, 1, 192)),
    ((0, 1728, 288, 1, 0),),
)
VECTOR_ROWS = ((0, 1, 2306, 2307), (0, 769, 770, 771), (1536, 1537, 1538, 1539), (2304, 2305, 2306, 2307))


PLANE = ("y", "x", "core")
EVERY = PLANE + ("z",)
HOPS = (1, 2, 3, 0)


def plane_permute(value, flips):
    return lax.ppermute(value, PLANE, [(i, i ^ flips[i % 2]) for i in range(REPS)])


def first_cross(value):
    return plane_permute(value, (2, 4))


def second_cross(value):
    return plane_permute(value, (4, 2))


def core_cross(value):
    return plane_permute(value, (1, 1))


def ring_step(value):
    return lax.ppermute(value, "z", [(i, (i + 1) % SHARDS) for i in range(SHARDS)])


def flips_of(rep):
    core = rep % 2
    first = 2 + 2 * core
    return (0, first, 6 - first, 6)


def spread_ids(rep):
    other = rep ^ 1
    return [rep ^ flip for flip in flips_of(rep)] + [other ^ flip for flip in flips_of(other)]


def window_of(row):
    return min(6 * row // 8 * 8, FLAT_ROWS - 16)


def pack_kernel(where, flat_ref, out_ref, *rest):
    vec_ref = rest[0] if len(rest) == 4 else None
    held, windows, sems = rest[-3:]
    shard = where[0]
    turns = out_ref.shape[0]
    for z in range(SHARDS):

        @pl.when(shard == z)
        def _(z=z):
            def copies_of(turn):
                slot = turn % 2
                rep = where[1 + turn]
                copies = []
                at = 0
                for part, (first, step, _, _, _) in enumerate(PARTS[z]):
                    lead = first % 8
                    count = step + (8 if lead else 0)
                    begin = pl.multiple_of(first - lead + step * rep, 8)
                    copies.append(
                        pltpu.make_async_copy(
                            flat_ref.at[pl.ds(begin, count)],
                            held.at[slot, pl.ds(at, count)],
                            sems.at[slot, part],
                        )
                    )
                    at += count
                return copies

            for copy in copies_of(0):
                copy.start()
            if vec_ref is not None:
                cuts = []
                for slot, row in enumerate(VECTOR_ROWS[z]):
                    cuts.append(
                        pltpu.make_async_copy(
                            flat_ref.at[pl.ds(window_of(row), 16)],
                            windows.at[slot],
                            sems.at[2 + slot // 2, slot % 2],
                        )
                    )
                    cuts[-1].start()
                vec_ref[...] = jnp.zeros_like(vec_ref)
                for slot, row in enumerate(VECTOR_ROWS[z]):
                    cuts[slot].wait()
                    lead = 6 * row - window_of(row)
                    for col in range(6):
                        got = windows[slot, lead + col : lead + col + 1, :]
                        vec_ref[slot : slot + 1, LANES * col : LANES * (col + 1)] = got.astype(
                            jnp.bfloat16
                        ).astype(jnp.float32)

            @pl.loop(0, turns)
            def _(turn):
                @pl.when(turn + 1 < turns)
                def _():
                    for copy in copies_of(turn + 1):
                        copy.start()

                slot = turn % 2
                at = 0
                for copy, (first, step, rows, blocks, place) in zip(copies_of(turn), PARTS[z]):
                    copy.wait()
                    lead = first % 8
                    for block in range(blocks):
                        for col in range(6):
                            begin = at + lead + 6 * block + col
                            got = held[slot, pl.ds(begin, rows, stride=6 * blocks), :]
                            out_ref[
                                turn,
                                place + rows * block : place + rows * (block + 1),
                                LANES * col : LANES * (col + 1),
                            ] = got.astype(jnp.bfloat16)
                    at += step + (8 if lead else 0)


def pack_pieces(params, shard, reps, vectors):
    pieces = jax.ShapeDtypeStruct((len(reps), PIECE, D), jnp.bfloat16)
    rows = jax.ShapeDtypeStruct((8, D), jnp.float32)
    vmem = pl.BlockSpec(memory_space=pltpu.VMEM)
    return pl.pallas_call(
        pack_kernel,
        grid_spec=pltpu.PrefetchScalarGridSpec(
            num_scalar_prefetch=1,
            in_specs=[pl.BlockSpec(memory_space=pltpu.HBM)],
            out_specs=[vmem, vmem] if vectors else [vmem],
            scratch_shapes=[
                pltpu.VMEM((2, MOVED + 16, LANES), jnp.float32),
                pltpu.VMEM((4, 16, LANES), jnp.float32),
                pltpu.SemaphoreType.DMA((4, 2)),
            ],
        ),
        out_shape=[pieces, rows] if vectors else [pieces],
        cost_estimate=pl.CostEstimate(
            flops=0, bytes_accessed=len(reps) * 3 * 2**20, transcendentals=0
        ),
        compiler_params=pltpu.CompilerParams(vmem_limit_bytes=56 * 2**20),
    )(jnp.stack([shard] + reps), params.reshape(FLAT_ROWS, LANES))


def prepare_kernel(tokens, cotangent, ids, freqs, normed, spread, grad_y, tables):
    x_wide = tokens[...].astype(jnp.float32)
    centered = x_wide - jnp.mean(x_wide, axis=1, keepdims=True)
    variance = jnp.mean(centered * centered, axis=1, keepdims=True)
    inv_std = lax.rsqrt(variance + EPS_NORM)
    normed[...] = centered * inv_std
    spread[...] = jnp.broadcast_to(inv_std, spread.shape)
    square = (TOK_DEV, TOK_DEV)
    across = jnp.broadcast_to(ids[...].astype(jnp.float32), square)
    down = across.T
    lane = lax.broadcasted_iota(jnp.int32, square, 1)
    row = lax.broadcasted_iota(jnp.int32, square, 0)
    begins = (across != pltpu.roll(across, 1, 1)) | (lane == 0)
    before = jnp.where(begins & (lane <= row), lane.astype(jnp.float32), 0.0)
    position = row.astype(jnp.float32) - jnp.max(before, axis=1, keepdims=True)
    angle = position * freqs[...]
    cosine, sine = jnp.cos(angle), jnp.sin(angle)
    within = lane % HD
    tables[0] = jnp.where(within < ROT, cosine, 1.0)
    tables[1] = jnp.where(within < ROT // 2, -sine, 0.0)
    tables[2] = jnp.where((within >= ROT // 2) & (within < ROT), sine, 0.0)
    tables[3] = jnp.where((across == down) & (lane <= row), 1.0, 0.0)
    cot = cotangent[...].astype(jnp.float32)
    grad_y[...] = jnp.where(down[:, 0:1] >= 0, cot, 0.0).astype(jnp.bfloat16)


def prepare(tokens, cotangent, segment_ids):
    steps = jnp.arange(LANES, dtype=jnp.int32) % (ROT // 2)
    freqs = jnp.power(jnp.float32(ROPE_BASE), -2.0 * steps.astype(jnp.float32) / ROT)
    return pl.pallas_call(
        prepare_kernel,
        out_shape=[
            jax.ShapeDtypeStruct((TOK_DEV, D), jnp.float32),
            jax.ShapeDtypeStruct((TOK_DEV, LANES), jnp.float32),
            jax.ShapeDtypeStruct((TOK_DEV, D), jnp.bfloat16),
            jax.ShapeDtypeStruct((4, TOK_DEV, TOK_DEV), jnp.float32),
        ],
        compiler_params=pltpu.CompilerParams(vmem_limit_bytes=16 * 2**20),
    )(tokens, cotangent, segment_ids.reshape(1, TOK_DEV), freqs.reshape(1, LANES))


PIECES = SHARDS * REPS
GROUPS = 12
ALL_ROWS = PIECES * PIECE


def fetch_pieces(ids, blocks, own, shard, held, sems):
    views = []
    for block in blocks:
        views += [block.at[p] for p in range(4)] if len(block.shape) == 3 else [block]
    ids = ids + [shard * REPS + r for r in range(REPS)]
    views += [own.at[pl.ds(r * PIECE, PIECE)] for r in range(REPS)]
    for early in (True, False):
        for which, view in zip(ids, views):

            @pl.when((which < 2 * REPS) == early)
            def _(which=which, view=view):
                row = pl.multiple_of(which * PIECE, 16)
                pltpu.make_async_copy(view, held.at[pl.ds(row, PIECE)], sems.at[which]).start()

    def arrive(owner):
        for r in range(REPS):
            at = owner * REPS + r
            pltpu.make_async_copy(
                own.at[pl.ds(0, PIECE)], held.at[pl.ds(at * PIECE, PIECE)], sems.at[at]
            ).wait()

    return arrive


def rows_of(held, shard, begin, rows):
    return jnp.concatenate(
        [held[pl.ds((shard * REPS + r) * PIECE + begin, rows), :] for r in range(REPS)], axis=0
    )


def w_qkv_of(held, j):
    return rows_of(held, 0, 96 * j, 96)


def w_out_of(held):
    return rows_of(held, 1, 0, 96)


def w_in_of(held, j):
    return jnp.concatenate([rows_of(held, 1, 96 + 48 * j, 48), rows_of(held, 2, 48 * j, 48)], axis=0)


def w_out2_of(held, j):
    if j == 0:
        return rows_of(held, 2, 192, 96)
    return held[pl.ds(3 * REPS * PIECE + D * (j - 1), D), :]


def dot32(a, b):
    return jnp.dot(a, b, preferred_element_type=jnp.float32)


def layer_kernel(where, *refs):
    count = PIECES - REPS
    blocks, own = refs[:GROUPS], refs[GROUPS]
    normed, grad_y, tables = refs[GROUPS + 1 : GROUPS + 4]
    hops = refs[GROUPS + 4 : GROUPS + 8]
    outs = refs[GROUPS + 8 : GROUPS + 24]
    (attn_out, mixed_out, low_sums, vecs, hidden_out, pre_out, high_sums) = refs[
        GROUPS + 24 : GROUPS + 31
    ]
    held, grads, query, key, value, grad_attn, sems, out_sems = refs[GROUPS + 31 :]
    rot_cos, rot_up, rot_down, bias = (tables.at[turn] for turn in range(4))
    shard = where[0]
    arrive = fetch_pieces([where[1 + t] for t in range(count)], blocks, own, shard, held, sems)
    low_sums[...] = jnp.zeros_like(low_sums)
    high_sums[...] = jnp.zeros_like(high_sums)
    for owner in range(SHARDS):
        rows = jnp.zeros((4, D), jnp.float32)
        for hop in range(SHARDS):
            met = (shard + SHARDS - owner) % SHARDS == hop
            rows = jnp.where(met, hops[hop][0:4, :], rows)
        vecs[4 * owner : 4 * owner + 4, :] = rows

    arrive(0)
    act1 = (normed[...] * vecs[0:1, :] + vecs[1:2, :]).astype(jnp.bfloat16)
    for j, out in enumerate((query, key, value)):
        got = dot32(act1, w_qkv_of(held, j)) + vecs[2 + j : 3 + j, :]
        if j < 2:
            for p in range(6):
                lanes = slice(LANES * p, LANES * (p + 1))
                part = got[:, lanes]
                part = (
                    part * rot_cos[...]
                    + pltpu.roll(part, LANES - 8, 1) * rot_up[...]
                    + pltpu.roll(part, 8, 1) * rot_down[...]
                )
                out[:, lanes] = part.astype(jnp.bfloat16)
        else:
            out[...] = got.astype(jnp.bfloat16)
    gy_t = grad_y[...].T
    arrive(1)
    grad_attn[...] = dot32(w_out_of(held), gy_t).T.astype(jnp.bfloat16)

    arrive(2)
    arrive(3)
    low = lax.broadcasted_iota(jnp.int32, (LANES, LANES), 1) < HD
    scale = HD ** (-0.5)
    for p in range(6):
        lanes = slice(LANES * p, LANES * (p + 1))
        q2, k2, v2, g2 = (ref[:, lanes] for ref in (query, key, value, grad_attn))
        k2_t, v2_t = k2.T, v2.T
        attn_parts, value_parts, query_parts, key_parts = [], [], [], []
        for half in range(2):
            here = low if half == 0 else ~low
            zero = jnp.zeros_like(q2)
            scores = dot32(jnp.where(here, q2, zero), k2_t) * scale
            scores = jnp.where(bias[...] > 0.5, scores, NEG_BIG)
            expd = jnp.exp(scores - jnp.max(scores, axis=1, keepdims=True))
            chances = expd / jnp.sum(expd, axis=1, keepdims=True)
            chances16 = chances.astype(jnp.bfloat16)
            attn = dot32(chances16, v2)
            attn16 = attn.astype(jnp.bfloat16)
            masked = jnp.where(here, g2, zero)
            delta = jnp.sum(
                masked.astype(jnp.float32) * attn16.astype(jnp.float32), axis=1, keepdims=True
            )
            grad_chance = dot32(masked, v2_t)
            slope = (chances * (grad_chance - delta) * scale).astype(jnp.bfloat16)
            attn_parts.append(attn16)
            value_parts.append(dot32(chances16.T, g2))
            query_parts.append(dot32(slope, k2))
            key_parts.append(dot32(slope.T, q2))
        attn_out[:, lanes] = jnp.where(low, *attn_parts)
        for j, parts in enumerate((query_parts, key_parts, value_parts)):
            part = jnp.where(low, *parts)
            if j < 2:
                part = (
                    part * rot_cos[...]
                    - pltpu.roll(part, LANES - 8, 1) * rot_up[...]
                    - pltpu.roll(part, 8, 1) * rot_down[...]
                )
            wide = slice(D * j + LANES * p, D * j + LANES * (p + 1))
            low_sums[j : j + 1, lanes] = jnp.sum(part, axis=0, keepdims=True)
            mixed_out[:, wide] = part.astype(jnp.bfloat16)


    def send_off(owner):
        for hop in range(SHARDS):

            @pl.when((shard + SHARDS - HOPS[hop]) % SHARDS == owner)
            def _(hop=hop):
                for turn in (2 * hop, 2 * hop + 1, 8 + 2 * hop, 9 + 2 * hop):
                    pltpu.make_async_copy(
                        grads.at[pl.ds(turn * 2 * PIECE, 2 * PIECE)],
                        outs[turn],
                        out_sems.at[turn],
                    ).start()

    slot_row = lambda z, r: pl.multiple_of(where[1 + count + z * REPS + r] * PIECE, 16)

    def keep_rows(z, begin, rows, part):
        for r in range(part.shape[0] // rows):
            grads[pl.ds(slot_row(z, r) + begin, rows), :] = part[rows * r : rows * (r + 1), :]

    gy = grad_y[...]
    act1_t = (normed[...] * vecs[0:1, :] + vecs[1:2, :]).astype(jnp.bfloat16).T
    for j in range(3):
        keep_rows(
            0, 96 * j, 96, dot32(act1_t, mixed_out[:, D * j : D * (j + 1)]).astype(jnp.bfloat16)
        )
    send_off(0)
    keep_rows(1, 0, 96, dot32(attn_out[...].T, gy).astype(jnp.bfloat16))

    act2 = (normed[...] * vecs[6:7, :] + vecs[7:8, :]).astype(jnp.bfloat16)
    act2_t = act2.T
    for j in range(4):
        wide = slice(D * j, D * (j + 1))
        pre = dot32(act2, w_in_of(held, j)) + vecs[8 + j : 9 + j, :]
        bell = 0.5 * (1.0 + lax.erf(pre * INV_ROOT_TWO))
        hidden = (pre * bell).astype(jnp.bfloat16)
        hidden_out[:, wide] = hidden
        grad_hidden = dot32(w_out2_of(held, j), gy_t).T
        grad_pre = grad_hidden * (bell + pre * jnp.exp(-0.5 * pre * pre) * INV_ROOT_TWO_PI)
        high_sums[j : j + 1, :] = jnp.sum(grad_pre, axis=0, keepdims=True)
        grad_pre16 = grad_pre.astype(jnp.bfloat16)
        pre_out[:, wide] = grad_pre16
        w2 = dot32(hidden.T, gy).astype(jnp.bfloat16)
        if j == 0:
            keep_rows(2, 192, 96, w2)
        else:
            at = D * (j - 1)
            while at < D * j:
                r, begin = divmod(at, PIECE)
                rows = min(PIECE - begin, D * j - at)
                grads[pl.ds(slot_row(3, r) + begin, rows), :] = w2[
                    at - D * (j - 1) : at - D * (j - 1) + rows, :
                ]
                at += rows
    send_off(3)
    for half, owner in enumerate((1, 2)):
        side = act2_t[D // 2 * half : D // 2 * (half + 1), :]
        for j in range(4):
            w1 = dot32(side, pre_out[:, D * j : D * (j + 1)]).astype(jnp.bfloat16)
            keep_rows(owner, (96 if owner == 1 else 0) + 48 * j, 48, w1)
        send_off(owner)
    for turn, out in enumerate(outs):
        pltpu.make_async_copy(
            grads.at[pl.ds(turn * 2 * PIECE, 2 * PIECE)], out, out_sems.at[turn]
        ).wait()


def layer_gradients(scalars, blocks, own, small):
    anywhere = pl.BlockSpec(memory_space=pl.ANY)
    vmem = pl.BlockSpec(memory_space=pltpu.VMEM)
    bf16 = jnp.bfloat16
    rows = jax.ShapeDtypeStruct((8, D), jnp.float32)
    return pl.pallas_call(
        layer_kernel,
        grid_spec=pltpu.PrefetchScalarGridSpec(
            num_scalar_prefetch=1,
            in_specs=[anywhere] * (len(blocks) + 1) + [vmem] * len(small),
            out_specs=[pl.BlockSpec(memory_space=pltpu.HBM)] * 16 + [vmem] * 7,
            scratch_shapes=[
                pltpu.VMEM((ALL_ROWS, D), bf16),
                pltpu.VMEM((ALL_ROWS, D), bf16),
                pltpu.VMEM((TOK_DEV, D), bf16),
                pltpu.VMEM((TOK_DEV, D), bf16),
                pltpu.VMEM((TOK_DEV, D), bf16),
                pltpu.VMEM((TOK_DEV, D), bf16),
                pltpu.SemaphoreType.DMA((PIECES,)),
                pltpu.SemaphoreType.DMA((16,)),
            ],
        ),
        out_shape=[jax.ShapeDtypeStruct((2 * PIECE, D), bf16)] * 16
        + [
            jax.ShapeDtypeStruct((TOK_DEV, D), bf16),
            jax.ShapeDtypeStruct((TOK_DEV, 3 * D), bf16),
            rows,
            jax.ShapeDtypeStruct((16, D), jnp.float32),
            jax.ShapeDtypeStruct((TOK_DEV, FF), bf16),
            jax.ShapeDtypeStruct((TOK_DEV, FF), bf16),
            rows,
        ],
        compiler_params=pltpu.CompilerParams(vmem_limit_bytes=60 * 2**20),
        cost_estimate=pl.CostEstimate(
            flops=2 * 10**10, bytes_accessed=80 * 2**20, transcendentals=10**6
        ),
    )(scalars, *blocks, own, *small)


def result_kernel(where, *refs):
    count = PIECES - REPS
    blocks, own = refs[:GROUPS], refs[GROUPS]
    (tokens, normed, spread, grad_y, attn, grad_mixed, low_sums, vecs, hidden, grad_pre, high_sums) = (
        refs[GROUPS + 1 : GROUPS + 12]
    )
    output, grad_input, vec_out, held, sems = refs[GROUPS + 12 :]
    ids = [where[1 + t] for t in range(count)]
    arrive = fetch_pieces(ids, blocks, own, where[0], held, sems)
    for owner in range(SHARDS):
        arrive(owner)
    total = dot32(attn[...], w_out_of(held)) + vecs[5:6, :]
    for j in range(4):
        total = total + dot32(hidden[:, D * j : D * (j + 1)], w_out2_of(held, j))
    output[...] = tokens[...].astype(jnp.float32) + (total + vecs[12:13, :])
    vec_out[2:5, :] = low_sums[0:3, :]
    vec_out[8:12, :] = high_sums[0:4, :]
    gy = grad_y[...].astype(jnp.float32)
    total = gy
    for norm, (parts, width, weights) in enumerate(
        ((grad_mixed, 3, w_qkv_of), (grad_pre, 4, w_in_of))
    ):
        back = None
        for j in range(width):
            part = dot32(weights(held, j), parts[:, D * j : D * (j + 1)].T)
            back = part if back is None else back + part
        grad_act = back.T
        gain_row = 0 if norm == 0 else 6
        unit = normed[...]
        vec_out[gain_row : gain_row + 1, :] = jnp.sum(grad_act * unit, axis=0, keepdims=True)
        vec_out[gain_row + 1 : gain_row + 2, :] = jnp.sum(grad_act, axis=0, keepdims=True)
        grad_norm = grad_act * vecs[gain_row : gain_row + 1, :]
        total = total + spread[:, 0:1] * (
            grad_norm
            - jnp.mean(grad_norm, axis=1, keepdims=True)
            - unit * jnp.mean(grad_norm * unit, axis=1, keepdims=True)
        )
    grad_input[...] = total
    bottom = jnp.sum(gy, axis=0, keepdims=True)
    vec_out[5:6, :] = bottom
    vec_out[12:13, :] = bottom
    vec_out[13:16, :] = jnp.zeros((3, D), jnp.float32)
    vec_out[...] = vec_out[...].astype(jnp.bfloat16).astype(jnp.float32)


def layer_results(scalars, blocks, own, small):
    anywhere = pl.BlockSpec(memory_space=pl.ANY)
    vmem = pl.BlockSpec(memory_space=pltpu.VMEM)
    rows = jax.ShapeDtypeStruct((TOK_DEV, D), jnp.float32)
    return pl.pallas_call(
        result_kernel,
        grid_spec=pltpu.PrefetchScalarGridSpec(
            num_scalar_prefetch=1,
            in_specs=[anywhere] * (len(blocks) + 1) + [vmem] * len(small),
            out_specs=[vmem] * 3,
            scratch_shapes=[
                pltpu.VMEM((ALL_ROWS, D), jnp.bfloat16),
                pltpu.SemaphoreType.DMA((PIECES,)),
            ],
        ),
        out_shape=[rows, rows, jax.ShapeDtypeStruct((16, D), jnp.float32)],
        compiler_params=pltpu.CompilerParams(vmem_limit_bytes=60 * 2**20),
        cost_estimate=pl.CostEstimate(
            flops=4 * 10**9, bytes_accessed=30 * 2**20, transcendentals=0
        ),
    )(scalars, *blocks, own, *small)


SHARE = FLAT_ROWS // REPS
BEGINS = tuple(SHARE * r // 16 * 16 for r in range(REPS)) + (FLAT_ROWS,)
SHARE_ROWS = 1760
STEP = 576


def align_kernel(where, one_ref, two_ref, out_ref, held):
    for r in range(REPS):

        @pl.when(where[0] == r)
        def _(r=r):
            lead = SHARE * r - BEGINS[r]
            for turn, ref in enumerate((one_ref, two_ref)):
                held[0:16, :] = jnp.zeros((16, LANES), jnp.float32)
                held[SHARE_ROWS - 32 :, :] = jnp.zeros((32, LANES), jnp.float32)
                held[lead : lead + SHARE, :] = ref[...]
                out_ref[turn] = held[...].astype(jnp.bfloat16)


def align_moments(moment_one, moment_two, rep):
    return pl.pallas_call(
        align_kernel,
        grid_spec=pltpu.PrefetchScalarGridSpec(
            num_scalar_prefetch=1,
            in_specs=[pl.BlockSpec(memory_space=pltpu.VMEM)] * 2,
            out_specs=pl.BlockSpec(memory_space=pltpu.VMEM),
            scratch_shapes=[pltpu.VMEM((SHARE_ROWS, LANES), jnp.float32)],
        ),
        out_shape=jax.ShapeDtypeStruct((2, SHARE_ROWS, LANES), jnp.bfloat16),
        compiler_params=pltpu.CompilerParams(vmem_limit_bytes=16 * 2**20),
        cost_estimate=pl.CostEstimate(flops=0, bytes_accessed=6 * 2**20, transcendentals=0),
    )(jnp.stack([rep]), moment_one.reshape(SHARE, LANES), moment_two.reshape(SHARE, LANES))


def update_kernel(factor, where, *refs):
    blocks = refs[:REPS]
    moments = refs[REPS : 2 * REPS]
    vec_ref, params, grad_out, params_out = refs[2 * REPS : 2 * REPS + 4]
    held, grad, weight, moment, sems, out_sems = refs[2 * REPS + 4 :]
    copies = []
    for turn in range(REPS):
        copies.append(
            pltpu.make_async_copy(blocks[turn], held.at[where[1 + turn]], sems.at[turn])
        )
    fetched = []
    for r in range(REPS):
        rows = pl.ds(BEGINS[r], BEGINS[r + 1] - BEGINS[r])
        fetched.append(
            pltpu.make_async_copy(params.at[rows], weight.at[rows], sems.at[REPS + r])
        )
    for turn in range(REPS):
        which = where[1 + turn]
        copies.append(
            pltpu.make_async_copy(
                moments[turn], moment.at[which], sems.at[2 * REPS + which]
            )
        )
    for copy in copies + fetched:
        copy.start()
    for copy in copies[:REPS]:
        copy.wait()
    shard = where[0]
    for z in range(SHARDS):

        @pl.when(shard == z)
        def _(z=z):
            for slot, row in enumerate(VECTOR_ROWS[z]):
                for col in range(6):
                    grad[6 * row + col : 6 * row + col + 1, :] = (
                        vec_ref[slot : slot + 1, LANES * col : LANES * (col + 1)] * factor
                    )

            @pl.loop(0, REPS)
            def _(rep):
                for first, step, rows, blocks, place in PARTS[z]:
                    for block in range(blocks):
                        for col in range(6):
                            got = held[
                                rep,
                                place + rows * block : place + rows * (block + 1),
                                LANES * col : LANES * (col + 1),
                            ]
                            begin = first + step * rep + 6 * block + col
                            grad[pl.ds(begin, rows, stride=6 * blocks), :] = (
                                got.astype(jnp.float32) * factor
                            )

    saving = []
    for r in range(REPS):
        rows = pl.ds(BEGINS[r], BEGINS[r + 1] - BEGINS[r])
        saving.append(
            pltpu.make_async_copy(grad.at[rows], grad_out.at[rows], out_sems.at[REPS + r])
        )
        saving[-1].start()
    for r in range(REPS):
        base = BEGINS[r]
        length = BEGINS[r + 1] - base
        pltpu.make_async_copy(moments[0], moment.at[r], sems.at[2 * REPS + r]).wait()
        fetched[r].wait()
        if r > 0:
            tail = base - BEGINS[r - 1]
            moment[r, :, 0:16, :] = moment[r, :, 0:16, :] + moment[r - 1, :, tail : tail + 16, :]

        def renew(at, rows, r=r, base=base):
            here = pl.ds(pl.multiple_of(base + at, 8), rows)
            there = pl.ds(pl.multiple_of(at, 16), rows)
            updated, _, _ = adam_update(
                weight[here, :],
                moment[r, 0, there, :].astype(jnp.float32),
                moment[r, 1, there, :].astype(jnp.float32),
                grad[here, :],
            )
            weight[here, :] = updated

        @pl.loop(0, length // STEP)
        def _(turn):
            renew(turn * STEP, STEP)

        if length % STEP:
            renew(length // STEP * STEP, length % STEP)
        rows = pl.ds(base, length)
        saving.append(
            pltpu.make_async_copy(weight.at[rows], params_out.at[rows], out_sems.at[r])
        )
        saving[-1].start()
    for copy in saving:
        copy.wait()


def update_shard(blocks, ids, vectors, params, moments, shard, factor):
    anywhere = pl.BlockSpec(memory_space=pl.ANY)
    flat = jax.ShapeDtypeStruct((FLAT_ROWS, LANES), jnp.float32)
    return pl.pallas_call(
        functools.partial(update_kernel, factor),
        grid_spec=pltpu.PrefetchScalarGridSpec(
            num_scalar_prefetch=1,
            in_specs=[anywhere] * (2 * REPS)
            + [pl.BlockSpec(memory_space=pltpu.VMEM), anywhere],
            out_specs=[anywhere] * 2,
            scratch_shapes=[
                pltpu.VMEM((REPS, PIECE, D), jnp.bfloat16),
                pltpu.VMEM((FLAT_ROWS, LANES), jnp.float32),
                pltpu.VMEM((FLAT_ROWS, LANES), jnp.float32),
                pltpu.VMEM((REPS, 2, SHARE_ROWS, LANES), jnp.bfloat16),
                pltpu.SemaphoreType.DMA((3 * REPS,)),
                pltpu.SemaphoreType.DMA((2 * REPS,)),
            ],
        ),
        out_shape=[flat, flat],
        compiler_params=pltpu.CompilerParams(vmem_limit_bytes=60 * 2**20),
    )(jnp.stack([shard] + ids), *blocks, *moments, vectors, params.reshape(FLAT_ROWS, LANES))


def ring_shift(value, hop):
    return lax.ppermute(value, "z", [(i, (i + hop) % SHARDS) for i in range(SHARDS)])


fence = lax.optimization_barrier


def gather_matrices(params, shard, rep, early, moment_one, moment_two):
    piece = pack_pieces(params, shard, [rep], False)[0][0]
    own, vec = pack_pieces(params, shard, [rep * 0 + turn for turn in range(REPS)], True)
    one = ring_step(piece)
    _, moment_one, moment_two = fence((piece, moment_one, moment_two))
    moments = align_moments(moment_one, moment_two, rep)
    first_moments = first_cross(moments)
    one, own, vec, first_moments = fence((one, own, vec, first_moments))
    two, first_one, second_one = ring_step(one), first_cross(one), second_cross(one)
    vec_one = ring_step(vec)
    two, first_one, second_one, vec_one, early = fence(
        (two, first_one, second_one, vec_one, early)
    )
    three, first_two, second_two = ring_step(two), first_cross(two), second_cross(two)
    both_one = second_cross(first_one)
    vec_two = ring_step(vec_one)
    three, first_two, second_two, both_one, vec_two = fence(
        (three, first_two, second_two, both_one, vec_two)
    )
    first_three, second_three = first_cross(three), second_cross(three)
    both_two = second_cross(first_two)
    mine_one = jnp.stack([one, first_one, second_one, both_one])
    other_one = core_cross(mine_one)
    vec_three = ring_step(vec_two)
    first_three, second_three, both_two, other_one, vec_three = fence(
        (first_three, second_three, both_two, other_one, vec_three)
    )
    both_three = second_cross(first_three)
    mine_two = jnp.stack([two, first_two, second_two, both_two])
    other_two = core_cross(mine_two)
    others = [core_cross(value) for value in (three, first_three, second_three)]
    others, both_three, other_two = fence((others, both_three, other_two))
    others.append(core_cross(both_three))
    threes = [three, first_three, second_three, both_three]
    blocks = [mine_one, other_one, mine_two, other_two] + threes + others
    ids = []
    for hop in range(1, SHARDS):
        owner = (shard + SHARDS - hop) % SHARDS
        ids += [owner * REPS + which for which in spread_ids(rep)]
    hops = [vec, vec_one, vec_two, vec_three]
    return blocks, own.reshape(REPS * PIECE, D), ids, hops, early, [moments, first_moments]


def slots_by_piece(shard, rep):
    slots = []
    for owner in range(SHARDS):
        hop = (shard + SHARDS - owner + 3) % SHARDS
        for which in range(REPS):
            apart = rep ^ which
            kept = 1 - apart % 2
            core = which % 2
            across = apart & 6
            first = 2 + 2 * core
            place = jnp.where(
                across == 0, 2, jnp.where(across == 6, 1, jnp.where(across == first, 0, 3))
            )
            slots.append((kept * SHARDS + hop) * 4 + place)
    return slots


def scatter_sums(parts, moments, small, results):
    sent_far, sent_near, kept_far, kept_near = (
        [parts[8 * half + 2 * turn + near] for turn in range(SHARDS)]
        for half in range(2)
        for near in range(2)
    )
    cores = [core_cross(sent_far[0]), core_cross(sent_near[0]), core_cross(sent_far[1])]
    cores = list(fence(cores))
    far = [kept_far[0] + cores[0], kept_far[1] + cores[2]]
    crossed = first_cross(far[0])
    others = [core_cross(v) for v in (sent_near[1], sent_far[2], sent_near[2], sent_far[3])]
    crossed, others, small = fence((crossed, others, small))
    near = [kept_near[0] + cores[1], kept_near[1] + others[0], kept_near[2] + others[2]]
    far += [kept_far[2] + others[1], kept_far[3] + others[3]]

    pair = near[0] + crossed
    final = second_cross(pair[1])
    kept = pair[0]
    crossed = first_cross(far[1])
    last_near = core_cross(sent_near[3])
    output, grad_input, vectors = results(small)
    final, crossed, last_near, vectors = fence((final, crossed, last_near, vectors))
    near.append(kept_near[3] + last_near)

    carried = None
    for turn in range(1, SHARDS):
        total = kept + final
        if carried is not None:
            total = total + carried
        carried = ring_step(total)
        pair = near[turn] + crossed
        kept = pair[0]
        final = second_cross(pair[1])
        met = plane_permute(vectors, ((1, 1), (2, 2), (4, 4))[turn - 1])
        if turn < SHARDS - 1:
            crossed = first_cross(far[turn + 1])
            final, crossed, carried, met, moments = fence(
                (final, crossed, carried, met, moments)
            )
        else:
            final, carried, met = fence((final, carried, met))
        if turn > 1:
            moments.append(core_cross(moments[turn]))
        vectors = vectors + met
    total = kept + final + carried

    first, second = first_cross(total), second_cross(total)
    shifted = [ring_shift(vectors, hop) for hop in range(1, SHARDS)]
    first, second, shifted = fence((first, second, shifted))
    vectors = vectors + shifted[0] + shifted[1] + shifted[2]
    both = second_cross(first)
    mine = [total, first, second]
    spread = [core_cross(value) for value in mine]
    both, spread = fence((both, spread))
    spread.append(core_cross(both))
    return mine + [both] + spread, moments, output, grad_input, vectors


def on_device_rows(tokens, segment_ids, cotangent, params, moment_one, moment_two):
    shard = lax.axis_index("z")
    rep = lax.axis_index(PLANE)
    early = prepare(tokens, cotangent, segment_ids)
    blocks, own, ids, hops, early, moments = gather_matrices(
        params, shard, rep, early, moment_one, moment_two
    )
    normed, inv_std, grad_y, tables = early
    moments, blocks = fence((moments, blocks))
    moments += [second_cross(value) for value in moments]
    moments += [core_cross(value) for value in moments[:2]]
    scalars = jnp.stack([shard] + ids + slots_by_piece(shard, rep))
    made = layer_gradients(scalars, blocks, own, (normed, grad_y, tables, *hops))
    made, moments = fence((made, moments))
    small = (tokens, normed, inv_std, grad_y) + tuple(made[16:])
    spread, moments, output, grad_input, vec_grads = scatter_sums(
        [part.reshape(2, PIECE, D) for part in made[:16]], moments, small, lambda small: layer_results(scalars, blocks, own, small)
    )
    own_vectors = lax.dynamic_index_in_dim(
        vec_grads.reshape(SHARDS, 4, D), shard, 0, keepdims=False
    )
    tokens_all = tokens.shape[0] * lax.axis_size(EVERY)
    grad_params, new_params = update_shard(
        spread,
        spread_ids(rep),
        own_vectors,
        params,
        moments,
        shard,
        1.0 / math.sqrt(tokens_all),
    )
    grad_params = grad_params.reshape(-1)
    width = moment_one.shape[0]
    grad_share = lax.dynamic_slice_in_dim(grad_params, rep * width, width)
    _, upd_first, upd_second = adam_update(moment_one, moment_one, moment_two, grad_share)
    return (output, grad_input, grad_params, new_params.reshape(-1), upd_first, upd_second)


def solution(mesh):
    in_rows = mesh.shape["rep"] == REPS and mesh.shape["shard"] == SHARDS
    if in_rows:
        rep, shard = PLANE, "z"
        mesh = Mesh(mesh.devices.reshape(2, 2, 2, SHARDS), EVERY)
        body = on_device_rows
    else:
        rep, shard = ("rep",), "shard"
        body = on_device
    rows = rep + (shard,)
    owner = (shard,) + rep
    in_specs = (P(rows, None), P(rows), P(rows, None), P(shard), P(owner), P(owner))
    out_specs = (P(rows, None), P(rows, None), P(shard), P(shard), P(owner), P(owner))
    return jax.shard_map(body, mesh=mesh, in_specs=in_specs, out_specs=out_specs, check_vma=False)
```

```python
import functools
import math

import jax
import jax.numpy as jnp
from jax import lax
from jax.experimental import pallas as pl
from jax.experimental.pallas import tpu as pltpu
from jax.sharding import Mesh
from jax.sharding import PartitionSpec as P

D = 768
HEADS = 12
HD = 64
ROT = 16
FF = 3072
TOK_DEV = 128


EPS_NORM = 1e-05
ROPE_BASE = 10000.0
NEG_BIG = -1e30
BETA_ONE = 0.9
BETA_TWO = 0.95
ADAM_STEP = 3.0
LEARN_RATE = 0.05
DECAY = 0.01
ADAM_EPS = 1e-08
INV_ROOT_TWO = 0.7071067811865476
INV_ROOT_TWO_PI = 0.3989422804014327


def layout_offsets():
    q_width = HEADS * HD
    o_wqkv = 2 * D
    o_bqkv = o_wqkv + 3 * q_width * D
    o_wout = o_bqkv + 3 * q_width
    o_bout = o_wout + q_width * D
    o_gain2 = o_bout + D
    o_shift2 = o_gain2 + D
    o_win = o_shift2 + D
    o_bin = o_win + D * FF
    o_wout2 = o_bin + FF
    o_bout2 = o_wout2 + FF * D
    return (
        o_wqkv,
        o_bqkv,
        o_wout,
        o_bout,
        o_gain2,
        o_shift2,
        o_win,
        o_bin,
        o_wout2,
        o_bout2,
        o_bout2 + D,
    )


def split_params(flat16):
    q_width = HEADS * HD
    o_wqkv, o_bqkv, o_wout, o_bout, o_gain2, o_shift2, o_win, o_bin, o_wout2, o_bout2, o_end = (
        layout_offsets()
    )
    return (
        flat16[0:D],
        flat16[D:o_wqkv],
        flat16[o_wqkv:o_bqkv].reshape(D, 3 * q_width),
        flat16[o_bqkv:o_wout],
        flat16[o_wout:o_bout].reshape(q_width, D),
        flat16[o_bout:o_gain2],
        flat16[o_gain2:o_shift2],
        flat16[o_shift2:o_win],
        flat16[o_win:o_bin].reshape(D, FF),
        flat16[o_bin:o_wout2],
        flat16[o_wout2:o_bout2].reshape(FF, D),
        flat16[o_bout2:o_end],
    )


def positions_of(segments):
    count = segments.shape[0]
    slot_ids = jnp.arange(count, dtype=jnp.int32)
    before = jnp.concatenate([jnp.full((1,), -2, jnp.int32), segments[:-1]])
    begins = segments != before
    first_slot = lax.cummax(jnp.where(begins, slot_ids, 0), axis=0)
    return slot_ids - first_slot


def rotary_tables(positions):
    half = ROT // 2
    steps_j = jnp.arange(half, dtype=jnp.float32)
    freqs = jnp.power(jnp.float32(ROPE_BASE), -2.0 * steps_j / ROT)
    angle = positions.astype(jnp.float32)[:, None] * freqs[None, :]
    return (jnp.cos(angle)[:, None, :], jnp.sin(angle)[:, None, :])


def rotate(values, cosine, sine, sign):
    half = cosine.shape[-1]
    lower = values[..., :half]
    upper = values[..., half : 2 * half]
    rest = values[..., 2 * half :]
    return jnp.concatenate(
        [lower * cosine - sign * upper * sine, upper * cosine + sign * lower * sine, rest], axis=-1
    )


def gelu_exact(value):
    return value * 0.5 * (1.0 + lax.erf(value * INV_ROOT_TWO))


def gelu_slope(value):
    return (
        0.5 * (1.0 + lax.erf(value * INV_ROOT_TWO))
        + value * jnp.exp(-0.5 * value * value) * INV_ROOT_TWO_PI
    )


def masked_scores(q_blk, keys, seg_rows, seg_cols, begin_row):
    scale = q_blk.shape[-1] ** (-0.5)
    raw_scores = jnp.einsum("qhd,khd->hqk", q_blk, keys, preferred_element_type=jnp.float32) * scale
    row_ids = begin_row + jnp.arange(q_blk.shape[0], dtype=jnp.int32)
    col_ids = jnp.arange(keys.shape[0], dtype=jnp.int32)
    allowed = (seg_rows[:, None] == seg_cols[None, :]) & (col_ids[None, :] <= row_ids[:, None])
    return jnp.where(allowed[None], raw_scores, NEG_BIG)


def attend_forward(query16, key16, value16, segments):
    scores = masked_scores(query16, key16, segments, segments, 0)
    row_max = jnp.max(scores, axis=-1, keepdims=True)
    expd = jnp.exp(scores - row_max)
    row_total = jnp.sum(expd, axis=-1, keepdims=True)
    probs16 = (expd / row_total).astype(jnp.bfloat16)
    attn_blk = jnp.einsum("hqk,khd->qhd", probs16, value16, preferred_element_type=jnp.float32)
    pieces_out = attn_blk.astype(jnp.bfloat16)
    lse_list = [row_max + jnp.log(row_total)]
    return (pieces_out, lse_list)


def attend_backward(query16, key16, value16, attn16, lse_list, segments, grad_attn16):
    count = query16.shape[0]
    block = min(512, count)
    scale = query16.shape[-1] ** (-0.5)
    grad_query = []
    grad_key = jnp.zeros(key16.shape, jnp.float32)
    grad_value = jnp.zeros(value16.shape, jnp.float32)
    for turn, begin_row in enumerate(range(0, count, block)):
        stop_row = begin_row + block
        scores = masked_scores(query16, key16, segments, segments, begin_row)
        chances = jnp.exp(scores - lse_list[turn])
        chances16 = chances.astype(jnp.bfloat16)
        grad_value = grad_value.at[:stop_row].add(
            jnp.einsum("hqk,qhd->khd", chances16, grad_attn16, preferred_element_type=jnp.float32)
        )
        grad_chance = jnp.einsum(
            "qhd,khd->hqk", grad_attn16, value16, preferred_element_type=jnp.float32
        )
        delta = jnp.sum(grad_attn16.astype(jnp.float32) * attn16.astype(jnp.float32), axis=-1)
        grad_scores = (chances * (grad_chance - jnp.transpose(delta)[:, :, None]) * scale).astype(
            jnp.bfloat16
        )
        grad_query.append(
            jnp.einsum("hqk,khd->qhd", grad_scores, key16, preferred_element_type=jnp.float32)
        )
        grad_key = grad_key.at[:stop_row].add(
            jnp.einsum("hqk,qhd->khd", grad_scores, query16, preferred_element_type=jnp.float32)
        )
    return (grad_query[0], grad_key, grad_value)


def norm_back(grad_act, normed, inv_std, gain):
    grad_gain = jnp.sum(grad_act * normed, axis=0)
    grad_shift = jnp.sum(grad_act, axis=0)
    grad_norm = grad_act * gain.astype(jnp.float32)
    grad_x = inv_std * (
        grad_norm
        - jnp.mean(grad_norm, axis=1, keepdims=True)
        - normed * jnp.mean(grad_norm * normed, axis=1, keepdims=True)
    )
    return (grad_gain, grad_shift, grad_x)


def layer_forward(tokens, segments, pieces):
    (
        gain_one,
        shift_one,
        w_qkv,
        b_qkv,
        w_out,
        b_out,
        gain_two,
        shift_two,
        w_in,
        b_in,
        w_out2,
        b_out2,
    ) = pieces
    count = tokens.shape[0]
    x_wide = tokens.astype(jnp.float32)
    row_mean = jnp.mean(x_wide, axis=1, keepdims=True)
    centered = x_wide - row_mean
    variance = jnp.mean(centered * centered, axis=1, keepdims=True)
    inv_std = lax.rsqrt(variance + EPS_NORM)
    normed = centered * inv_std
    act_one = (normed * gain_one.astype(jnp.float32) + shift_one.astype(jnp.float32)).astype(
        jnp.bfloat16
    )
    act_two = (normed * gain_two.astype(jnp.float32) + shift_two.astype(jnp.float32)).astype(
        jnp.bfloat16
    )
    mixed = jnp.dot(act_one, w_qkv, preferred_element_type=jnp.float32) + b_qkv.astype(jnp.float32)
    mixed = mixed.reshape(count, 3, HEADS, HD)
    cosine, sine = rotary_tables(positions_of(segments))
    query16 = rotate(mixed[:, 0], cosine, sine, 1.0).astype(jnp.bfloat16)
    key16 = rotate(mixed[:, 1], cosine, sine, 1.0).astype(jnp.bfloat16)
    value16 = mixed[:, 2].astype(jnp.bfloat16)
    attn16, lse_list = attend_forward(query16, key16, value16, segments)
    proj = jnp.dot(
        attn16.reshape(count, HEADS * HD), w_out, preferred_element_type=jnp.float32
    ) + b_out.astype(jnp.float32)
    pre = jnp.dot(act_two, w_in, preferred_element_type=jnp.float32) + b_in.astype(jnp.float32)
    hidden16 = gelu_exact(pre).astype(jnp.bfloat16)
    feed = jnp.dot(hidden16, w_out2, preferred_element_type=jnp.float32) + b_out2.astype(
        jnp.float32
    )
    output = x_wide + proj + feed
    saved = (
        normed,
        inv_std,
        act_one,
        act_two,
        query16,
        key16,
        value16,
        attn16,
        lse_list,
        cosine,
        sine,
        pre,
        hidden16,
    )
    return (output, saved)


def layer_backward(cotangent, segments, pieces, saved):
    (
        gain_one,
        shift_one,
        w_qkv,
        b_qkv,
        w_out,
        b_out,
        gain_two,
        shift_two,
        w_in,
        b_in,
        w_out2,
        b_out2,
    ) = pieces
    (
        normed,
        inv_std,
        act_one,
        act_two,
        query16,
        key16,
        value16,
        attn16,
        lse_list,
        cosine,
        sine,
        pre,
        hidden16,
    ) = saved
    count = cotangent.shape[0]
    contract_rows = (((0,), (0,)), ((), ()))
    contract_cols = (((1,), (1,)), ((), ()))
    live_rows = (segments >= 0).astype(jnp.float32)[:, None]
    grad_y = cotangent.astype(jnp.float32) * live_rows
    grad_y16 = grad_y.astype(jnp.bfloat16)
    grad_b_out = jnp.sum(grad_y, axis=0)
    attn_flat = attn16.reshape(count, HEADS * HD)
    grad_w_out = lax.dot_general(
        attn_flat, grad_y16, contract_rows, preferred_element_type=jnp.float32
    )
    grad_w_out2 = lax.dot_general(
        hidden16, grad_y16, contract_rows, preferred_element_type=jnp.float32
    )
    grad_hidden = lax.dot_general(
        grad_y16, w_out2, contract_cols, preferred_element_type=jnp.float32
    )
    grad_pre = grad_hidden * gelu_slope(pre)
    grad_b_in = jnp.sum(grad_pre, axis=0)
    grad_pre16 = grad_pre.astype(jnp.bfloat16)
    grad_w_in = lax.dot_general(
        act_two, grad_pre16, contract_rows, preferred_element_type=jnp.float32
    )
    grad_act_two = lax.dot_general(
        grad_pre16, w_in, contract_cols, preferred_element_type=jnp.float32
    )
    grad_attn16 = (
        lax.dot_general(grad_y16, w_out, contract_cols, preferred_element_type=jnp.float32)
        .astype(jnp.bfloat16)
        .reshape(count, HEADS, HD)
    )
    grad_query, grad_key, grad_value = attend_backward(
        query16, key16, value16, attn16, lse_list, segments, grad_attn16
    )
    grad_query = rotate(grad_query, cosine, sine, -1.0)
    grad_key = rotate(grad_key, cosine, sine, -1.0)
    grad_mixed = jnp.stack([grad_query, grad_key, grad_value], axis=1).reshape(
        count, 3 * HEADS * HD
    )
    grad_b_qkv = jnp.sum(grad_mixed, axis=0)
    grad_mixed16 = grad_mixed.astype(jnp.bfloat16)
    grad_w_qkv = lax.dot_general(
        act_one, grad_mixed16, contract_rows, preferred_element_type=jnp.float32
    )
    grad_act_one = lax.dot_general(
        grad_mixed16, w_qkv, contract_cols, preferred_element_type=jnp.float32
    )
    gain_grad_one, shift_grad_one, grad_x_one = norm_back(grad_act_one, normed, inv_std, gain_one)
    gain_grad_two, shift_grad_two, grad_x_two = norm_back(grad_act_two, normed, inv_std, gain_two)
    grad_in = grad_y + grad_x_one + grad_x_two
    return (
        grad_in,
        [
            gain_grad_one,
            shift_grad_one,
            grad_w_qkv,
            grad_b_qkv,
            grad_w_out,
            grad_b_out,
            gain_grad_two,
            shift_grad_two,
            grad_w_in,
            grad_b_in,
            grad_w_out2,
            grad_b_out,
        ],
    )


def flatten_grads(parts, total_len):
    used = layout_offsets()[-1]
    rounded = [part.astype(jnp.bfloat16).reshape(-1) for part in parts]
    return jnp.concatenate(rounded + [jnp.zeros((total_len - used,), jnp.bfloat16)])


def adam_update(weights, first_moment, second_moment, gradient):
    new_first = BETA_ONE * first_moment + (1.0 - BETA_ONE) * gradient
    new_second = BETA_TWO * second_moment + (1.0 - BETA_TWO) * gradient * gradient
    unbiased_first = new_first / (1.0 - BETA_ONE**ADAM_STEP)
    unbiased_second = new_second / (1.0 - BETA_TWO**ADAM_STEP)
    new_weights = weights - LEARN_RATE * (
        unbiased_first / (jnp.sqrt(unbiased_second) + ADAM_EPS) + DECAY * weights
    )
    return (new_weights, new_first, new_second)


def on_device(tokens, segment_ids, cotangent, params, moment_one, moment_two):
    gathered = lax.all_gather(params.astype(jnp.bfloat16), "shard", axis=0, tiled=True)
    total_len = gathered.shape[0]
    pieces = split_params(gathered)
    output, saved = layer_forward(tokens, segment_ids, pieces)
    grad_input, parts = layer_backward(cotangent, segment_ids, pieces, saved)
    local_grad = flatten_grads(parts, total_len)
    owned = lax.psum_scatter(local_grad, "shard", scatter_dimension=0, tiled=True).astype(
        jnp.float32
    )
    tokens_all = tokens.shape[0] * lax.axis_size("rep") * lax.axis_size("shard")
    factor = 1.0 / math.sqrt(tokens_all)
    width = moment_one.shape[0]
    begin = lax.axis_index("rep") * width
    param_share = lax.dynamic_slice_in_dim(params, begin, width)
    share = lax.psum_scatter(owned, "rep", scatter_dimension=0, tiled=True)
    grad_share = share * factor
    upd_params, upd_first, upd_second = adam_update(param_share, moment_one, moment_two, grad_share)
    grad_params, new_params = (
        lax.all_gather(grad_share, "rep", axis=0, tiled=True),
        lax.all_gather(upd_params, "rep", axis=0, tiled=True),
    )
    return (output, grad_input, grad_params, new_params, upd_first, upd_second)


LANES = 128
REPS = 8
SHARDS = 4
PIECE = 288
FLAT_ROWS = 13848
MOVED = PIECE * D // LANES


PARTS = (
    ((12, 1728, 96, 3, 0),),
    ((6, 576, 96, 1, 0), (4632, 1152, 48, 4, 96)),
    ((0, 1152, 48, 4, 0), (9240, 576, 96, 1, 192)),
    ((0, 1728, 288, 1, 0),),
)
VECTOR_ROWS = ((0, 1, 2306, 2307), (0, 769, 770, 771), (1536, 1537, 1538, 1539), (2304, 2305, 2306, 2307))


PLANE = ("y", "x", "core")
EVERY = PLANE + ("z",)
HOPS = (1, 2, 3, 0)


def plane_permute(value, flips):
    return lax.ppermute(value, PLANE, [(i, i ^ flips[i % 2]) for i in range(REPS)])


def first_cross(value):
    return plane_permute(value, (2, 4))


def second_cross(value):
    return plane_permute(value, (4, 2))


def core_cross(value):
    return plane_permute(value, (1, 1))


def ring_step(value):
    return lax.ppermute(value, "z", [(i, (i + 1) % SHARDS) for i in range(SHARDS)])


def flips_of(rep):
    core = rep % 2
    first = 2 + 2 * core
    return (0, first, 6 - first, 6)


def spread_ids(rep):
    other = rep ^ 1
    return [rep ^ flip for flip in flips_of(rep)] + [other ^ flip for flip in flips_of(other)]


def window_of(row):
    return min(6 * row // 8 * 8, FLAT_ROWS - 16)


def pack_kernel(where, flat_ref, out_ref, *rest):
    vec_ref = rest[0] if len(rest) == 4 else None
    held, windows, sems = rest[-3:]
    shard = where[0]
    turns = out_ref.shape[0]
    for z in range(SHARDS):

        @pl.when(shard == z)
        def _(z=z):
            def copies_of(turn):
                slot = turn % 2
                rep = where[1 + turn]
                copies = []
                at = 0
                for part, (first, step, _, _, _) in enumerate(PARTS[z]):
                    lead = first % 8
                    count = step + (8 if lead else 0)
                    begin = pl.multiple_of(first - lead + step * rep, 8)
                    copies.append(
                        pltpu.make_async_copy(
                            flat_ref.at[pl.ds(begin, count)],
                            held.at[slot, pl.ds(at, count)],
                            sems.at[slot, part],
                        )
                    )
                    at += count
                return copies

            for copy in copies_of(0):
                copy.start()
            if vec_ref is not None:
                cuts = []
                for slot, row in enumerate(VECTOR_ROWS[z]):
                    cuts.append(
                        pltpu.make_async_copy(
                            flat_ref.at[pl.ds(window_of(row), 16)],
                            windows.at[slot],
                            sems.at[2 + slot // 2, slot % 2],
                        )
                    )
                    cuts[-1].start()
                vec_ref[...] = jnp.zeros_like(vec_ref)
                for slot, row in enumerate(VECTOR_ROWS[z]):
                    cuts[slot].wait()
                    lead = 6 * row - window_of(row)
                    for col in range(6):
                        got = windows[slot, lead + col : lead + col + 1, :]
                        vec_ref[slot : slot + 1, LANES * col : LANES * (col + 1)] = got.astype(
                            jnp.bfloat16
                        ).astype(jnp.float32)

            @pl.loop(0, turns)
            def _(turn):
                @pl.when(turn + 1 < turns)
                def _():
                    for copy in copies_of(turn + 1):
                        copy.start()

                slot = turn % 2
                at = 0
                for copy, (first, step, rows, blocks, place) in zip(copies_of(turn), PARTS[z]):
                    copy.wait()
                    lead = first % 8
                    for block in range(blocks):
                        for col in range(6):
                            begin = at + lead + 6 * block + col
                            got = held[slot, pl.ds(begin, rows, stride=6 * blocks), :]
                            out_ref[
                                turn,
                                place + rows * block : place + rows * (block + 1),
                                LANES * col : LANES * (col + 1),
                            ] = got.astype(jnp.bfloat16)
                    at += step + (8 if lead else 0)


def pack_pieces(params, shard, reps, vectors):
    pieces = jax.ShapeDtypeStruct((len(reps), PIECE, D), jnp.bfloat16)
    rows = jax.ShapeDtypeStruct((8, D), jnp.float32)
    vmem = pl.BlockSpec(memory_space=pltpu.VMEM)
    return pl.pallas_call(
        pack_kernel,
        grid_spec=pltpu.PrefetchScalarGridSpec(
            num_scalar_prefetch=1,
            in_specs=[pl.BlockSpec(memory_space=pltpu.HBM)],
            out_specs=[vmem, vmem] if vectors else [vmem],
            scratch_shapes=[
                pltpu.VMEM((2, MOVED + 16, LANES), jnp.float32),
                pltpu.VMEM((4, 16, LANES), jnp.float32),
                pltpu.SemaphoreType.DMA((4, 2)),
            ],
        ),
        out_shape=[pieces, rows] if vectors else [pieces],
        cost_estimate=pl.CostEstimate(
            flops=0, bytes_accessed=len(reps) * 3 * 2**20, transcendentals=0
        ),
        compiler_params=pltpu.CompilerParams(vmem_limit_bytes=56 * 2**20),
    )(jnp.stack([shard] + reps), params.reshape(FLAT_ROWS, LANES))


def prepare_kernel(tokens, cotangent, ids, freqs, normed, spread, grad_y, tables):
    x_wide = tokens[...].astype(jnp.float32)
    centered = x_wide - jnp.mean(x_wide, axis=1, keepdims=True)
    variance = jnp.mean(centered * centered, axis=1, keepdims=True)
    inv_std = lax.rsqrt(variance + EPS_NORM)
    normed[...] = centered * inv_std
    spread[...] = jnp.broadcast_to(inv_std, spread.shape)
    square = (TOK_DEV, TOK_DEV)
    across = jnp.broadcast_to(ids[...].astype(jnp.float32), square)
    down = across.T
    lane = lax.broadcasted_iota(jnp.int32, square, 1)
    row = lax.broadcasted_iota(jnp.int32, square, 0)
    begins = (across != pltpu.roll(across, 1, 1)) | (lane == 0)
    before = jnp.where(begins & (lane <= row), lane.astype(jnp.float32), 0.0)
    position = row.astype(jnp.float32) - jnp.max(before, axis=1, keepdims=True)
    angle = position * freqs[...]
    cosine, sine = jnp.cos(angle), jnp.sin(angle)
    within = lane % HD
    tables[0] = jnp.where(within < ROT, cosine, 1.0)
    tables[1] = jnp.where(within < ROT // 2, -sine, 0.0)
    tables[2] = jnp.where((within >= ROT // 2) & (within < ROT), sine, 0.0)
    tables[3] = jnp.where((across == down) & (lane <= row), 1.0, 0.0)
    cot = cotangent[...].astype(jnp.float32)
    grad_y[...] = jnp.where(down[:, 0:1] >= 0, cot, 0.0).astype(jnp.bfloat16)


def prepare(tokens, cotangent, segment_ids):
    steps = jnp.arange(LANES, dtype=jnp.int32) % (ROT // 2)
    freqs = jnp.power(jnp.float32(ROPE_BASE), -2.0 * steps.astype(jnp.float32) / ROT)
    return pl.pallas_call(
        prepare_kernel,
        out_shape=[
            jax.ShapeDtypeStruct((TOK_DEV, D), jnp.float32),
            jax.ShapeDtypeStruct((TOK_DEV, LANES), jnp.float32),
            jax.ShapeDtypeStruct((TOK_DEV, D), jnp.bfloat16),
            jax.ShapeDtypeStruct((4, TOK_DEV, TOK_DEV), jnp.float32),
        ],
        compiler_params=pltpu.CompilerParams(vmem_limit_bytes=16 * 2**20),
    )(tokens, cotangent, segment_ids.reshape(1, TOK_DEV), freqs.reshape(1, LANES))


PIECES = SHARDS * REPS
GROUPS = 12
ALL_ROWS = PIECES * PIECE


def fetch_pieces(ids, blocks, own, shard, held, sems):
    views = []
    for block in blocks:
        views += [block.at[p] for p in range(4)] if len(block.shape) == 3 else [block]
    ids = ids + [shard * REPS + r for r in range(REPS)]
    views += [own.at[pl.ds(r * PIECE, PIECE)] for r in range(REPS)]
    for early in (True, False):
        for which, view in zip(ids, views):

            @pl.when((which < 2 * REPS) == early)
            def _(which=which, view=view):
                row = pl.multiple_of(which * PIECE, 16)
                pltpu.make_async_copy(view, held.at[pl.ds(row, PIECE)], sems.at[which]).start()

    def arrive(owner):
        for r in range(REPS):
            at = owner * REPS + r
            pltpu.make_async_copy(
                own.at[pl.ds(0, PIECE)], held.at[pl.ds(at * PIECE, PIECE)], sems.at[at]
            ).wait()

    return arrive


def rows_of(held, shard, begin, rows):
    return jnp.concatenate(
        [held[pl.ds((shard * REPS + r) * PIECE + begin, rows), :] for r in range(REPS)], axis=0
    )


def w_qkv_of(held, j):
    return rows_of(held, 0, 96 * j, 96)


def w_out_of(held):
    return rows_of(held, 1, 0, 96)


def w_in_of(held, j):
    return jnp.concatenate([rows_of(held, 1, 96 + 48 * j, 48), rows_of(held, 2, 48 * j, 48)], axis=0)


def w_out2_of(held, j):
    if j == 0:
        return rows_of(held, 2, 192, 96)
    return held[pl.ds(3 * REPS * PIECE + D * (j - 1), D), :]


def dot32(a, b):
    return jnp.dot(a, b, preferred_element_type=jnp.float32)


def layer_kernel(where, *refs):
    count = PIECES - REPS
    blocks, own = refs[:GROUPS], refs[GROUPS]
    normed, grad_y, tables = refs[GROUPS + 1 : GROUPS + 4]
    hops = refs[GROUPS + 4 : GROUPS + 8]
    outs = refs[GROUPS + 8 : GROUPS + 24]
    (attn_out, mixed_out, low_sums, vecs, hidden_out, pre_out, high_sums) = refs[
        GROUPS + 24 : GROUPS + 31
    ]
    held, grads, query, key, value, grad_attn, sems, out_sems = refs[GROUPS + 31 :]
    rot_cos, rot_up, rot_down, bias = (tables.at[turn] for turn in range(4))
    shard = where[0]
    arrive = fetch_pieces([where[1 + t] for t in range(count)], blocks, own, shard, held, sems)
    low_sums[...] = jnp.zeros_like(low_sums)
    high_sums[...] = jnp.zeros_like(high_sums)
    for owner in range(SHARDS):
        rows = jnp.zeros((4, D), jnp.float32)
        for hop in range(SHARDS):
            met = (shard + SHARDS - owner) % SHARDS == hop
            rows = jnp.where(met, hops[hop][0:4, :], rows)
        vecs[4 * owner : 4 * owner + 4, :] = rows

    arrive(0)
    act1 = (normed[...] * vecs[0:1, :] + vecs[1:2, :]).astype(jnp.bfloat16)
    for j, out in enumerate((query, key, value)):
        got = dot32(act1, w_qkv_of(held, j)) + vecs[2 + j : 3 + j, :]
        if j < 2:
            for p in range(6):
                lanes = slice(LANES * p, LANES * (p + 1))
                part = got[:, lanes]
                part = (
                    part * rot_cos[...]
                    + pltpu.roll(part, LANES - 8, 1) * rot_up[...]
                    + pltpu.roll(part, 8, 1) * rot_down[...]
                )
                out[:, lanes] = part.astype(jnp.bfloat16)
        else:
            out[...] = got.astype(jnp.bfloat16)
    gy_t = grad_y[...].T
    arrive(1)
    grad_attn[...] = dot32(w_out_of(held), gy_t).T.astype(jnp.bfloat16)

    arrive(2)
    arrive(3)
    low = lax.broadcasted_iota(jnp.int32, (LANES, LANES), 1) < HD
    scale = HD ** (-0.5)
    for p in range(6):
        lanes = slice(LANES * p, LANES * (p + 1))
        q2, k2, v2, g2 = (ref[:, lanes] for ref in (query, key, value, grad_attn))
        k2_t, v2_t = k2.T, v2.T
        attn_parts, value_parts, query_parts, key_parts = [], [], [], []
        for half in range(2):
            here = low if half == 0 else ~low
            zero = jnp.zeros_like(q2)
            scores = dot32(jnp.where(here, q2, zero), k2_t) * scale
            scores = jnp.where(bias[...] > 0.5, scores, NEG_BIG)
            expd = jnp.exp(scores - jnp.max(scores, axis=1, keepdims=True))
            chances = expd / jnp.sum(expd, axis=1, keepdims=True)
            chances16 = chances.astype(jnp.bfloat16)
            attn = dot32(chances16, v2)
            attn16 = attn.astype(jnp.bfloat16)
            masked = jnp.where(here, g2, zero)
            delta = jnp.sum(
                masked.astype(jnp.float32) * attn16.astype(jnp.float32), axis=1, keepdims=True
            )
            grad_chance = dot32(masked, v2_t)
            slope = (chances * (grad_chance - delta) * scale).astype(jnp.bfloat16)
            attn_parts.append(attn16)
            value_parts.append(dot32(chances16.T, g2))
            query_parts.append(dot32(slope, k2))
            key_parts.append(dot32(slope.T, q2))
        attn_out[:, lanes] = jnp.where(low, *attn_parts)
        for j, parts in enumerate((query_parts, key_parts, value_parts)):
            part = jnp.where(low, *parts)
            if j < 2:
                part = (
                    part * rot_cos[...]
                    - pltpu.roll(part, LANES - 8, 1) * rot_up[...]
                    - pltpu.roll(part, 8, 1) * rot_down[...]
                )
            wide = slice(D * j + LANES * p, D * j + LANES * (p + 1))
            low_sums[j : j + 1, lanes] = jnp.sum(part, axis=0, keepdims=True)
            mixed_out[:, wide] = part.astype(jnp.bfloat16)


    def send_off(owner):
        for hop in range(SHARDS):

            @pl.when((shard + SHARDS - HOPS[hop]) % SHARDS == owner)
            def _(hop=hop):
                for turn in (2 * hop, 2 * hop + 1, 8 + 2 * hop, 9 + 2 * hop):
                    pltpu.make_async_copy(
                        grads.at[pl.ds(turn * 2 * PIECE, 2 * PIECE)],
                        outs[turn],
                        out_sems.at[turn],
                    ).start()

    slot_row = lambda z, r: pl.multiple_of(where[1 + count + z * REPS + r] * PIECE, 16)

    def keep_rows(z, begin, rows, part):
        for r in range(part.shape[0] // rows):
            grads[pl.ds(slot_row(z, r) + begin, rows), :] = part[rows * r : rows * (r + 1), :]

    gy = grad_y[...]
    act1_t = (normed[...] * vecs[0:1, :] + vecs[1:2, :]).astype(jnp.bfloat16).T
    for j in range(3):
        keep_rows(
            0, 96 * j, 96, dot32(act1_t, mixed_out[:, D * j : D * (j + 1)]).astype(jnp.bfloat16)
        )
    send_off(0)
    keep_rows(1, 0, 96, dot32(attn_out[...].T, gy).astype(jnp.bfloat16))

    act2 = (normed[...] * vecs[6:7, :] + vecs[7:8, :]).astype(jnp.bfloat16)
    act2_t = act2.T
    for j in range(4):
        wide = slice(D * j, D * (j + 1))
        pre = dot32(act2, w_in_of(held, j)) + vecs[8 + j : 9 + j, :]
        bell = 0.5 * (1.0 + lax.erf(pre * INV_ROOT_TWO))
        hidden = (pre * bell).astype(jnp.bfloat16)
        hidden_out[:, wide] = hidden
        grad_hidden = dot32(w_out2_of(held, j), gy_t).T
        grad_pre = grad_hidden * (bell + pre * jnp.exp(-0.5 * pre * pre) * INV_ROOT_TWO_PI)
        high_sums[j : j + 1, :] = jnp.sum(grad_pre, axis=0, keepdims=True)
        grad_pre16 = grad_pre.astype(jnp.bfloat16)
        pre_out[:, wide] = grad_pre16
        w2 = dot32(hidden.T, gy).astype(jnp.bfloat16)
        if j == 0:
            keep_rows(2, 192, 96, w2)
        else:
            at = D * (j - 1)
            while at < D * j:
                r, begin = divmod(at, PIECE)
                rows = min(PIECE - begin, D * j - at)
                grads[pl.ds(slot_row(3, r) + begin, rows), :] = w2[
                    at - D * (j - 1) : at - D * (j - 1) + rows, :
                ]
                at += rows
    send_off(3)
    for half, owner in enumerate((1, 2)):
        side = act2_t[D // 2 * half : D // 2 * (half + 1), :]
        for j in range(4):
            w1 = dot32(side, pre_out[:, D * j : D * (j + 1)]).astype(jnp.bfloat16)
            keep_rows(owner, (96 if owner == 1 else 0) + 48 * j, 48, w1)
        send_off(owner)
    for turn, out in enumerate(outs):
        pltpu.make_async_copy(
            grads.at[pl.ds(turn * 2 * PIECE, 2 * PIECE)], out, out_sems.at[turn]
        ).wait()


def layer_gradients(scalars, blocks, own, small):
    anywhere = pl.BlockSpec(memory_space=pl.ANY)
    vmem = pl.BlockSpec(memory_space=pltpu.VMEM)
    bf16 = jnp.bfloat16
    rows = jax.ShapeDtypeStruct((8, D), jnp.float32)
    return pl.pallas_call(
        layer_kernel,
        grid_spec=pltpu.PrefetchScalarGridSpec(
            num_scalar_prefetch=1,
            in_specs=[anywhere] * (len(blocks) + 1) + [vmem] * len(small),
            out_specs=[pl.BlockSpec(memory_space=pltpu.HBM)] * 16 + [vmem] * 7,
            scratch_shapes=[
                pltpu.VMEM((ALL_ROWS, D), bf16),
                pltpu.VMEM((ALL_ROWS, D), bf16),
                pltpu.VMEM((TOK_DEV, D), bf16),
                pltpu.VMEM((TOK_DEV, D), bf16),
                pltpu.VMEM((TOK_DEV, D), bf16),
                pltpu.VMEM((TOK_DEV, D), bf16),
                pltpu.SemaphoreType.DMA((PIECES,)),
                pltpu.SemaphoreType.DMA((16,)),
            ],
        ),
        out_shape=[jax.ShapeDtypeStruct((2 * PIECE, D), bf16)] * 16
        + [
            jax.ShapeDtypeStruct((TOK_DEV, D), bf16),
            jax.ShapeDtypeStruct((TOK_DEV, 3 * D), bf16),
            rows,
            jax.ShapeDtypeStruct((16, D), jnp.float32),
            jax.ShapeDtypeStruct((TOK_DEV, FF), bf16),
            jax.ShapeDtypeStruct((TOK_DEV, FF), bf16),
            rows,
        ],
        compiler_params=pltpu.CompilerParams(vmem_limit_bytes=60 * 2**20),
        cost_estimate=pl.CostEstimate(
            flops=2 * 10**10, bytes_accessed=80 * 2**20, transcendentals=10**6
        ),
    )(scalars, *blocks, own, *small)


def result_kernel(where, *refs):
    count = PIECES - REPS
    blocks, own = refs[:GROUPS], refs[GROUPS]
    (tokens, normed, spread, grad_y, attn, grad_mixed, low_sums, vecs, hidden, grad_pre, high_sums) = (
        refs[GROUPS + 1 : GROUPS + 12]
    )
    output, grad_input, vec_out, held, sems = refs[GROUPS + 12 :]
    ids = [where[1 + t] for t in range(count)]
    arrive = fetch_pieces(ids, blocks, own, where[0], held, sems)
    for owner in range(SHARDS):
        arrive(owner)
    total = dot32(attn[...], w_out_of(held)) + vecs[5:6, :]
    for j in range(4):
        total = total + dot32(hidden[:, D * j : D * (j + 1)], w_out2_of(held, j))
    output[...] = tokens[...].astype(jnp.float32) + (total + vecs[12:13, :])
    vec_out[2:5, :] = low_sums[0:3, :]
    vec_out[8:12, :] = high_sums[0:4, :]
    gy = grad_y[...].astype(jnp.float32)
    total = gy
    for norm, (parts, width, weights) in enumerate(
        ((grad_mixed, 3, w_qkv_of), (grad_pre, 4, w_in_of))
    ):
        back = None
        for j in range(width):
            part = dot32(weights(held, j), parts[:, D * j : D * (j + 1)].T)
            back = part if back is None else back + part
        grad_act = back.T
        gain_row = 0 if norm == 0 else 6
        unit = normed[...]
        vec_out[gain_row : gain_row + 1, :] = jnp.sum(grad_act * unit, axis=0, keepdims=True)
        vec_out[gain_row + 1 : gain_row + 2, :] = jnp.sum(grad_act, axis=0, keepdims=True)
        grad_norm = grad_act * vecs[gain_row : gain_row + 1, :]
        total = total + spread[:, 0:1] * (
            grad_norm
            - jnp.mean(grad_norm, axis=1, keepdims=True)
            - unit * jnp.mean(grad_norm * unit, axis=1, keepdims=True)
        )
    grad_input[...] = total
    bottom = jnp.sum(gy, axis=0, keepdims=True)
    vec_out[5:6, :] = bottom
    vec_out[12:13, :] = bottom
    vec_out[13:16, :] = jnp.zeros((3, D), jnp.float32)
    vec_out[...] = vec_out[...].astype(jnp.bfloat16).astype(jnp.float32)


def layer_results(scalars, blocks, own, small):
    anywhere = pl.BlockSpec(memory_space=pl.ANY)
    vmem = pl.BlockSpec(memory_space=pltpu.VMEM)
    rows = jax.ShapeDtypeStruct((TOK_DEV, D), jnp.float32)
    return pl.pallas_call(
        result_kernel,
        grid_spec=pltpu.PrefetchScalarGridSpec(
            num_scalar_prefetch=1,
            in_specs=[anywhere] * (len(blocks) + 1) + [vmem] * len(small),
            out_specs=[vmem] * 3,
            scratch_shapes=[
                pltpu.VMEM((ALL_ROWS, D), jnp.bfloat16),
                pltpu.SemaphoreType.DMA((PIECES,)),
            ],
        ),
        out_shape=[rows, rows, jax.ShapeDtypeStruct((16, D), jnp.float32)],
        compiler_params=pltpu.CompilerParams(vmem_limit_bytes=60 * 2**20),
        cost_estimate=pl.CostEstimate(
            flops=4 * 10**9, bytes_accessed=30 * 2**20, transcendentals=0
        ),
    )(scalars, *blocks, own, *small)


SHARE = FLAT_ROWS // REPS
BEGINS = tuple(SHARE * r // 16 * 16 for r in range(REPS)) + (FLAT_ROWS,)
SHARE_ROWS = 1760
STEP = 576


def align_kernel(where, one_ref, two_ref, out_ref, held):
    for r in range(REPS):

        @pl.when(where[0] == r)
        def _(r=r):
            lead = SHARE * r - BEGINS[r]
            for turn, ref in enumerate((one_ref, two_ref)):
                held[0:16, :] = jnp.zeros((16, LANES), jnp.float32)
                held[SHARE_ROWS - 32 :, :] = jnp.zeros((32, LANES), jnp.float32)
                held[lead : lead + SHARE, :] = ref[...]
                out_ref[turn] = held[...].astype(jnp.bfloat16)


def align_moments(moment_one, moment_two, rep):
    return pl.pallas_call(
        align_kernel,
        grid_spec=pltpu.PrefetchScalarGridSpec(
            num_scalar_prefetch=1,
            in_specs=[pl.BlockSpec(memory_space=pltpu.VMEM)] * 2,
            out_specs=pl.BlockSpec(memory_space=pltpu.VMEM),
            scratch_shapes=[pltpu.VMEM((SHARE_ROWS, LANES), jnp.float32)],
        ),
        out_shape=jax.ShapeDtypeStruct((2, SHARE_ROWS, LANES), jnp.bfloat16),
        compiler_params=pltpu.CompilerParams(vmem_limit_bytes=16 * 2**20),
        cost_estimate=pl.CostEstimate(flops=0, bytes_accessed=6 * 2**20, transcendentals=0),
    )(jnp.stack([rep]), moment_one.reshape(SHARE, LANES), moment_two.reshape(SHARE, LANES))


def update_kernel(factor, where, *refs):
    blocks = refs[:REPS]
    moments = refs[REPS : 2 * REPS]
    vec_ref, params, grad_out, params_out = refs[2 * REPS : 2 * REPS + 4]
    held, grad, weight, moment, sems, out_sems = refs[2 * REPS + 4 :]
    copies = []
    for turn in range(REPS):
        copies.append(
            pltpu.make_async_copy(blocks[turn], held.at[where[1 + turn]], sems.at[turn])
        )
    fetched = []
    for r in range(REPS):
        rows = pl.ds(BEGINS[r], BEGINS[r + 1] - BEGINS[r])
        fetched.append(
            pltpu.make_async_copy(params.at[rows], weight.at[rows], sems.at[REPS + r])
        )
    for turn in range(REPS):
        which = where[1 + turn]
        copies.append(
            pltpu.make_async_copy(
                moments[turn], moment.at[which], sems.at[2 * REPS + which]
            )
        )
    for copy in copies + fetched:
        copy.start()
    for copy in copies[:REPS]:
        copy.wait()
    shard = where[0]
    for z in range(SHARDS):

        @pl.when(shard == z)
        def _(z=z):
            for slot, row in enumerate(VECTOR_ROWS[z]):
                for col in range(6):
                    grad[6 * row + col : 6 * row + col + 1, :] = (
                        vec_ref[slot : slot + 1, LANES * col : LANES * (col + 1)] * factor
                    )

            @pl.loop(0, REPS)
            def _(rep):
                for first, step, rows, blocks, place in PARTS[z]:
                    for block in range(blocks):
                        for col in range(6):
                            got = held[
                                rep,
                                place + rows * block : place + rows * (block + 1),
                                LANES * col : LANES * (col + 1),
                            ]
                            begin = first + step * rep + 6 * block + col
                            grad[pl.ds(begin, rows, stride=6 * blocks), :] = (
                                got.astype(jnp.float32) * factor
                            )

    saving = []
    for r in range(REPS):
        rows = pl.ds(BEGINS[r], BEGINS[r + 1] - BEGINS[r])
        saving.append(
            pltpu.make_async_copy(grad.at[rows], grad_out.at[rows], out_sems.at[REPS + r])
        )
        saving[-1].start()
    for r in range(REPS):
        base = BEGINS[r]
        length = BEGINS[r + 1] - base
        pltpu.make_async_copy(moments[0], moment.at[r], sems.at[2 * REPS + r]).wait()
        fetched[r].wait()
        if r > 0:
            tail = base - BEGINS[r - 1]
            moment[r, :, 0:16, :] = moment[r, :, 0:16, :] + moment[r - 1, :, tail : tail + 16, :]

        def renew(at, rows, r=r, base=base):
            here = pl.ds(pl.multiple_of(base + at, 8), rows)
            there = pl.ds(pl.multiple_of(at, 16), rows)
            updated, _, _ = adam_update(
                weight[here, :],
                moment[r, 0, there, :].astype(jnp.float32),
                moment[r, 1, there, :].astype(jnp.float32),
                grad[here, :],
            )
            weight[here, :] = updated

        @pl.loop(0, length // STEP)
        def _(turn):
            renew(turn * STEP, STEP)

        if length % STEP:
            renew(length // STEP * STEP, length % STEP)
        rows = pl.ds(base, length)
        saving.append(
            pltpu.make_async_copy(weight.at[rows], params_out.at[rows], out_sems.at[r])
        )
        saving[-1].start()
    for copy in saving:
        copy.wait()


def update_shard(blocks, ids, vectors, params, moments, shard, factor):
    anywhere = pl.BlockSpec(memory_space=pl.ANY)
    flat = jax.ShapeDtypeStruct((FLAT_ROWS, LANES), jnp.float32)
    return pl.pallas_call(
        functools.partial(update_kernel, factor),
        grid_spec=pltpu.PrefetchScalarGridSpec(
            num_scalar_prefetch=1,
            in_specs=[anywhere] * (2 * REPS)
            + [pl.BlockSpec(memory_space=pltpu.VMEM), anywhere],
            out_specs=[anywhere] * 2,
            scratch_shapes=[
                pltpu.VMEM((REPS, PIECE, D), jnp.bfloat16),
                pltpu.VMEM((FLAT_ROWS, LANES), jnp.float32),
                pltpu.VMEM((FLAT_ROWS, LANES), jnp.float32),
                pltpu.VMEM((REPS, 2, SHARE_ROWS, LANES), jnp.bfloat16),
                pltpu.SemaphoreType.DMA((3 * REPS,)),
                pltpu.SemaphoreType.DMA((2 * REPS,)),
            ],
        ),
        out_shape=[flat, flat],
        compiler_params=pltpu.CompilerParams(vmem_limit_bytes=60 * 2**20),
    )(jnp.stack([shard] + ids), *blocks, *moments, vectors, params.reshape(FLAT_ROWS, LANES))


def ring_shift(value, hop):
    return lax.ppermute(value, "z", [(i, (i + hop) % SHARDS) for i in range(SHARDS)])


fence = lax.optimization_barrier


def gather_matrices(params, shard, rep, early):
    piece = pack_pieces(params, shard, [rep], False)[0][0]
    own, vec = pack_pieces(params, shard, [rep * 0 + turn for turn in range(REPS)], True)
    one = ring_step(piece)
    one, own, vec = fence((one, own, vec))
    two, first_one, second_one = ring_step(one), first_cross(one), second_cross(one)
    vec_one = ring_step(vec)
    two, first_one, second_one, vec_one, early = fence(
        (two, first_one, second_one, vec_one, early)
    )
    three, first_two, second_two = ring_step(two), first_cross(two), second_cross(two)
    both_one = second_cross(first_one)
    vec_two = ring_step(vec_one)
    three, first_two, second_two, both_one, vec_two = fence(
        (three, first_two, second_two, both_one, vec_two)
    )
    first_three, second_three = first_cross(three), second_cross(three)
    both_two = second_cross(first_two)
    mine_one = jnp.stack([one, first_one, second_one, both_one])
    other_one = core_cross(mine_one)
    vec_three = ring_step(vec_two)
    first_three, second_three, both_two, other_one, vec_three = fence(
        (first_three, second_three, both_two, other_one, vec_three)
    )
    both_three = second_cross(first_three)
    mine_two = jnp.stack([two, first_two, second_two, both_two])
    other_two = core_cross(mine_two)
    others = [core_cross(value) for value in (three, first_three, second_three)]
    others, both_three, other_two = fence((others, both_three, other_two))
    others.append(core_cross(both_three))
    threes = [three, first_three, second_three, both_three]
    blocks = [mine_one, other_one, mine_two, other_two] + threes + others
    ids = []
    for hop in range(1, SHARDS):
        owner = (shard + SHARDS - hop) % SHARDS
        ids += [owner * REPS + which for which in spread_ids(rep)]
    hops = [vec, vec_one, vec_two, vec_three]
    return blocks, own.reshape(REPS * PIECE, D), ids, hops, early


def slots_by_piece(shard, rep):
    slots = []
    for owner in range(SHARDS):
        hop = (shard + SHARDS - owner + 3) % SHARDS
        for which in range(REPS):
            apart = rep ^ which
            kept = 1 - apart % 2
            core = which % 2
            across = apart & 6
            first = 2 + 2 * core
            place = jnp.where(
                across == 0, 2, jnp.where(across == 6, 1, jnp.where(across == first, 0, 3))
            )
            slots.append((kept * SHARDS + hop) * 4 + place)
    return slots


def scatter_sums(parts, moments, small, results):
    sent_far, sent_near, kept_far, kept_near = (
        [parts[8 * half + 2 * turn + near] for turn in range(SHARDS)]
        for half in range(2)
        for near in range(2)
    )
    cores = [core_cross(sent_far[0]), core_cross(sent_near[0]), core_cross(sent_far[1])]
    cores = list(fence(cores))
    far = [kept_far[0] + cores[0], kept_far[1] + cores[2]]
    crossed = first_cross(far[0])
    others = [core_cross(v) for v in (sent_near[1], sent_far[2], sent_near[2], sent_far[3])]
    crossed, others, small = fence((crossed, others, small))
    near = [kept_near[0] + cores[1], kept_near[1] + others[0], kept_near[2] + others[2]]
    far += [kept_far[2] + others[1], kept_far[3] + others[3]]

    pair = near[0] + crossed
    final = second_cross(pair[1])
    kept = pair[0]
    crossed = first_cross(far[1])
    last_near = core_cross(sent_near[3])
    output, grad_input, vectors = results(small)
    final, crossed, last_near, vectors = fence((final, crossed, last_near, vectors))
    near.append(kept_near[3] + last_near)

    carried = None
    for turn in range(1, SHARDS):
        total = kept + final
        if carried is not None:
            total = total + carried
        carried = ring_step(total)
        pair = near[turn] + crossed
        kept = pair[0]
        final = second_cross(pair[1])
        met = plane_permute(vectors, ((1, 1), (2, 2), (4, 4))[turn - 1])
        if turn == 1:
            crossed = first_cross(far[turn + 1])
            final, crossed, carried, met = fence((final, crossed, carried, met))
        elif turn == 2:
            crossed = first_cross(far[turn + 1])
            first_other = core_cross(moments[1])
            final, crossed, carried, met, moments, first_other = fence(
                (final, crossed, carried, met, moments, first_other)
            )
        else:
            both_moments, second_other = second_cross(moments[1]), core_cross(moments[2])
            final, carried, met, both_moments, second_other = fence(
                (final, carried, met, both_moments, second_other)
            )
        vectors = vectors + met
    total = kept + final + carried

    first, second = first_cross(total), second_cross(total)
    shifted = [ring_shift(vectors, hop) for hop in range(1, SHARDS)]
    first, second, shifted = fence((first, second, shifted))
    vectors = vectors + shifted[0] + shifted[1] + shifted[2]
    both = second_cross(first)
    mine = [total, first, second]
    spread = [core_cross(value) for value in mine]
    both_other = core_cross(both_moments)
    both, spread = fence((both, spread))
    spread.append(core_cross(both))
    moments = moments[:3] + [both_moments, moments[3], first_other, second_other, both_other]
    return mine + [both] + spread, moments, output, grad_input, vectors


def on_device_rows(tokens, segment_ids, cotangent, params, moment_one, moment_two):
    shard = lax.axis_index("z")
    rep = lax.axis_index(PLANE)
    early = (prepare(tokens, cotangent, segment_ids), align_moments(moment_one, moment_two, rep))
    blocks, own, ids, hops, early = gather_matrices(params, shard, rep, early)
    (normed, inv_std, grad_y, tables), moments = early
    moments, blocks = fence((moments, blocks))
    moments = [moments, first_cross(moments), second_cross(moments), core_cross(moments)]
    scalars = jnp.stack([shard] + ids + slots_by_piece(shard, rep))
    made = layer_gradients(scalars, blocks, own, (normed, grad_y, tables, *hops))
    made, moments = fence((made, moments))
    small = (tokens, normed, inv_std, grad_y) + tuple(made[16:])
    spread, moments, output, grad_input, vec_grads = scatter_sums(
        [part.reshape(2, PIECE, D) for part in made[:16]], moments, small, lambda small: layer_results(scalars, blocks, own, small)
    )
    own_vectors = lax.dynamic_index_in_dim(
        vec_grads.reshape(SHARDS, 4, D), shard, 0, keepdims=False
    )
    tokens_all = tokens.shape[0] * lax.axis_size(EVERY)
    grad_params, new_params = update_shard(
        spread,
        spread_ids(rep),
        own_vectors,
        params,
        moments,
        shard,
        1.0 / math.sqrt(tokens_all),
    )
    grad_params = grad_params.reshape(-1)
    width = moment_one.shape[0]
    grad_share = lax.dynamic_slice_in_dim(grad_params, rep * width, width)
    _, upd_first, upd_second = adam_update(moment_one, moment_one, moment_two, grad_share)
    return (output, grad_input, grad_params, new_params.reshape(-1), upd_first, upd_second)


def solution(mesh):
    in_rows = mesh.shape["rep"] == REPS and mesh.shape["shard"] == SHARDS
    if in_rows:
        rep, shard = PLANE, "z"
        mesh = Mesh(mesh.devices.reshape(2, 2, 2, SHARDS), EVERY)
        body = on_device_rows
    else:
        rep, shard = ("rep",), "shard"
        body = on_device
    rows = rep + (shard,)
    owner = (shard,) + rep
    in_specs = (P(rows, None), P(rows), P(rows, None), P(shard), P(owner), P(owner))
    out_specs = (P(rows, None), P(rows, None), P(shard), P(shard), P(owner), P(owner))
    return jax.shard_map(body, mesh=mesh, in_specs=in_specs, out_specs=out_specs, check_vma=False)
```

```python
import functools
import math

import jax
import jax.numpy as jnp
from jax import lax
from jax.experimental import pallas as pl
from jax.experimental.pallas import tpu as pltpu
from jax.sharding import Mesh
from jax.sharding import PartitionSpec as P

D = 768
HEADS = 12
HD = 64
ROT = 16
FF = 3072
TOK_DEV = 128


EPS_NORM = 1e-05
ROPE_BASE = 10000.0
NEG_BIG = -1e30
BETA_ONE = 0.9
BETA_TWO = 0.95
ADAM_STEP = 3.0
LEARN_RATE = 0.05
DECAY = 0.01
ADAM_EPS = 1e-08
INV_ROOT_TWO = 0.7071067811865476
INV_ROOT_TWO_PI = 0.3989422804014327


def layout_offsets():
    q_width = HEADS * HD
    o_wqkv = 2 * D
    o_bqkv = o_wqkv + 3 * q_width * D
    o_wout = o_bqkv + 3 * q_width
    o_bout = o_wout + q_width * D
    o_gain2 = o_bout + D
    o_shift2 = o_gain2 + D
    o_win = o_shift2 + D
    o_bin = o_win + D * FF
    o_wout2 = o_bin + FF
    o_bout2 = o_wout2 + FF * D
    return (
        o_wqkv,
        o_bqkv,
        o_wout,
        o_bout,
        o_gain2,
        o_shift2,
        o_win,
        o_bin,
        o_wout2,
        o_bout2,
        o_bout2 + D,
    )


def split_params(flat16):
    q_width = HEADS * HD
    o_wqkv, o_bqkv, o_wout, o_bout, o_gain2, o_shift2, o_win, o_bin, o_wout2, o_bout2, o_end = (
        layout_offsets()
    )
    return (
        flat16[0:D],
        flat16[D:o_wqkv],
        flat16[o_wqkv:o_bqkv].reshape(D, 3 * q_width),
        flat16[o_bqkv:o_wout],
        flat16[o_wout:o_bout].reshape(q_width, D),
        flat16[o_bout:o_gain2],
        flat16[o_gain2:o_shift2],
        flat16[o_shift2:o_win],
        flat16[o_win:o_bin].reshape(D, FF),
        flat16[o_bin:o_wout2],
        flat16[o_wout2:o_bout2].reshape(FF, D),
        flat16[o_bout2:o_end],
    )


def positions_of(segments):
    count = segments.shape[0]
    slot_ids = jnp.arange(count, dtype=jnp.int32)
    before = jnp.concatenate([jnp.full((1,), -2, jnp.int32), segments[:-1]])
    begins = segments != before
    first_slot = lax.cummax(jnp.where(begins, slot_ids, 0), axis=0)
    return slot_ids - first_slot


def rotary_tables(positions):
    half = ROT // 2
    steps_j = jnp.arange(half, dtype=jnp.float32)
    freqs = jnp.power(jnp.float32(ROPE_BASE), -2.0 * steps_j / ROT)
    angle = positions.astype(jnp.float32)[:, None] * freqs[None, :]
    return (jnp.cos(angle)[:, None, :], jnp.sin(angle)[:, None, :])


def rotate(values, cosine, sine, sign):
    half = cosine.shape[-1]
    lower = values[..., :half]
    upper = values[..., half : 2 * half]
    rest = values[..., 2 * half :]
    return jnp.concatenate(
        [lower * cosine - sign * upper * sine, upper * cosine + sign * lower * sine, rest], axis=-1
    )


def gelu_exact(value):
    return value * 0.5 * (1.0 + lax.erf(value * INV_ROOT_TWO))


def gelu_slope(value):
    return (
        0.5 * (1.0 + lax.erf(value * INV_ROOT_TWO))
        + value * jnp.exp(-0.5 * value * value) * INV_ROOT_TWO_PI
    )


def masked_scores(q_blk, keys, seg_rows, seg_cols, begin_row):
    scale = q_blk.shape[-1] ** (-0.5)
    raw_scores = jnp.einsum("qhd,khd->hqk", q_blk, keys, preferred_element_type=jnp.float32) * scale
    row_ids = begin_row + jnp.arange(q_blk.shape[0], dtype=jnp.int32)
    col_ids = jnp.arange(keys.shape[0], dtype=jnp.int32)
    allowed = (seg_rows[:, None] == seg_cols[None, :]) & (col_ids[None, :] <= row_ids[:, None])
    return jnp.where(allowed[None], raw_scores, NEG_BIG)


def attend_forward(query16, key16, value16, segments):
    scores = masked_scores(query16, key16, segments, segments, 0)
    row_max = jnp.max(scores, axis=-1, keepdims=True)
    expd = jnp.exp(scores - row_max)
    row_total = jnp.sum(expd, axis=-1, keepdims=True)
    probs16 = (expd / row_total).astype(jnp.bfloat16)
    attn_blk = jnp.einsum("hqk,khd->qhd", probs16, value16, preferred_element_type=jnp.float32)
    pieces_out = attn_blk.astype(jnp.bfloat16)
    lse_list = [row_max + jnp.log(row_total)]
    return (pieces_out, lse_list)


def attend_backward(query16, key16, value16, attn16, lse_list, segments, grad_attn16):
    count = query16.shape[0]
    block = min(512, count)
    scale = query16.shape[-1] ** (-0.5)
    grad_query = []
    grad_key = jnp.zeros(key16.shape, jnp.float32)
    grad_value = jnp.zeros(value16.shape, jnp.float32)
    for turn, begin_row in enumerate(range(0, count, block)):
        stop_row = begin_row + block
        scores = masked_scores(query16, key16, segments, segments, begin_row)
        chances = jnp.exp(scores - lse_list[turn])
        chances16 = chances.astype(jnp.bfloat16)
        grad_value = grad_value.at[:stop_row].add(
            jnp.einsum("hqk,qhd->khd", chances16, grad_attn16, preferred_element_type=jnp.float32)
        )
        grad_chance = jnp.einsum(
            "qhd,khd->hqk", grad_attn16, value16, preferred_element_type=jnp.float32
        )
        delta = jnp.sum(grad_attn16.astype(jnp.float32) * attn16.astype(jnp.float32), axis=-1)
        grad_scores = (chances * (grad_chance - jnp.transpose(delta)[:, :, None]) * scale).astype(
            jnp.bfloat16
        )
        grad_query.append(
            jnp.einsum("hqk,khd->qhd", grad_scores, key16, preferred_element_type=jnp.float32)
        )
        grad_key = grad_key.at[:stop_row].add(
            jnp.einsum("hqk,qhd->khd", grad_scores, query16, preferred_element_type=jnp.float32)
        )
    return (grad_query[0], grad_key, grad_value)


def norm_back(grad_act, normed, inv_std, gain):
    grad_gain = jnp.sum(grad_act * normed, axis=0)
    grad_shift = jnp.sum(grad_act, axis=0)
    grad_norm = grad_act * gain.astype(jnp.float32)
    grad_x = inv_std * (
        grad_norm
        - jnp.mean(grad_norm, axis=1, keepdims=True)
        - normed * jnp.mean(grad_norm * normed, axis=1, keepdims=True)
    )
    return (grad_gain, grad_shift, grad_x)


def layer_forward(tokens, segments, pieces):
    (
        gain_one,
        shift_one,
        w_qkv,
        b_qkv,
        w_out,
        b_out,
        gain_two,
        shift_two,
        w_in,
        b_in,
        w_out2,
        b_out2,
    ) = pieces
    count = tokens.shape[0]
    x_wide = tokens.astype(jnp.float32)
    row_mean = jnp.mean(x_wide, axis=1, keepdims=True)
    centered = x_wide - row_mean
    variance = jnp.mean(centered * centered, axis=1, keepdims=True)
    inv_std = lax.rsqrt(variance + EPS_NORM)
    normed = centered * inv_std
    act_one = (normed * gain_one.astype(jnp.float32) + shift_one.astype(jnp.float32)).astype(
        jnp.bfloat16
    )
    act_two = (normed * gain_two.astype(jnp.float32) + shift_two.astype(jnp.float32)).astype(
        jnp.bfloat16
    )
    mixed = jnp.dot(act_one, w_qkv, preferred_element_type=jnp.float32) + b_qkv.astype(jnp.float32)
    mixed = mixed.reshape(count, 3, HEADS, HD)
    cosine, sine = rotary_tables(positions_of(segments))
    query16 = rotate(mixed[:, 0], cosine, sine, 1.0).astype(jnp.bfloat16)
    key16 = rotate(mixed[:, 1], cosine, sine, 1.0).astype(jnp.bfloat16)
    value16 = mixed[:, 2].astype(jnp.bfloat16)
    attn16, lse_list = attend_forward(query16, key16, value16, segments)
    proj = jnp.dot(
        attn16.reshape(count, HEADS * HD), w_out, preferred_element_type=jnp.float32
    ) + b_out.astype(jnp.float32)
    pre = jnp.dot(act_two, w_in, preferred_element_type=jnp.float32) + b_in.astype(jnp.float32)
    hidden16 = gelu_exact(pre).astype(jnp.bfloat16)
    feed = jnp.dot(hidden16, w_out2, preferred_element_type=jnp.float32) + b_out2.astype(
        jnp.float32
    )
    output = x_wide + proj + feed
    saved = (
        normed,
        inv_std,
        act_one,
        act_two,
        query16,
        key16,
        value16,
        attn16,
        lse_list,
        cosine,
        sine,
        pre,
        hidden16,
    )
    return (output, saved)


def layer_backward(cotangent, segments, pieces, saved):
    (
        gain_one,
        shift_one,
        w_qkv,
        b_qkv,
        w_out,
        b_out,
        gain_two,
        shift_two,
        w_in,
        b_in,
        w_out2,
        b_out2,
    ) = pieces
    (
        normed,
        inv_std,
        act_one,
        act_two,
        query16,
        key16,
        value16,
        attn16,
        lse_list,
        cosine,
        sine,
        pre,
        hidden16,
    ) = saved
    count = cotangent.shape[0]
    contract_rows = (((0,), (0,)), ((), ()))
    contract_cols = (((1,), (1,)), ((), ()))
    live_rows = (segments >= 0).astype(jnp.float32)[:, None]
    grad_y = cotangent.astype(jnp.float32) * live_rows
    grad_y16 = grad_y.astype(jnp.bfloat16)
    grad_b_out = jnp.sum(grad_y, axis=0)
    attn_flat = attn16.reshape(count, HEADS * HD)
    grad_w_out = lax.dot_general(
        attn_flat, grad_y16, contract_rows, preferred_element_type=jnp.float32
    )
    grad_w_out2 = lax.dot_general(
        hidden16, grad_y16, contract_rows, preferred_element_type=jnp.float32
    )
    grad_hidden = lax.dot_general(
        grad_y16, w_out2, contract_cols, preferred_element_type=jnp.float32
    )
    grad_pre = grad_hidden * gelu_slope(pre)
    grad_b_in = jnp.sum(grad_pre, axis=0)
    grad_pre16 = grad_pre.astype(jnp.bfloat16)
    grad_w_in = lax.dot_general(
        act_two, grad_pre16, contract_rows, preferred_element_type=jnp.float32
    )
    grad_act_two = lax.dot_general(
        grad_pre16, w_in, contract_cols, preferred_element_type=jnp.float32
    )
    grad_attn16 = (
        lax.dot_general(grad_y16, w_out, contract_cols, preferred_element_type=jnp.float32)
        .astype(jnp.bfloat16)
        .reshape(count, HEADS, HD)
    )
    grad_query, grad_key, grad_value = attend_backward(
        query16, key16, value16, attn16, lse_list, segments, grad_attn16
    )
    grad_query = rotate(grad_query, cosine, sine, -1.0)
    grad_key = rotate(grad_key, cosine, sine, -1.0)
    grad_mixed = jnp.stack([grad_query, grad_key, grad_value], axis=1).reshape(
        count, 3 * HEADS * HD
    )
    grad_b_qkv = jnp.sum(grad_mixed, axis=0)
    grad_mixed16 = grad_mixed.astype(jnp.bfloat16)
    grad_w_qkv = lax.dot_general(
        act_one, grad_mixed16, contract_rows, preferred_element_type=jnp.float32
    )
    grad_act_one = lax.dot_general(
        grad_mixed16, w_qkv, contract_cols, preferred_element_type=jnp.float32
    )
    gain_grad_one, shift_grad_one, grad_x_one = norm_back(grad_act_one, normed, inv_std, gain_one)
    gain_grad_two, shift_grad_two, grad_x_two = norm_back(grad_act_two, normed, inv_std, gain_two)
    grad_in = grad_y + grad_x_one + grad_x_two
    return (
        grad_in,
        [
            gain_grad_one,
            shift_grad_one,
            grad_w_qkv,
            grad_b_qkv,
            grad_w_out,
            grad_b_out,
            gain_grad_two,
            shift_grad_two,
            grad_w_in,
            grad_b_in,
            grad_w_out2,
            grad_b_out,
        ],
    )


def flatten_grads(parts, total_len):
    used = layout_offsets()[-1]
    rounded = [part.astype(jnp.bfloat16).reshape(-1) for part in parts]
    return jnp.concatenate(rounded + [jnp.zeros((total_len - used,), jnp.bfloat16)])


def adam_update(weights, first_moment, second_moment, gradient):
    new_first = BETA_ONE * first_moment + (1.0 - BETA_ONE) * gradient
    new_second = BETA_TWO * second_moment + (1.0 - BETA_TWO) * gradient * gradient
    unbiased_first = new_first / (1.0 - BETA_ONE**ADAM_STEP)
    unbiased_second = new_second / (1.0 - BETA_TWO**ADAM_STEP)
    new_weights = weights - LEARN_RATE * (
        unbiased_first / (jnp.sqrt(unbiased_second) + ADAM_EPS) + DECAY * weights
    )
    return (new_weights, new_first, new_second)


def on_device(tokens, segment_ids, cotangent, params, moment_one, moment_two):
    gathered = lax.all_gather(params.astype(jnp.bfloat16), "shard", axis=0, tiled=True)
    total_len = gathered.shape[0]
    pieces = split_params(gathered)
    output, saved = layer_forward(tokens, segment_ids, pieces)
    grad_input, parts = layer_backward(cotangent, segment_ids, pieces, saved)
    local_grad = flatten_grads(parts, total_len)
    owned = lax.psum_scatter(local_grad, "shard", scatter_dimension=0, tiled=True).astype(
        jnp.float32
    )
    tokens_all = tokens.shape[0] * lax.axis_size("rep") * lax.axis_size("shard")
    factor = 1.0 / math.sqrt(tokens_all)
    width = moment_one.shape[0]
    begin = lax.axis_index("rep") * width
    param_share = lax.dynamic_slice_in_dim(params, begin, width)
    share = lax.psum_scatter(owned, "rep", scatter_dimension=0, tiled=True)
    grad_share = share * factor
    upd_params, upd_first, upd_second = adam_update(param_share, moment_one, moment_two, grad_share)
    grad_params, new_params = (
        lax.all_gather(grad_share, "rep", axis=0, tiled=True),
        lax.all_gather(upd_params, "rep", axis=0, tiled=True),
    )
    return (output, grad_input, grad_params, new_params, upd_first, upd_second)


LANES = 128
REPS = 8
SHARDS = 4
PIECE = 288
FLAT_ROWS = 13848
MOVED = PIECE * D // LANES


PARTS = (
    ((12, 1728, 96, 3, 0),),
    ((6, 576, 96, 1, 0), (4632, 1152, 48, 4, 96)),
    ((0, 1152, 48, 4, 0), (9240, 576, 96, 1, 192)),
    ((0, 1728, 288, 1, 0),),
)
VECTOR_ROWS = ((0, 1, 2306, 2307), (0, 769, 770, 771), (1536, 1537, 1538, 1539), (2304, 2305, 2306, 2307))


PLANE = ("y", "x", "core")
EVERY = PLANE + ("z",)
HOPS = (1, 2, 3, 0)


def plane_permute(value, flips):
    return lax.ppermute(value, PLANE, [(i, i ^ flips[i % 2]) for i in range(REPS)])


def first_cross(value):
    return plane_permute(value, (2, 4))


def second_cross(value):
    return plane_permute(value, (4, 2))


def core_cross(value):
    return plane_permute(value, (1, 1))


def ring_step(value):
    return lax.ppermute(value, "z", [(i, (i + 1) % SHARDS) for i in range(SHARDS)])


def flips_of(rep):
    core = rep % 2
    first = 2 + 2 * core
    return (0, first, 6 - first, 6)


def spread_ids(rep):
    other = rep ^ 1
    return [rep ^ flip for flip in flips_of(rep)] + [other ^ flip for flip in flips_of(other)]


def window_of(row):
    return min(6 * row // 8 * 8, FLAT_ROWS - 16)


def pack_kernel(where, flat_ref, out_ref, *rest):
    vec_ref = rest[0] if len(rest) == 4 else None
    held, windows, sems = rest[-3:]
    shard = where[0]
    turns = out_ref.shape[0]
    for z in range(SHARDS):

        @pl.when(shard == z)
        def _(z=z):
            def copies_of(turn):
                slot = turn % 2
                rep = where[1 + turn]
                copies = []
                at = 0
                for part, (first, step, _, _, _) in enumerate(PARTS[z]):
                    lead = first % 8
                    count = step + (8 if lead else 0)
                    begin = pl.multiple_of(first - lead + step * rep, 8)
                    copies.append(
                        pltpu.make_async_copy(
                            flat_ref.at[pl.ds(begin, count)],
                            held.at[slot, pl.ds(at, count)],
                            sems.at[slot, part],
                        )
                    )
                    at += count
                return copies

            for copy in copies_of(0):
                copy.start()
            if vec_ref is not None:
                cuts = []
                for slot, row in enumerate(VECTOR_ROWS[z]):
                    cuts.append(
                        pltpu.make_async_copy(
                            flat_ref.at[pl.ds(window_of(row), 16)],
                            windows.at[slot],
                            sems.at[2 + slot // 2, slot % 2],
                        )
                    )
                    cuts[-1].start()
                vec_ref[...] = jnp.zeros_like(vec_ref)
                for slot, row in enumerate(VECTOR_ROWS[z]):
                    cuts[slot].wait()
                    lead = 6 * row - window_of(row)
                    for col in range(6):
                        got = windows[slot, lead + col : lead + col + 1, :]
                        vec_ref[slot : slot + 1, LANES * col : LANES * (col + 1)] = got.astype(
                            jnp.bfloat16
                        ).astype(jnp.float32)

            @pl.loop(0, turns)
            def _(turn):
                @pl.when(turn + 1 < turns)
                def _():
                    for copy in copies_of(turn + 1):
                        copy.start()

                slot = turn % 2
                at = 0
                for copy, (first, step, rows, blocks, place) in zip(copies_of(turn), PARTS[z]):
                    copy.wait()
                    lead = first % 8
                    for block in range(blocks):
                        for col in range(6):
                            begin = at + lead + 6 * block + col
                            got = held[slot, pl.ds(begin, rows, stride=6 * blocks), :]
                            out_ref[
                                turn,
                                place + rows * block : place + rows * (block + 1),
                                LANES * col : LANES * (col + 1),
                            ] = got.astype(jnp.bfloat16)
                    at += step + (8 if lead else 0)


def pack_pieces(params, shard, reps, vectors):
    pieces = jax.ShapeDtypeStruct((len(reps), PIECE, D), jnp.bfloat16)
    rows = jax.ShapeDtypeStruct((8, D), jnp.float32)
    vmem = pl.BlockSpec(memory_space=pltpu.VMEM)
    return pl.pallas_call(
        pack_kernel,
        grid_spec=pltpu.PrefetchScalarGridSpec(
            num_scalar_prefetch=1,
            in_specs=[pl.BlockSpec(memory_space=pltpu.HBM)],
            out_specs=[vmem, vmem] if vectors else [vmem],
            scratch_shapes=[
                pltpu.VMEM((2, MOVED + 16, LANES), jnp.float32),
                pltpu.VMEM((4, 16, LANES), jnp.float32),
                pltpu.SemaphoreType.DMA((4, 2)),
            ],
        ),
        out_shape=[pieces, rows] if vectors else [pieces],
        cost_estimate=pl.CostEstimate(
            flops=0, bytes_accessed=len(reps) * 3 * 2**20, transcendentals=0
        ),
        compiler_params=pltpu.CompilerParams(vmem_limit_bytes=56 * 2**20),
    )(jnp.stack([shard] + reps), params.reshape(FLAT_ROWS, LANES))


def prepare_kernel(tokens, cotangent, ids, freqs, normed, spread, grad_y, tables):
    x_wide = tokens[...].astype(jnp.float32)
    centered = x_wide - jnp.mean(x_wide, axis=1, keepdims=True)
    variance = jnp.mean(centered * centered, axis=1, keepdims=True)
    inv_std = lax.rsqrt(variance + EPS_NORM)
    normed[...] = centered * inv_std
    spread[...] = jnp.broadcast_to(inv_std, spread.shape)
    square = (TOK_DEV, TOK_DEV)
    across = jnp.broadcast_to(ids[...].astype(jnp.float32), square)
    down = across.T
    lane = lax.broadcasted_iota(jnp.int32, square, 1)
    row = lax.broadcasted_iota(jnp.int32, square, 0)
    begins = (across != pltpu.roll(across, 1, 1)) | (lane == 0)
    before = jnp.where(begins & (lane <= row), lane.astype(jnp.float32), 0.0)
    position = row.astype(jnp.float32) - jnp.max(before, axis=1, keepdims=True)
    angle = position * freqs[...]
    cosine, sine = jnp.cos(angle), jnp.sin(angle)
    within = lane % HD
    tables[0] = jnp.where(within < ROT, cosine, 1.0)
    tables[1] = jnp.where(within < ROT // 2, -sine, 0.0)
    tables[2] = jnp.where((within >= ROT // 2) & (within < ROT), sine, 0.0)
    tables[3] = jnp.where((across == down) & (lane <= row), 1.0, 0.0)
    cot = cotangent[...].astype(jnp.float32)
    grad_y[...] = jnp.where(down[:, 0:1] >= 0, cot, 0.0).astype(jnp.bfloat16)


def prepare(tokens, cotangent, segment_ids):
    steps = jnp.arange(LANES, dtype=jnp.int32) % (ROT // 2)
    freqs = jnp.power(jnp.float32(ROPE_BASE), -2.0 * steps.astype(jnp.float32) / ROT)
    return pl.pallas_call(
        prepare_kernel,
        out_shape=[
            jax.ShapeDtypeStruct((TOK_DEV, D), jnp.float32),
            jax.ShapeDtypeStruct((TOK_DEV, LANES), jnp.float32),
            jax.ShapeDtypeStruct((TOK_DEV, D), jnp.bfloat16),
            jax.ShapeDtypeStruct((4, TOK_DEV, TOK_DEV), jnp.float32),
        ],
        compiler_params=pltpu.CompilerParams(vmem_limit_bytes=16 * 2**20),
    )(tokens, cotangent, segment_ids.reshape(1, TOK_DEV), freqs.reshape(1, LANES))


PIECES = SHARDS * REPS
GROUPS = 12
ALL_ROWS = PIECES * PIECE


def fetch_pieces(ids, blocks, own, shard, held, sems):
    views = []
    for block in blocks:
        views += [block.at[p] for p in range(4)] if len(block.shape) == 3 else [block]
    ids = ids + [shard * REPS + r for r in range(REPS)]
    views += [own.at[pl.ds(r * PIECE, PIECE)] for r in range(REPS)]
    for early in (True, False):
        for which, view in zip(ids, views):

            @pl.when((which < 2 * REPS) == early)
            def _(which=which, view=view):
                row = pl.multiple_of(which * PIECE, 16)
                pltpu.make_async_copy(view, held.at[pl.ds(row, PIECE)], sems.at[which]).start()

    def arrive(owner):
        for r in range(REPS):
            at = owner * REPS + r
            pltpu.make_async_copy(
                own.at[pl.ds(0, PIECE)], held.at[pl.ds(at * PIECE, PIECE)], sems.at[at]
            ).wait()

    return arrive


def rows_of(held, shard, begin, rows):
    return jnp.concatenate(
        [held[pl.ds((shard * REPS + r) * PIECE + begin, rows), :] for r in range(REPS)], axis=0
    )


def w_qkv_of(held, j):
    return rows_of(held, 0, 96 * j, 96)


def w_out_of(held):
    return rows_of(held, 1, 0, 96)


def w_in_of(held, j):
    return jnp.concatenate([rows_of(held, 1, 96 + 48 * j, 48), rows_of(held, 2, 48 * j, 48)], axis=0)


def w_out2_of(held, j):
    if j == 0:
        return rows_of(held, 2, 192, 96)
    return held[pl.ds(3 * REPS * PIECE + D * (j - 1), D), :]


def dot32(a, b):
    return jnp.dot(a, b, preferred_element_type=jnp.float32)


def layer_kernel(where, *refs):
    count = PIECES - REPS
    blocks, own = refs[:GROUPS], refs[GROUPS]
    normed, grad_y, tables = refs[GROUPS + 1 : GROUPS + 4]
    hops = refs[GROUPS + 4 : GROUPS + 8]
    outs = refs[GROUPS + 8 : GROUPS + 24]
    (attn_out, mixed_out, low_sums, vecs, hidden_out, pre_out, high_sums) = refs[
        GROUPS + 24 : GROUPS + 31
    ]
    held, grads, query, key, value, grad_attn, sems, out_sems = refs[GROUPS + 31 :]
    rot_cos, rot_up, rot_down, bias = (tables.at[turn] for turn in range(4))
    shard = where[0]
    arrive = fetch_pieces([where[1 + t] for t in range(count)], blocks, own, shard, held, sems)
    low_sums[...] = jnp.zeros_like(low_sums)
    high_sums[...] = jnp.zeros_like(high_sums)
    for owner in range(SHARDS):
        rows = jnp.zeros((4, D), jnp.float32)
        for hop in range(SHARDS):
            met = (shard + SHARDS - owner) % SHARDS == hop
            rows = jnp.where(met, hops[hop][0:4, :], rows)
        vecs[4 * owner : 4 * owner + 4, :] = rows

    arrive(0)
    act1 = (normed[...] * vecs[0:1, :] + vecs[1:2, :]).astype(jnp.bfloat16)
    for j, out in enumerate((query, key, value)):
        got = dot32(act1, w_qkv_of(held, j)) + vecs[2 + j : 3 + j, :]
        if j < 2:
            for p in range(6):
                lanes = slice(LANES * p, LANES * (p + 1))
                part = got[:, lanes]
                part = (
                    part * rot_cos[...]
                    + pltpu.roll(part, LANES - 8, 1) * rot_up[...]
                    + pltpu.roll(part, 8, 1) * rot_down[...]
                )
                out[:, lanes] = part.astype(jnp.bfloat16)
        else:
            out[...] = got.astype(jnp.bfloat16)
    gy_t = grad_y[...].T
    arrive(1)
    grad_attn[...] = dot32(w_out_of(held), gy_t).T.astype(jnp.bfloat16)

    arrive(2)
    arrive(3)
    low = lax.broadcasted_iota(jnp.int32, (LANES, LANES), 1) < HD
    scale = HD ** (-0.5)
    for p in range(6):
        lanes = slice(LANES * p, LANES * (p + 1))
        q2, k2, v2, g2 = (ref[:, lanes] for ref in (query, key, value, grad_attn))
        k2_t, v2_t = k2.T, v2.T
        attn_parts, value_parts, query_parts, key_parts = [], [], [], []
        for half in range(2):
            here = low if half == 0 else ~low
            zero = jnp.zeros_like(q2)
            scores = dot32(jnp.where(here, q2, zero), k2_t) * scale
            scores = jnp.where(bias[...] > 0.5, scores, NEG_BIG)
            expd = jnp.exp(scores - jnp.max(scores, axis=1, keepdims=True))
            chances = expd / jnp.sum(expd, axis=1, keepdims=True)
            chances16 = chances.astype(jnp.bfloat16)
            attn = dot32(chances16, v2)
            attn16 = attn.astype(jnp.bfloat16)
            masked = jnp.where(here, g2, zero)
            delta = jnp.sum(
                masked.astype(jnp.float32) * attn16.astype(jnp.float32), axis=1, keepdims=True
            )
            grad_chance = dot32(masked, v2_t)
            slope = (chances * (grad_chance - delta) * scale).astype(jnp.bfloat16)
            attn_parts.append(attn16)
            value_parts.append(dot32(chances16.T, g2))
            query_parts.append(dot32(slope, k2))
            key_parts.append(dot32(slope.T, q2))
        attn_out[:, lanes] = jnp.where(low, *attn_parts)
        for j, parts in enumerate((query_parts, key_parts, value_parts)):
            part = jnp.where(low, *parts)
            if j < 2:
                part = (
                    part * rot_cos[...]
                    - pltpu.roll(part, LANES - 8, 1) * rot_up[...]
                    - pltpu.roll(part, 8, 1) * rot_down[...]
                )
            wide = slice(D * j + LANES * p, D * j + LANES * (p + 1))
            low_sums[j : j + 1, lanes] = jnp.sum(part, axis=0, keepdims=True)
            mixed_out[:, wide] = part.astype(jnp.bfloat16)


    def send_off(owner):
        for hop in range(SHARDS):

            @pl.when((shard + SHARDS - HOPS[hop]) % SHARDS == owner)
            def _(hop=hop):
                for turn in (2 * hop, 2 * hop + 1, 8 + 2 * hop, 9 + 2 * hop):
                    pltpu.make_async_copy(
                        grads.at[pl.ds(turn * 2 * PIECE, 2 * PIECE)],
                        outs[turn],
                        out_sems.at[turn],
                    ).start()

    slot_row = lambda z, r: pl.multiple_of(where[1 + count + z * REPS + r] * PIECE, 16)

    def keep_rows(z, begin, rows, part):
        for r in range(part.shape[0] // rows):
            grads[pl.ds(slot_row(z, r) + begin, rows), :] = part[rows * r : rows * (r + 1), :]

    gy = grad_y[...]
    act1_t = (normed[...] * vecs[0:1, :] + vecs[1:2, :]).astype(jnp.bfloat16).T
    for j in range(3):
        keep_rows(
            0, 96 * j, 96, dot32(act1_t, mixed_out[:, D * j : D * (j + 1)]).astype(jnp.bfloat16)
        )
    send_off(0)
    keep_rows(1, 0, 96, dot32(attn_out[...].T, gy).astype(jnp.bfloat16))

    act2 = (normed[...] * vecs[6:7, :] + vecs[7:8, :]).astype(jnp.bfloat16)
    act2_t = act2.T
    for j in range(4):
        wide = slice(D * j, D * (j + 1))
        pre = dot32(act2, w_in_of(held, j)) + vecs[8 + j : 9 + j, :]
        bell = 0.5 * (1.0 + lax.erf(pre * INV_ROOT_TWO))
        hidden = (pre * bell).astype(jnp.bfloat16)
        hidden_out[:, wide] = hidden
        grad_hidden = dot32(w_out2_of(held, j), gy_t).T
        grad_pre = grad_hidden * (bell + pre * jnp.exp(-0.5 * pre * pre) * INV_ROOT_TWO_PI)
        high_sums[j : j + 1, :] = jnp.sum(grad_pre, axis=0, keepdims=True)
        grad_pre16 = grad_pre.astype(jnp.bfloat16)
        pre_out[:, wide] = grad_pre16
        w2 = dot32(hidden.T, gy).astype(jnp.bfloat16)
        if j == 0:
            keep_rows(2, 192, 96, w2)
        else:
            at = D * (j - 1)
            while at < D * j:
                r, begin = divmod(at, PIECE)
                rows = min(PIECE - begin, D * j - at)
                grads[pl.ds(slot_row(3, r) + begin, rows), :] = w2[
                    at - D * (j - 1) : at - D * (j - 1) + rows, :
                ]
                at += rows
    send_off(3)
    for half, owner in enumerate((1, 2)):
        side = act2_t[D // 2 * half : D // 2 * (half + 1), :]
        for j in range(4):
            w1 = dot32(side, pre_out[:, D * j : D * (j + 1)]).astype(jnp.bfloat16)
            keep_rows(owner, (96 if owner == 1 else 0) + 48 * j, 48, w1)
        send_off(owner)
    for turn, out in enumerate(outs):
        pltpu.make_async_copy(
            grads.at[pl.ds(turn * 2 * PIECE, 2 * PIECE)], out, out_sems.at[turn]
        ).wait()


def layer_gradients(scalars, blocks, own, small):
    anywhere = pl.BlockSpec(memory_space=pl.ANY)
    vmem = pl.BlockSpec(memory_space=pltpu.VMEM)
    bf16 = jnp.bfloat16
    rows = jax.ShapeDtypeStruct((8, D), jnp.float32)
    return pl.pallas_call(
        layer_kernel,
        grid_spec=pltpu.PrefetchScalarGridSpec(
            num_scalar_prefetch=1,
            in_specs=[anywhere] * (len(blocks) + 1) + [vmem] * len(small),
            out_specs=[pl.BlockSpec(memory_space=pltpu.HBM)] * 16 + [vmem] * 7,
            scratch_shapes=[
                pltpu.VMEM((ALL_ROWS, D), bf16),
                pltpu.VMEM((ALL_ROWS, D), bf16),
                pltpu.VMEM((TOK_DEV, D), bf16),
                pltpu.VMEM((TOK_DEV, D), bf16),
                pltpu.VMEM((TOK_DEV, D), bf16),
                pltpu.VMEM((TOK_DEV, D), bf16),
                pltpu.SemaphoreType.DMA((PIECES,)),
                pltpu.SemaphoreType.DMA((16,)),
            ],
        ),
        out_shape=[jax.ShapeDtypeStruct((2 * PIECE, D), bf16)] * 16
        + [
            jax.ShapeDtypeStruct((TOK_DEV, D), bf16),
            jax.ShapeDtypeStruct((TOK_DEV, 3 * D), bf16),
            rows,
            jax.ShapeDtypeStruct((16, D), jnp.float32),
            jax.ShapeDtypeStruct((TOK_DEV, FF), bf16),
            jax.ShapeDtypeStruct((TOK_DEV, FF), bf16),
            rows,
        ],
        compiler_params=pltpu.CompilerParams(vmem_limit_bytes=60 * 2**20),
        cost_estimate=pl.CostEstimate(
            flops=2 * 10**10, bytes_accessed=80 * 2**20, transcendentals=10**6
        ),
    )(scalars, *blocks, own, *small)


def result_kernel(where, *refs):
    count = PIECES - REPS
    blocks, own = refs[:GROUPS], refs[GROUPS]
    (tokens, normed, spread, grad_y, attn, grad_mixed, low_sums, vecs, hidden, grad_pre, high_sums) = (
        refs[GROUPS + 1 : GROUPS + 12]
    )
    output, grad_input, vec_out, held, sems = refs[GROUPS + 12 :]
    ids = [where[1 + t] for t in range(count)]
    arrive = fetch_pieces(ids, blocks, own, where[0], held, sems)
    for owner in range(SHARDS):
        arrive(owner)
    total = dot32(attn[...], w_out_of(held)) + vecs[5:6, :]
    for j in range(4):
        total = total + dot32(hidden[:, D * j : D * (j + 1)], w_out2_of(held, j))
    output[...] = tokens[...].astype(jnp.float32) + (total + vecs[12:13, :])
    vec_out[2:5, :] = low_sums[0:3, :]
    vec_out[8:12, :] = high_sums[0:4, :]
    gy = grad_y[...].astype(jnp.float32)
    total = gy
    for norm, (parts, width, weights) in enumerate(
        ((grad_mixed, 3, w_qkv_of), (grad_pre, 4, w_in_of))
    ):
        back = None
        for j in range(width):
            part = dot32(weights(held, j), parts[:, D * j : D * (j + 1)].T)
            back = part if back is None else back + part
        grad_act = back.T
        gain_row = 0 if norm == 0 else 6
        unit = normed[...]
        vec_out[gain_row : gain_row + 1, :] = jnp.sum(grad_act * unit, axis=0, keepdims=True)
        vec_out[gain_row + 1 : gain_row + 2, :] = jnp.sum(grad_act, axis=0, keepdims=True)
        grad_norm = grad_act * vecs[gain_row : gain_row + 1, :]
        total = total + spread[:, 0:1] * (
            grad_norm
            - jnp.mean(grad_norm, axis=1, keepdims=True)
            - unit * jnp.mean(grad_norm * unit, axis=1, keepdims=True)
        )
    grad_input[...] = total
    bottom = jnp.sum(gy, axis=0, keepdims=True)
    vec_out[5:6, :] = bottom
    vec_out[12:13, :] = bottom
    vec_out[13:16, :] = jnp.zeros((3, D), jnp.float32)
    vec_out[...] = vec_out[...].astype(jnp.bfloat16).astype(jnp.float32)


def layer_results(scalars, blocks, own, small):
    anywhere = pl.BlockSpec(memory_space=pl.ANY)
    vmem = pl.BlockSpec(memory_space=pltpu.VMEM)
    rows = jax.ShapeDtypeStruct((TOK_DEV, D), jnp.float32)
    return pl.pallas_call(
        result_kernel,
        grid_spec=pltpu.PrefetchScalarGridSpec(
            num_scalar_prefetch=1,
            in_specs=[anywhere] * (len(blocks) + 1) + [vmem] * len(small),
            out_specs=[vmem] * 3,
            scratch_shapes=[
                pltpu.VMEM((ALL_ROWS, D), jnp.bfloat16),
                pltpu.SemaphoreType.DMA((PIECES,)),
            ],
        ),
        out_shape=[rows, rows, jax.ShapeDtypeStruct((16, D), jnp.float32)],
        compiler_params=pltpu.CompilerParams(vmem_limit_bytes=60 * 2**20),
        cost_estimate=pl.CostEstimate(
            flops=4 * 10**9, bytes_accessed=30 * 2**20, transcendentals=0
        ),
    )(scalars, *blocks, own, *small)


SHARE = FLAT_ROWS // REPS
BEGINS = tuple(SHARE * r // 16 * 16 for r in range(REPS)) + (FLAT_ROWS,)
SHARE_ROWS = 1760
STEP = 576


def align_kernel(where, one_ref, two_ref, out_ref, held):
    for r in range(REPS):

        @pl.when(where[0] == r)
        def _(r=r):
            lead = SHARE * r - BEGINS[r]
            for turn, ref in enumerate((one_ref, two_ref)):
                held[0:16, :] = jnp.zeros((16, LANES), jnp.float32)
                held[SHARE_ROWS - 32 :, :] = jnp.zeros((32, LANES), jnp.float32)
                held[lead : lead + SHARE, :] = ref[...]
                out_ref[turn] = held[...].astype(jnp.bfloat16)


def align_moments(moment_one, moment_two, rep):
    return pl.pallas_call(
        align_kernel,
        grid_spec=pltpu.PrefetchScalarGridSpec(
            num_scalar_prefetch=1,
            in_specs=[pl.BlockSpec(memory_space=pltpu.VMEM)] * 2,
            out_specs=pl.BlockSpec(memory_space=pltpu.VMEM),
            scratch_shapes=[pltpu.VMEM((SHARE_ROWS, LANES), jnp.float32)],
        ),
        out_shape=jax.ShapeDtypeStruct((2, SHARE_ROWS, LANES), jnp.bfloat16),
        compiler_params=pltpu.CompilerParams(vmem_limit_bytes=16 * 2**20),
        cost_estimate=pl.CostEstimate(flops=0, bytes_accessed=6 * 2**20, transcendentals=0),
    )(jnp.stack([rep]), moment_one.reshape(SHARE, LANES), moment_two.reshape(SHARE, LANES))


def update_kernel(factor, where, *refs):
    blocks = refs[:REPS]
    moments = refs[REPS : 2 * REPS]
    vec_ref, params, grad_out, params_out = refs[2 * REPS : 2 * REPS + 4]
    held, grad, weight, moment, sems, out_sems = refs[2 * REPS + 4 :]
    copies = []
    for turn in range(REPS):
        copies.append(
            pltpu.make_async_copy(blocks[turn], held.at[where[1 + turn]], sems.at[turn])
        )
    fetched = []
    for r in range(REPS):
        rows = pl.ds(BEGINS[r], BEGINS[r + 1] - BEGINS[r])
        fetched.append(
            pltpu.make_async_copy(params.at[rows], weight.at[rows], sems.at[REPS + r])
        )
    for turn in range(REPS):
        which = where[1 + turn]
        copies.append(
            pltpu.make_async_copy(
                moments[turn], moment.at[which], sems.at[2 * REPS + which]
            )
        )
    for copy in copies + fetched:
        copy.start()
    for copy in copies[:REPS]:
        copy.wait()
    shard = where[0]
    for z in range(SHARDS):

        @pl.when(shard == z)
        def _(z=z):
            for slot, row in enumerate(VECTOR_ROWS[z]):
                for col in range(6):
                    grad[6 * row + col : 6 * row + col + 1, :] = (
                        vec_ref[slot : slot + 1, LANES * col : LANES * (col + 1)] * factor
                    )

            @pl.loop(0, REPS)
            def _(rep):
                for first, step, rows, blocks, place in PARTS[z]:
                    for block in range(blocks):
                        for col in range(6):
                            got = held[
                                rep,
                                place + rows * block : place + rows * (block + 1),
                                LANES * col : LANES * (col + 1),
                            ]
                            begin = first + step * rep + 6 * block + col
                            grad[pl.ds(begin, rows, stride=6 * blocks), :] = (
                                got.astype(jnp.float32) * factor
                            )

    saving = []
    for r in range(REPS):
        rows = pl.ds(BEGINS[r], BEGINS[r + 1] - BEGINS[r])
        saving.append(
            pltpu.make_async_copy(grad.at[rows], grad_out.at[rows], out_sems.at[REPS + r])
        )
        saving[-1].start()
    for r in range(REPS):
        base = BEGINS[r]
        length = BEGINS[r + 1] - base
        pltpu.make_async_copy(moments[0], moment.at[r], sems.at[2 * REPS + r]).wait()
        fetched[r].wait()
        if r > 0:
            tail = base - BEGINS[r - 1]
            moment[r, :, 0:16, :] = moment[r, :, 0:16, :] + moment[r - 1, :, tail : tail + 16, :]

        def renew(at, rows, r=r, base=base):
            here = pl.ds(pl.multiple_of(base + at, 8), rows)
            there = pl.ds(pl.multiple_of(at, 16), rows)
            updated, _, _ = adam_update(
                weight[here, :],
                moment[r, 0, there, :].astype(jnp.float32),
                moment[r, 1, there, :].astype(jnp.float32),
                grad[here, :],
            )
            weight[here, :] = updated

        @pl.loop(0, length // STEP)
        def _(turn):
            renew(turn * STEP, STEP)

        if length % STEP:
            renew(length // STEP * STEP, length % STEP)
        rows = pl.ds(base, length)
        saving.append(
            pltpu.make_async_copy(weight.at[rows], params_out.at[rows], out_sems.at[r])
        )
        saving[-1].start()
    for copy in saving:
        copy.wait()


def update_shard(blocks, ids, vectors, params, moments, shard, factor):
    anywhere = pl.BlockSpec(memory_space=pl.ANY)
    flat = jax.ShapeDtypeStruct((FLAT_ROWS, LANES), jnp.float32)
    return pl.pallas_call(
        functools.partial(update_kernel, factor),
        grid_spec=pltpu.PrefetchScalarGridSpec(
            num_scalar_prefetch=1,
            in_specs=[anywhere] * (2 * REPS)
            + [pl.BlockSpec(memory_space=pltpu.VMEM), anywhere],
            out_specs=[anywhere] * 2,
            scratch_shapes=[
                pltpu.VMEM((REPS, PIECE, D), jnp.bfloat16),
                pltpu.VMEM((FLAT_ROWS, LANES), jnp.float32),
                pltpu.VMEM((FLAT_ROWS, LANES), jnp.float32),
                pltpu.VMEM((REPS, 2, SHARE_ROWS, LANES), jnp.bfloat16),
                pltpu.SemaphoreType.DMA((3 * REPS,)),
                pltpu.SemaphoreType.DMA((2 * REPS,)),
            ],
        ),
        out_shape=[flat, flat],
        compiler_params=pltpu.CompilerParams(vmem_limit_bytes=60 * 2**20),
    )(jnp.stack([shard] + ids), *blocks, *moments, vectors, params.reshape(FLAT_ROWS, LANES))


def ring_shift(value, hop):
    return lax.ppermute(value, "z", [(i, (i + hop) % SHARDS) for i in range(SHARDS)])


fence = lax.optimization_barrier


def gather_matrices(params, shard, rep, early):
    piece = pack_pieces(params, shard, [rep], False)[0][0]
    own, vec = pack_pieces(params, shard, [rep * 0 + turn for turn in range(REPS)], True)
    one = ring_step(piece)
    one, own, vec = fence((one, own, vec))
    two, first_one, second_one = ring_step(one), first_cross(one), second_cross(one)
    vec_one = ring_step(vec)
    two, first_one, second_one, vec_one, early = fence(
        (two, first_one, second_one, vec_one, early)
    )
    three, first_two, second_two = ring_step(two), first_cross(two), second_cross(two)
    both_one = second_cross(first_one)
    vec_two = ring_step(vec_one)
    three, first_two, second_two, both_one, vec_two = fence(
        (three, first_two, second_two, both_one, vec_two)
    )
    first_three, second_three = first_cross(three), second_cross(three)
    both_two = second_cross(first_two)
    mine_one = jnp.stack([one, first_one, second_one, both_one])
    other_one = core_cross(mine_one)
    vec_three = ring_step(vec_two)
    first_three, second_three, both_two, other_one, vec_three, moments = fence(
        (first_three, second_three, both_two, other_one, vec_three, early[1])
    )
    first_moments = first_cross(moments)
    both_three = second_cross(first_three)
    mine_two = jnp.stack([two, first_two, second_two, both_two])
    other_two = core_cross(mine_two)
    others = [core_cross(value) for value in (three, first_three, second_three)]
    others, both_three, other_two, first_moments = fence(
        (others, both_three, other_two, first_moments)
    )
    others.append(core_cross(both_three))
    threes = [three, first_three, second_three, both_three]
    blocks = [mine_one, other_one, mine_two, other_two] + threes + others
    ids = []
    for hop in range(1, SHARDS):
        owner = (shard + SHARDS - hop) % SHARDS
        ids += [owner * REPS + which for which in spread_ids(rep)]
    hops = [vec, vec_one, vec_two, vec_three]
    return blocks, own.reshape(REPS * PIECE, D), ids, hops, early[0], [moments, first_moments]


def slots_by_piece(shard, rep):
    slots = []
    for owner in range(SHARDS):
        hop = (shard + SHARDS - owner + 3) % SHARDS
        for which in range(REPS):
            apart = rep ^ which
            kept = 1 - apart % 2
            core = which % 2
            across = apart & 6
            first = 2 + 2 * core
            place = jnp.where(
                across == 0, 2, jnp.where(across == 6, 1, jnp.where(across == first, 0, 3))
            )
            slots.append((kept * SHARDS + hop) * 4 + place)
    return slots


def scatter_sums(parts, moments, small, results):
    sent_far, sent_near, kept_far, kept_near = (
        [parts[8 * half + 2 * turn + near] for turn in range(SHARDS)]
        for half in range(2)
        for near in range(2)
    )
    cores = [core_cross(sent_far[0]), core_cross(sent_near[0]), core_cross(sent_far[1])]
    cores = list(fence(cores))
    far = [kept_far[0] + cores[0], kept_far[1] + cores[2]]
    crossed = first_cross(far[0])
    others = [core_cross(v) for v in (sent_near[1], sent_far[2], sent_near[2], sent_far[3])]
    crossed, others, small = fence((crossed, others, small))
    near = [kept_near[0] + cores[1], kept_near[1] + others[0], kept_near[2] + others[2]]
    far += [kept_far[2] + others[1], kept_far[3] + others[3]]

    pair = near[0] + crossed
    final = second_cross(pair[1])
    kept = pair[0]
    crossed = first_cross(far[1])
    last_near = core_cross(sent_near[3])
    output, grad_input, vectors = results(small)
    final, crossed, last_near, vectors = fence((final, crossed, last_near, vectors))
    near.append(kept_near[3] + last_near)

    carried = None
    for turn in range(1, SHARDS):
        total = kept + final
        if carried is not None:
            total = total + carried
        carried = ring_step(total)
        pair = near[turn] + crossed
        kept = pair[0]
        final = second_cross(pair[1])
        met = plane_permute(vectors, ((1, 1), (2, 2), (4, 4))[turn - 1])
        if turn < SHARDS - 1:
            crossed = first_cross(far[turn + 1])
            final, crossed, carried, met, moments = fence(
                (final, crossed, carried, met, moments)
            )
        else:
            final, carried, met = fence((final, carried, met))
        if turn > 1:
            moments.append(core_cross(moments[turn]))
        vectors = vectors + met
    total = kept + final + carried

    first, second = first_cross(total), second_cross(total)
    shifted = [ring_shift(vectors, hop) for hop in range(1, SHARDS)]
    first, second, shifted = fence((first, second, shifted))
    vectors = vectors + shifted[0] + shifted[1] + shifted[2]
    both = second_cross(first)
    mine = [total, first, second]
    spread = [core_cross(value) for value in mine]
    both, spread = fence((both, spread))
    spread.append(core_cross(both))
    return mine + [both] + spread, moments, output, grad_input, vectors


def on_device_rows(tokens, segment_ids, cotangent, params, moment_one, moment_two):
    shard = lax.axis_index("z")
    rep = lax.axis_index(PLANE)
    early = (prepare(tokens, cotangent, segment_ids), align_moments(moment_one, moment_two, rep))
    blocks, own, ids, hops, early, moments = gather_matrices(params, shard, rep, early)
    normed, inv_std, grad_y, tables = early
    moments, blocks = fence((moments, blocks))
    moments += [second_cross(value) for value in moments]
    moments += [core_cross(value) for value in moments[:2]]
    scalars = jnp.stack([shard] + ids + slots_by_piece(shard, rep))
    made = layer_gradients(scalars, blocks, own, (normed, grad_y, tables, *hops))
    made, moments = fence((made, moments))
    small = (tokens, normed, inv_std, grad_y) + tuple(made[16:])
    spread, moments, output, grad_input, vec_grads = scatter_sums(
        [part.reshape(2, PIECE, D) for part in made[:16]], moments, small, lambda small: layer_results(scalars, blocks, own, small)
    )
    own_vectors = lax.dynamic_index_in_dim(
        vec_grads.reshape(SHARDS, 4, D), shard, 0, keepdims=False
    )
    tokens_all = tokens.shape[0] * lax.axis_size(EVERY)
    grad_params, new_params = update_shard(
        spread,
        spread_ids(rep),
        own_vectors,
        params,
        moments,
        shard,
        1.0 / math.sqrt(tokens_all),
    )
    grad_params = grad_params.reshape(-1)
    width = moment_one.shape[0]
    grad_share = lax.dynamic_slice_in_dim(grad_params, rep * width, width)
    _, upd_first, upd_second = adam_update(moment_one, moment_one, moment_two, grad_share)
    return (output, grad_input, grad_params, new_params.reshape(-1), upd_first, upd_second)


def solution(mesh):
    in_rows = mesh.shape["rep"] == REPS and mesh.shape["shard"] == SHARDS
    if in_rows:
        rep, shard = PLANE, "z"
        mesh = Mesh(mesh.devices.reshape(2, 2, 2, SHARDS), EVERY)
        body = on_device_rows
    else:
        rep, shard = ("rep",), "shard"
        body = on_device
    rows = rep + (shard,)
    owner = (shard,) + rep
    in_specs = (P(rows, None), P(rows), P(rows, None), P(shard), P(owner), P(owner))
    out_specs = (P(rows, None), P(rows, None), P(shard), P(shard), P(owner), P(owner))
    return jax.shard_map(body, mesh=mesh, in_specs=in_specs, out_specs=out_specs, check_vma=False)
```
